32 devices in a mesh: slab: 8 (over z, y), grp: 4 (over x, core).
Axes of the slice: x: 2, y: 2, z: 4, core: 2. Of those that a mesh axis runs over, the one named last changes fastest.
Arguments:
- u_now: float32 [3, 128, 32, 128], P(None, 'slab', 'grp'), may hold values from -6 to 6
- u_prev: float32 [3, 128, 32, 128], P(None, 'slab', 'grp'), may hold values from -6 to 6
- force: float32 [3, 128, 32, 128], P(None, 'slab', 'grp'), may hold values from -6 to 6
- stiffness: float32 [128, 32, 128], P('slab', 'grp'), may hold values from 0.5 to 2
- broken: int32 [32, 8, 32], P('slab', 'grp'), may hold values 0 or 1
- flags: int32 [32, 8, 32], P('slab', 'grp'), may hold values 0 or 1
Outputs:
- displacement: float32 [3, 128, 32, 128], P(None, 'slab', 'grp')
- coeffs: float32 [6, 32, 128, 128], P(None, 'grp', 'slab')
The draws below stay inside these ranges and needn't reach their ends.
All inputs are finite; a program needn't handle non-finite values. No bound on the sum of `broken` or of `flags` on one device may be relied on, other than what follows from the above.
Results may differ from the reference program's by a relative error of at most 0.0001.
Values sent between devices are 32-bit elements; how exact they have to be, the bound alone decides.
A program may use at most 64 MiB of HBM per device.

```python
import math
import jax
import jax.numpy as jnp
import numpy as np
from jax import lax

NZ = 128
STEPS = 2
ITERS = 2
LEVELS = 3
NX = 128
NY = 32


def place_ends(values, stream_key, low, largest):
    longest = values.shape.index(max(values.shape))
    spots = []
    for shift in (0, 1):
        where = [jax.random.randint(jax.random.fold_in(stream_key, axis), (), 0, length) for axis, length in enumerate(values.shape)]
        where[longest] = (where[longest] + shift) % values.shape[longest]
        spots.append(tuple(where))
    return values.at[spots[0]].set(low).at[spots[1]].set(largest)


def level_of(stream_key, extent, split, least, largest):
    gain, own = 1.0, jax.random.fold_in(stream_key, 6)
    for axis_at, parts in split:
        steps = jnp.exp(jax.random.uniform(jax.random.fold_in(own, axis_at), (parts,), jnp.float32, least / len(split), largest / len(split)))
        gain = gain * jnp.repeat(steps, extent[axis_at] // parts).reshape([-1 if axis == axis_at else 1 for axis in range(len(extent))])
    return gain


def gaussian(rng, dims, deviation, reach, split=(), held_as=jnp.bfloat16):
    loudness = level_of(rng, dims, split, -0.22, 0.18) if split else 1.0
    entries = jax.random.normal(rng, dims, jnp.float32) * deviation * loudness
    return jnp.minimum(jnp.maximum(entries, -reach), reach).astype(held_as)


def setup_inputs(seed: int = 0) -> dict:
    key_of = jax.random.split(jax.random.key(seed), 7)
    u_now = gaussian(key_of[0], (3, NX, NY, NZ), 1.0, 6.0, ((1, 8), (2, 4)), jnp.float32)
    u_prev = gaussian(key_of[1], (3, NX, NY, NZ), 1.0, 6.0, ((1, 8), (2, 4)), jnp.float32)
    force = gaussian(key_of[2], (3, NX, NY, NZ), 1.0, 6.0, ((1, 8), (2, 4)), jnp.float32)
    stiffness = jnp.clip(jnp.exp(math.log(2.0) - 1.3862944 * jax.random.uniform(key_of[3], (NX, NY, NZ), jnp.float32) ** level_of(key_of[3], (NX, NY, NZ), ((0, 8), (1, 4)), -0.2, 0.2)), 0.5, 2.0)
    broken = place_ends((jax.random.randint(key_of[4], (NX // 4, NY // 4, NZ // 4), 0, 4) < 1).astype(jnp.int32), jax.random.fold_in(key_of[4], 1), 0, 1)
    flags = place_ends((jax.random.randint(key_of[5], (NX // 4, NY // 4, NZ // 4), 0, 3) < 2).astype(jnp.int32), jax.random.fold_in(key_of[5], 1), 0, 1)
    return {"u_now": u_now, "u_prev": u_prev, "force": force, "stiffness": stiffness, "broken": broken, "flags": flags}


SPRING_NORMAL = 1.0
SPRING_SHEAR = 0.4
MASS_TERM = 1.0
CRACK_CUT = 0.9

def cosine_table():
    freq = np.arange(4)[:, None]
    place = np.arange(4)[None, :]
    factor = np.where(freq == 0, 0.5, np.sqrt(0.5))
    return factor * np.cos(np.pi * (2 * place + 1) * freq / 8.0)

def spread(mask):
    values = mask.astype(jnp.float32)
    size_a, size_b, size_c = values.shape
    wide = jnp.broadcast_to(values[:, None, :, None, :, None], (size_a, 4, size_b, 4, size_c, 4))
    return wide.reshape(size_a * 4, size_b * 4, size_c * 4)

def sides(padded, axis_index):
    leading = padded.ndim - 3

    def cut(offset):
        index_list = [slice(None)] * leading + [slice(1, -1)] * 3
        length = padded.shape[leading + axis_index]
        index_list[leading + axis_index] = slice(1 + offset, length - 1 + offset)
        return padded[tuple(index_list)]
    return (cut(1), cut(-1))

def springs(field, weight, field_pad, weight_pad):
    result = MASS_TERM * field
    for axis_index in range(3):
        upper_v, lower_v = sides(field_pad, axis_index)
        upper_w, lower_w = sides(weight_pad, axis_index)
        k_upper = 0.5 * (weight + upper_w)
        k_lower = 0.5 * (weight + lower_w)
        change = k_upper * (field - upper_v) + k_lower * (field - lower_v)
        coupling = jnp.array([SPRING_NORMAL if comp == axis_index else SPRING_SHEAR for comp in range(3)], jnp.float32).reshape(3, 1, 1, 1)
        result = result + coupling * change
    return result

def stresses(field, carry, field_pad):
    rows_out = []
    for axis_index in range(3):
        upper_v, lower_v = sides(field_pad, axis_index)
        rows_out.append(SPRING_NORMAL * carry * 0.5 * (upper_v[axis_index] - lower_v[axis_index]))
    return jnp.stack(rows_out)

def lift(signal):
    even = signal[..., 0::2]
    odd = signal[..., 1::2]
    detail = odd - 0.5 * (even + jnp.roll(even, -1, axis=-1))
    approx = even + 0.25 * (jnp.roll(detail, 1, axis=-1) + detail)
    return (approx, detail)

def wavelet(signal):
    pieces = []
    approx = signal
    for level_index in range(LEVELS):
        approx, detail = lift(approx)
        pieces.insert(0, detail)
    return jnp.concatenate([approx] + pieces, axis=-1)

def block_transform(fields):
    table = jnp.asarray(cosine_table(), jnp.float32)
    chans, size_x, size_y, size_z = fields.shape
    grid = fields.reshape(chans, size_x // 4, 4, size_y // 4, 4, size_z // 4, 4)
    grid = jnp.einsum('ai,hpiqjrk->hpaqjrk', table, grid, precision=lax.Precision.HIGHEST)
    grid = jnp.einsum('bj,hpaqjrk->hpaqbrk', table, grid, precision=lax.Precision.HIGHEST)
    grid = jnp.einsum('ck,hpaqbrk->hpaqbrc', table, grid, precision=lax.Precision.HIGHEST)
    return grid.reshape(fields.shape)

def reference(u_now, u_prev, force, stiffness, broken, flags):
    weight = stiffness * (1.0 - CRACK_CUT * spread(broken))
    carry = spread(flags) * weight
    weight_pad = jnp.pad(weight, 1)

    def operate(field):
        field_pad = jnp.pad(field, ((0, 0), (1, 1), (1, 1), (1, 1)))
        return springs(field, weight, field_pad, weight_pad)
    for step_index in range(STEPS):
        rhs = MASS_TERM * (2.0 * u_now - u_prev) + force
        guess = u_now
        residual = rhs - operate(guess)
        direction = residual
        norm_now = jnp.sum(residual * residual)
        for turn_index in range(ITERS):
            image = operate(direction)
            alpha = norm_now / jnp.sum(direction * image)
            guess = guess + alpha * direction
            residual = residual - alpha * image
            if turn_index + 1 < ITERS:
                norm_next = jnp.sum(residual * residual)
                direction = residual + norm_next / norm_now * direction
                norm_now = norm_next
        u_prev = u_now
        u_now = guess
    field_pad = jnp.pad(u_now, ((0, 0), (1, 1), (1, 1), (1, 1)))
    fields = jnp.concatenate([u_now, stresses(u_now, carry, field_pad)], axis=0)
    blockc = block_transform(fields)
    coeffs = wavelet(jnp.transpose(blockc, (0, 2, 3, 1)))
    return (u_now, coeffs)
```

```python
import jax
import jax.numpy as jnp
import numpy as np
from jax import lax
from jax.experimental import pallas as pl
from jax.experimental.pallas import tpu as pltpu
from jax.sharding import PartitionSpec as P

STEPS = 2
ITERS = 2
LEVELS = 3


SPRING_NORMAL = 1.0
SPRING_SHEAR = 0.4
MASS_TERM = 1.0
CRACK_CUT = 0.9


def with_halo(block, sides, width):
    for axis, dim in sides:
        count = lax.axis_size(axis)
        forward = [(i, i + 1) for i in range(count - 1)]
        backward = [(target, source) for source, target in forward]
        low = lax.ppermute(
            lax.slice_in_dim(block, block.shape[dim] - width, None, axis=dim), axis, forward
        )
        high = lax.ppermute(lax.slice_in_dim(block, 0, width, axis=dim), axis, backward)
        block = jnp.concatenate([low, block, high], axis=dim)
    return block


def cosine_table():
    freq = np.arange(4)[:, None]
    place = np.arange(4)[None, :]
    factor = np.where(freq == 0, 0.5, np.sqrt(0.5))
    return factor * np.cos(np.pi * (2 * place + 1) * freq / 8.0)


def block_table(count):
    return jnp.asarray(np.kron(np.eye(count // 4), cosine_table()), jnp.float32)


def spread(mask):
    values = mask.astype(jnp.float32)
    size_a, size_b, size_c = values.shape
    wide = jnp.broadcast_to(values[:, None, :, None, :, None], (size_a, 4, size_b, 4, size_c, 4))
    return wide.reshape(size_a * 4, size_b * 4, size_c * 4)


def sides(padded, axis_index):
    leading = padded.ndim - 3

    def cut(offset):
        index_list = [slice(None)] * leading + [slice(1, -1)] * 3
        length = padded.shape[leading + axis_index]
        index_list[leading + axis_index] = slice(1 + offset, length - 1 + offset)
        return padded[tuple(index_list)]

    return (cut(1), cut(-1))


def springs(field, weight, field_pad, weight_pad):
    result = MASS_TERM * field
    for axis_index in range(3):
        upper_v, lower_v = sides(field_pad, axis_index)
        upper_w, lower_w = sides(weight_pad, axis_index)
        k_upper = 0.5 * (weight + upper_w)
        k_lower = 0.5 * (weight + lower_w)
        change = k_upper * (field - upper_v) + k_lower * (field - lower_v)
        coupling = jnp.array(
            [SPRING_NORMAL if comp == axis_index else SPRING_SHEAR for comp in range(3)],
            jnp.float32,
        ).reshape(3, 1, 1, 1)
        result = result + coupling * change
    return result


def faces(field):
    padded = with_halo(field, (("slab", 1), ("grp", 2)), 1)
    return jnp.pad(padded, ((0, 0), (0, 0), (0, 0), (1, 1)))


def stresses(carry, field_pad):
    rows_out = []
    for axis_index in range(3):
        upper_v, lower_v = sides(field_pad, axis_index)
        rows_out.append(SPRING_NORMAL * carry * 0.5 * (upper_v[axis_index] - lower_v[axis_index]))
    return jnp.stack(rows_out)


def paired_sum(residual, image):
    return lax.psum((jnp.sum(residual * residual), jnp.sum(residual * image)), ("slab", "grp"))


def lift(signal):
    even = signal[..., 0::2]
    odd = signal[..., 1::2]
    detail = odd - 0.5 * (even + jnp.roll(even, -1, axis=-1))
    approx = even + 0.25 * (jnp.roll(detail, 1, axis=-1) + detail)
    return (approx, detail)


def wavelet(signal):
    pieces = []
    approx = signal
    for level_index in range(LEVELS):
        approx, detail = lift(approx)
        pieces.insert(0, detail)
    return jnp.concatenate([approx] + pieces, axis=-1)


def body(u_now, u_prev, force, stiffness, broken, flags):
    weight = stiffness * (1.0 - CRACK_CUT * spread(broken))
    carry = spread(flags) * weight
    weight_pad = with_halo(weight, (("slab", 0), ("grp", 1)), 1)
    weight_pad = jnp.pad(weight_pad, ((0, 0), (0, 0), (1, 1)))

    def operate(field):
        return springs(field, weight, faces(field), weight_pad)

    for step_index in range(STEPS):
        rhs = MASS_TERM * (2.0 * u_now - u_prev) + force
        guess = u_now
        residual = rhs - operate(guess)
        image = operate(residual)
        norm_now, product = paired_sum(residual, image)
        alpha = norm_now / product
        direction, along = (residual, image)
        for turn_index in range(ITERS):
            guess = guess + alpha * direction
            residual = residual - alpha * along
            if turn_index + 1 < ITERS:
                image = operate(residual)
                norm_next, product = paired_sum(residual, image)
                ratio = norm_next / norm_now
                alpha = norm_next / (product - ratio * norm_next / alpha)
                direction = residual + ratio * direction
                along = image + ratio * along
                norm_now = norm_next
        u_prev = u_now
        u_now = guess
    stress = stresses(carry, faces(u_now))
    fields = jnp.concatenate([u_now, stress], axis=0)
    table_x = block_table(fields.shape[1])
    table_y = block_table(fields.shape[2])
    table_z = block_table(fields.shape[3])
    blockc = jnp.einsum("ax,hxyz->hayz", table_x, fields, precision=lax.Precision.HIGHEST)
    blockc = jnp.einsum("by,hxyz->hxbz", table_y, blockc, precision=lax.Precision.HIGHEST)
    blockc = jnp.einsum("hxyz,cz->hxyc", blockc, table_z, precision=lax.Precision.HIGHEST)
    moved = jnp.transpose(blockc, (0, 2, 3, 1))
    shipped = lax.all_to_all(moved, "slab", split_axis=2, concat_axis=3, tiled=True)
    coeffs = wavelet(shipped)
    return (u_now, coeffs)


MESH = pl.DeviceIdType.MESH
HALO = 4
REACH = 3
SHEAR_REST = SPRING_NORMAL - SPRING_SHEAR


def wavelet_table(count):
    table = np.kron(np.eye(count // 4), cosine_table())
    pieces = []
    approx = table
    for level_index in range(LEVELS):
        even, odd = approx[0::2], approx[1::2]
        detail = odd - 0.5 * (even + np.roll(even, -1, axis=0))
        approx = even + 0.25 * (np.roll(detail, 1, axis=0) + detail)
        pieces.insert(0, detail)
    return np.concatenate([approx] + pieces, axis=0)


def split_table(table):
    high = table.astype(jnp.bfloat16).astype(np.float64)
    return high, (table - high).astype(jnp.bfloat16).astype(np.float64)


def sub_index():
    return lax.broadcasted_iota(jnp.int32, (8, 128), 0)


def lane_index():
    return lax.broadcasted_iota(jnp.int32, (8, 128), 1)


def up_y(a, b):
    ra, rb = pltpu.roll(a, 7, 0), pltpu.roll(b, 7, 0)
    last = sub_index() == 7
    return jnp.where(last, rb, ra), jnp.where(last, ra, rb)


def down_y(a, b):
    ra, rb = pltpu.roll(a, 1, 0), pltpu.roll(b, 1, 0)
    first = sub_index() == 0
    return jnp.where(first, rb, ra), jnp.where(first, ra, rb)


def up_z(v):
    return pltpu.roll(v, 127, 1)


def down_z(v):
    return pltpu.roll(v, 1, 1)


def total(v):
    return jnp.sum(jnp.sum(v, axis=0, keepdims=True), axis=1, keepdims=True)


def kernel(ns, ng, u_in, p_in, f_in, k_in, br_in, fl_in, ez_in, cz_in, gt_in,
           disp_ref, coef_ref,
           u_ref, p_ref, f_ref, k_ref, br_ref, fl_ref, ez_ref, cz_ref, gt_ref, isem,
           e1a, e1b, s1, h1, e2a, e2b, s2, h2, rqa, rqb, e3a, s3, h3,
           u1a, u1b, carry, dga, dgb, kca, kcb, gath, rows, outb, inb,
           ctake, cland, csend, crecv, send4, recv4, send0, recv0, send1, recv1, send2, recv2, send3, recv3, asend, arecv, tsend, trecv):
    X, Y = u_ref.shape[1], u_ref.shape[2]
    si, gi = lax.axis_index("slab"), lax.axis_index("grp")
    me = si * ng + gi
    count = ns * ng
    fetched = []
    for at, (source, target) in enumerate((
        (br_in, br_ref), (fl_in, fl_ref), (ez_in, ez_ref), (k_in, k_ref), (u_in, u_ref), (p_in, p_ref),
        (f_in, f_ref), (cz_in, cz_ref), (gt_in, gt_ref),
    )):
        fetch = pltpu.make_async_copy(source, target, isem.at[at])
        fetch.start()
        fetched.append(fetch)
    barrier = pltpu.get_barrier_semaphore()

    others = []
    for k in sorted(range(ns), key=lambda k: -min(k, ns - k)):
        for g in range(ng):
            if k or g:
                others.append((lax.rem(si + k, ns), lax.rem(gi + g, ng)))
    for other in others:
        pl.semaphore_signal(barrier, inc=1, device_id=other, device_id_type=MESH)

    sub, lane = sub_index(), lane_index()
    upper = sub < 4

    steps = [(-1, 0), (1, 0), (0, -1), (0, 1), (-1, -1), (-1, 1), (1, -1), (1, 1)]

    def inside(ds, dg):
        ok = None
        if ds:
            ok = (si >= 1) if ds < 0 else (si <= ns - 2)
        if dg:
            more = (gi >= 1) if dg < 0 else (gi <= ng - 2)
            ok = more if ok is None else jnp.logical_and(ok, more)
        return ok

    def copies(ea, dst_a, stage, land, send, recv, low=0, high=None, ways=8, reach=REACH):
        half = X // 2
        edge = HALO // 2
        made = []
        chans = pl.ds(low, (ea.shape[0] if high is None else high) - low)
        for at, (ds, dg) in enumerate(steps[:ways]):
            if dg == 0:
                if ds < 0:
                    source = ea.at[chans, pl.ds(HALO, reach)]
                    target = dst_a.at[chans, pl.ds(HALO + X, reach)]
                else:
                    source = ea.at[chans, pl.ds(HALO + X - reach, reach)]
                    target = dst_a.at[chans, pl.ds(HALO - reach, reach)]
            else:
                side = 0 if dg < 0 else 1
                if ds == 0:
                    source, target = stage.at[side, chans], land.at[side, chans, pl.ds(edge, half)]
                elif ds < 0:
                    source = stage.at[side, chans, pl.ds(0, 1)]
                    target = land.at[side, chans, pl.ds(edge + half, 1)]
                else:
                    source = stage.at[side, chans, pl.ds(half - 1, 1)]
                    target = land.at[side, chans, pl.ds(edge - 1, 1)]
            made.append((ds, dg, pltpu.make_async_remote_copy(
                src_ref=source, dst_ref=target, send_sem=send.at[at], recv_sem=recv.at[at ^ 1 if at < 4 else 11 - at],
                device_id=(si + ds, gi + dg), device_id_type=MESH)))
        return made

    def begin(made):
        for ds, dg, copy in made:
            @pl.when(inside(ds, dg))
            def _():
                copy.start()

    def finish_recv(made, recv):
        for at, (ds, dg) in enumerate(steps[:len(made)]):
            back = made[at ^ 1 if at < 4 else 11 - at][2]

            @pl.when(inside(ds, dg))
            def _():
                back.wait_recv()

    def finish_send(made):
        for ds, dg, copy in made:
            @pl.when(inside(ds, dg))
            def _():
                copy.wait_send()

    def blank(dst_a, land):
        zero_a = jnp.zeros((dst_a.shape[0], HALO) + dst_a.shape[2:], jnp.float32)
        half, edge = X // 2, HALO // 2
        zero_l = jnp.zeros((land.shape[1], edge, 8, 128), jnp.float32)

        @pl.when(si == 0)
        def _():
            dst_a[:, pl.ds(0, HALO)] = zero_a
            for side in range(2):
                land[side, :, pl.ds(0, edge)] = zero_l

        @pl.when(si == ns - 1)
        def _():
            dst_a[:, pl.ds(HALO + X, HALO)] = zero_a
            for side in range(2):
                land[side, :, pl.ds(edge + half, edge)] = zero_l

        for side, edge_here in ((0, gi == ng - 1), (1, gi == 0)):
            @pl.when(edge_here)
            def _(side=side):
                land[side] = jnp.zeros(land.shape[1:], jnp.float32)

    def pack(stage, ch, pair, even, odd):
        stage[0, ch, pair] = jnp.where(upper, even, pltpu.roll(odd, 4, 0))
        stage[1, ch, pair] = jnp.where(upper, pltpu.roll(even, 4, 0), odd)

    def unpack(land, ch, pair):
        high, low = land[0, ch, pair], land[1, ch, pair]
        return (jnp.where(upper, high, pltpu.roll(low, 4, 0)),
                jnp.where(upper, pltpu.roll(high, 4, 0), low))

    def spread_rows(mask):
        wide = jnp.dot(mask.astype(jnp.float32), ez_ref[...], preferred_element_type=jnp.float32)
        return jnp.where(upper, jnp.broadcast_to(wide[0:1], (8, 128)), jnp.broadcast_to(wide[1:2], (8, 128)))

    for at in range(4):
        fetched[at].wait()
    for bx in range(X // 4):
        cut = 1.0 - CRACK_CUT * spread_rows(br_ref[bx])
        flag = spread_rows(fl_ref[bx])
        for at in range(4):
            x = bx * 4 + at
            w = k_ref[x] * cut
            e1a[6, HALO + x] = w
            carry[x] = flag * w

    def own(i, _):
        for c in range(3):
            tiles = []
            for o in range(2):
                x = 2 * i + o
                u = u_ref[c, x]
                f = f_ref[c, x]
                rhs = MASS_TERM * (2.0 * u - p_ref[c, x]) + f
                e1a[c, HALO + x] = u
                e1a[3 + c, HALO + x] = rhs
                e2a[c, HALO + x] = f
                tiles.append((u, rhs, f))
            pack(s1, c, i, tiles[0][0], tiles[1][0])
            pack(s1, 3 + c, i, tiles[0][1], tiles[1][1])
            pack(s2, c, i, tiles[0][2], tiles[1][2])
        pack(s1, 6, i, e1a[6, HALO + 2 * i], e1a[6, HALO + 2 * i + 1])
        return 0

    for at in range(4, 7):
        fetched[at].wait()
    lax.fori_loop(0, X // 2, own, 0)
    blank(e1a, h1)
    blank(e2a, h2)
    blank(e3a, h3)

    def corner_copies():
        made = []
        for at, (ds, dg) in enumerate(steps[4:]):
            side, end = (0 if dg < 0 else 1), (0 if ds < 0 else 1)
            made.append((ds, dg, pltpu.make_async_remote_copy(
                src_ref=ctake.at[side, end], dst_ref=cland.at[side, 1 - end],
                send_sem=csend.at[at], recv_sem=crecv.at[3 - at],
                device_id=(si + ds, gi + dg), device_id_type=MESH)))
        return made

    near = sub % 4 < 2
    for side in range(2):
        for end in range(2):
            for t in range((7 + 1) // 2):
                tile = s1[side, 2 * t, end * (X // 2 - 1)]
                if 2 * t + 1 < 7:
                    other = s1[side, 2 * t + 1, end * (X // 2 - 1)]
                    tile = (jnp.where(near, tile, pltpu.roll(other, 2, 0)) if side == 0
                            else jnp.where(near, pltpu.roll(other, 6, 0), tile))
                ctake[side, end, t] = tile

    def corner_unpack(made):
        for at, (ds, dg) in enumerate(steps[4:]):
            side, end = (0 if dg > 0 else 1), (1 if ds > 0 else 0)
            pair = HALO // 2 + X // 2 if ds > 0 else HALO // 2 - 1
            back = made[3 - at][2]

            @pl.when(inside(ds, dg))
            def _():
                back.wait_recv()
                for ch in range(7):
                    tile = cland[side, end, ch // 2]
                    h1[side, ch, pair] = tile if ch % 2 == 0 else pltpu.roll(tile, 6 if side == 0 else 2, 0)

    corners = corner_copies()
    zeroth = copies(e1a, e1a, s1, h1, send0, recv0, 6, 7, 4)
    first = copies(e1a, e1a, s1, h1, send1, recv1, 0, 3, 4)
    rest = copies(e1a, e1a, s1, h1, send4, recv4, 3, 6, 4, REACH - 1)
    second = copies(e2a, e2a, s2, h2, send2, recv2)
    third = copies(rqa, e3a, s3, h3, send3, recv3)
    pl.semaphore_wait(barrier, count - 1)
    begin(zeroth)
    begin(corners)
    begin(first)
    begin(rest)
    finish_recv(zeroth, recv0)
    corner_unpack(corners)

    def open0(i, _):
        e1b[6, 2 * i], e1b[6, 2 * i + 1] = unpack(h1, 6, i)
        return 0

    def open1(i, _):
        for ch in range(6):
            e1b[ch, 2 * i], e1b[ch, 2 * i + 1] = unpack(h1, ch, i)
        return 0

    lax.fori_loop(0, (X + 2 * HALO) // 2, open0, 0)

    def link(w, other):
        return jnp.where(jnp.minimum(w, other) > 0.0, 0.5 * (w + other), 0.0)

    not_last, not_first = lane < 127, lane > 0

    def coefficients(x, _):
        wa, wb = e1a[6, x], e1b[6, x]
        ya, yb = up_y(wa, wb)
        da, db = down_y(wa, wb)
        for w, wu, wd, yu, yd, dg, kc in (
            (wa, e1a[6, x + 1], e1a[6, x - 1], ya, da, dga, kca),
            (wb, e1b[6, x + 1], e1b[6, x - 1], yb, db, dgb, kcb),
        ):
            zu = jnp.where(not_last, up_z(w), 0.0)
            zd = jnp.where(not_first, down_z(w), 0.0)
            kc[0, x] = link(w, wu)
            kc[1, x] = link(w, yu)
            kc[2, x] = link(w, yd)
            kc[3, x] = link(w, zu)
            kc[4, x] = link(w, zd)
            sx = w + 0.5 * (wu + wd)
            sy = w + 0.5 * (yu + yd)
            sz = w + 0.5 * (zu + zd)
            every = MASS_TERM + SPRING_SHEAR * (sx + sy + sz)
            dg[0, x] = every + SHEAR_REST * sx
            dg[1, x] = every + SHEAR_REST * sy
            dg[2, x] = every + SHEAR_REST * sz
        return 0

    kca[0, HALO - REACH] = link(e1a[6, HALO - REACH], e1a[6, HALO - REACH + 1])
    kcb[0, HALO - REACH] = link(e1b[6, HALO - REACH], e1b[6, HALO - REACH + 1])
    lax.fori_loop(HALO - 2, HALO + X + 2, coefficients, 0)
    finish_recv(first, recv1)
    finish_recv(rest, recv4)
    begin(second)
    lax.fori_loop(0, (X + 2 * HALO) // 2, open1, 0)

    def operate(x, va, vb, base, both=True):
        result = []
        coef = [[kc[j, x] for j in range(5)] + [kc[0, x - 1]] for kc in (kca, kcb)]
        for c in range(3):
            a, b = va[base + c, x], vb[base + c, x]
            ua, ub = up_y(a, b)
            la, lb = down_y(a, b)
            pair = []
            halves = ((a, va, ua, la, coef[0], dga), (b, vb, ub, lb, coef[1], dgb))
            for v, ref, u, l, k, dg in halves if both else halves[:1]:
                parts = (
                    k[0] * ref[base + c, x + 1] + k[5] * ref[base + c, x - 1],
                    k[1] * u + k[2] * l,
                    k[3] * up_z(v) + k[4] * down_z(v),
                )
                every = parts[0] + parts[1] + parts[2]
                pair.append(dg[c, x] * v - (SPRING_SHEAR * every + SHEAR_REST * parts[c]))
            result.append(pair)
        return result

    def solve(step, va, vb, rhs_of):
        def residual(i, _):
            done = []
            for x in (2 * i, 2 * i + 1):
                image = operate(x, va, vb, 0)
                for c in range(3):
                    ra, rb = rhs_of(c, x)
                    done.append((c, x, ra - image[c][0], rb - image[c][1]))
            for c, x, ra, rb in done:
                rqa[c, x] = ra
                rqb[c, x] = rb
            return 0

        lax.fori_loop((HALO - 2) // 2, (HALO + X + 2) // 2, residual, 0)

        def put(x, image):
            for c in range(3):
                rqa[3 + c, x] = image[c][0]
                rqb[3 + c, x] = image[c][1]

        def apply(i, sums):
            rr, rq = sums
            at = (2 * i, 2 * i + 1)
            images = [operate(x, rqa, rqb, 0) for x in at]
            for x, image in zip(at, images):
                for c in range(3):
                    r = rqa[c, x]
                    rr, rq = rr + r * r, rq + r * image[c][0]
            for x, image in zip(at, images):
                put(x, image)
            return rr, rq

        zero = jnp.zeros((8, 128), jnp.float32)
        images = [operate(x, rqa, rqb, 0) for x in (HALO - 1, HALO + X)]
        put(HALO - 1, images[0])
        put(HALO + X, images[1])
        rr, rq = lax.fori_loop(HALO // 2, (HALO + X) // 2, apply, (zero, zero))
        rr, rq = total(rr), total(rq)
        mu = jnp.where(rr > 0.0, rq / jnp.where(rr > 0.0, rr, 1.0), 0.0)

        def centred(i, sums):
            ww, wr, mix, wt = sums
            for x in (2 * i, 2 * i + 1):
                image = operate(x, rqa, rqb, 3, False)
                for c in range(3):
                    r, q, s = rqa[c, x], rqa[3 + c, x], image[c][0]
                    w, t = q - mu * r, s - mu * q
                    ww, wr, mix, wt = ww + w * w, wr + w * r, mix + (r * t + w * q), wt + w * t
            return ww, wr, mix, wt

        sums = lax.fori_loop(HALO // 2, (HALO + X) // 2, centred, (zero,) * 4)
        ww, wr, mix, wt = [total(v) for v in sums]
        one = lax.broadcasted_iota(jnp.int32, (1, 128), 1)
        row = jnp.zeros((1, 128), jnp.float32)
        for at, value in enumerate((rr, rq, mu, ww, wr, mix, wt)):
            row = jnp.where(one == at, value, row)
        gath[step, me] = row

        for other in others:
            pltpu.make_async_remote_copy(
                src_ref=gath.at[step, me], dst_ref=gath.at[step, me], send_sem=asend.at[step], recv_sem=arecv.at[step],
                device_id=other, device_id_type=MESH).start()

    def collect(step):
        block = gath.at[step, pl.ds(0, count - 1)]
        pltpu.make_async_copy(block, block, arecv.at[step]).wait()
        table = gath[step].reshape(count, 128)
        rr, rq, mu, ww, wr, mix, wt = [table[:, at:at + 1] for at in range(7)]

        def down(v):
            return jnp.sum(v, axis=0, keepdims=True)

        norm = down(rr)
        alpha = norm / down(rq)
        rest = 1.0 - alpha * mu
        after = down(alpha * alpha * ww - 2.0 * alpha * rest * wr + rest * rest * rr)
        curved = down(rest * rest * rq - alpha * rest * mix + alpha * alpha * wt)
        ratio = after / norm
        beta = after / (curved - ratio * after / alpha)
        return alpha + beta * (1.0 + ratio), -beta * alpha

    def drain(step):
        block = gath.at[step, pl.ds(0, count - 1)]
        pltpu.make_async_copy(block, block, asend.at[step]).wait()

    solve(0, e1a, e1b, lambda c, x: (e1a[3 + c, x], e1b[3 + c, x]))

    def pack3(i, _):
        for ch in range(6):
            pack(s3, ch, i, rqa[ch, HALO + 2 * i], rqa[ch, HALO + 2 * i + 1])
        return 0

    lax.fori_loop(0, X // 2, pack3, 0)
    begin(third)

    finish_recv(second, recv2)

    def open2(i, _):
        for ch in range(3):
            e2b[ch, 2 * i], e2b[ch, 2 * i + 1] = unpack(h2, ch, i)
        return 0

    lax.fori_loop(0, (X + 2 * HALO) // 2, open2, 0)
    finish_recv(third, recv3)
    c0, c1 = collect(0)

    def step_b(i, _):
        for c in range(3):
            r0, r1 = unpack(h3, c, i)
            q0, q1 = unpack(h3, 3 + c, i)
            u1b[c, 2 * i] = e1b[c, 2 * i] + (c0 * r0 + c1 * q0)
            u1b[c, 2 * i + 1] = e1b[c, 2 * i + 1] + (c0 * r1 + c1 * q1)
        return 0

    lax.fori_loop(0, (X + 2 * HALO) // 2, step_b, 0)

    def step_a(i, _):
        for x in (2 * i, 2 * i + 1):
            for c in range(3):
                u1a[c, x] = e1a[c, x] + (c0 * rqa[c, x] + c1 * rqa[3 + c, x])
        return 0

    lax.fori_loop(HALO // 2, (HALO + X) // 2, step_a, 0)
    for x in list(range(HALO - REACH, HALO)) + list(range(HALO + X, HALO + X + REACH)):
        for c in range(3):
            u1a[c, x] = e1a[c, x] + (c0 * e3a[c, x] + c1 * e3a[3 + c, x])
    finish_send(zeroth)
    finish_send(corners)
    finish_send(rest)
    finish_send(first)
    finish_send(second)
    finish_send(third)

    def rhs2(c, x):
        return (MASS_TERM * (2.0 * u1a[c, x] - e1a[c, x]) + e2a[c, x],
                MASS_TERM * (2.0 * u1b[c, x] - e1b[c, x]) + e2b[c, x])

    solve(1, u1a, u1b, rhs2)
    c0, c1 = collect(1)

    def step2(x, _):
        for c in range(3):
            va = u1a[c, x] + (c0 * rqa[c, x] + c1 * rqa[3 + c, x])
            vb = u1b[c, x] + (c0 * rqb[c, x] + c1 * rqb[3 + c, x])
            u1a[c, x] = va
            u1b[c, x] = vb
        return 0

    step2(HALO - 1, 0)
    step2(HALO + X, 0)

    def step2_own(i, _):
        for x in (2 * i, 2 * i + 1):
            step2(x, 0)
            for c in range(3):
                v = u1a[c, x]
                disp_ref[c, x - HALO] = v
                rows[c, pl.ds(x - HALO, 8, stride=X), :] = v
        return 0

    lax.fori_loop(HALO // 2, (HALO + X) // 2, step2_own, 0)
    zrows = coef_ref.shape[2]
    nt = (((1,), (1,)), ((), ()))

    def halves(v):
        high = v.astype(jnp.bfloat16)
        return high, (v - high.astype(jnp.float32)).astype(jnp.bfloat16)

    def transform(c, _):
        high, low = halves(rows[c])
        turned = lax.dot_general(cz_ref[:, 0:256], jnp.concatenate([high, low], axis=1), nt,
                                 preferred_element_type=jnp.float32)
        turned += lax.dot_general(cz_ref[:, 256:384], high, nt, preferred_element_type=jnp.float32)
        for j in range(ns):
            outb[j, c] = turned[j * zrows:(j + 1) * zrows]
        return 0

    def trade(part, i):
        to = lax.rem(si + i, ns)
        return pltpu.make_async_remote_copy(
            src_ref=outb.at[to, pl.ds(3 * part, 3)], dst_ref=inb.at[si, pl.ds(3 * part, 3)],
            send_sem=tsend.at[part, i], recv_sem=trecv.at[part, i],
            device_id=(to, gi), device_id_type=MESH)

    trades = [[trade(part, i) for i in range(1, ns)] for part in range(2)]

    def ship(part):
        lax.fori_loop(3 * part, 3 * part + 3, transform, 0)
        for copy in trades[part]:
            copy.start()
        for c in range(3 * part, 3 * part + 3):
            inb[si, c] = outb[si, c]

    fetched[7].wait()
    ship(0)

    def finals(i, _):
        for x in (2 * i, 2 * i + 1):
            at = x - HALO
            scale = SPRING_NORMAL * carry[at] * 0.5
            a1, a2, b1 = u1a[1, x], u1a[2, x], u1b[1, x]
            dx = u1a[0, x + 1] - u1a[0, x - 1]
            dy = up_y(a1, b1)[0] - down_y(a1, b1)[0]
            dz = jnp.where(not_last, up_z(a2), 0.0) - jnp.where(not_first, down_z(a2), 0.0)
            for c, d in enumerate((dx, dy, dz)):
                rows[3 + c, pl.ds(at, 8, stride=X), :] = scale * d
        return 0

    lax.fori_loop(HALO // 2, (HALO + X) // 2, finals, 0)
    ship(1)
    fetched[8].wait()

    zlane = lax.broadcasted_iota(jnp.int32, (zrows, 128), 1)
    c1t, c3t = float(np.sqrt(0.5) * np.cos(np.pi / 8)), float(np.sqrt(0.5) * np.cos(3 * np.pi / 8))

    def gather_back(c, _):
        pieces = [inb[j, c] for j in range(ns)]
        gap = ns // 2
        while gap:
            keep = (zlane // (X * gap)) % 2 == 0
            mixed = list(pieces)
            for j in range(ns):
                if (j // gap) % 2 == 0:
                    a, b = pieces[j], pieces[j + gap]
                    mixed[j] = jnp.where(keep, a, pltpu.roll(b, X * gap, 1))
                    mixed[j + gap] = jnp.where(keep, pltpu.roll(a, 128 - X * gap, 1), b)
            pieces = mixed
            gap //= 2
        coded = []
        for b in range(Y // 4):
            v0, v1, v2, v3 = pieces[4 * b:4 * b + 4]
            s03, s12, d03, d12 = v0 + v3, v1 + v2, v0 - v3, v1 - v2
            coded += [0.5 * (s03 + s12), c1t * d03 + c3t * d12, 0.5 * (s03 - s12), c3t * d03 - c1t * d12]
        high, low = halves(jnp.concatenate(coded, axis=0))
        done = jnp.dot(jnp.concatenate([high, low], axis=1), gt_ref[...], preferred_element_type=jnp.float32)
        coef_ref[c] = (done[:, 0:128] + done[:, 128:256]).reshape(Y, zrows, 128)
        return 0

    for part in range(2):
        for copy in trades[part]:
            copy.wait_recv()
        for c in range(3 * part, 3 * part + 3):
            gather_back(c, 0)
    drain(0)
    drain(1)
    for part in range(2):
        for copy in trades[part]:
            copy.wait_send()


def store(disp_in, coef_in, disp_out, coef_out, sems):
    copies = [pltpu.make_async_copy(disp_in, disp_out, sems.at[0]), pltpu.make_async_copy(coef_in, coef_out, sems.at[1])]
    for copy in copies:
        copy.start()
    for copy in copies:
        copy.wait()


def fused(mesh, u_now, u_prev, force, stiffness, broken, flags):
    ns, ng = mesh.shape["slab"], mesh.shape["grp"]
    _, X, Y, Z = u_now.shape
    xe, pairs, half = X + 2 * HALO, X // 2 + HALO, X // 2
    zrows = Z // ns
    ez = jnp.asarray(np.kron(np.eye(Z // 4), np.ones((1, 4))), jnp.float32)
    czh, czl = split_table(np.kron(np.eye(Z // 4), cosine_table()))
    cz = jnp.asarray(np.concatenate([czh, czh, czl], axis=1), jnp.bfloat16)
    gth, gtl = split_table(wavelet_table(X * ns).T)
    gt = jnp.asarray(np.block([[gth, gtl], [gth, np.zeros_like(gtl)]]), jnp.bfloat16)

    def vm(*shape):
        return pltpu.VMEM(shape, jnp.float32)

    def ext(n):
        return vm(n, xe, Y, Z)

    def stage(n):
        return vm(2, n, half, Y, Z)

    def land(n):
        return vm(2, n, pairs, Y, Z)

    dma = pltpu.SemaphoreType.DMA
    shapes = (u_now.shape, (6, Y, zrows, X * ns))
    operands = [pltpu.with_memory_space_constraint(v, pltpu.HBM)
                for v in (u_now, u_prev, force, stiffness, broken, flags, ez, cz, gt)]
    results = pl.pallas_call(
        lambda *refs: kernel(ns, ng, *refs),
        name="lattice",
        out_shape=tuple(vm(*shape) for shape in shapes),
        in_specs=[pl.BlockSpec(memory_space=pltpu.MemorySpace.HBM)] * 9,
        out_specs=(pl.BlockSpec(memory_space=pltpu.VMEM),) * 2,
        scratch_shapes=[
            vm(*u_now.shape), vm(*u_now.shape), vm(*u_now.shape), vm(*stiffness.shape),
            pltpu.VMEM(broken.shape, broken.dtype), pltpu.VMEM(flags.shape, flags.dtype),
            vm(*ez.shape), pltpu.VMEM(cz.shape, cz.dtype), pltpu.VMEM(gt.shape, gt.dtype), pltpu.SemaphoreType.DMA((9,)),
            ext(7), ext(7), stage(7), land(7),
            ext(3), ext(3), stage(3), land(3),
            ext(6), ext(6), ext(6), stage(6), land(6),
            ext(3), ext(3), vm(X, Y, Z), ext(3), ext(3), ext(5), ext(5),
            vm(2, ns * ng, 1, 128), vm(6, Y * X, Z), vm(ns, 6, zrows, 128), vm(ns, 6, zrows, 128),
            vm(2, 2, 4, Y, Z), vm(2, 2, 4, Y, Z), dma((4,)), dma((4,)), dma((8,)), dma((8,)),
            dma((8,)), dma((8,)), dma((8,)), dma((8,)), dma((8,)), dma((8,)), dma((8,)), dma((8,)),
            dma((2,)), dma((2,)), dma((2, ns)), dma((2, ns)),
        ],
        compiler_params=pltpu.CompilerParams(collective_id=0, has_side_effects=True, vmem_limit_bytes=24 << 20),
    )(*operands)
    return pl.pallas_call(
        store,
        name="store",
        out_shape=tuple(jax.ShapeDtypeStruct(shape, jnp.float32) for shape in shapes),
        in_specs=[pl.BlockSpec(memory_space=pltpu.VMEM)] * 2,
        out_specs=(pl.BlockSpec(memory_space=pltpu.MemorySpace.HBM),) * 2,
        scratch_shapes=[dma((2,))],
        compiler_params=pltpu.CompilerParams(vmem_limit_bytes=1 << 20),
    )(*[pltpu.with_memory_space_constraint(v, pltpu.VMEM) for v in results])


def fits(mesh, shape):
    ns, ng = mesh.shape["slab"], mesh.shape["grp"]
    x, y, z = shape[1] // ns, shape[2] // ng, shape[3]
    return y == 8 and z == 128 and x * y == 128 and x * ns == 128 and z % (8 * ns) == 0


def entry(mesh, *args):
    ns, ng = mesh.shape["slab"], mesh.shape["grp"]
    _, x, y, z = args[0].shape
    if fits(mesh, (3, x * ns, y * ng, z)):
        return fused(mesh, *args)
    return body(*args)


def solution(mesh):
    return jax.shard_map(
        lambda *args: entry(mesh, *args),
        mesh=mesh,
        in_specs=(
            P(None, "slab", "grp", None),
            P(None, "slab", "grp", None),
            P(None, "slab", "grp", None),
            P("slab", "grp", None),
            P("slab", "grp", None),
            P("slab", "grp", None),
        ),
        out_specs=(P(None, "slab", "grp", None), P(None, "grp", "slab", None)),
        check_vma=False,
    )
```

```python
import jax
import jax.numpy as jnp
import numpy as np
from jax import lax
from jax.experimental import pallas as pl
from jax.experimental.pallas import tpu as pltpu
from jax.sharding import PartitionSpec as P

STEPS = 2
ITERS = 2
LEVELS = 3


SPRING_NORMAL = 1.0
SPRING_SHEAR = 0.4
MASS_TERM = 1.0
CRACK_CUT = 0.9


def with_halo(block, sides, width):
    for axis, dim in sides:
        count = lax.axis_size(axis)
        forward = [(i, i + 1) for i in range(count - 1)]
        backward = [(target, source) for source, target in forward]
        low = lax.ppermute(
            lax.slice_in_dim(block, block.shape[dim] - width, None, axis=dim), axis, forward
        )
        high = lax.ppermute(lax.slice_in_dim(block, 0, width, axis=dim), axis, backward)
        block = jnp.concatenate([low, block, high], axis=dim)
    return block


def cosine_table():
    freq = np.arange(4)[:, None]
    place = np.arange(4)[None, :]
    factor = np.where(freq == 0, 0.5, np.sqrt(0.5))
    return factor * np.cos(np.pi * (2 * place + 1) * freq / 8.0)


def block_table(count):
    return jnp.asarray(np.kron(np.eye(count // 4), cosine_table()), jnp.float32)


def spread(mask):
    values = mask.astype(jnp.float32)
    size_a, size_b, size_c = values.shape
    wide = jnp.broadcast_to(values[:, None, :, None, :, None], (size_a, 4, size_b, 4, size_c, 4))
    return wide.reshape(size_a * 4, size_b * 4, size_c * 4)


def sides(padded, axis_index):
    leading = padded.ndim - 3

    def cut(offset):
        index_list = [slice(None)] * leading + [slice(1, -1)] * 3
        length = padded.shape[leading + axis_index]
        index_list[leading + axis_index] = slice(1 + offset, length - 1 + offset)
        return padded[tuple(index_list)]

    return (cut(1), cut(-1))


def springs(field, weight, field_pad, weight_pad):
    result = MASS_TERM * field
    for axis_index in range(3):
        upper_v, lower_v = sides(field_pad, axis_index)
        upper_w, lower_w = sides(weight_pad, axis_index)
        k_upper = 0.5 * (weight + upper_w)
        k_lower = 0.5 * (weight + lower_w)
        change = k_upper * (field - upper_v) + k_lower * (field - lower_v)
        coupling = jnp.array(
            [SPRING_NORMAL if comp == axis_index else SPRING_SHEAR for comp in range(3)],
            jnp.float32,
        ).reshape(3, 1, 1, 1)
        result = result + coupling * change
    return result


def faces(field):
    padded = with_halo(field, (("slab", 1), ("grp", 2)), 1)
    return jnp.pad(padded, ((0, 0), (0, 0), (0, 0), (1, 1)))


def stresses(carry, field_pad):
    rows_out = []
    for axis_index in range(3):
        upper_v, lower_v = sides(field_pad, axis_index)
        rows_out.append(SPRING_NORMAL * carry * 0.5 * (upper_v[axis_index] - lower_v[axis_index]))
    return jnp.stack(rows_out)


def paired_sum(residual, image):
    return lax.psum((jnp.sum(residual * residual), jnp.sum(residual * image)), ("slab", "grp"))


def lift(signal):
    even = signal[..., 0::2]
    odd = signal[..., 1::2]
    detail = odd - 0.5 * (even + jnp.roll(even, -1, axis=-1))
    approx = even + 0.25 * (jnp.roll(detail, 1, axis=-1) + detail)
    return (approx, detail)


def wavelet(signal):
    pieces = []
    approx = signal
    for level_index in range(LEVELS):
        approx, detail = lift(approx)
        pieces.insert(0, detail)
    return jnp.concatenate([approx] + pieces, axis=-1)


def body(u_now, u_prev, force, stiffness, broken, flags):
    weight = stiffness * (1.0 - CRACK_CUT * spread(broken))
    carry = spread(flags) * weight
    weight_pad = with_halo(weight, (("slab", 0), ("grp", 1)), 1)
    weight_pad = jnp.pad(weight_pad, ((0, 0), (0, 0), (1, 1)))

    def operate(field):
        return springs(field, weight, faces(field), weight_pad)

    for step_index in range(STEPS):
        rhs = MASS_TERM * (2.0 * u_now - u_prev) + force
        guess = u_now
        residual = rhs - operate(guess)
        image = operate(residual)
        norm_now, product = paired_sum(residual, image)
        alpha = norm_now / product
        direction, along = (residual, image)
        for turn_index in range(ITERS):
            guess = guess + alpha * direction
            residual = residual - alpha * along
            if turn_index + 1 < ITERS:
                image = operate(residual)
                norm_next, product = paired_sum(residual, image)
                ratio = norm_next / norm_now
                alpha = norm_next / (product - ratio * norm_next / alpha)
                direction = residual + ratio * direction
                along = image + ratio * along
                norm_now = norm_next
        u_prev = u_now
        u_now = guess
    stress = stresses(carry, faces(u_now))
    fields = jnp.concatenate([u_now, stress], axis=0)
    table_x = block_table(fields.shape[1])
    table_y = block_table(fields.shape[2])
    table_z = block_table(fields.shape[3])
    blockc = jnp.einsum("ax,hxyz->hayz", table_x, fields, precision=lax.Precision.HIGHEST)
    blockc = jnp.einsum("by,hxyz->hxbz", table_y, blockc, precision=lax.Precision.HIGHEST)
    blockc = jnp.einsum("hxyz,cz->hxyc", blockc, table_z, precision=lax.Precision.HIGHEST)
    moved = jnp.transpose(blockc, (0, 2, 3, 1))
    shipped = lax.all_to_all(moved, "slab", split_axis=2, concat_axis=3, tiled=True)
    coeffs = wavelet(shipped)
    return (u_now, coeffs)


MESH = pl.DeviceIdType.MESH
HALO = 4
REACH = 3
SHEAR_REST = SPRING_NORMAL - SPRING_SHEAR


def wavelet_table(count):
    table = np.kron(np.eye(count // 4), cosine_table())
    pieces = []
    approx = table
    for level_index in range(LEVELS):
        even, odd = approx[0::2], approx[1::2]
        detail = odd - 0.5 * (even + np.roll(even, -1, axis=0))
        approx = even + 0.25 * (np.roll(detail, 1, axis=0) + detail)
        pieces.insert(0, detail)
    return np.concatenate([approx] + pieces, axis=0)


def split_table(table):
    high = table.astype(jnp.bfloat16).astype(np.float64)
    return high, (table - high).astype(jnp.bfloat16).astype(np.float64)


def sub_index():
    return lax.broadcasted_iota(jnp.int32, (8, 128), 0)


def lane_index():
    return lax.broadcasted_iota(jnp.int32, (8, 128), 1)


def up_y(a, b):
    ra, rb = pltpu.roll(a, 7, 0), pltpu.roll(b, 7, 0)
    last = sub_index() == 7
    return jnp.where(last, rb, ra), jnp.where(last, ra, rb)


def down_y(a, b):
    ra, rb = pltpu.roll(a, 1, 0), pltpu.roll(b, 1, 0)
    first = sub_index() == 0
    return jnp.where(first, rb, ra), jnp.where(first, ra, rb)


def up_z(v):
    return pltpu.roll(v, 127, 1)


def down_z(v):
    return pltpu.roll(v, 1, 1)


def total(v):
    return jnp.sum(jnp.sum(v, axis=0, keepdims=True), axis=1, keepdims=True)


def kernel(ns, ng, u_in, p_in, f_in, k_in, br_in, fl_in, ez_in, cz_in, gt_in,
           disp_ref, coef_ref,
           u_ref, p_ref, f_ref, k_ref, br_ref, fl_ref, ez_ref, cz_ref, gt_ref, isem,
           e1a, e1b, s1, h1, e2a, e2b, s2, h2, rqa, rqb, s3, h3, k3,
           u1a, u1b, carry, dga, dgb, kca, kcb, gath, rows, outb, inb,
           ctake, cland, csend, crecv, send4, recv4, send0, recv0, send1, recv1, send2, recv2, send3, recv3, sendq, recvq, sendk, recvk, asend, arecv, tsend, trecv):
    X, Y = u_ref.shape[1], u_ref.shape[2]
    si, gi = lax.axis_index("slab"), lax.axis_index("grp")
    me = si * ng + gi
    count = ns * ng
    fetched = []
    for at, (source, target) in enumerate((
        (br_in, br_ref), (fl_in, fl_ref), (ez_in, ez_ref), (k_in, k_ref), (u_in, u_ref), (p_in, p_ref),
        (f_in, f_ref), (cz_in, cz_ref), (gt_in, gt_ref),
    )):
        fetch = pltpu.make_async_copy(source, target, isem.at[at])
        fetch.start()
        fetched.append(fetch)
    barrier = pltpu.get_barrier_semaphore()

    others = []
    for k in sorted(range(ns), key=lambda k: -min(k, ns - k)):
        for g in range(ng):
            if k or g:
                others.append((lax.rem(si + k, ns), lax.rem(gi + g, ng)))
    for other in others:
        pl.semaphore_signal(barrier, inc=1, device_id=other, device_id_type=MESH)

    sub, lane = sub_index(), lane_index()
    upper = sub < 4

    steps = [(-1, 0), (1, 0), (0, -1), (0, 1), (-1, -1), (-1, 1), (1, -1), (1, 1)]

    def inside(ds, dg):
        ok = None
        if ds:
            ok = (si >= 1) if ds < 0 else (si <= ns - 2)
        if dg:
            more = (gi >= 1) if dg < 0 else (gi <= ng - 2)
            ok = more if ok is None else jnp.logical_and(ok, more)
        return ok

    def copies(ea, dst_a, stage, land, send, recv, low=0, high=None, ways=8, reach=REACH, depth=None):
        depth = reach if depth is None else depth
        half = X // 2
        edge = HALO // 2
        made = []
        chans = pl.ds(low, (ea.shape[0] if high is None else high) - low)
        for at, (ds, dg) in enumerate(steps[:ways]):
            if dg == 0:
                if ds < 0:
                    source = ea.at[chans, pl.ds(HALO + depth - reach, reach)]
                    target = dst_a.at[chans, pl.ds(HALO + X + depth - reach, reach)]
                else:
                    source = ea.at[chans, pl.ds(HALO + X - depth, reach)]
                    target = dst_a.at[chans, pl.ds(HALO - depth, reach)]
            else:
                side = 0 if dg < 0 else 1
                if ds == 0:
                    source, target = stage.at[side, chans], land.at[side, chans, pl.ds(edge, half)]
                elif ds < 0:
                    source = stage.at[side, chans, pl.ds(0, 1)]
                    target = land.at[side, chans, pl.ds(edge + half, 1)]
                else:
                    source = stage.at[side, chans, pl.ds(half - 1, 1)]
                    target = land.at[side, chans, pl.ds(edge - 1, 1)]
            made.append((ds, dg, pltpu.make_async_remote_copy(
                src_ref=source, dst_ref=target, send_sem=send.at[at], recv_sem=recv.at[at ^ 1 if at < 4 else 11 - at],
                device_id=(si + ds, gi + dg), device_id_type=MESH)))
        return made

    def begin(made):
        for ds, dg, copy in made:
            @pl.when(inside(ds, dg))
            def _():
                copy.start()

    def finish_recv(made, recv):
        for at, (ds, dg) in enumerate(steps[:len(made)]):
            back = made[at ^ 1 if at < 4 else 11 - at][2]

            @pl.when(inside(ds, dg))
            def _():
                back.wait_recv()

    def finish_send(made):
        for ds, dg, copy in made:
            @pl.when(inside(ds, dg))
            def _():
                copy.wait_send()

    def blank(dst_a, land):
        zero_a = jnp.zeros((dst_a.shape[0], HALO) + dst_a.shape[2:], jnp.float32)
        half, edge = X // 2, HALO // 2
        zero_l = jnp.zeros((land.shape[1], edge, 8, 128), jnp.float32)

        @pl.when(si == 0)
        def _():
            dst_a[:, pl.ds(0, HALO)] = zero_a
            for side in range(2):
                land[side, :, pl.ds(0, edge)] = zero_l

        @pl.when(si == ns - 1)
        def _():
            dst_a[:, pl.ds(HALO + X, HALO)] = zero_a
            for side in range(2):
                land[side, :, pl.ds(edge + half, edge)] = zero_l

        for side, edge_here in ((0, gi == ng - 1), (1, gi == 0)):
            @pl.when(edge_here)
            def _(side=side):
                land[side] = jnp.zeros(land.shape[1:], jnp.float32)

    def pack(stage, ch, pair, even, odd):
        stage[0, ch, pair] = jnp.where(upper, even, pltpu.roll(odd, 4, 0))
        stage[1, ch, pair] = jnp.where(upper, pltpu.roll(even, 4, 0), odd)

    def unpack(land, ch, pair):
        high, low = land[0, ch, pair], land[1, ch, pair]
        return (jnp.where(upper, high, pltpu.roll(low, 4, 0)),
                jnp.where(upper, pltpu.roll(high, 4, 0), low))

    def spread_rows(mask):
        wide = jnp.dot(mask.astype(jnp.float32), ez_ref[...], preferred_element_type=jnp.float32)
        return jnp.where(upper, jnp.broadcast_to(wide[0:1], (8, 128)), jnp.broadcast_to(wide[1:2], (8, 128)))

    for at in range(4):
        fetched[at].wait()
    for bx in range(X // 4):
        cut = 1.0 - CRACK_CUT * spread_rows(br_ref[bx])
        flag = spread_rows(fl_ref[bx])
        for at in range(4):
            x = bx * 4 + at
            w = k_ref[x] * cut
            e1a[6, HALO + x] = w
            carry[x] = flag * w

    def own(i, _):
        for c in range(3):
            tiles = []
            for o in range(2):
                x = 2 * i + o
                u = u_ref[c, x]
                f = f_ref[c, x]
                rhs = MASS_TERM * (2.0 * u - p_ref[c, x]) + f
                e1a[c, HALO + x] = u
                e1a[3 + c, HALO + x] = rhs
                e2a[c, HALO + x] = f
                tiles.append((u, rhs, f))
            pack(s1, c, i, tiles[0][0], tiles[1][0])
            pack(s1, 3 + c, i, tiles[0][1], tiles[1][1])
            pack(s2, c, i, tiles[0][2], tiles[1][2])
        pack(s1, 6, i, e1a[6, HALO + 2 * i], e1a[6, HALO + 2 * i + 1])
        return 0

    for at in range(4, 7):
        fetched[at].wait()
    lax.fori_loop(0, X // 2, own, 0)
    blank(e1a, h1)
    blank(e2a, h2)
    blank(rqa, h3)

    def wedge_copies():
        made = []
        for at, (ds, dg) in enumerate(steps[4:]):
            side, end = (0 if dg < 0 else 1), (0 if ds < 0 else 1)
            pair = HALO // 2 + X // 2 if ds < 0 else HALO // 2 - 1
            made.append((ds, dg, pltpu.make_async_remote_copy(
                src_ref=k3.at[side, end], dst_ref=h3.at[side, :, pl.ds(pair, 1)],
                send_sem=sendk.at[at], recv_sem=recvk.at[3 - at],
                device_id=(si + ds, gi + dg), device_id_type=MESH)))
        return made

    def corner_copies():
        made = []
        for at, (ds, dg) in enumerate(steps[4:]):
            side, end = (0 if dg < 0 else 1), (0 if ds < 0 else 1)
            made.append((ds, dg, pltpu.make_async_remote_copy(
                src_ref=ctake.at[side, end], dst_ref=cland.at[side, 1 - end],
                send_sem=csend.at[at], recv_sem=crecv.at[3 - at],
                device_id=(si + ds, gi + dg), device_id_type=MESH)))
        return made

    near = sub % 4 < 2
    for side in range(2):
        for end in range(2):
            for t in range((7 + 1) // 2):
                tile = s1[side, 2 * t, end * (X // 2 - 1)]
                if 2 * t + 1 < 7:
                    other = s1[side, 2 * t + 1, end * (X // 2 - 1)]
                    tile = (jnp.where(near, tile, pltpu.roll(other, 2, 0)) if side == 0
                            else jnp.where(near, pltpu.roll(other, 6, 0), tile))
                ctake[side, end, t] = tile

    def corner_unpack(made):
        for at, (ds, dg) in enumerate(steps[4:]):
            side, end = (0 if dg > 0 else 1), (1 if ds > 0 else 0)
            pair = HALO // 2 + X // 2 if ds > 0 else HALO // 2 - 1
            back = made[3 - at][2]

            @pl.when(inside(ds, dg))
            def _():
                back.wait_recv()
                for ch in range(7):
                    tile = cland[side, end, ch // 2]
                    h1[side, ch, pair] = tile if ch % 2 == 0 else pltpu.roll(tile, 6 if side == 0 else 2, 0)

    corners = corner_copies()
    zeroth = copies(e1a, e1a, s1, h1, send0, recv0, 6, 7, 4)
    first = copies(e1a, e1a, s1, h1, send1, recv1, 0, 3, 4)
    rest = copies(e1a, e1a, s1, h1, send4, recv4, 3, 6, 4, REACH - 1)
    second = copies(e2a, e2a, s2, h2, send2, recv2, reach=REACH - 1)
    third = copies(rqa, rqa, s3, h3, send3, recv3, 0, 3, 4, 1, REACH)
    outer = copies(rqa, rqa, s3, h3, sendq, recvq, 3, 6, 2, REACH - 1, REACH)
    wedges = wedge_copies()
    pl.semaphore_wait(barrier, count - 1)
    begin(zeroth)
    begin(corners)
    begin(first)
    begin(rest)
    finish_recv(zeroth, recv0)
    corner_unpack(corners)

    def open0(i, _):
        e1b[6, 2 * i], e1b[6, 2 * i + 1] = unpack(h1, 6, i)
        return 0

    def open1(i, _):
        for ch in range(6):
            e1b[ch, 2 * i], e1b[ch, 2 * i + 1] = unpack(h1, ch, i)
        return 0

    lax.fori_loop(0, (X + 2 * HALO) // 2, open0, 0)

    def link(w, other):
        return jnp.where(jnp.minimum(w, other) > 0.0, 0.5 * (w + other), 0.0)

    not_last, not_first = lane < 127, lane > 0

    def coefficients(x, _):
        wa, wb = e1a[6, x], e1b[6, x]
        ya, yb = up_y(wa, wb)
        da, db = down_y(wa, wb)
        for w, wu, wd, yu, yd, dg, kc in (
            (wa, e1a[6, x + 1], e1a[6, x - 1], ya, da, dga, kca),
            (wb, e1b[6, x + 1], e1b[6, x - 1], yb, db, dgb, kcb),
        ):
            zu = jnp.where(not_last, up_z(w), 0.0)
            zd = jnp.where(not_first, down_z(w), 0.0)
            kc[0, x] = link(w, wu)
            kc[1, x] = link(w, yu)
            kc[2, x] = link(w, yd)
            kc[3, x] = link(w, zu)
            kc[4, x] = link(w, zd)
            sx = w + 0.5 * (wu + wd)
            sy = w + 0.5 * (yu + yd)
            sz = w + 0.5 * (zu + zd)
            every = MASS_TERM + SPRING_SHEAR * (sx + sy + sz)
            dg[0, x] = every + SHEAR_REST * sx
            dg[1, x] = every + SHEAR_REST * sy
            dg[2, x] = every + SHEAR_REST * sz
        return 0

    kca[0, HALO - REACH] = link(e1a[6, HALO - REACH], e1a[6, HALO - REACH + 1])
    kcb[0, HALO - REACH] = link(e1b[6, HALO - REACH], e1b[6, HALO - REACH + 1])
    lax.fori_loop(HALO - 2, HALO + X + 2, coefficients, 0)
    finish_recv(first, recv1)
    finish_recv(rest, recv4)
    begin(second)
    lax.fori_loop(0, (X + 2 * HALO) // 2, open1, 0)

    def operate(x, va, vb, base, both=True):
        result = []
        coef = [[kc[j, x] for j in range(5)] + [kc[0, x - 1]] for kc in (kca, kcb)]
        for c in range(3):
            a, b = va[base + c, x], vb[base + c, x]
            ua, ub = up_y(a, b)
            la, lb = down_y(a, b)
            pair = []
            halves = ((a, va, ua, la, coef[0], dga), (b, vb, ub, lb, coef[1], dgb))
            for v, ref, u, l, k, dg in halves if both else halves[:1]:
                parts = (
                    k[0] * ref[base + c, x + 1] + k[5] * ref[base + c, x - 1],
                    k[1] * u + k[2] * l,
                    k[3] * up_z(v) + k[4] * down_z(v),
                )
                every = parts[0] + parts[1] + parts[2]
                pair.append(dg[c, x] * v - (SPRING_SHEAR * every + SHEAR_REST * parts[c]))
            result.append(pair)
        return result

    def solve(step, va, vb, rhs_of, ship_halo=None):
        def residual(i, _):
            done = []
            for x in (2 * i, 2 * i + 1):
                image = operate(x, va, vb, 0)
                for c in range(3):
                    ra, rb = rhs_of(c, x)
                    done.append((c, x, ra - image[c][0], rb - image[c][1]))
            for c, x, ra, rb in done:
                rqa[c, x] = ra
                rqb[c, x] = rb
            return 0

        lax.fori_loop((HALO - 2) // 2, (HALO + X + 2) // 2, residual, 0)

        def put(x, image):
            for c in range(3):
                rqa[3 + c, x] = image[c][0]
                rqb[3 + c, x] = image[c][1]

        def apply(i, sums):
            rr, rq = sums
            at = (2 * i, 2 * i + 1)
            images = [operate(x, rqa, rqb, 0) for x in at]
            for x, image in zip(at, images):
                for c in range(3):
                    r = rqa[c, x]
                    rr, rq = rr + r * r, rq + r * image[c][0]
            for x, image in zip(at, images):
                put(x, image)
            return rr, rq

        zero = jnp.zeros((8, 128), jnp.float32)
        images = [operate(x, rqa, rqb, 0) for x in (HALO - 1, HALO + X)]
        put(HALO - 1, images[0])
        put(HALO + X, images[1])
        rr, rq = lax.fori_loop(HALO // 2, (HALO + X) // 2, apply, (zero, zero))
        if ship_halo is not None:
            ship_halo()
        rr, rq = total(rr), total(rq)
        mu = jnp.where(rr > 0.0, rq / jnp.where(rr > 0.0, rr, 1.0), 0.0)

        def centred(i, sums):
            ww, wr, mix, wt = sums
            for x in (2 * i, 2 * i + 1):
                image = operate(x, rqa, rqb, 3, False)
                for c in range(3):
                    r, q, s = rqa[c, x], rqa[3 + c, x], image[c][0]
                    w, t = q - mu * r, s - mu * q
                    ww, wr, mix, wt = ww + w * w, wr + w * r, mix + (r * t + w * q), wt + w * t
            return ww, wr, mix, wt

        sums = lax.fori_loop(HALO // 2, (HALO + X) // 2, centred, (zero,) * 4)
        ww, wr, mix, wt = [total(v) for v in sums]
        one = lax.broadcasted_iota(jnp.int32, (1, 128), 1)
        row = jnp.zeros((1, 128), jnp.float32)
        for at, value in enumerate((rr, rq, mu, ww, wr, mix, wt)):
            row = jnp.where(one == at, value, row)
        gath[step, me] = row

        for other in others:
            pltpu.make_async_remote_copy(
                src_ref=gath.at[step, me], dst_ref=gath.at[step, me], send_sem=asend.at[step], recv_sem=arecv.at[step],
                device_id=other, device_id_type=MESH).start()

    def collect(step):
        block = gath.at[step, pl.ds(0, count - 1)]
        pltpu.make_async_copy(block, block, arecv.at[step]).wait()
        table = gath[step].reshape(count, 128)
        rr, rq, mu, ww, wr, mix, wt = [table[:, at:at + 1] for at in range(7)]

        def down(v):
            return jnp.sum(v, axis=0, keepdims=True)

        norm = down(rr)
        alpha = norm / down(rq)
        rest = 1.0 - alpha * mu
        after = down(alpha * alpha * ww - 2.0 * alpha * rest * wr + rest * rest * rr)
        curved = down(rest * rest * rq - alpha * rest * mix + alpha * alpha * wt)
        ratio = after / norm
        beta = after / (curved - ratio * after / alpha)
        return alpha + beta * (1.0 + ratio), -beta * alpha

    def drain(step):
        block = gath.at[step, pl.ds(0, count - 1)]
        pltpu.make_async_copy(block, block, asend.at[step]).wait()

    def joined(c, x, near, far):
        r, q = rqa[c, x], rqa[3 + c, x]
        return jnp.where(sub == 3, pltpu.roll(r, near, 0), jnp.where(sub == 4, pltpu.roll(r, far, 0), q))

    def split(c, x, tile, row, near, far):
        r = rqb[c, x]
        rqb[c, x] = jnp.where(sub == row, pltpu.roll(tile, near, 0), jnp.where(sub == 7 - row, pltpu.roll(tile, far, 0), r))
        rqb[3 + c, x] = tile

    def ship_halo():
        def pack3(i, _):
            x = HALO + 2 * i
            for c in range(3):
                pack(s3, c, i, joined(c, x, 1, 7), joined(c, x + 1, 1, 7))
            return 0

        lax.fori_loop(0, X // 2, pack3, 0)
        for end, x in ((0, HALO), (1, HALO + X - 2)):
            for c in range(3):
                even, odd = [joined(c, x + o, 2, 6) if o == end else joined(c, x + o, 3, 5) for o in range(2)]
                k3[0, end, c, 0] = jnp.where(upper, even, pltpu.roll(odd, 4, 0))
                k3[1, end, c, 0] = jnp.where(upper, pltpu.roll(even, 4, 0), odd)
        begin(third)
        begin(wedges)
        begin(outer)

    solve(0, e1a, e1b, lambda c, x: (e1a[3 + c, x], e1b[3 + c, x]), ship_halo)
    finish_recv(second, recv2)

    def open2(i, _):
        for ch in range(3):
            e2b[ch, 2 * i], e2b[ch, 2 * i + 1] = unpack(h2, ch, i)
        return 0

    lax.fori_loop(0, (X + 2 * HALO) // 2, open2, 0)
    finish_recv(third, recv3)
    for at, (ds, dg) in enumerate(steps[4:]):
        back = wedges[3 - at][2]

        @pl.when(inside(ds, dg))
        def _():
            back.wait_recv()

    def open3(i, _):
        for c in range(3):
            even, odd = unpack(h3, c, i)
            split(c, 2 * i, even, 2, 7, 1)
            split(c, 2 * i + 1, odd, 2, 7, 1)
        return 0

    lax.fori_loop(HALO // 2, (HALO + X) // 2, open3, 0)
    for pair, one in ((HALO // 2 - 1, 1), ((HALO + X) // 2, 0)):
        for c in range(3):
            for o, tile in enumerate(unpack(h3, c, pair)):
                if o == one:
                    split(c, 2 * pair + o, tile, 1, 6, 2)
                else:
                    split(c, 2 * pair + o, tile, 0, 5, 3)
    finish_recv(outer, recvq)
    c0, c1 = collect(0)

    def step1(x, both=True):
        for c in range(3):
            u1a[c, x] = e1a[c, x] + (c0 * rqa[c, x] + c1 * rqa[3 + c, x])
            u1b[c, x] = e1b[c, x] + (c0 * rqb[c, x] + c1 * rqb[3 + c, x]) if both else jnp.zeros((8, 128), jnp.float32)

    def step1_pair(i, _):
        step1(2 * i)
        step1(2 * i + 1)
        return 0

    lax.fori_loop(HALO // 2 - 1, (HALO + X) // 2 + 1, step1_pair, 0)
    step1(HALO - REACH, False)
    step1(HALO + X + REACH - 1, False)
    finish_send(zeroth)
    finish_send(corners)
    finish_send(rest)
    finish_send(first)
    finish_send(second)
    finish_send(third)
    finish_send(outer)
    finish_send(wedges)

    def rhs2(c, x):
        return (MASS_TERM * (2.0 * u1a[c, x] - e1a[c, x]) + e2a[c, x],
                MASS_TERM * (2.0 * u1b[c, x] - e1b[c, x]) + e2b[c, x])

    solve(1, u1a, u1b, rhs2)
    c0, c1 = collect(1)

    def step2(x, _):
        for c in range(3):
            va = u1a[c, x] + (c0 * rqa[c, x] + c1 * rqa[3 + c, x])
            vb = u1b[c, x] + (c0 * rqb[c, x] + c1 * rqb[3 + c, x])
            u1a[c, x] = va
            u1b[c, x] = vb
        return 0

    step2(HALO - 1, 0)
    step2(HALO + X, 0)

    def step2_own(i, _):
        for x in (2 * i, 2 * i + 1):
            step2(x, 0)
            for c in range(3):
                v = u1a[c, x]
                disp_ref[c, x - HALO] = v
                rows[c, pl.ds(x - HALO, 8, stride=X), :] = v
        return 0

    lax.fori_loop(HALO // 2, (HALO + X) // 2, step2_own, 0)
    zrows = coef_ref.shape[2]
    nt = (((1,), (1,)), ((), ()))

    def halves(v):
        high = v.astype(jnp.bfloat16)
        return high, (v - high.astype(jnp.float32)).astype(jnp.bfloat16)

    def transform(c, _):
        high, low = halves(rows[c])
        turned = lax.dot_general(cz_ref[:, 0:256], jnp.concatenate([high, low], axis=1), nt,
                                 preferred_element_type=jnp.float32)
        turned += lax.dot_general(cz_ref[:, 256:384], high, nt, preferred_element_type=jnp.float32)
        for j in range(ns):
            outb[j, c] = turned[j * zrows:(j + 1) * zrows]
        return 0

    def trade(part, i):
        to = lax.rem(si + i, ns)
        return pltpu.make_async_remote_copy(
            src_ref=outb.at[to, pl.ds(3 * part, 3)], dst_ref=inb.at[si, pl.ds(3 * part, 3)],
            send_sem=tsend.at[part, i], recv_sem=trecv.at[part, i],
            device_id=(to, gi), device_id_type=MESH)

    trades = [[trade(part, i) for i in range(1, ns)] for part in range(2)]

    def ship(part):
        lax.fori_loop(3 * part, 3 * part + 3, transform, 0)
        for copy in trades[part]:
            copy.start()
        for c in range(3 * part, 3 * part + 3):
            inb[si, c] = outb[si, c]

    fetched[7].wait()
    ship(0)

    def finals(i, _):
        for x in (2 * i, 2 * i + 1):
            at = x - HALO
            scale = SPRING_NORMAL * carry[at] * 0.5
            a1, a2, b1 = u1a[1, x], u1a[2, x], u1b[1, x]
            dx = u1a[0, x + 1] - u1a[0, x - 1]
            dy = up_y(a1, b1)[0] - down_y(a1, b1)[0]
            dz = jnp.where(not_last, up_z(a2), 0.0) - jnp.where(not_first, down_z(a2), 0.0)
            for c, d in enumerate((dx, dy, dz)):
                rows[3 + c, pl.ds(at, 8, stride=X), :] = scale * d
        return 0

    lax.fori_loop(HALO // 2, (HALO + X) // 2, finals, 0)
    ship(1)
    fetched[8].wait()

    zlane = lax.broadcasted_iota(jnp.int32, (zrows, 128), 1)
    c1t, c3t = float(np.sqrt(0.5) * np.cos(np.pi / 8)), float(np.sqrt(0.5) * np.cos(3 * np.pi / 8))

    def gather_back(c, _):
        pieces = [inb[j, c] for j in range(ns)]
        gap = ns // 2
        while gap:
            keep = (zlane // (X * gap)) % 2 == 0
            mixed = list(pieces)
            for j in range(ns):
                if (j // gap) % 2 == 0:
                    a, b = pieces[j], pieces[j + gap]
                    mixed[j] = jnp.where(keep, a, pltpu.roll(b, X * gap, 1))
                    mixed[j + gap] = jnp.where(keep, pltpu.roll(a, 128 - X * gap, 1), b)
            pieces = mixed
            gap //= 2
        coded = []
        for b in range(Y // 4):
            v0, v1, v2, v3 = pieces[4 * b:4 * b + 4]
            s03, s12, d03, d12 = v0 + v3, v1 + v2, v0 - v3, v1 - v2
            coded += [0.5 * (s03 + s12), c1t * d03 + c3t * d12, 0.5 * (s03 - s12), c3t * d03 - c1t * d12]
        high, low = halves(jnp.concatenate(coded, axis=0))
        done = jnp.dot(jnp.concatenate([high, low], axis=1), gt_ref[...], preferred_element_type=jnp.float32)
        coef_ref[c] = (done[:, 0:128] + done[:, 128:256]).reshape(Y, zrows, 128)
        return 0

    for part in range(2):
        for copy in trades[part]:
            copy.wait_recv()
        for c in range(3 * part, 3 * part + 3):
            gather_back(c, 0)
    drain(0)
    drain(1)
    for part in range(2):
        for copy in trades[part]:
            copy.wait_send()


def store(disp_in, coef_in, disp_out, coef_out, sems):
    copies = [pltpu.make_async_copy(disp_in, disp_out, sems.at[0]), pltpu.make_async_copy(coef_in, coef_out, sems.at[1])]
    for copy in copies:
        copy.start()
    for copy in copies:
        copy.wait()


def fused(mesh, u_now, u_prev, force, stiffness, broken, flags):
    ns, ng = mesh.shape["slab"], mesh.shape["grp"]
    _, X, Y, Z = u_now.shape
    xe, pairs, half = X + 2 * HALO, X // 2 + HALO, X // 2
    zrows = Z // ns
    ez = jnp.asarray(np.kron(np.eye(Z // 4), np.ones((1, 4))), jnp.float32)
    czh, czl = split_table(np.kron(np.eye(Z // 4), cosine_table()))
    cz = jnp.asarray(np.concatenate([czh, czh, czl], axis=1), jnp.bfloat16)
    gth, gtl = split_table(wavelet_table(X * ns).T)
    gt = jnp.asarray(np.block([[gth, gtl], [gth, np.zeros_like(gtl)]]), jnp.bfloat16)

    def vm(*shape):
        return pltpu.VMEM(shape, jnp.float32)

    def ext(n):
        return vm(n, xe, Y, Z)

    def stage(n):
        return vm(2, n, half, Y, Z)

    def land(n):
        return vm(2, n, pairs, Y, Z)

    dma = pltpu.SemaphoreType.DMA
    shapes = (u_now.shape, (6, Y, zrows, X * ns))
    operands = [pltpu.with_memory_space_constraint(v, pltpu.HBM)
                for v in (u_now, u_prev, force, stiffness, broken, flags, ez, cz, gt)]
    results = pl.pallas_call(
        lambda *refs: kernel(ns, ng, *refs),
        name="lattice",
        out_shape=tuple(vm(*shape) for shape in shapes),
        in_specs=[pl.BlockSpec(memory_space=pltpu.MemorySpace.HBM)] * 9,
        out_specs=(pl.BlockSpec(memory_space=pltpu.VMEM),) * 2,
        scratch_shapes=[
            vm(*u_now.shape), vm(*u_now.shape), vm(*u_now.shape), vm(*stiffness.shape),
            pltpu.VMEM(broken.shape, broken.dtype), pltpu.VMEM(flags.shape, flags.dtype),
            vm(*ez.shape), pltpu.VMEM(cz.shape, cz.dtype), pltpu.VMEM(gt.shape, gt.dtype), pltpu.SemaphoreType.DMA((9,)),
            ext(7), ext(7), stage(7), land(7),
            ext(3), ext(3), stage(3), land(3),
            ext(6), ext(6), stage(3), land(3), vm(2, 2, 3, 1, Y, Z),
            ext(3), ext(3), vm(X, Y, Z), ext(3), ext(3), ext(5), ext(5),
            vm(2, ns * ng, 1, 128), vm(6, Y * X, Z), vm(ns, 6, zrows, 128), vm(ns, 6, zrows, 128),
            vm(2, 2, 4, Y, Z), vm(2, 2, 4, Y, Z), dma((4,)), dma((4,)), dma((4,)), dma((4,)),
            dma((4,)), dma((4,)), dma((4,)), dma((4,)), dma((8,)), dma((8,)), dma((4,)), dma((4,)), dma((2,)), dma((2,)), dma((4,)), dma((4,)),
            dma((2,)), dma((2,)), dma((2, ns)), dma((2, ns)),
        ],
        compiler_params=pltpu.CompilerParams(collective_id=0, has_side_effects=True, vmem_limit_bytes=24 << 20),
    )(*operands)
    return pl.pallas_call(
        store,
        name="store",
        out_shape=tuple(jax.ShapeDtypeStruct(shape, jnp.float32) for shape in shapes),
        in_specs=[pl.BlockSpec(memory_space=pltpu.VMEM)] * 2,
        out_specs=(pl.BlockSpec(memory_space=pltpu.MemorySpace.HBM),) * 2,
        scratch_shapes=[dma((2,))],
        compiler_params=pltpu.CompilerParams(vmem_limit_bytes=1 << 20),
    )(*[pltpu.with_memory_space_constraint(v, pltpu.VMEM) for v in results])


def fits(mesh, shape):
    ns, ng = mesh.shape["slab"], mesh.shape["grp"]
    x, y, z = shape[1] // ns, shape[2] // ng, shape[3]
    return y == 8 and z == 128 and x * y == 128 and x * ns == 128 and z % (8 * ns) == 0


def entry(mesh, *args):
    ns, ng = mesh.shape["slab"], mesh.shape["grp"]
    _, x, y, z = args[0].shape
    if fits(mesh, (3, x * ns, y * ng, z)):
        return fused(mesh, *args)
    return body(*args)


def solution(mesh):
    return jax.shard_map(
        lambda *args: entry(mesh, *args),
        mesh=mesh,
        in_specs=(
            P(None, "slab", "grp", None),
            P(None, "slab", "grp", None),
            P(None, "slab", "grp", None),
            P("slab", "grp", None),
            P("slab", "grp", None),
            P("slab", "grp", None),
        ),
        out_specs=(P(None, "slab", "grp", None), P(None, "grp", "slab", None)),
        check_vma=False,
    )
```

```python
import jax
import jax.numpy as jnp
import numpy as np
from jax import lax
from jax.experimental import pallas as pl
from jax.experimental.pallas import tpu as pltpu
from jax.sharding import PartitionSpec as P

STEPS = 2
ITERS = 2
LEVELS = 3


SPRING_NORMAL = 1.0
SPRING_SHEAR = 0.4
MASS_TERM = 1.0
CRACK_CUT = 0.9


def with_halo(block, sides, width):
    for axis, dim in sides:
        count = lax.axis_size(axis)
        forward = [(i, i + 1) for i in range(count - 1)]
        backward = [(target, source) for source, target in forward]
        low = lax.ppermute(
            lax.slice_in_dim(block, block.shape[dim] - width, None, axis=dim), axis, forward
        )
        high = lax.ppermute(lax.slice_in_dim(block, 0, width, axis=dim), axis, backward)
        block = jnp.concatenate([low, block, high], axis=dim)
    return block


def cosine_table():
    freq = np.arange(4)[:, None]
    place = np.arange(4)[None, :]
    factor = np.where(freq == 0, 0.5, np.sqrt(0.5))
    return factor * np.cos(np.pi * (2 * place + 1) * freq / 8.0)


def block_table(count):
    return jnp.asarray(np.kron(np.eye(count // 4), cosine_table()), jnp.float32)


def spread(mask):
    values = mask.astype(jnp.float32)
    size_a, size_b, size_c = values.shape
    wide = jnp.broadcast_to(values[:, None, :, None, :, None], (size_a, 4, size_b, 4, size_c, 4))
    return wide.reshape(size_a * 4, size_b * 4, size_c * 4)


def sides(padded, axis_index):
    leading = padded.ndim - 3

    def cut(offset):
        index_list = [slice(None)] * leading + [slice(1, -1)] * 3
        length = padded.shape[leading + axis_index]
        index_list[leading + axis_index] = slice(1 + offset, length - 1 + offset)
        return padded[tuple(index_list)]

    return (cut(1), cut(-1))


def springs(field, weight, field_pad, weight_pad):
    result = MASS_TERM * field
    for axis_index in range(3):
        upper_v, lower_v = sides(field_pad, axis_index)
        upper_w, lower_w = sides(weight_pad, axis_index)
        k_upper = 0.5 * (weight + upper_w)
        k_lower = 0.5 * (weight + lower_w)
        change = k_upper * (field - upper_v) + k_lower * (field - lower_v)
        coupling = jnp.array(
            [SPRING_NORMAL if comp == axis_index else SPRING_SHEAR for comp in range(3)],
            jnp.float32,
        ).reshape(3, 1, 1, 1)
        result = result + coupling * change
    return result


def faces(field):
    padded = with_halo(field, (("slab", 1), ("grp", 2)), 1)
    return jnp.pad(padded, ((0, 0), (0, 0), (0, 0), (1, 1)))


def stresses(carry, field_pad):
    rows_out = []
    for axis_index in range(3):
        upper_v, lower_v = sides(field_pad, axis_index)
        rows_out.append(SPRING_NORMAL * carry * 0.5 * (upper_v[axis_index] - lower_v[axis_index]))
    return jnp.stack(rows_out)


def paired_sum(residual, image):
    return lax.psum((jnp.sum(residual * residual), jnp.sum(residual * image)), ("slab", "grp"))


def lift(signal):
    even = signal[..., 0::2]
    odd = signal[..., 1::2]
    detail = odd - 0.5 * (even + jnp.roll(even, -1, axis=-1))
    approx = even + 0.25 * (jnp.roll(detail, 1, axis=-1) + detail)
    return (approx, detail)


def wavelet(signal):
    pieces = []
    approx = signal
    for level_index in range(LEVELS):
        approx, detail = lift(approx)
        pieces.insert(0, detail)
    return jnp.concatenate([approx] + pieces, axis=-1)


def body(u_now, u_prev, force, stiffness, broken, flags):
    weight = stiffness * (1.0 - CRACK_CUT * spread(broken))
    carry = spread(flags) * weight
    weight_pad = with_halo(weight, (("slab", 0), ("grp", 1)), 1)
    weight_pad = jnp.pad(weight_pad, ((0, 0), (0, 0), (1, 1)))

    def operate(field):
        return springs(field, weight, faces(field), weight_pad)

    for step_index in range(STEPS):
        rhs = MASS_TERM * (2.0 * u_now - u_prev) + force
        guess = u_now
        residual = rhs - operate(guess)
        image = operate(residual)
        norm_now, product = paired_sum(residual, image)
        alpha = norm_now / product
        direction, along = (residual, image)
        for turn_index in range(ITERS):
            guess = guess + alpha * direction
            residual = residual - alpha * along
            if turn_index + 1 < ITERS:
                image = operate(residual)
                norm_next, product = paired_sum(residual, image)
                ratio = norm_next / norm_now
                alpha = norm_next / (product - ratio * norm_next / alpha)
                direction = residual + ratio * direction
                along = image + ratio * along
                norm_now = norm_next
        u_prev = u_now
        u_now = guess
    stress = stresses(carry, faces(u_now))
    fields = jnp.concatenate([u_now, stress], axis=0)
    table_x = block_table(fields.shape[1])
    table_y = block_table(fields.shape[2])
    table_z = block_table(fields.shape[3])
    blockc = jnp.einsum("ax,hxyz->hayz", table_x, fields, precision=lax.Precision.HIGHEST)
    blockc = jnp.einsum("by,hxyz->hxbz", table_y, blockc, precision=lax.Precision.HIGHEST)
    blockc = jnp.einsum("hxyz,cz->hxyc", blockc, table_z, precision=lax.Precision.HIGHEST)
    moved = jnp.transpose(blockc, (0, 2, 3, 1))
    shipped = lax.all_to_all(moved, "slab", split_axis=2, concat_axis=3, tiled=True)
    coeffs = wavelet(shipped)
    return (u_now, coeffs)


MESH = pl.DeviceIdType.MESH
HALO = 4
REACH = 3
SHEAR_REST = SPRING_NORMAL - SPRING_SHEAR


def wavelet_table(count):
    table = np.kron(np.eye(count // 4), cosine_table())
    pieces = []
    approx = table
    for level_index in range(LEVELS):
        even, odd = approx[0::2], approx[1::2]
        detail = odd - 0.5 * (even + np.roll(even, -1, axis=0))
        approx = even + 0.25 * (np.roll(detail, 1, axis=0) + detail)
        pieces.insert(0, detail)
    return np.concatenate([approx] + pieces, axis=0)


def split_table(table):
    high = table.astype(jnp.bfloat16).astype(np.float64)
    return high, (table - high).astype(jnp.bfloat16).astype(np.float64)


def sub_index():
    return lax.broadcasted_iota(jnp.int32, (8, 128), 0)


def lane_index():
    return lax.broadcasted_iota(jnp.int32, (8, 128), 1)


def up_y(a, b):
    ra, rb = pltpu.roll(a, 7, 0), pltpu.roll(b, 7, 0)
    last = sub_index() == 7
    return jnp.where(last, rb, ra), jnp.where(last, ra, rb)


def down_y(a, b):
    ra, rb = pltpu.roll(a, 1, 0), pltpu.roll(b, 1, 0)
    first = sub_index() == 0
    return jnp.where(first, rb, ra), jnp.where(first, ra, rb)


def up_z(v):
    return pltpu.roll(v, 127, 1)


def down_z(v):
    return pltpu.roll(v, 1, 1)


def total(v):
    return jnp.sum(jnp.sum(v, axis=0, keepdims=True), axis=1, keepdims=True)


def kernel(ns, ng, u_in, p_in, f_in, k_in, br_in, fl_in, ez_in, gt_in,
           disp_ref, coef_ref,
           u_ref, p_ref, f_ref, k_ref, br_ref, fl_ref, ez_ref, gt_ref, isem,
           e1a, e1b, s1, h1, e2a, e2b, s2, h2, rqa, rqb, s3, h3, k3,
           u1a, u1b, scale, dga, dgb, kca, kcb, gath, rows, outb, inb, outx, inx, work,
           ctake, cland, csend, crecv, send4, recv4, send0, recv0, send1, recv1, send2, recv2, send3, recv3, sendq, recvq, sendk, recvk, asend, arecv, tsend, trecv):
    X, Y, Z = u_ref.shape[1:]
    si, gi = lax.axis_index("slab"), lax.axis_index("grp")
    me = si * ng + gi
    count = ns * ng
    fetched = []
    for at, (source, target) in enumerate((
        (br_in, br_ref), (fl_in, fl_ref), (ez_in, ez_ref), (k_in, k_ref), (u_in, u_ref), (p_in, p_ref),
        (f_in, f_ref), (gt_in, gt_ref),
    )):
        fetch = pltpu.make_async_copy(source, target, isem.at[at])
        fetch.start()
        fetched.append(fetch)
    barrier = pltpu.get_barrier_semaphore()

    others = []
    for k in sorted(range(ns), key=lambda k: -min(k, ns - k)):
        for g in range(ng):
            if k or g:
                others.append((lax.rem(si + k, ns), lax.rem(gi + g, ng)))
    for other in others:
        pl.semaphore_signal(barrier, inc=1, device_id=other, device_id_type=MESH)

    sub, lane = sub_index(), lane_index()
    upper = sub < 4

    steps = [(-1, 0), (1, 0), (0, -1), (0, 1), (-1, -1), (-1, 1), (1, -1), (1, 1)]

    def inside(ds, dg):
        ok = None
        if ds:
            ok = (si >= 1) if ds < 0 else (si <= ns - 2)
        if dg:
            more = (gi >= 1) if dg < 0 else (gi <= ng - 2)
            ok = more if ok is None else jnp.logical_and(ok, more)
        return ok

    def copies(ea, dst_a, stage, land, send, recv, low=0, high=None, ways=8, reach=REACH, depth=None):
        depth = reach if depth is None else depth
        half = X // 2
        edge = HALO // 2
        made = []
        chans = pl.ds(low, (ea.shape[0] if high is None else high) - low)
        for at, (ds, dg) in enumerate(steps[:ways]):
            if dg == 0:
                if ds < 0:
                    source = ea.at[chans, pl.ds(HALO + depth - reach, reach)]
                    target = dst_a.at[chans, pl.ds(HALO + X + depth - reach, reach)]
                else:
                    source = ea.at[chans, pl.ds(HALO + X - depth, reach)]
                    target = dst_a.at[chans, pl.ds(HALO - depth, reach)]
            else:
                side = 0 if dg < 0 else 1
                if ds == 0:
                    source, target = stage.at[side, chans], land.at[side, chans, pl.ds(edge, half)]
                elif ds < 0:
                    source = stage.at[side, chans, pl.ds(0, 1)]
                    target = land.at[side, chans, pl.ds(edge + half, 1)]
                else:
                    source = stage.at[side, chans, pl.ds(half - 1, 1)]
                    target = land.at[side, chans, pl.ds(edge - 1, 1)]
            made.append((ds, dg, pltpu.make_async_remote_copy(
                src_ref=source, dst_ref=target, send_sem=send.at[at], recv_sem=recv.at[at ^ 1 if at < 4 else 11 - at],
                device_id=(si + ds, gi + dg), device_id_type=MESH)))
        return made

    def begin(made):
        for ds, dg, copy in made:
            @pl.when(inside(ds, dg))
            def _():
                copy.start()

    def finish_recv(made, recv):
        for at, (ds, dg) in enumerate(steps[:len(made)]):
            back = made[at ^ 1 if at < 4 else 11 - at][2]

            @pl.when(inside(ds, dg))
            def _():
                back.wait_recv()

    def finish_send(made):
        for ds, dg, copy in made:
            @pl.when(inside(ds, dg))
            def _():
                copy.wait_send()

    def blank(dst_a, land):
        zero_a = jnp.zeros((dst_a.shape[0], HALO) + dst_a.shape[2:], jnp.float32)
        half, edge = X // 2, HALO // 2
        zero_l = jnp.zeros((land.shape[1], edge, 8, 128), jnp.float32)

        @pl.when(si == 0)
        def _():
            dst_a[:, pl.ds(0, HALO)] = zero_a
            for side in range(2):
                land[side, :, pl.ds(0, edge)] = zero_l

        @pl.when(si == ns - 1)
        def _():
            dst_a[:, pl.ds(HALO + X, HALO)] = zero_a
            for side in range(2):
                land[side, :, pl.ds(edge + half, edge)] = zero_l

        for side, edge_here in ((0, gi == ng - 1), (1, gi == 0)):
            @pl.when(edge_here)
            def _(side=side):
                land[side] = jnp.zeros(land.shape[1:], jnp.float32)

    def pack(stage, ch, pair, even, odd):
        stage[0, ch, pair] = jnp.where(upper, even, pltpu.roll(odd, 4, 0))
        stage[1, ch, pair] = jnp.where(upper, pltpu.roll(even, 4, 0), odd)

    def unpack(land, ch, pair):
        high, low = land[0, ch, pair], land[1, ch, pair]
        return (jnp.where(upper, high, pltpu.roll(low, 4, 0)),
                jnp.where(upper, pltpu.roll(high, 4, 0), low))

    def spread_rows(mask):
        wide = jnp.dot(mask.astype(jnp.float32), ez_ref[...], preferred_element_type=jnp.float32)
        return jnp.where(upper, jnp.broadcast_to(wide[0:1], (8, 128)), jnp.broadcast_to(wide[1:2], (8, 128)))

    for at in range(4):
        fetched[at].wait()
    for bx in range(X // 4):
        cut = 1.0 - CRACK_CUT * spread_rows(br_ref[bx])
        flag = spread_rows(fl_ref[bx])
        for at in range(4):
            x = bx * 4 + at
            w = k_ref[x] * cut
            e1a[6, HALO + x] = w
            rows[3, pl.ds(x, 8, stride=X), :] = (SPRING_NORMAL * 0.5) * (flag * w)

    def own(i, _):
        for c in range(3):
            tiles = []
            for o in range(2):
                x = 2 * i + o
                u = u_ref[c, x]
                f = f_ref[c, x]
                rhs = MASS_TERM * (2.0 * u - p_ref[c, x]) + f
                e1a[c, HALO + x] = u
                e1a[3 + c, HALO + x] = rhs
                e2a[c, HALO + x] = f
                tiles.append((u, rhs, f))
            pack(s1, c, i, tiles[0][0], tiles[1][0])
            pack(s1, 3 + c, i, tiles[0][1], tiles[1][1])
            pack(s2, c, i, tiles[0][2], tiles[1][2])
        pack(s1, 6, i, e1a[6, HALO + 2 * i], e1a[6, HALO + 2 * i + 1])
        return 0

    for at in range(4, 7):
        fetched[at].wait()
    lax.fori_loop(0, X // 2, own, 0)
    blank(e1a, h1)
    blank(e2a, h2)
    blank(rqa, h3)

    zrows = Z // ns

    def turn_out(value, out):
        turned = value.T
        for j in range(ns):
            out[j] = turned[j * zrows:(j + 1) * zrows]
        return turned

    def spread_out(source, target, at):
        for i in range(1, ns):
            to = lax.rem(si + i, ns)
            pltpu.make_async_remote_copy(
                src_ref=source.at[to], dst_ref=target.at[si], send_sem=tsend.at[at], recv_sem=trecv.at[at],
                device_id=(to, gi), device_id_type=MESH).start()

    def landed(target, sem):
        block = target.at[pl.ds(0, ns - 1)]
        pltpu.make_async_copy(block, block, sem).wait()

    def regroup(pieces):
        lanes = lax.broadcasted_iota(jnp.int32, pieces[0].shape, 1)
        gap = ns // 2
        while gap:
            keep = (lanes // (X * gap)) % 2 == 0
            mixed = list(pieces)
            for j in range(ns):
                if (j // gap) % 2 == 0:
                    a, b = pieces[j], pieces[j + gap]
                    mixed[j] = jnp.where(keep, a, pltpu.roll(b, X * gap, 1))
                    mixed[j + gap] = jnp.where(keep, pltpu.roll(a, 128 - X * gap, 1), b)
            pieces = mixed
            gap //= 2
        return pieces

    def wedge_copies():
        made = []
        for at, (ds, dg) in enumerate(steps[4:]):
            side, end = (0 if dg < 0 else 1), (0 if ds < 0 else 1)
            pair = HALO // 2 + X // 2 if ds < 0 else HALO // 2 - 1
            made.append((ds, dg, pltpu.make_async_remote_copy(
                src_ref=k3.at[side, end], dst_ref=h3.at[side, :, pl.ds(pair, 1)],
                send_sem=sendk.at[at], recv_sem=recvk.at[3 - at],
                device_id=(si + ds, gi + dg), device_id_type=MESH)))
        return made

    def corner_copies():
        made = []
        for at, (ds, dg) in enumerate(steps[4:]):
            side, end = (0 if dg < 0 else 1), (0 if ds < 0 else 1)
            made.append((ds, dg, pltpu.make_async_remote_copy(
                src_ref=ctake.at[side, end], dst_ref=cland.at[side, 1 - end],
                send_sem=csend.at[at], recv_sem=crecv.at[3 - at],
                device_id=(si + ds, gi + dg), device_id_type=MESH)))
        return made

    near = sub % 4 < 2
    for side in range(2):
        for end in range(2):
            for t in range((7 + 1) // 2):
                tile = s1[side, 2 * t, end * (X // 2 - 1)]
                if 2 * t + 1 < 7:
                    other = s1[side, 2 * t + 1, end * (X // 2 - 1)]
                    tile = (jnp.where(near, tile, pltpu.roll(other, 2, 0)) if side == 0
                            else jnp.where(near, pltpu.roll(other, 6, 0), tile))
                ctake[side, end, t] = tile

    def corner_unpack(made):
        for at, (ds, dg) in enumerate(steps[4:]):
            side, end = (0 if dg > 0 else 1), (1 if ds > 0 else 0)
            pair = HALO // 2 + X // 2 if ds > 0 else HALO // 2 - 1
            back = made[3 - at][2]

            @pl.when(inside(ds, dg))
            def _():
                back.wait_recv()
                for ch in range(7):
                    tile = cland[side, end, ch // 2]
                    h1[side, ch, pair] = tile if ch % 2 == 0 else pltpu.roll(tile, 6 if side == 0 else 2, 0)

    corners = corner_copies()
    zeroth = copies(e1a, e1a, s1, h1, send0, recv0, 6, 7, 4)
    first = copies(e1a, e1a, s1, h1, send1, recv1, 0, 3, 4)
    rest = copies(e1a, e1a, s1, h1, send4, recv4, 3, 6, 4, REACH - 1)
    second = copies(e2a, e2a, s2, h2, send2, recv2, reach=REACH - 1)
    third = copies(rqa, rqa, s3, h3, send3, recv3, 0, 3, 4, 1, REACH)
    outer = copies(rqa, rqa, s3, h3, sendq, recvq, 3, 6, 2, REACH - 1, REACH)
    wedges = wedge_copies()
    pl.semaphore_wait(barrier, count - 1)
    begin(zeroth)
    begin(corners)
    begin(first)
    begin(rest)
    turn_out(rows[3], outb.at[3])
    inb[3, si] = outb[3, si]
    finish_recv(zeroth, recv0)
    corner_unpack(corners)

    def open0(i, _):
        e1b[6, 2 * i], e1b[6, 2 * i + 1] = unpack(h1, 6, i)
        return 0

    def open1(i, _):
        for ch in range(6):
            e1b[ch, 2 * i], e1b[ch, 2 * i + 1] = unpack(h1, ch, i)
        return 0

    lax.fori_loop(0, (X + 2 * HALO) // 2, open0, 0)

    def link(w, other):
        return jnp.where(jnp.minimum(w, other) > 0.0, 0.5 * (w + other), 0.0)

    not_last, not_first = lane < 127, lane > 0

    def coefficients(x, _):
        wa, wb = e1a[6, x], e1b[6, x]
        ya, yb = up_y(wa, wb)
        da, db = down_y(wa, wb)
        for w, wu, wd, yu, yd, dg, kc in (
            (wa, e1a[6, x + 1], e1a[6, x - 1], ya, da, dga, kca),
            (wb, e1b[6, x + 1], e1b[6, x - 1], yb, db, dgb, kcb),
        ):
            zu = jnp.where(not_last, up_z(w), 0.0)
            zd = jnp.where(not_first, down_z(w), 0.0)
            kc[0, x] = link(w, wu)
            kc[1, x] = link(w, yu)
            kc[2, x] = link(w, yd)
            kc[3, x] = link(w, zu)
            kc[4, x] = link(w, zd)
            sx = w + 0.5 * (wu + wd)
            sy = w + 0.5 * (yu + yd)
            sz = w + 0.5 * (zu + zd)
            every = MASS_TERM + SPRING_SHEAR * (sx + sy + sz)
            dg[0, x] = every + SHEAR_REST * sx
            dg[1, x] = every + SHEAR_REST * sy
            dg[2, x] = every + SHEAR_REST * sz
        return 0

    kca[0, HALO - REACH] = link(e1a[6, HALO - REACH], e1a[6, HALO - REACH + 1])
    kcb[0, HALO - REACH] = link(e1b[6, HALO - REACH], e1b[6, HALO - REACH + 1])
    lax.fori_loop(HALO - 2, HALO + X + 2, coefficients, 0)
    finish_recv(first, recv1)
    finish_recv(rest, recv4)
    begin(second)
    spread_out(outb.at[3], inb.at[3], 3)
    lax.fori_loop(0, (X + 2 * HALO) // 2, open1, 0)

    def operate(x, va, vb, base, both=True):
        result = []
        coef = [[kc[j, x] for j in range(5)] + [kc[0, x - 1]] for kc in (kca, kcb)]
        for c in range(3):
            a, b = va[base + c, x], vb[base + c, x]
            ua, ub = up_y(a, b)
            la, lb = down_y(a, b)
            pair = []
            halves = ((a, va, ua, la, coef[0], dga), (b, vb, ub, lb, coef[1], dgb))
            for v, ref, u, l, k, dg in halves if both else halves[:1]:
                parts = (
                    k[0] * ref[base + c, x + 1] + k[5] * ref[base + c, x - 1],
                    k[1] * u + k[2] * l,
                    k[3] * up_z(v) + k[4] * down_z(v),
                )
                every = parts[0] + parts[1] + parts[2]
                pair.append(dg[c, x] * v - (SPRING_SHEAR * every + SHEAR_REST * parts[c]))
            result.append(pair)
        return result

    def solve(step, va, vb, rhs_of, ship_halo=None):
        def residual(i, _):
            done = []
            for x in (2 * i, 2 * i + 1):
                image = operate(x, va, vb, 0)
                for c in range(3):
                    ra, rb = rhs_of(c, x)
                    done.append((c, x, ra - image[c][0], rb - image[c][1]))
            for c, x, ra, rb in done:
                rqa[c, x] = ra
                rqb[c, x] = rb
            return 0

        lax.fori_loop((HALO - 2) // 2, (HALO + X + 2) // 2, residual, 0)

        def put(x, image):
            for c in range(3):
                rqa[3 + c, x] = image[c][0]
                rqb[3 + c, x] = image[c][1]

        def apply(i, sums):
            rr, rq = sums
            at = (2 * i, 2 * i + 1)
            images = [operate(x, rqa, rqb, 0) for x in at]
            for x, image in zip(at, images):
                for c in range(3):
                    r = rqa[c, x]
                    rr, rq = rr + r * r, rq + r * image[c][0]
            for x, image in zip(at, images):
                put(x, image)
            return rr, rq

        zero = jnp.zeros((8, 128), jnp.float32)
        images = [operate(x, rqa, rqb, 0) for x in (HALO - 1, HALO + X)]
        put(HALO - 1, images[0])
        put(HALO + X, images[1])
        rr, rq = lax.fori_loop(HALO // 2, (HALO + X) // 2, apply, (zero, zero))
        if ship_halo is not None:
            ship_halo()
        rr, rq = total(rr), total(rq)
        mu = jnp.where(rr > 0.0, rq / jnp.where(rr > 0.0, rr, 1.0), 0.0)

        def centred(i, sums):
            ww, wr, mix, wt = sums
            for x in (2 * i, 2 * i + 1):
                image = operate(x, rqa, rqb, 3, False)
                for c in range(3):
                    r, q, s = rqa[c, x], rqa[3 + c, x], image[c][0]
                    w, t = q - mu * r, s - mu * q
                    ww, wr, mix, wt = ww + w * w, wr + w * r, mix + (r * t + w * q), wt + w * t
            return ww, wr, mix, wt

        sums = lax.fori_loop(HALO // 2, (HALO + X) // 2, centred, (zero,) * 4)
        ww, wr, mix, wt = [total(v) for v in sums]
        one = lax.broadcasted_iota(jnp.int32, (1, 128), 1)
        row = jnp.zeros((1, 128), jnp.float32)
        for at, value in enumerate((rr, rq, mu, ww, wr, mix, wt)):
            row = jnp.where(one == at, value, row)
        gath[step, me] = row

        for other in others:
            pltpu.make_async_remote_copy(
                src_ref=gath.at[step, me], dst_ref=gath.at[step, me], send_sem=asend.at[step], recv_sem=arecv.at[step],
                device_id=other, device_id_type=MESH).start()

    def collect(step):
        block = gath.at[step, pl.ds(0, count - 1)]
        pltpu.make_async_copy(block, block, arecv.at[step]).wait()
        table = gath[step].reshape(count, 128)
        rr, rq, mu, ww, wr, mix, wt = [table[:, at:at + 1] for at in range(7)]

        def down(v):
            return jnp.sum(v, axis=0, keepdims=True)

        norm = down(rr)
        alpha = norm / down(rq)
        rest = 1.0 - alpha * mu
        after = down(alpha * alpha * ww - 2.0 * alpha * rest * wr + rest * rest * rr)
        curved = down(rest * rest * rq - alpha * rest * mix + alpha * alpha * wt)
        ratio = after / norm
        beta = after / (curved - ratio * after / alpha)
        return alpha + beta * (1.0 + ratio), -beta * alpha

    def drain(step):
        block = gath.at[step, pl.ds(0, count - 1)]
        pltpu.make_async_copy(block, block, asend.at[step]).wait()

    def joined(c, x, near, far):
        r, q = rqa[c, x], rqa[3 + c, x]
        return jnp.where(sub == 3, pltpu.roll(r, near, 0), jnp.where(sub == 4, pltpu.roll(r, far, 0), q))

    def split(c, x, tile, row, near, far):
        r = rqb[c, x]
        rqb[c, x] = jnp.where(sub == row, pltpu.roll(tile, near, 0), jnp.where(sub == 7 - row, pltpu.roll(tile, far, 0), r))
        rqb[3 + c, x] = tile

    def ship_halo():
        def pack3(i, _):
            x = HALO + 2 * i
            for c in range(3):
                pack(s3, c, i, joined(c, x, 1, 7), joined(c, x + 1, 1, 7))
            return 0

        lax.fori_loop(0, X // 2, pack3, 0)
        for end, x in ((0, HALO), (1, HALO + X - 2)):
            for c in range(3):
                even, odd = [joined(c, x + o, 2, 6) if o == end else joined(c, x + o, 3, 5) for o in range(2)]
                k3[0, end, c, 0] = jnp.where(upper, even, pltpu.roll(odd, 4, 0))
                k3[1, end, c, 0] = jnp.where(upper, pltpu.roll(even, 4, 0), odd)
        begin(third)
        begin(wedges)
        begin(outer)

    solve(0, e1a, e1b, lambda c, x: (e1a[3 + c, x], e1b[3 + c, x]), ship_halo)
    finish_recv(second, recv2)

    def open2(i, _):
        for ch in range(3):
            e2b[ch, 2 * i], e2b[ch, 2 * i + 1] = unpack(h2, ch, i)
        return 0

    lax.fori_loop(0, (X + 2 * HALO) // 2, open2, 0)
    finish_recv(third, recv3)
    for at, (ds, dg) in enumerate(steps[4:]):
        back = wedges[3 - at][2]

        @pl.when(inside(ds, dg))
        def _():
            back.wait_recv()

    def open3(i, _):
        for c in range(3):
            even, odd = unpack(h3, c, i)
            split(c, 2 * i, even, 2, 7, 1)
            split(c, 2 * i + 1, odd, 2, 7, 1)
        return 0

    lax.fori_loop(HALO // 2, (HALO + X) // 2, open3, 0)
    for pair, one in ((HALO // 2 - 1, 1), ((HALO + X) // 2, 0)):
        for c in range(3):
            for o, tile in enumerate(unpack(h3, c, pair)):
                if o == one:
                    split(c, 2 * pair + o, tile, 1, 6, 2)
                else:
                    split(c, 2 * pair + o, tile, 0, 5, 3)
    finish_recv(outer, recvq)
    c0, c1 = collect(0)

    def step1(x, both=True):
        for c in range(3):
            u1a[c, x] = e1a[c, x] + (c0 * rqa[c, x] + c1 * rqa[3 + c, x])
            u1b[c, x] = e1b[c, x] + (c0 * rqb[c, x] + c1 * rqb[3 + c, x]) if both else jnp.zeros((8, 128), jnp.float32)

    def step1_pair(i, _):
        step1(2 * i)
        step1(2 * i + 1)
        return 0

    lax.fori_loop(HALO // 2 - 1, (HALO + X) // 2 + 1, step1_pair, 0)
    step1(HALO - REACH, False)
    step1(HALO + X + REACH - 1, False)
    finish_send(zeroth)
    finish_send(corners)
    finish_send(rest)
    finish_send(first)
    finish_send(second)
    finish_send(third)
    finish_send(outer)
    finish_send(wedges)

    def rhs2(c, x):
        return (MASS_TERM * (2.0 * u1a[c, x] - e1a[c, x]) + e2a[c, x],
                MASS_TERM * (2.0 * u1b[c, x] - e1b[c, x]) + e2b[c, x])

    solve(1, u1a, u1b, rhs2)
    landed(inb.at[3], trecv.at[3])
    for y, piece in enumerate(regroup([inb[3, j] for j in range(ns)])):
        scale[y] = piece
    c0, c1 = collect(1)

    def step2(ra, rb, c, x):
        return ra[c, x] + (c0 * rb[c, x] + c1 * rb[3 + c, x])

    def halves(v):
        high = v.astype(jnp.bfloat16)
        return high, (v - high.astype(jnp.float32)).astype(jnp.bfloat16)

    def finish(c):
        for x in range(X):
            v = step2(u1a, rqa, c, HALO + x)
            disp_ref[c, x] = v
            rows[c, pl.ds(x, 8, stride=X), :] = v
        turned = turn_out(rows[c], outb.at[c])
        spread_out(outb.at[c], inb.at[c], c)
        inb[c, si] = outb[c, si]
        return turned

    def finish_edges(turned):
        for x in range(X):
            rows[4, pl.ds(x, 8, stride=X), :] = step2(u1b, rqb, 1, HALO + x)
        sides_y = rows[4].T
        zero = jnp.zeros((8, 128), jnp.float32)
        for j in range(ns):
            low, high = sides_y[zrows * j:zrows * j + 8], sides_y[zrows * j + 8:zrows * j + 16]
            tile = jnp.where(lane < 32, pltpu.roll(low, 16, 1),
                             jnp.where(lane < 64, pltpu.roll(pltpu.roll(low, 4, 0), 48, 1),
                                       jnp.where(lane < 96, pltpu.roll(high, 80, 1),
                                                 pltpu.roll(pltpu.roll(high, 4, 0), 112, 1))))
            before = pltpu.roll(turned[zrows * j - 8:zrows * j], 5, 0) if j else zero
            after = pltpu.roll(turned[zrows * (j + 1):zrows * (j + 1) + 8], 5, 0) if j + 1 < ns else zero
            outx[j] = jnp.where(sub == 4, before, jnp.where(sub == 5, after, tile))
        spread_out(outx, inx, 4)
        inx[si] = outx[si]

    finish_edges(finish(2))
    finish(0)
    finish(1)
    fetched[7].wait()

    c1t, c3t = float(np.sqrt(0.5) * np.cos(np.pi / 8)), float(np.sqrt(0.5) * np.cos(3 * np.pi / 8))

    def cosine(v0, v1, v2, v3):
        s03, s12, d03, d12 = v0 + v3, v1 + v2, v0 - v3, v1 - v2
        return [0.5 * (s03 + s12), c1t * d03 + c3t * d12, 0.5 * (s03 - s12), c3t * d03 - c1t * d12]

    def encode(ch, fields):
        for b in range(Y // 4):
            for k, v in enumerate(cosine(*fields[4 * b:4 * b + 4])):
                work[ch, (4 * b + k) * zrows:(4 * b + k + 1) * zrows] = v
        parts = []
        for p in range(Y * zrows // 32):
            parts += cosine(*[work[ch, pl.ds(32 * p + n, 8, stride=4), :] for n in range(4)])
        high, low = halves(jnp.concatenate(parts, axis=0))
        done = jnp.dot(jnp.concatenate([high, low], axis=1), gt_ref[...], preferred_element_type=jnp.float32)
        done = done[:, 0:128] + done[:, 128:256]
        for p in range(Y * zrows // 32):
            for n in range(4):
                coef_ref[ch, pl.ds(32 * p + n, 8, stride=4), :] = done[(4 * p + n) * 8:(4 * p + n + 1) * 8]

    def arrived(c):
        landed(inb.at[c], trecv.at[c])
        return regroup([inb[c, j] for j in range(ns)])

    field = arrived(2)
    encode(2, field)
    landed(inx, trecv.at[4])
    edges = regroup([inx[j] for j in range(ns)])
    stress = []
    for y in range(Y):
        low, high = field[y][0:8], field[y][8:16]
        ul, uh, dl, dh = pltpu.roll(low, 7, 0), pltpu.roll(high, 7, 0), pltpu.roll(low, 1, 0), pltpu.roll(high, 1, 0)
        first, last = sub == 0, sub == 7
        low = jnp.where(last, uh, ul) - jnp.where(first, pltpu.roll(edges[y], 4, 0), dl)
        high = jnp.where(last, pltpu.roll(edges[y], 2, 0), uh) - jnp.where(first, dl, dh)
        stress.append(scale[y] * jnp.concatenate([low, high], axis=0))
    encode(5, stress)
    field = arrived(0)
    encode(0, field)
    wide = lax.broadcasted_iota(jnp.int32, (zrows, 128), 1)
    encode(3, [scale[y] * (jnp.where(wide < 127, up_z(field[y]), 0.0) - jnp.where(wide > 0, down_z(field[y]), 0.0))
               for y in range(Y)])
    field = arrived(1)
    encode(1, field)
    outside = []
    for side in range(2):
        quarter = [edges[2 * q + side] for q in range(4)]
        outside.append(jnp.concatenate([jnp.where(upper, quarter[q], pltpu.roll(quarter[q + 1], 4, 0)) for q in (0, 2)], axis=0))
    field = [outside[0]] + field + [outside[1]]
    encode(4, [scale[y] * (field[y + 2] - field[y]) for y in range(Y)])
    drain(0)
    drain(1)
    for at in range(4):
        landed(inb.at[at], tsend.at[at])
    landed(inx, tsend.at[4])


def store(disp_in, coef_in, disp_out, coef_out, sems):
    copies = [pltpu.make_async_copy(disp_in, disp_out, sems.at[0]), pltpu.make_async_copy(coef_in, coef_out, sems.at[1])]
    for copy in copies:
        copy.start()
    for copy in copies:
        copy.wait()


def fused(mesh, u_now, u_prev, force, stiffness, broken, flags):
    ns, ng = mesh.shape["slab"], mesh.shape["grp"]
    _, X, Y, Z = u_now.shape
    xe, pairs, half = X + 2 * HALO, X // 2 + HALO, X // 2
    zrows = Z // ns
    ez = jnp.asarray(np.kron(np.eye(Z // 4), np.ones((1, 4))), jnp.float32)
    gth, gtl = split_table(wavelet_table(X * ns).T)
    gt = jnp.asarray(np.block([[gth, gtl], [gth, np.zeros_like(gtl)]]), jnp.bfloat16)

    def vm(*shape):
        return pltpu.VMEM(shape, jnp.float32)

    def ext(n):
        return vm(n, xe, Y, Z)

    def stage(n):
        return vm(2, n, half, Y, Z)

    def land(n):
        return vm(2, n, pairs, Y, Z)

    dma = pltpu.SemaphoreType.DMA
    shapes = (u_now.shape, (6, Y * zrows, X * ns))
    operands = [pltpu.with_memory_space_constraint(v, pltpu.HBM)
                for v in (u_now, u_prev, force, stiffness, broken, flags, ez, gt)]
    results = pl.pallas_call(
        lambda *refs: kernel(ns, ng, *refs),
        name="lattice",
        out_shape=tuple(vm(*shape) for shape in shapes),
        in_specs=[pl.BlockSpec(memory_space=pltpu.MemorySpace.HBM)] * 8,
        out_specs=(pl.BlockSpec(memory_space=pltpu.VMEM),) * 2,
        scratch_shapes=[
            vm(*u_now.shape), vm(*u_now.shape), vm(*u_now.shape), vm(*stiffness.shape),
            pltpu.VMEM(broken.shape, broken.dtype), pltpu.VMEM(flags.shape, flags.dtype),
            vm(*ez.shape), pltpu.VMEM(gt.shape, gt.dtype), pltpu.SemaphoreType.DMA((8,)),
            ext(7), ext(7), stage(7), land(7),
            ext(3), ext(3), stage(3), land(3),
            ext(6), ext(6), stage(3), land(3), vm(2, 2, 3, 1, Y, Z),
            ext(3), ext(3), vm(Y, zrows, X * ns), ext(3), ext(3), ext(5), ext(5),
            vm(2, ns * ng, 1, 128), vm(5, Y * X, Z), vm(4, ns, zrows, 128), vm(4, ns, zrows, 128), vm(ns, 8, 128), vm(ns, 8, 128), vm(6, Y * zrows, X * ns),
            vm(2, 2, 4, Y, Z), vm(2, 2, 4, Y, Z), dma((4,)), dma((4,)), dma((4,)), dma((4,)),
            dma((4,)), dma((4,)), dma((4,)), dma((4,)), dma((8,)), dma((8,)), dma((4,)), dma((4,)), dma((2,)), dma((2,)), dma((4,)), dma((4,)),
            dma((2,)), dma((2,)), dma((5,)), dma((5,)),
        ],
        compiler_params=pltpu.CompilerParams(collective_id=0, has_side_effects=True, vmem_limit_bytes=24 << 20),
    )(*operands)
    disp, coef = pl.pallas_call(
        store,
        name="store",
        out_shape=tuple(jax.ShapeDtypeStruct(shape, jnp.float32) for shape in shapes),
        in_specs=[pl.BlockSpec(memory_space=pltpu.VMEM)] * 2,
        out_specs=(pl.BlockSpec(memory_space=pltpu.MemorySpace.HBM),) * 2,
        scratch_shapes=[dma((2,))],
        compiler_params=pltpu.CompilerParams(vmem_limit_bytes=1 << 20),
    )(*[pltpu.with_memory_space_constraint(v, pltpu.VMEM) for v in results])
    return disp, coef.reshape(6, Y, zrows, X * ns)


def fits(mesh, shape):
    ns, ng = mesh.shape["slab"], mesh.shape["grp"]
    x, y, z = shape[1] // ns, shape[2] // ng, shape[3]
    return y == 8 and z == 128 and x * y == 128 and x * ns == 128 and z % (8 * ns) == 0


def entry(mesh, *args):
    ns, ng = mesh.shape["slab"], mesh.shape["grp"]
    _, x, y, z = args[0].shape
    if fits(mesh, (3, x * ns, y * ng, z)):
        return fused(mesh, *args)
    return body(*args)


def solution(mesh):
    return jax.shard_map(
        lambda *args: entry(mesh, *args),
        mesh=mesh,
        in_specs=(
            P(None, "slab", "grp", None),
            P(None, "slab", "grp", None),
            P(None, "slab", "grp", None),
            P("slab", "grp", None),
            P("slab", "grp", None),
            P("slab", "grp", None),
        ),
        out_specs=(P(None, "slab", "grp", None), P(None, "grp", "slab", None)),
        check_vma=False,
    )
```

```python
import jax
import jax.numpy as jnp
import numpy as np
from jax import lax
from jax.experimental import pallas as pl
from jax.experimental.pallas import tpu as pltpu
from jax.sharding import PartitionSpec as P

STEPS = 2
ITERS = 2
LEVELS = 3


SPRING_NORMAL = 1.0
SPRING_SHEAR = 0.4
MASS_TERM = 1.0
CRACK_CUT = 0.9


def with_halo(block, sides, width):
    for axis, dim in sides:
        count = lax.axis_size(axis)
        forward = [(i, i + 1) for i in range(count - 1)]
        backward = [(target, source) for source, target in forward]
        low = lax.ppermute(
            lax.slice_in_dim(block, block.shape[dim] - width, None, axis=dim), axis, forward
        )
        high = lax.ppermute(lax.slice_in_dim(block, 0, width, axis=dim), axis, backward)
        block = jnp.concatenate([low, block, high], axis=dim)
    return block


def cosine_table():
    freq = np.arange(4)[:, None]
    place = np.arange(4)[None, :]
    factor = np.where(freq == 0, 0.5, np.sqrt(0.5))
    return factor * np.cos(np.pi * (2 * place + 1) * freq / 8.0)


def block_table(count):
    return jnp.asarray(np.kron(np.eye(count // 4), cosine_table()), jnp.float32)


def spread(mask):
    values = mask.astype(jnp.float32)
    size_a, size_b, size_c = values.shape
    wide = jnp.broadcast_to(values[:, None, :, None, :, None], (size_a, 4, size_b, 4, size_c, 4))
    return wide.reshape(size_a * 4, size_b * 4, size_c * 4)


def sides(padded, axis_index):
    leading = padded.ndim - 3

    def cut(offset):
        index_list = [slice(None)] * leading + [slice(1, -1)] * 3
        length = padded.shape[leading + axis_index]
        index_list[leading + axis_index] = slice(1 + offset, length - 1 + offset)
        return padded[tuple(index_list)]

    return (cut(1), cut(-1))


def springs(field, weight, field_pad, weight_pad):
    result = MASS_TERM * field
    for axis_index in range(3):
        upper_v, lower_v = sides(field_pad, axis_index)
        upper_w, lower_w = sides(weight_pad, axis_index)
        k_upper = 0.5 * (weight + upper_w)
        k_lower = 0.5 * (weight + lower_w)
        change = k_upper * (field - upper_v) + k_lower * (field - lower_v)
        coupling = jnp.array(
            [SPRING_NORMAL if comp == axis_index else SPRING_SHEAR for comp in range(3)],
            jnp.float32,
        ).reshape(3, 1, 1, 1)
        result = result + coupling * change
    return result


def faces(field):
    padded = with_halo(field, (("slab", 1), ("grp", 2)), 1)
    return jnp.pad(padded, ((0, 0), (0, 0), (0, 0), (1, 1)))


def stresses(carry, field_pad):
    rows_out = []
    for axis_index in range(3):
        upper_v, lower_v = sides(field_pad, axis_index)
        rows_out.append(SPRING_NORMAL * carry * 0.5 * (upper_v[axis_index] - lower_v[axis_index]))
    return jnp.stack(rows_out)


def paired_sum(residual, image):
    return lax.psum((jnp.sum(residual * residual), jnp.sum(residual * image)), ("slab", "grp"))


def lift(signal):
    even = signal[..., 0::2]
    odd = signal[..., 1::2]
    detail = odd - 0.5 * (even + jnp.roll(even, -1, axis=-1))
    approx = even + 0.25 * (jnp.roll(detail, 1, axis=-1) + detail)
    return (approx, detail)


def wavelet(signal):
    pieces = []
    approx = signal
    for level_index in range(LEVELS):
        approx, detail = lift(approx)
        pieces.insert(0, detail)
    return jnp.concatenate([approx] + pieces, axis=-1)


def body(u_now, u_prev, force, stiffness, broken, flags):
    weight = stiffness * (1.0 - CRACK_CUT * spread(broken))
    carry = spread(flags) * weight
    weight_pad = with_halo(weight, (("slab", 0), ("grp", 1)), 1)
    weight_pad = jnp.pad(weight_pad, ((0, 0), (0, 0), (1, 1)))

    def operate(field):
        return springs(field, weight, faces(field), weight_pad)

    for step_index in range(STEPS):
        rhs = MASS_TERM * (2.0 * u_now - u_prev) + force
        guess = u_now
        residual = rhs - operate(guess)
        image = operate(residual)
        norm_now, product = paired_sum(residual, image)
        alpha = norm_now / product
        direction, along = (residual, image)
        for turn_index in range(ITERS):
            guess = guess + alpha * direction
            residual = residual - alpha * along
            if turn_index + 1 < ITERS:
                image = operate(residual)
                norm_next, product = paired_sum(residual, image)
                ratio = norm_next / norm_now
                alpha = norm_next / (product - ratio * norm_next / alpha)
                direction = residual + ratio * direction
                along = image + ratio * along
                norm_now = norm_next
        u_prev = u_now
        u_now = guess
    stress = stresses(carry, faces(u_now))
    fields = jnp.concatenate([u_now, stress], axis=0)
    table_x = block_table(fields.shape[1])
    table_y = block_table(fields.shape[2])
    table_z = block_table(fields.shape[3])
    blockc = jnp.einsum("ax,hxyz->hayz", table_x, fields, precision=lax.Precision.HIGHEST)
    blockc = jnp.einsum("by,hxyz->hxbz", table_y, blockc, precision=lax.Precision.HIGHEST)
    blockc = jnp.einsum("hxyz,cz->hxyc", blockc, table_z, precision=lax.Precision.HIGHEST)
    moved = jnp.transpose(blockc, (0, 2, 3, 1))
    shipped = lax.all_to_all(moved, "slab", split_axis=2, concat_axis=3, tiled=True)
    coeffs = wavelet(shipped)
    return (u_now, coeffs)


MESH = pl.DeviceIdType.MESH
HALO = 4
REACH = 3
SHEAR_REST = SPRING_NORMAL - SPRING_SHEAR
WIDE_R, WIDE_A, WIDE_C, WIDE_K = 10, 8, 8, 10


def wavelet_table(count):
    table = np.kron(np.eye(count // 4), cosine_table())
    pieces = []
    approx = table
    for level_index in range(LEVELS):
        even, odd = approx[0::2], approx[1::2]
        detail = odd - 0.5 * (even + np.roll(even, -1, axis=0))
        approx = even + 0.25 * (np.roll(detail, 1, axis=0) + detail)
        pieces.insert(0, detail)
    return np.concatenate([approx] + pieces, axis=0)


def split_table(table):
    high = table.astype(jnp.bfloat16).astype(np.float64)
    return high, (table - high).astype(jnp.bfloat16).astype(np.float64)


def sub_index():
    return lax.broadcasted_iota(jnp.int32, (8, 128), 0)


def lane_index():
    return lax.broadcasted_iota(jnp.int32, (8, 128), 1)


def up_y(a, b):
    ra, rb = pltpu.roll(a, 7, 0), pltpu.roll(b, 7, 0)
    last = sub_index() == 7
    return jnp.where(last, rb, ra), jnp.where(last, ra, rb)


def down_y(a, b):
    ra, rb = pltpu.roll(a, 1, 0), pltpu.roll(b, 1, 0)
    first = sub_index() == 0
    return jnp.where(first, rb, ra), jnp.where(first, ra, rb)


def up_z(v):
    return pltpu.roll(v, 127, 1)


def down_z(v):
    return pltpu.roll(v, 1, 1)


def total(v):
    return jnp.sum(jnp.sum(v, axis=0, keepdims=True), axis=1, keepdims=True)


def kernel(ns, ng, u_in, p_in, f_in, k_in, br_in, fl_in, ez_in, gt_in,
           disp_ref, coef_ref,
           u_ref, p_ref, f_ref, k_ref, br_ref, fl_ref, ez_ref, gt_ref, isem,
           e1a, e1b, s1, h1, e2a, e2b, s2, h2, rqa, rqb, s3, h3, k3,
           u1a, u1b, scale, dga, dgb, kca, kcb, gath, rows, outb, inb, outx, inx, work,
           ctake, cland, csend, crecv, send4, recv4, send0, recv0, send1, recv1, send2, recv2, send3, recv3, sendq, recvq, sendk, recvk, asend, arecv, tsend, trecv):
    X, Y, Z = u_ref.shape[1:]
    si, gi = lax.axis_index("slab"), lax.axis_index("grp")
    me = si * ng + gi
    count = ns * ng
    fetched = []
    for at, (source, target) in enumerate((
        (br_in, br_ref), (fl_in, fl_ref), (ez_in, ez_ref), (k_in, k_ref), (u_in, u_ref), (p_in, p_ref),
        (f_in, f_ref), (gt_in, gt_ref),
    )):
        fetch = pltpu.make_async_copy(source, target, isem.at[at])
        fetch.start()
        fetched.append(fetch)
    barrier = pltpu.get_barrier_semaphore()

    others = []
    for k in sorted(range(ns), key=lambda k: -min(k, ns - k)):
        for g in range(ng):
            if k or g:
                others.append((lax.rem(si + k, ns), lax.rem(gi + g, ng)))
    for other in others:
        pl.semaphore_signal(barrier, inc=1, device_id=other, device_id_type=MESH)

    sub, lane = sub_index(), lane_index()
    upper = sub < 4

    steps = [(-1, 0), (1, 0), (0, -1), (0, 1), (-1, -1), (-1, 1), (1, -1), (1, 1)]

    def inside(ds, dg):
        ok = None
        if ds:
            ok = (si >= 1) if ds < 0 else (si <= ns - 2)
        if dg:
            more = (gi >= 1) if dg < 0 else (gi <= ng - 2)
            ok = more if ok is None else jnp.logical_and(ok, more)
        return ok

    def copies(ea, dst_a, stage, land, send, recv, low=0, high=None, ways=8, reach=REACH, depth=None):
        depth = reach if depth is None else depth
        half = X // 2
        edge = HALO // 2
        made = []
        chans = pl.ds(low, (ea.shape[0] if high is None else high) - low)
        for at, (ds, dg) in enumerate(steps[:ways]):
            if dg == 0:
                if ds < 0:
                    source = ea.at[chans, pl.ds(HALO + depth - reach, reach)]
                    target = dst_a.at[chans, pl.ds(HALO + X + depth - reach, reach)]
                else:
                    source = ea.at[chans, pl.ds(HALO + X - depth, reach)]
                    target = dst_a.at[chans, pl.ds(HALO - depth, reach)]
            else:
                side = 0 if dg < 0 else 1
                if ds == 0:
                    source, target = stage.at[side, chans], land.at[side, chans, pl.ds(edge, half)]
                elif ds < 0:
                    source = stage.at[side, chans, pl.ds(0, 1)]
                    target = land.at[side, chans, pl.ds(edge + half, 1)]
                else:
                    source = stage.at[side, chans, pl.ds(half - 1, 1)]
                    target = land.at[side, chans, pl.ds(edge - 1, 1)]
            made.append((ds, dg, pltpu.make_async_remote_copy(
                src_ref=source, dst_ref=target, send_sem=send.at[at], recv_sem=recv.at[at ^ 1 if at < 4 else 11 - at],
                device_id=(si + ds, gi + dg), device_id_type=MESH)))
        return made

    def begin(made):
        for ds, dg, copy in made:
            @pl.when(inside(ds, dg))
            def _():
                copy.start()

    def finish_recv(made, recv):
        for at, (ds, dg) in enumerate(steps[:len(made)]):
            back = made[at ^ 1 if at < 4 else 11 - at][2]

            @pl.when(inside(ds, dg))
            def _():
                back.wait_recv()

    def finish_send(made):
        for ds, dg, copy in made:
            @pl.when(inside(ds, dg))
            def _():
                copy.wait_send()

    def blank(dst_a, land):
        zero_a = jnp.zeros((dst_a.shape[0], HALO) + dst_a.shape[2:], jnp.float32)
        half, edge = X // 2, HALO // 2
        zero_l = jnp.zeros((land.shape[1], edge, 8, 128), jnp.float32)

        @pl.when(si == 0)
        def _():
            dst_a[:, pl.ds(0, HALO)] = zero_a
            for side in range(2):
                land[side, :, pl.ds(0, edge)] = zero_l

        @pl.when(si == ns - 1)
        def _():
            dst_a[:, pl.ds(HALO + X, HALO)] = zero_a
            for side in range(2):
                land[side, :, pl.ds(edge + half, edge)] = zero_l

        for side, edge_here in ((0, gi == ng - 1), (1, gi == 0)):
            @pl.when(edge_here)
            def _(side=side):
                land[side] = jnp.zeros(land.shape[1:], jnp.float32)

    def pack(stage, ch, pair, even, odd):
        stage[0, ch, pair] = jnp.where(upper, even, pltpu.roll(odd, 4, 0))
        stage[1, ch, pair] = jnp.where(upper, pltpu.roll(even, 4, 0), odd)

    def unpack(land, ch, pair):
        high, low = land[0, ch, pair], land[1, ch, pair]
        return (jnp.where(upper, high, pltpu.roll(low, 4, 0)),
                jnp.where(upper, pltpu.roll(high, 4, 0), low))

    def spread_rows(mask):
        wide = jnp.dot(mask.astype(jnp.float32), ez_ref[...], preferred_element_type=jnp.float32)
        return jnp.where(upper, jnp.broadcast_to(wide[0:1], (8, 128)), jnp.broadcast_to(wide[1:2], (8, 128)))

    for at in range(4):
        fetched[at].wait()
    for bx in range(X // 4):
        cut = 1.0 - CRACK_CUT * spread_rows(br_ref[bx])
        flag = spread_rows(fl_ref[bx])
        for at in range(4):
            x = bx * 4 + at
            w = k_ref[x] * cut
            e1a[6, HALO + x] = w
            rows[3, pl.ds(x, 8, stride=X), :] = (SPRING_NORMAL * 0.5) * (flag * w)

    def own(i, _):
        for c in range(3):
            tiles = []
            for o in range(2):
                x = 2 * i + o
                u = u_ref[c, x]
                f = f_ref[c, x]
                rhs = MASS_TERM * (2.0 * u - p_ref[c, x]) + f
                e1a[c, HALO + x] = u
                e1a[3 + c, HALO + x] = rhs
                e2a[c, HALO + x] = f
                tiles.append((u, rhs, f))
            pack(s1, c, i, tiles[0][0], tiles[1][0])
            pack(s1, 3 + c, i, tiles[0][1], tiles[1][1])
            pack(s2, c, i, tiles[0][2], tiles[1][2])
        pack(s1, 6, i, e1a[6, HALO + 2 * i], e1a[6, HALO + 2 * i + 1])
        return 0

    for at in range(4, 7):
        fetched[at].wait()
    lax.fori_loop(0, X // 2, own, 0)
    blank(e1a, h1)
    blank(e2a, h2)
    blank(rqa, h3)

    zrows = Z // ns

    def turn_out(value, out):
        turned = value.T
        for j in range(ns):
            out[j] = turned[j * zrows:(j + 1) * zrows]
        return turned

    def spread_out(source, target, at):
        for i in range(1, ns):
            to = lax.rem(si + i, ns)
            pltpu.make_async_remote_copy(
                src_ref=source.at[to], dst_ref=target.at[si], send_sem=tsend.at[at], recv_sem=trecv.at[at],
                device_id=(to, gi), device_id_type=MESH).start()

    def landed(target, sem):
        block = target.at[pl.ds(0, ns - 1)]
        pltpu.make_async_copy(block, block, sem).wait()

    def regroup(pieces):
        lanes = lax.broadcasted_iota(jnp.int32, pieces[0].shape, 1)
        gap = ns // 2
        while gap:
            keep = (lanes // (X * gap)) % 2 == 0
            mixed = list(pieces)
            for j in range(ns):
                if (j // gap) % 2 == 0:
                    a, b = pieces[j], pieces[j + gap]
                    mixed[j] = jnp.where(keep, a, pltpu.roll(b, X * gap, 1))
                    mixed[j + gap] = jnp.where(keep, pltpu.roll(a, 128 - X * gap, 1), b)
            pieces = mixed
            gap //= 2
        return pieces

    def wedge_copies():
        made = []
        for at, (ds, dg) in enumerate(steps[4:]):
            side, end = (0 if dg < 0 else 1), (0 if ds < 0 else 1)
            pair = HALO // 2 + X // 2 if ds < 0 else HALO // 2 - 1
            made.append((ds, dg, pltpu.make_async_remote_copy(
                src_ref=k3.at[side, end], dst_ref=h3.at[side, :, pl.ds(pair, 1)],
                send_sem=sendk.at[at], recv_sem=recvk.at[3 - at],
                device_id=(si + ds, gi + dg), device_id_type=MESH)))
        return made

    def corner_copies():
        made = []
        for at, (ds, dg) in enumerate(steps[4:]):
            side, end = (0 if dg < 0 else 1), (0 if ds < 0 else 1)
            made.append((ds, dg, pltpu.make_async_remote_copy(
                src_ref=ctake.at[side, end], dst_ref=cland.at[side, 1 - end],
                send_sem=csend.at[at], recv_sem=crecv.at[3 - at],
                device_id=(si + ds, gi + dg), device_id_type=MESH)))
        return made

    near = sub % 4 < 2
    for side in range(2):
        for end in range(2):
            for t in range((7 + 1) // 2):
                tile = s1[side, 2 * t, end * (X // 2 - 1)]
                if 2 * t + 1 < 7:
                    other = s1[side, 2 * t + 1, end * (X // 2 - 1)]
                    tile = (jnp.where(near, tile, pltpu.roll(other, 2, 0)) if side == 0
                            else jnp.where(near, pltpu.roll(other, 6, 0), tile))
                ctake[side, end, t] = tile

    def corner_unpack(made):
        for at, (ds, dg) in enumerate(steps[4:]):
            side, end = (0 if dg > 0 else 1), (1 if ds > 0 else 0)
            pair = HALO // 2 + X // 2 if ds > 0 else HALO // 2 - 1
            back = made[3 - at][2]

            @pl.when(inside(ds, dg))
            def _():
                back.wait_recv()
                for ch in range(7):
                    tile = cland[side, end, ch // 2]
                    h1[side, ch, pair] = tile if ch % 2 == 0 else pltpu.roll(tile, 6 if side == 0 else 2, 0)

    corners = corner_copies()
    zeroth = copies(e1a, e1a, s1, h1, send0, recv0, 6, 7, 4)
    first = copies(e1a, e1a, s1, h1, send1, recv1, 0, 3, 4)
    rest = copies(e1a, e1a, s1, h1, send4, recv4, 3, 6, 4, REACH - 1)
    second = copies(e2a, e2a, s2, h2, send2, recv2, reach=REACH - 1)
    third = copies(rqa, rqa, s3, h3, send3, recv3, 0, 3, 4, 1, REACH)
    outer = copies(rqa, rqa, s3, h3, sendq, recvq, 3, 6, 2, REACH - 1, REACH)
    wedges = wedge_copies()
    pl.semaphore_wait(barrier, count - 1)
    begin(zeroth)
    begin(corners)
    begin(first)
    begin(rest)
    turn_out(rows[3], outb.at[3])
    inb[3, si] = outb[3, si]
    finish_recv(zeroth, recv0)
    corner_unpack(corners)

    def open0(i, _):
        e1b[6, 2 * i], e1b[6, 2 * i + 1] = unpack(h1, 6, i)
        return 0

    def open1(i, _):
        for ch in range(6):
            e1b[ch, 2 * i], e1b[ch, 2 * i + 1] = unpack(h1, ch, i)
        return 0

    lax.fori_loop(0, (X + 2 * HALO) // 2, open0, 0)

    def link(w, other):
        return jnp.where(jnp.minimum(w, other) > 0.0, (0.5 * SPRING_SHEAR) * (w + other), 0.0)

    not_last, not_first = lane < 127, lane > 0

    def over_rows(low, high, width, body, carried=0):
        width = max(v for v in range(1, width + 1) if (high - low) % v == 0)

        def chunk(i, state):
            return body([low + i * width + o for o in range(width)], state)

        return lax.fori_loop(0, (high - low) // width, chunk, carried)

    def all_coefficients(rows_here, _):
        for x in rows_here:
            coefficients(x)
        return 0

    def coefficients(x):
        wa, wb = e1a[6, x], e1b[6, x]
        ya, yb = up_y(wa, wb)
        da, db = down_y(wa, wb)
        for w, wu, wd, yu, yd, dg, kc in (
            (wa, e1a[6, x + 1], e1a[6, x - 1], ya, da, dga, kca),
            (wb, e1b[6, x + 1], e1b[6, x - 1], yb, db, dgb, kcb),
        ):
            zu = jnp.where(not_last, up_z(w), 0.0)
            zd = jnp.where(not_first, down_z(w), 0.0)
            kc[0, x] = link(w, wu)
            kc[1, x] = link(w, yu)
            kc[2, x] = link(w, yd)
            kc[3, x] = link(w, zu)
            kc[4, x] = link(w, zd)
            sx = w + 0.5 * (wu + wd)
            sy = w + 0.5 * (yu + yd)
            sz = w + 0.5 * (zu + zd)
            every = MASS_TERM + SPRING_SHEAR * (sx + sy + sz)
            dg[0, x] = every + SHEAR_REST * sx
            dg[1, x] = every + SHEAR_REST * sy
            dg[2, x] = every + SHEAR_REST * sz

    kca[0, HALO - REACH] = link(e1a[6, HALO - REACH], e1a[6, HALO - REACH + 1])
    kcb[0, HALO - REACH] = link(e1b[6, HALO - REACH], e1b[6, HALO - REACH + 1])
    over_rows(HALO - 2, HALO + X + 2, WIDE_K, all_coefficients)
    finish_recv(first, recv1)
    finish_recv(rest, recv4)
    begin(second)
    spread_out(outb.at[3], inb.at[3], 3)
    lax.fori_loop(0, (X + 2 * HALO) // 2, open1, 0)

    def operate(x, va, vb, base, both=True):
        result = []
        coef = [[kc[j, x] for j in range(5)] + [kc[0, x - 1]] for kc in (kca, kcb)]
        for c in range(3):
            a, b = va[base + c, x], vb[base + c, x]
            ua, ub = up_y(a, b)
            la, lb = down_y(a, b)
            pair = []
            halves = ((a, va, ua, la, coef[0], dga), (b, vb, ub, lb, coef[1], dgb))
            for v, ref, u, l, k, dg in halves if both else halves[:1]:
                parts = (
                    k[0] * ref[base + c, x + 1] + k[5] * ref[base + c, x - 1],
                    k[1] * u + k[2] * l,
                    k[3] * up_z(v) + k[4] * down_z(v),
                )
                shear = parts[(c + 1) % 3] + parts[(c + 2) % 3]
                pair.append(dg[c, x] * v - (shear + (SPRING_NORMAL / SPRING_SHEAR) * parts[c]))
            result.append(pair)
        return result

    def solve(step, va, vb, rhs_of, ship_halo=None):
        def residual(rows_here, _):
            for x in rows_here:
                image = operate(x, va, vb, 0)
                for c in range(3):
                    ra, rb = rhs_of(c, x)
                    rqa[c, x] = ra - image[c][0]
                    rqb[c, x] = rb - image[c][1]
            return 0

        over_rows(HALO - 2, HALO + X + 2, WIDE_R, residual)

        def put(x, image):
            for c in range(3):
                rqa[3 + c, x] = image[c][0]
                rqb[3 + c, x] = image[c][1]

        def apply(rows_here, sums):
            rr, rq = sums
            for x in rows_here:
                image = operate(x, rqa, rqb, 0)
                for c in range(3):
                    r = rqa[c, x]
                    rr, rq = rr + r * r, rq + r * image[c][0]
                put(x, image)
            return rr, rq

        zero = jnp.zeros((8, 128), jnp.float32)
        images = [operate(x, rqa, rqb, 0) for x in (HALO - 1, HALO + X)]
        put(HALO - 1, images[0])
        put(HALO + X, images[1])
        rr, rq = over_rows(HALO, HALO + X, WIDE_A, apply, (zero, zero))
        if ship_halo is not None:
            ship_halo()
        rr, rq = total(rr), total(rq)
        mu = jnp.where(rr > 0.0, rq / jnp.where(rr > 0.0, rr, 1.0), 0.0)

        def centred(rows_here, sums):
            ww, wr, mix, wt = sums
            for x in rows_here:
                image = operate(x, rqa, rqb, 3, False)
                for c in range(3):
                    r, q, s = rqa[c, x], rqa[3 + c, x], image[c][0]
                    w, t = q - mu * r, s - mu * q
                    ww, wr, mix, wt = ww + w * w, wr + w * r, mix + (r * t + w * q), wt + w * t
            return ww, wr, mix, wt

        sums = over_rows(HALO, HALO + X, WIDE_C, centred, (zero,) * 4)
        ww, wr, mix, wt = [total(v) for v in sums]
        one = lax.broadcasted_iota(jnp.int32, (1, 128), 1)
        row = jnp.zeros((1, 128), jnp.float32)
        for at, value in enumerate((rr, rq, mu, ww, wr, mix, wt)):
            row = jnp.where(one == at, value, row)
        gath[step, me] = row

        for other in others:
            pltpu.make_async_remote_copy(
                src_ref=gath.at[step, me], dst_ref=gath.at[step, me], send_sem=asend.at[step], recv_sem=arecv.at[step],
                device_id=other, device_id_type=MESH).start()

    def collect(step):
        block = gath.at[step, pl.ds(0, count - 1)]
        pltpu.make_async_copy(block, block, arecv.at[step]).wait()
        table = gath[step].reshape(count, 128)
        rr, rq, mu, ww, wr, mix, wt = [table[:, at:at + 1] for at in range(7)]

        def down(v):
            return jnp.sum(v, axis=0, keepdims=True)

        norm = down(rr)
        alpha = norm / down(rq)
        rest = 1.0 - alpha * mu
        after = down(alpha * alpha * ww - 2.0 * alpha * rest * wr + rest * rest * rr)
        curved = down(rest * rest * rq - alpha * rest * mix + alpha * alpha * wt)
        ratio = after / norm
        beta = after / (curved - ratio * after / alpha)
        return alpha + beta * (1.0 + ratio), -beta * alpha

    def drain(step):
        block = gath.at[step, pl.ds(0, count - 1)]
        pltpu.make_async_copy(block, block, asend.at[step]).wait()

    def joined(c, x, near, far):
        r, q = rqa[c, x], rqa[3 + c, x]
        return jnp.where(sub == 3, pltpu.roll(r, near, 0), jnp.where(sub == 4, pltpu.roll(r, far, 0), q))

    def split(c, x, tile, row, near, far):
        r = rqb[c, x]
        rqb[c, x] = jnp.where(sub == row, pltpu.roll(tile, near, 0), jnp.where(sub == 7 - row, pltpu.roll(tile, far, 0), r))
        rqb[3 + c, x] = tile

    def ship_halo():
        def pack3(i, _):
            x = HALO + 2 * i
            for c in range(3):
                pack(s3, c, i, joined(c, x, 1, 7), joined(c, x + 1, 1, 7))
            return 0

        lax.fori_loop(0, X // 2, pack3, 0)
        for end, x in ((0, HALO), (1, HALO + X - 2)):
            for c in range(3):
                even, odd = [joined(c, x + o, 2, 6) if o == end else joined(c, x + o, 3, 5) for o in range(2)]
                k3[0, end, c, 0] = jnp.where(upper, even, pltpu.roll(odd, 4, 0))
                k3[1, end, c, 0] = jnp.where(upper, pltpu.roll(even, 4, 0), odd)
        begin(third)
        begin(wedges)
        begin(outer)

    solve(0, e1a, e1b, lambda c, x: (e1a[3 + c, x], e1b[3 + c, x]), ship_halo)
    finish_recv(second, recv2)

    def open2(i, _):
        for ch in range(3):
            e2b[ch, 2 * i], e2b[ch, 2 * i + 1] = unpack(h2, ch, i)
        return 0

    lax.fori_loop(0, (X + 2 * HALO) // 2, open2, 0)
    finish_recv(third, recv3)
    for at, (ds, dg) in enumerate(steps[4:]):
        back = wedges[3 - at][2]

        @pl.when(inside(ds, dg))
        def _():
            back.wait_recv()

    def open3(i, _):
        for c in range(3):
            even, odd = unpack(h3, c, i)
            split(c, 2 * i, even, 2, 7, 1)
            split(c, 2 * i + 1, odd, 2, 7, 1)
        return 0

    lax.fori_loop(HALO // 2, (HALO + X) // 2, open3, 0)
    for pair, one in ((HALO // 2 - 1, 1), ((HALO + X) // 2, 0)):
        for c in range(3):
            for o, tile in enumerate(unpack(h3, c, pair)):
                if o == one:
                    split(c, 2 * pair + o, tile, 1, 6, 2)
                else:
                    split(c, 2 * pair + o, tile, 0, 5, 3)
    finish_recv(outer, recvq)
    c0, c1 = collect(0)

    def step1(x, both=True):
        for c in range(3):
            u1a[c, x] = e1a[c, x] + (c0 * rqa[c, x] + c1 * rqa[3 + c, x])
            u1b[c, x] = e1b[c, x] + (c0 * rqb[c, x] + c1 * rqb[3 + c, x]) if both else jnp.zeros((8, 128), jnp.float32)

    def step1_pair(i, _):
        step1(2 * i)
        step1(2 * i + 1)
        return 0

    lax.fori_loop(HALO // 2 - 1, (HALO + X) // 2 + 1, step1_pair, 0)
    step1(HALO - REACH, False)
    step1(HALO + X + REACH - 1, False)
    finish_send(zeroth)
    finish_send(corners)
    finish_send(rest)
    finish_send(first)
    finish_send(second)
    finish_send(third)
    finish_send(outer)
    finish_send(wedges)

    def rhs2(c, x):
        return (MASS_TERM * (2.0 * u1a[c, x] - e1a[c, x]) + e2a[c, x],
                MASS_TERM * (2.0 * u1b[c, x] - e1b[c, x]) + e2b[c, x])

    solve(1, u1a, u1b, rhs2)
    landed(inb.at[3], trecv.at[3])
    for y, piece in enumerate(regroup([inb[3, j] for j in range(ns)])):
        scale[y] = piece
    c0, c1 = collect(1)

    def step2(ra, rb, c, x):
        return ra[c, x] + (c0 * rb[c, x] + c1 * rb[3 + c, x])

    def halves(v):
        high = v.astype(jnp.bfloat16)
        return high, (v - high.astype(jnp.float32)).astype(jnp.bfloat16)

    def finish(c):
        for x in range(X):
            v = step2(u1a, rqa, c, HALO + x)
            disp_ref[c, x] = v
            rows[c, pl.ds(x, 8, stride=X), :] = v
        turned = turn_out(rows[c], outb.at[c])
        spread_out(outb.at[c], inb.at[c], c)
        inb[c, si] = outb[c, si]
        return turned

    def finish_edges(turned):
        for x in range(X):
            rows[4, pl.ds(x, 8, stride=X), :] = step2(u1b, rqb, 1, HALO + x)
        sides_y = rows[4].T
        zero = jnp.zeros((8, 128), jnp.float32)
        for j in range(ns):
            low, high = sides_y[zrows * j:zrows * j + 8], sides_y[zrows * j + 8:zrows * j + 16]
            tile = jnp.where(lane < 32, pltpu.roll(low, 16, 1),
                             jnp.where(lane < 64, pltpu.roll(pltpu.roll(low, 4, 0), 48, 1),
                                       jnp.where(lane < 96, pltpu.roll(high, 80, 1),
                                                 pltpu.roll(pltpu.roll(high, 4, 0), 112, 1))))
            before = pltpu.roll(turned[zrows * j - 8:zrows * j], 5, 0) if j else zero
            after = pltpu.roll(turned[zrows * (j + 1):zrows * (j + 1) + 8], 5, 0) if j + 1 < ns else zero
            outx[j] = jnp.where(sub == 4, before, jnp.where(sub == 5, after, tile))
        spread_out(outx, inx, 4)
        inx[si] = outx[si]

    finish_edges(finish(2))
    finish(0)
    finish(1)
    fetched[7].wait()

    c1t, c3t = float(np.sqrt(0.5) * np.cos(np.pi / 8)), float(np.sqrt(0.5) * np.cos(3 * np.pi / 8))

    def cosine(v0, v1, v2, v3):
        s03, s12, d03, d12 = v0 + v3, v1 + v2, v0 - v3, v1 - v2
        return [0.5 * (s03 + s12), c1t * d03 + c3t * d12, 0.5 * (s03 - s12), c3t * d03 - c1t * d12]

    def encode(ch, fields):
        for b in range(Y // 4):
            for k, v in enumerate(cosine(*fields[4 * b:4 * b + 4])):
                work[ch, (4 * b + k) * zrows:(4 * b + k + 1) * zrows] = v
        parts = []
        for p in range(Y * zrows // 32):
            parts += cosine(*[work[ch, pl.ds(32 * p + n, 8, stride=4), :] for n in range(4)])
        high, low = halves(jnp.concatenate(parts, axis=0))
        done = jnp.dot(jnp.concatenate([high, low], axis=1), gt_ref[...], preferred_element_type=jnp.float32)
        done = done[:, 0:128] + done[:, 128:256]
        for p in range(Y * zrows // 32):
            for n in range(4):
                coef_ref[ch, pl.ds(32 * p + n, 8, stride=4), :] = done[(4 * p + n) * 8:(4 * p + n + 1) * 8]

    def arrived(c):
        landed(inb.at[c], trecv.at[c])
        return regroup([inb[c, j] for j in range(ns)])

    field = arrived(2)
    encode(2, field)
    landed(inx, trecv.at[4])
    edges = regroup([inx[j] for j in range(ns)])
    stress = []
    for y in range(Y):
        low, high = field[y][0:8], field[y][8:16]
        ul, uh, dl, dh = pltpu.roll(low, 7, 0), pltpu.roll(high, 7, 0), pltpu.roll(low, 1, 0), pltpu.roll(high, 1, 0)
        first, last = sub == 0, sub == 7
        low = jnp.where(last, uh, ul) - jnp.where(first, pltpu.roll(edges[y], 4, 0), dl)
        high = jnp.where(last, pltpu.roll(edges[y], 2, 0), uh) - jnp.where(first, dl, dh)
        stress.append(scale[y] * jnp.concatenate([low, high], axis=0))
    encode(5, stress)
    field = arrived(0)
    encode(0, field)
    wide = lax.broadcasted_iota(jnp.int32, (zrows, 128), 1)
    encode(3, [scale[y] * (jnp.where(wide < 127, up_z(field[y]), 0.0) - jnp.where(wide > 0, down_z(field[y]), 0.0))
               for y in range(Y)])
    field = arrived(1)
    encode(1, field)
    outside = []
    for side in range(2):
        quarter = [edges[2 * q + side] for q in range(4)]
        outside.append(jnp.concatenate([jnp.where(upper, quarter[q], pltpu.roll(quarter[q + 1], 4, 0)) for q in (0, 2)], axis=0))
    field = [outside[0]] + field + [outside[1]]
    encode(4, [scale[y] * (field[y + 2] - field[y]) for y in range(Y)])
    drain(0)
    drain(1)
    for at in range(4):
        landed(inb.at[at], tsend.at[at])
    landed(inx, tsend.at[4])


def store(disp_in, coef_in, disp_out, coef_out, sems):
    copies = [pltpu.make_async_copy(disp_in, disp_out, sems.at[0]), pltpu.make_async_copy(coef_in, coef_out, sems.at[1])]
    for copy in copies:
        copy.start()
    for copy in copies:
        copy.wait()


def fused(mesh, u_now, u_prev, force, stiffness, broken, flags):
    ns, ng = mesh.shape["slab"], mesh.shape["grp"]
    _, X, Y, Z = u_now.shape
    xe, pairs, half = X + 2 * HALO, X // 2 + HALO, X // 2
    zrows = Z // ns
    ez = jnp.asarray(np.kron(np.eye(Z // 4), np.ones((1, 4))), jnp.float32)
    gth, gtl = split_table(wavelet_table(X * ns).T)
    gt = jnp.asarray(np.block([[gth, gtl], [gth, np.zeros_like(gtl)]]), jnp.bfloat16)

    def vm(*shape):
        return pltpu.VMEM(shape, jnp.float32)

    def ext(n):
        return vm(n, xe, Y, Z)

    def stage(n):
        return vm(2, n, half, Y, Z)

    def land(n):
        return vm(2, n, pairs, Y, Z)

    dma = pltpu.SemaphoreType.DMA
    shapes = (u_now.shape, (6, Y * zrows, X * ns))
    operands = [pltpu.with_memory_space_constraint(v, pltpu.HBM)
                for v in (u_now, u_prev, force, stiffness, broken, flags, ez, gt)]
    results = pl.pallas_call(
        lambda *refs: kernel(ns, ng, *refs),
        name="lattice",
        out_shape=tuple(vm(*shape) for shape in shapes),
        in_specs=[pl.BlockSpec(memory_space=pltpu.MemorySpace.HBM)] * 8,
        out_specs=(pl.BlockSpec(memory_space=pltpu.VMEM),) * 2,
        scratch_shapes=[
            vm(*u_now.shape), vm(*u_now.shape), vm(*u_now.shape), vm(*stiffness.shape),
            pltpu.VMEM(broken.shape, broken.dtype), pltpu.VMEM(flags.shape, flags.dtype),
            vm(*ez.shape), pltpu.VMEM(gt.shape, gt.dtype), pltpu.SemaphoreType.DMA((8,)),
            ext(7), ext(7), stage(7), land(7),
            ext(3), ext(3), stage(3), land(3),
            ext(6), ext(6), stage(3), land(3), vm(2, 2, 3, 1, Y, Z),
            ext(3), ext(3), vm(Y, zrows, X * ns), ext(3), ext(3), ext(5), ext(5),
            vm(2, ns * ng, 1, 128), vm(5, Y * X, Z), vm(4, ns, zrows, 128), vm(4, ns, zrows, 128), vm(ns, 8, 128), vm(ns, 8, 128), vm(6, Y * zrows, X * ns),
            vm(2, 2, 4, Y, Z), vm(2, 2, 4, Y, Z), dma((4,)), dma((4,)), dma((4,)), dma((4,)),
            dma((4,)), dma((4,)), dma((4,)), dma((4,)), dma((8,)), dma((8,)), dma((4,)), dma((4,)), dma((2,)), dma((2,)), dma((4,)), dma((4,)),
            dma((2,)), dma((2,)), dma((5,)), dma((5,)),
        ],
        compiler_params=pltpu.CompilerParams(collective_id=0, has_side_effects=True, vmem_limit_bytes=24 << 20),
    )(*operands)
    disp, coef = pl.pallas_call(
        store,
        name="store",
        out_shape=tuple(jax.ShapeDtypeStruct(shape, jnp.float32) for shape in shapes),
        in_specs=[pl.BlockSpec(memory_space=pltpu.VMEM)] * 2,
        out_specs=(pl.BlockSpec(memory_space=pltpu.MemorySpace.HBM),) * 2,
        scratch_shapes=[dma((2,))],
        compiler_params=pltpu.CompilerParams(vmem_limit_bytes=1 << 20),
    )(*[pltpu.with_memory_space_constraint(v, pltpu.VMEM) for v in results])
    return disp, coef.reshape(6, Y, zrows, X * ns)


def fits(mesh, shape):
    ns, ng = mesh.shape["slab"], mesh.shape["grp"]
    x, y, z = shape[1] // ns, shape[2] // ng, shape[3]
    return y == 8 and z == 128 and x * y == 128 and x * ns == 128 and z % (8 * ns) == 0


def entry(mesh, *args):
    ns, ng = mesh.shape["slab"], mesh.shape["grp"]
    _, x, y, z = args[0].shape
    if fits(mesh, (3, x * ns, y * ng, z)):
        return fused(mesh, *args)
    return body(*args)


def solution(mesh):
    return jax.shard_map(
        lambda *args: entry(mesh, *args),
        mesh=mesh,
        in_specs=(
            P(None, "slab", "grp", None),
            P(None, "slab", "grp", None),
            P(None, "slab", "grp", None),
            P("slab", "grp", None),
            P("slab", "grp", None),
            P("slab", "grp", None),
        ),
        out_specs=(P(None, "slab", "grp", None), P(None, "grp", "slab", None)),
        check_vma=False,
    )
```

```python
import jax
import jax.numpy as jnp
import numpy as np
from jax import lax
from jax.experimental import pallas as pl
from jax.experimental.pallas import tpu as pltpu
from jax.sharding import PartitionSpec as P

STEPS = 2
ITERS = 2
LEVELS = 3


SPRING_NORMAL = 1.0
SPRING_SHEAR = 0.4
MASS_TERM = 1.0
CRACK_CUT = 0.9


def with_halo(block, sides, width):
    for axis, dim in sides:
        count = lax.axis_size(axis)
        forward = [(i, i + 1) for i in range(count - 1)]
        backward = [(target, source) for source, target in forward]
        low = lax.ppermute(
            lax.slice_in_dim(block, block.shape[dim] - width, None, axis=dim), axis, forward
        )
        high = lax.ppermute(lax.slice_in_dim(block, 0, width, axis=dim), axis, backward)
        block = jnp.concatenate([low, block, high], axis=dim)
    return block


def cosine_table():
    freq = np.arange(4)[:, None]
    place = np.arange(4)[None, :]
    factor = np.where(freq == 0, 0.5, np.sqrt(0.5))
    return factor * np.cos(np.pi * (2 * place + 1) * freq / 8.0)


def block_table(count):
    return jnp.asarray(np.kron(np.eye(count // 4), cosine_table()), jnp.float32)


def spread(mask):
    values = mask.astype(jnp.float32)
    size_a, size_b, size_c = values.shape
    wide = jnp.broadcast_to(values[:, None, :, None, :, None], (size_a, 4, size_b, 4, size_c, 4))
    return wide.reshape(size_a * 4, size_b * 4, size_c * 4)


def sides(padded, axis_index):
    leading = padded.ndim - 3

    def cut(offset):
        index_list = [slice(None)] * leading + [slice(1, -1)] * 3
        length = padded.shape[leading + axis_index]
        index_list[leading + axis_index] = slice(1 + offset, length - 1 + offset)
        return padded[tuple(index_list)]

    return (cut(1), cut(-1))


def springs(field, weight, field_pad, weight_pad):
    result = MASS_TERM * field
    for axis_index in range(3):
        upper_v, lower_v = sides(field_pad, axis_index)
        upper_w, lower_w = sides(weight_pad, axis_index)
        k_upper = 0.5 * (weight + upper_w)
        k_lower = 0.5 * (weight + lower_w)
        change = k_upper * (field - upper_v) + k_lower * (field - lower_v)
        coupling = jnp.array(
            [SPRING_NORMAL if comp == axis_index else SPRING_SHEAR for comp in range(3)],
            jnp.float32,
        ).reshape(3, 1, 1, 1)
        result = result + coupling * change
    return result


def faces(field):
    padded = with_halo(field, (("slab", 1), ("grp", 2)), 1)
    return jnp.pad(padded, ((0, 0), (0, 0), (0, 0), (1, 1)))


def stresses(carry, field_pad):
    rows_out = []
    for axis_index in range(3):
        upper_v, lower_v = sides(field_pad, axis_index)
        rows_out.append(SPRING_NORMAL * carry * 0.5 * (upper_v[axis_index] - lower_v[axis_index]))
    return jnp.stack(rows_out)


def paired_sum(residual, image):
    return lax.psum((jnp.sum(residual * residual), jnp.sum(residual * image)), ("slab", "grp"))


def lift(signal):
    even = signal[..., 0::2]
    odd = signal[..., 1::2]
    detail = odd - 0.5 * (even + jnp.roll(even, -1, axis=-1))
    approx = even + 0.25 * (jnp.roll(detail, 1, axis=-1) + detail)
    return (approx, detail)


def wavelet(signal):
    pieces = []
    approx = signal
    for level_index in range(LEVELS):
        approx, detail = lift(approx)
        pieces.insert(0, detail)
    return jnp.concatenate([approx] + pieces, axis=-1)


def body(u_now, u_prev, force, stiffness, broken, flags):
    weight = stiffness * (1.0 - CRACK_CUT * spread(broken))
    carry = spread(flags) * weight
    weight_pad = with_halo(weight, (("slab", 0), ("grp", 1)), 1)
    weight_pad = jnp.pad(weight_pad, ((0, 0), (0, 0), (1, 1)))

    def operate(field):
        return springs(field, weight, faces(field), weight_pad)

    for step_index in range(STEPS):
        rhs = MASS_TERM * (2.0 * u_now - u_prev) + force
        guess = u_now
        residual = rhs - operate(guess)
        image = operate(residual)
        norm_now, product = paired_sum(residual, image)
        alpha = norm_now / product
        direction, along = (residual, image)
        for turn_index in range(ITERS):
            guess = guess + alpha * direction
            residual = residual - alpha * along
            if turn_index + 1 < ITERS:
                image = operate(residual)
                norm_next, product = paired_sum(residual, image)
                ratio = norm_next / norm_now
                alpha = norm_next / (product - ratio * norm_next / alpha)
                direction = residual + ratio * direction
                along = image + ratio * along
                norm_now = norm_next
        u_prev = u_now
        u_now = guess
    stress = stresses(carry, faces(u_now))
    fields = jnp.concatenate([u_now, stress], axis=0)
    table_x = block_table(fields.shape[1])
    table_y = block_table(fields.shape[2])
    table_z = block_table(fields.shape[3])
    blockc = jnp.einsum("ax,hxyz->hayz", table_x, fields, precision=lax.Precision.HIGHEST)
    blockc = jnp.einsum("by,hxyz->hxbz", table_y, blockc, precision=lax.Precision.HIGHEST)
    blockc = jnp.einsum("hxyz,cz->hxyc", blockc, table_z, precision=lax.Precision.HIGHEST)
    moved = jnp.transpose(blockc, (0, 2, 3, 1))
    shipped = lax.all_to_all(moved, "slab", split_axis=2, concat_axis=3, tiled=True)
    coeffs = wavelet(shipped)
    return (u_now, coeffs)


MESH = pl.DeviceIdType.MESH
HALO = 4
REACH = 3
SHEAR_REST = SPRING_NORMAL - SPRING_SHEAR
WIDE_R, WIDE_A, WIDE_C, WIDE_K = 20, 16, 16, 20


def wavelet_table(count):
    table = np.kron(np.eye(count // 4), cosine_table())
    pieces = []
    approx = table
    for level_index in range(LEVELS):
        even, odd = approx[0::2], approx[1::2]
        detail = odd - 0.5 * (even + np.roll(even, -1, axis=0))
        approx = even + 0.25 * (np.roll(detail, 1, axis=0) + detail)
        pieces.insert(0, detail)
    return np.concatenate([approx] + pieces, axis=0)


def split_table(table):
    high = table.astype(jnp.bfloat16).astype(np.float64)
    return high, (table - high).astype(jnp.bfloat16).astype(np.float64)


def sub_index():
    return lax.broadcasted_iota(jnp.int32, (8, 128), 0)


def lane_index():
    return lax.broadcasted_iota(jnp.int32, (8, 128), 1)


def up_y(a, b):
    ra, rb = pltpu.roll(a, 7, 0), pltpu.roll(b, 7, 0)
    last = sub_index() == 7
    return jnp.where(last, rb, ra), jnp.where(last, ra, rb)


def down_y(a, b):
    ra, rb = pltpu.roll(a, 1, 0), pltpu.roll(b, 1, 0)
    first = sub_index() == 0
    return jnp.where(first, rb, ra), jnp.where(first, ra, rb)


def up_z(v):
    return pltpu.roll(v, 127, 1)


def down_z(v):
    return pltpu.roll(v, 1, 1)


def total(v):
    return jnp.sum(jnp.sum(v, axis=0, keepdims=True), axis=1, keepdims=True)


def kernel(ns, ng, u_in, p_in, f_in, k_in, br_in, fl_in, ez_in, gt_in,
           disp_ref, coef_ref,
           u_ref, p_ref, f_ref, k_ref, br_ref, fl_ref, ez_ref, gt_ref, isem,
           e1a, e1b, s1, h1, e2a, e2b, s2, h2, rqa, rqb, s3, h3, k3,
           u1a, u1b, scale, dga, dgb, kca, kcb, known, gath, rows, outb, inb, outx, inx, work,
           ctake, cland, csend, crecv, send4, recv4, send0, recv0, send1, recv1, send2, recv2, send3, recv3, sendq, recvq, sendk, recvk, asend, arecv, tsend, trecv):
    X, Y, Z = u_ref.shape[1:]
    si, gi = lax.axis_index("slab"), lax.axis_index("grp")
    me = si * ng + gi
    count = ns * ng
    barrier = pltpu.get_barrier_semaphore()

    others = []
    for k in sorted(range(ns), key=lambda k: -min(k, ns - k)):
        for g in range(ng):
            if k or g:
                others.append((lax.rem(si + k, ns), lax.rem(gi + g, ng)))
    sub, lane = sub_index(), lane_index()
    upper = sub < 4

    steps = [(-1, 0), (1, 0), (0, -1), (0, 1), (-1, -1), (-1, 1), (1, -1), (1, 1)]

    def inside(ds, dg):
        ok = None
        if ds:
            ok = (si >= -ds) if ds < 0 else (si <= ns - 1 - ds)
        if dg:
            more = (gi >= -dg) if dg < 0 else (gi <= ng - 1 - dg)
            ok = more if ok is None else jnp.logical_and(ok, more)
        return ok

    def around(reach):
        return [(ds, dg) for ds in (-reach, 0, reach) for dg in (-reach, 0, reach)
                if (ds or dg) and abs(ds) < ns and abs(dg) < ng]

    def greet(sem, reach):
        for ds, dg in around(reach):
            @pl.when(inside(ds, dg))
            def _():
                pl.semaphore_signal(sem, inc=1, device_id=(si + ds, gi + dg), device_id_type=MESH)

    def meet(sem, reach):
        pl.semaphore_wait(sem, sum(jnp.where(inside(ds, dg), 1, 0) for ds, dg in around(reach)))

    rounds = []
    while (rounds[-1] * 2 if rounds else 1) < max(ns, ng):
        rounds.append(rounds[-1] * 2 if rounds else 1)

    greet(barrier, 1)
    fetched = []
    for at, (source, target) in enumerate((
        (br_in, br_ref), (fl_in, fl_ref), (ez_in, ez_ref), (k_in, k_ref), (u_in, u_ref), (p_in, p_ref),
        (f_in, f_ref), (gt_in, gt_ref),
    )):
        fetch = pltpu.make_async_copy(source, target, isem.at[at])
        fetch.start()
        fetched.append(fetch)

    def copies(ea, dst_a, stage, land, send, recv, low=0, high=None, ways=8, reach=REACH, depth=None):
        depth = reach if depth is None else depth
        half = X // 2
        edge = HALO // 2
        made = []
        chans = pl.ds(low, (ea.shape[0] if high is None else high) - low)
        for at, (ds, dg) in enumerate(steps[:ways]):
            if dg == 0:
                if ds < 0:
                    source = ea.at[chans, pl.ds(HALO + depth - reach, reach)]
                    target = dst_a.at[chans, pl.ds(HALO + X + depth - reach, reach)]
                else:
                    source = ea.at[chans, pl.ds(HALO + X - depth, reach)]
                    target = dst_a.at[chans, pl.ds(HALO - depth, reach)]
            else:
                side = 0 if dg < 0 else 1
                if ds == 0:
                    source, target = stage.at[side, chans], land.at[side, chans, pl.ds(edge, half)]
                elif ds < 0:
                    source = stage.at[side, chans, pl.ds(0, 1)]
                    target = land.at[side, chans, pl.ds(edge + half, 1)]
                else:
                    source = stage.at[side, chans, pl.ds(half - 1, 1)]
                    target = land.at[side, chans, pl.ds(edge - 1, 1)]
            made.append((ds, dg, pltpu.make_async_remote_copy(
                src_ref=source, dst_ref=target, send_sem=send.at[at], recv_sem=recv.at[at ^ 1 if at < 4 else 11 - at],
                device_id=(si + ds, gi + dg), device_id_type=MESH)))
        return made

    def begin(made):
        for ds, dg, copy in made:
            @pl.when(inside(ds, dg))
            def _():
                copy.start()

    def finish_recv(made, recv):
        for at, (ds, dg) in enumerate(steps[:len(made)]):
            back = made[at ^ 1 if at < 4 else 11 - at][2]

            @pl.when(inside(ds, dg))
            def _():
                back.wait_recv()

    def finish_send(made):
        for ds, dg, copy in made:
            @pl.when(inside(ds, dg))
            def _():
                copy.wait_send()

    def blank(dst_a, land):
        zero_a = jnp.zeros((dst_a.shape[0], HALO) + dst_a.shape[2:], jnp.float32)
        half, edge = X // 2, HALO // 2
        zero_l = jnp.zeros((land.shape[1], edge, 8, 128), jnp.float32)

        @pl.when(si == 0)
        def _():
            dst_a[:, pl.ds(0, HALO)] = zero_a
            for side in range(2):
                land[side, :, pl.ds(0, edge)] = zero_l

        @pl.when(si == ns - 1)
        def _():
            dst_a[:, pl.ds(HALO + X, HALO)] = zero_a
            for side in range(2):
                land[side, :, pl.ds(edge + half, edge)] = zero_l

        for side, edge_here in ((0, gi == ng - 1), (1, gi == 0)):
            @pl.when(edge_here)
            def _(side=side):
                land[side] = jnp.zeros(land.shape[1:], jnp.float32)

    def pack(stage, ch, pair, even, odd):
        stage[0, ch, pair] = jnp.where(upper, even, pltpu.roll(odd, 4, 0))
        stage[1, ch, pair] = jnp.where(upper, pltpu.roll(even, 4, 0), odd)

    def unpack(land, ch, pair):
        high, low = land[0, ch, pair], land[1, ch, pair]
        return (jnp.where(upper, high, pltpu.roll(low, 4, 0)),
                jnp.where(upper, pltpu.roll(high, 4, 0), low))

    def spread_rows(mask):
        wide = jnp.dot(mask.astype(jnp.float32), ez_ref[...], preferred_element_type=jnp.float32)
        return jnp.where(upper, jnp.broadcast_to(wide[0:1], (8, 128)), jnp.broadcast_to(wide[1:2], (8, 128)))

    for at in range(4):
        fetched[at].wait()
    for bx in range(X // 4):
        cut = 1.0 - CRACK_CUT * spread_rows(br_ref[bx])
        flag = spread_rows(fl_ref[bx])
        for at in range(4):
            x = bx * 4 + at
            w = k_ref[x] * cut
            e1a[6, HALO + x] = w
            rows[3, pl.ds(x, 8, stride=X), :] = (SPRING_NORMAL * 0.5) * (flag * w)

    def own(i, _):
        for c in range(3):
            tiles = []
            for o in range(2):
                x = 2 * i + o
                u = u_ref[c, x]
                f = f_ref[c, x]
                rhs = MASS_TERM * (2.0 * u - p_ref[c, x]) + f
                e1a[c, HALO + x] = u
                e1a[3 + c, HALO + x] = rhs
                e2a[c, HALO + x] = f
                tiles.append((u, rhs, f))
            pack(s1, c, i, tiles[0][0], tiles[1][0])
            pack(s1, 3 + c, i, tiles[0][1], tiles[1][1])
            pack(s2, c, i, tiles[0][2], tiles[1][2])
        pack(s1, 6, i, e1a[6, HALO + 2 * i], e1a[6, HALO + 2 * i + 1])
        return 0

    for at in range(4, 7):
        fetched[at].wait()
    lax.fori_loop(0, X // 2, own, 0)
    blank(e1a, h1)
    blank(e2a, h2)
    blank(rqa, h3)

    zrows = Z // ns

    def turn_out(value, out):
        turned = value.T
        for j in range(ns):
            out[j] = turned[j * zrows:(j + 1) * zrows]
        return turned

    def spread_out(source, target, at):
        for i in range(1, ns):
            to = lax.rem(si + i, ns)
            pltpu.make_async_remote_copy(
                src_ref=source.at[to], dst_ref=target.at[si], send_sem=tsend.at[at], recv_sem=trecv.at[at],
                device_id=(to, gi), device_id_type=MESH).start()

    def landed(target, sem):
        block = target.at[pl.ds(0, ns - 1)]
        pltpu.make_async_copy(block, block, sem).wait()

    def regroup(pieces):
        lanes = lax.broadcasted_iota(jnp.int32, pieces[0].shape, 1)
        gap = ns // 2
        while gap:
            keep = (lanes // (X * gap)) % 2 == 0
            mixed = list(pieces)
            for j in range(ns):
                if (j // gap) % 2 == 0:
                    a, b = pieces[j], pieces[j + gap]
                    mixed[j] = jnp.where(keep, a, pltpu.roll(b, X * gap, 1))
                    mixed[j + gap] = jnp.where(keep, pltpu.roll(a, 128 - X * gap, 1), b)
            pieces = mixed
            gap //= 2
        return pieces

    def wedge_copies():
        made = []
        for at, (ds, dg) in enumerate(steps[4:]):
            side, end = (0 if dg < 0 else 1), (0 if ds < 0 else 1)
            pair = HALO // 2 + X // 2 if ds < 0 else HALO // 2 - 1
            made.append((ds, dg, pltpu.make_async_remote_copy(
                src_ref=k3.at[side, end], dst_ref=h3.at[side, :, pl.ds(pair, 1)],
                send_sem=sendk.at[at], recv_sem=recvk.at[3 - at],
                device_id=(si + ds, gi + dg), device_id_type=MESH)))
        return made

    def corner_copies():
        made = []
        for at, (ds, dg) in enumerate(steps[4:]):
            side, end = (0 if dg < 0 else 1), (0 if ds < 0 else 1)
            made.append((ds, dg, pltpu.make_async_remote_copy(
                src_ref=ctake.at[side, end], dst_ref=cland.at[side, 1 - end],
                send_sem=csend.at[at], recv_sem=crecv.at[3 - at],
                device_id=(si + ds, gi + dg), device_id_type=MESH)))
        return made

    near = sub % 4 < 2
    for side in range(2):
        for end in range(2):
            for t in range((7 + 1) // 2):
                tile = s1[side, 2 * t, end * (X // 2 - 1)]
                if 2 * t + 1 < 7:
                    other = s1[side, 2 * t + 1, end * (X // 2 - 1)]
                    tile = (jnp.where(near, tile, pltpu.roll(other, 2, 0)) if side == 0
                            else jnp.where(near, pltpu.roll(other, 6, 0), tile))
                ctake[side, end, t] = tile

    def corner_unpack(made):
        for at, (ds, dg) in enumerate(steps[4:]):
            side, end = (0 if dg > 0 else 1), (1 if ds > 0 else 0)
            pair = HALO // 2 + X // 2 if ds > 0 else HALO // 2 - 1
            back = made[3 - at][2]

            @pl.when(inside(ds, dg))
            def _():
                back.wait_recv()
                for ch in range(7):
                    tile = cland[side, end, ch // 2]
                    h1[side, ch, pair] = tile if ch % 2 == 0 else pltpu.roll(tile, 6 if side == 0 else 2, 0)

    corners = corner_copies()
    zeroth = copies(e1a, e1a, s1, h1, send0, recv0, 6, 7, 4)
    first = copies(e1a, e1a, s1, h1, send1, recv1, 0, 3, 4)
    rest = copies(e1a, e1a, s1, h1, send4, recv4, 3, 6, 4, REACH - 1)
    second = copies(e2a, e2a, s2, h2, send2, recv2, reach=REACH - 1)
    third = copies(rqa, rqa, s3, h3, send3, recv3, 0, 3, 4, 1, REACH)
    outer = copies(rqa, rqa, s3, h3, sendq, recvq, 3, 6, 2, REACH - 1, REACH)
    wedges = wedge_copies()
    meet(barrier, 1)
    begin(zeroth)
    begin(corners)
    begin(first)
    begin(rest)
    greet(known.at[0], rounds[0])
    turn_out(rows[3], outb.at[3])
    inb[3, si] = outb[3, si]
    for at in range(len(rounds) - 2):
        meet(known.at[at], rounds[at])
        greet(known.at[at + 1], rounds[at + 1])
    finish_recv(zeroth, recv0)
    corner_unpack(corners)
    meet(known.at[len(rounds) - 2], rounds[-2])
    greet(known.at[len(rounds) - 1], rounds[-1])

    def open0(i, _):
        e1b[6, 2 * i], e1b[6, 2 * i + 1] = unpack(h1, 6, i)
        return 0

    def open1(i, _):
        for ch in range(6):
            e1b[ch, 2 * i], e1b[ch, 2 * i + 1] = unpack(h1, ch, i)
        return 0

    lax.fori_loop(0, (X + 2 * HALO) // 2, open0, 0)

    def link(w, other):
        return jnp.where(jnp.minimum(w, other) > 0.0, (0.5 * SPRING_SHEAR) * (w + other), 0.0)

    not_last, not_first = lane < 127, lane > 0

    def over_rows(low, high, width, body, carried=0):
        width = max(v for v in range(1, width + 1) if (high - low) % v == 0)

        def chunk(i, state):
            return body([low + i * width + o for o in range(width)], state)

        return lax.fori_loop(0, (high - low) // width, chunk, carried)

    def all_coefficients(rows_here, _):
        for x in rows_here:
            coefficients(x)
        return 0

    def coefficients(x):
        wa, wb = e1a[6, x], e1b[6, x]
        ya, yb = up_y(wa, wb)
        da, db = down_y(wa, wb)
        for w, wu, wd, yu, yd, dg, kc in (
            (wa, e1a[6, x + 1], e1a[6, x - 1], ya, da, dga, kca),
            (wb, e1b[6, x + 1], e1b[6, x - 1], yb, db, dgb, kcb),
        ):
            zu = jnp.where(not_last, up_z(w), 0.0)
            zd = jnp.where(not_first, down_z(w), 0.0)
            kc[0, x] = link(w, wu)
            kc[1, x] = link(w, yu)
            kc[2, x] = link(w, yd)
            kc[3, x] = link(w, zu)
            kc[4, x] = link(w, zd)
            sx = w + 0.5 * (wu + wd)
            sy = w + 0.5 * (yu + yd)
            sz = w + 0.5 * (zu + zd)
            every = MASS_TERM + SPRING_SHEAR * (sx + sy + sz)
            dg[0, x] = every + SHEAR_REST * sx
            dg[1, x] = every + SHEAR_REST * sy
            dg[2, x] = every + SHEAR_REST * sz

    kca[0, HALO - REACH] = link(e1a[6, HALO - REACH], e1a[6, HALO - REACH + 1])
    kcb[0, HALO - REACH] = link(e1b[6, HALO - REACH], e1b[6, HALO - REACH + 1])
    over_rows(HALO - 2, HALO + X + 2, WIDE_K, all_coefficients)
    finish_recv(first, recv1)
    finish_recv(rest, recv4)
    begin(second)
    lax.fori_loop(0, (X + 2 * HALO) // 2, open1, 0)

    def operate(x, va, vb, base, both=True):
        result = []
        coef = [[kc[j, x] for j in range(5)] + [kc[0, x - 1]] for kc in (kca, kcb)]
        for c in range(3):
            a, b = va[base + c, x], vb[base + c, x]
            ua, ub = up_y(a, b)
            la, lb = down_y(a, b)
            pair = []
            halves = ((a, va, ua, la, coef[0], dga), (b, vb, ub, lb, coef[1], dgb))
            for v, ref, u, l, k, dg in halves if both else halves[:1]:
                parts = (
                    k[0] * ref[base + c, x + 1] + k[5] * ref[base + c, x - 1],
                    k[1] * u + k[2] * l,
                    k[3] * up_z(v) + k[4] * down_z(v),
                )
                shear = parts[(c + 1) % 3] + parts[(c + 2) % 3]
                pair.append(dg[c, x] * v - (shear + (SPRING_NORMAL / SPRING_SHEAR) * parts[c]))
            result.append(pair)
        return result

    def solve(step, va, vb, rhs_of, ship_halo=None):
        def residual(rows_here, _):
            for x in rows_here:
                image = operate(x, va, vb, 0)
                for c in range(3):
                    ra, rb = rhs_of(c, x)
                    rqa[c, x] = ra - image[c][0]
                    rqb[c, x] = rb - image[c][1]
            return 0

        over_rows(HALO - 2, HALO + X + 2, WIDE_R, residual)

        def put(x, image):
            for c in range(3):
                rqa[3 + c, x] = image[c][0]
                rqb[3 + c, x] = image[c][1]

        def apply(rows_here, sums):
            rr, rq = sums
            for x in rows_here:
                image = operate(x, rqa, rqb, 0)
                for c in range(3):
                    r = rqa[c, x]
                    rr, rq = rr + r * r, rq + r * image[c][0]
                put(x, image)
            return rr, rq

        zero = jnp.zeros((8, 128), jnp.float32)
        images = [operate(x, rqa, rqb, 0) for x in (HALO - 1, HALO + X)]
        put(HALO - 1, images[0])
        put(HALO + X, images[1])
        rr, rq = over_rows(HALO, HALO + X, WIDE_A, apply, (zero, zero))
        if ship_halo is not None:
            ship_halo()
        rr, rq = total(rr), total(rq)
        mu = jnp.where(rr > 0.0, rq / jnp.where(rr > 0.0, rr, 1.0), 0.0)

        def centred(rows_here, sums):
            ww, wr, mix, wt = sums
            for x in rows_here:
                image = operate(x, rqa, rqb, 3, False)
                for c in range(3):
                    r, q, s = rqa[c, x], rqa[3 + c, x], image[c][0]
                    w, t = q - mu * r, s - mu * q
                    ww, wr, mix, wt = ww + w * w, wr + w * r, mix + (r * t + w * q), wt + w * t
            return ww, wr, mix, wt

        sums = over_rows(HALO, HALO + X, WIDE_C, centred, (zero,) * 4)
        ww, wr, mix, wt = [total(v) for v in sums]
        one = lax.broadcasted_iota(jnp.int32, (1, 128), 1)
        row = jnp.zeros((1, 128), jnp.float32)
        for at, value in enumerate((rr, rq, mu, ww, wr, mix, wt)):
            row = jnp.where(one == at, value, row)
        gath[step, me] = row

        if step == 0:
            meet(known.at[len(rounds) - 1], rounds[-1])
        for other in others:
            pltpu.make_async_remote_copy(
                src_ref=gath.at[step, me], dst_ref=gath.at[step, me], send_sem=asend.at[step], recv_sem=arecv.at[step],
                device_id=other, device_id_type=MESH).start()

    def collect(step):
        block = gath.at[step, pl.ds(0, count - 1)]
        pltpu.make_async_copy(block, block, arecv.at[step]).wait()
        table = gath[step].reshape(count, 128)
        rr, rq, mu, ww, wr, mix, wt = [table[:, at:at + 1] for at in range(7)]

        def down(v):
            return jnp.sum(v, axis=0, keepdims=True)

        norm = down(rr)
        alpha = norm / down(rq)
        rest = 1.0 - alpha * mu
        after = down(alpha * alpha * ww - 2.0 * alpha * rest * wr + rest * rest * rr)
        curved = down(rest * rest * rq - alpha * rest * mix + alpha * alpha * wt)
        ratio = after / norm
        beta = after / (curved - ratio * after / alpha)
        return jnp.broadcast_to(alpha + beta * (1.0 + ratio), (8, 128)), jnp.broadcast_to(-beta * alpha, (8, 128))

    def drain(step):
        block = gath.at[step, pl.ds(0, count - 1)]
        pltpu.make_async_copy(block, block, asend.at[step]).wait()

    def joined(c, x, near, far):
        r, q = rqa[c, x], rqa[3 + c, x]
        return jnp.where(sub == 3, pltpu.roll(r, near, 0), jnp.where(sub == 4, pltpu.roll(r, far, 0), q))

    def split(c, x, tile, row, near, far):
        r = rqb[c, x]
        rqb[c, x] = jnp.where(sub == row, pltpu.roll(tile, near, 0), jnp.where(sub == 7 - row, pltpu.roll(tile, far, 0), r))
        rqb[3 + c, x] = tile

    def ship_halo():
        def pack3(i, _):
            x = HALO + 2 * i
            for c in range(3):
                pack(s3, c, i, joined(c, x, 1, 7), joined(c, x + 1, 1, 7))
            return 0

        lax.fori_loop(0, X // 2, pack3, 0)
        for end, x in ((0, HALO), (1, HALO + X - 2)):
            for c in range(3):
                even, odd = [joined(c, x + o, 2, 6) if o == end else joined(c, x + o, 3, 5) for o in range(2)]
                k3[0, end, c, 0] = jnp.where(upper, even, pltpu.roll(odd, 4, 0))
                k3[1, end, c, 0] = jnp.where(upper, pltpu.roll(even, 4, 0), odd)
        begin(third)
        begin(wedges)
        begin(outer)

    solve(0, e1a, e1b, lambda c, x: (e1a[3 + c, x], e1b[3 + c, x]), ship_halo)
    spread_out(outb.at[3], inb.at[3], 3)
    finish_recv(second, recv2)

    def open2(i, _):
        for ch in range(3):
            e2b[ch, 2 * i], e2b[ch, 2 * i + 1] = unpack(h2, ch, i)
        return 0

    lax.fori_loop(0, (X + 2 * HALO) // 2, open2, 0)
    finish_recv(third, recv3)
    for at, (ds, dg) in enumerate(steps[4:]):
        back = wedges[3 - at][2]

        @pl.when(inside(ds, dg))
        def _():
            back.wait_recv()

    def open3(i, _):
        for c in range(3):
            even, odd = unpack(h3, c, i)
            split(c, 2 * i, even, 2, 7, 1)
            split(c, 2 * i + 1, odd, 2, 7, 1)
        return 0

    lax.fori_loop(HALO // 2, (HALO + X) // 2, open3, 0)
    for pair, one in ((HALO // 2 - 1, 1), ((HALO + X) // 2, 0)):
        for c in range(3):
            for o, tile in enumerate(unpack(h3, c, pair)):
                if o == one:
                    split(c, 2 * pair + o, tile, 1, 6, 2)
                else:
                    split(c, 2 * pair + o, tile, 0, 5, 3)
    finish_recv(outer, recvq)
    c0, c1 = collect(0)

    def step1(x, both=True):
        for c in range(3):
            u1a[c, x] = e1a[c, x] + (c0 * rqa[c, x] + c1 * rqa[3 + c, x])
            u1b[c, x] = e1b[c, x] + (c0 * rqb[c, x] + c1 * rqb[3 + c, x]) if both else jnp.zeros((8, 128), jnp.float32)

    for x in range(HALO - REACH + 1, HALO + X + REACH - 1):
        step1(x)
    step1(HALO - REACH, False)
    step1(HALO + X + REACH - 1, False)
    finish_send(zeroth)
    finish_send(corners)
    finish_send(rest)
    finish_send(first)
    finish_send(second)
    finish_send(third)
    finish_send(outer)
    finish_send(wedges)

    def rhs2(c, x):
        return (MASS_TERM * (2.0 * u1a[c, x] - e1a[c, x]) + e2a[c, x],
                MASS_TERM * (2.0 * u1b[c, x] - e1b[c, x]) + e2b[c, x])

    solve(1, u1a, u1b, rhs2)
    landed(inb.at[3], trecv.at[3])
    for y, piece in enumerate(regroup([inb[3, j] for j in range(ns)])):
        scale[y] = piece
    c0, c1 = collect(1)

    def step2(ra, rb, c, x):
        return ra[c, x] + (c0 * rb[c, x] + c1 * rb[3 + c, x])

    def halves(v):
        high = v.astype(jnp.bfloat16)
        return high, (v - high.astype(jnp.float32)).astype(jnp.bfloat16)

    def finish(c):
        for x in range(X):
            v = step2(u1a, rqa, c, HALO + x)
            disp_ref[c, x] = v
            rows[c, pl.ds(x, 8, stride=X), :] = v
        turned = turn_out(rows[c], outb.at[c])
        spread_out(outb.at[c], inb.at[c], c)
        inb[c, si] = outb[c, si]
        return turned

    def finish_edges(turned):
        for x in range(X):
            rows[4, pl.ds(x, 8, stride=X), :] = step2(u1b, rqb, 1, HALO + x)
        sides_y = rows[4].T
        zero = jnp.zeros((8, 128), jnp.float32)
        for j in range(ns):
            low, high = sides_y[zrows * j:zrows * j + 8], sides_y[zrows * j + 8:zrows * j + 16]
            tile = jnp.where(lane < 32, pltpu.roll(low, 16, 1),
                             jnp.where(lane < 64, pltpu.roll(pltpu.roll(low, 4, 0), 48, 1),
                                       jnp.where(lane < 96, pltpu.roll(high, 80, 1),
                                                 pltpu.roll(pltpu.roll(high, 4, 0), 112, 1))))
            before = pltpu.roll(turned[zrows * j - 8:zrows * j], 5, 0) if j else zero
            after = pltpu.roll(turned[zrows * (j + 1):zrows * (j + 1) + 8], 5, 0) if j + 1 < ns else zero
            outx[j] = jnp.where(sub == 4, before, jnp.where(sub == 5, after, tile))
        spread_out(outx, inx, 4)
        inx[si] = outx[si]

    finish_edges(finish(2))
    finish(0)
    finish(1)
    fetched[7].wait()

    c1t, c3t = float(np.sqrt(0.5) * np.cos(np.pi / 8)), float(np.sqrt(0.5) * np.cos(3 * np.pi / 8))

    def cosine(v0, v1, v2, v3):
        s03, s12, d03, d12 = v0 + v3, v1 + v2, v0 - v3, v1 - v2
        return [0.5 * (s03 + s12), c1t * d03 + c3t * d12, 0.5 * (s03 - s12), c3t * d03 - c1t * d12]

    def encode(ch, fields):
        for b in range(Y // 4):
            for k, v in enumerate(cosine(*fields[4 * b:4 * b + 4])):
                work[ch, (4 * b + k) * zrows:(4 * b + k + 1) * zrows] = v
        parts = []
        for p in range(Y * zrows // 32):
            parts += cosine(*[work[ch, pl.ds(32 * p + n, 8, stride=4), :] for n in range(4)])
        high, low = halves(jnp.concatenate(parts, axis=0))
        done = jnp.dot(jnp.concatenate([high, low], axis=1), gt_ref[...], preferred_element_type=jnp.float32)
        done = done[:, 0:128] + done[:, 128:256]
        for p in range(Y * zrows // 32):
            for n in range(4):
                coef_ref[ch, pl.ds(32 * p + n, 8, stride=4), :] = done[(4 * p + n) * 8:(4 * p + n + 1) * 8]

    def arrived(c):
        landed(inb.at[c], trecv.at[c])
        return regroup([inb[c, j] for j in range(ns)])

    field = arrived(2)
    encode(2, field)
    landed(inx, trecv.at[4])
    edges = regroup([inx[j] for j in range(ns)])
    stress = []
    for y in range(Y):
        low, high = field[y][0:8], field[y][8:16]
        ul, uh, dl, dh = pltpu.roll(low, 7, 0), pltpu.roll(high, 7, 0), pltpu.roll(low, 1, 0), pltpu.roll(high, 1, 0)
        first, last = sub == 0, sub == 7
        low = jnp.where(last, uh, ul) - jnp.where(first, pltpu.roll(edges[y], 4, 0), dl)
        high = jnp.where(last, pltpu.roll(edges[y], 2, 0), uh) - jnp.where(first, dl, dh)
        stress.append(scale[y] * jnp.concatenate([low, high], axis=0))
    encode(5, stress)
    field = arrived(0)
    encode(0, field)
    wide = lax.broadcasted_iota(jnp.int32, (zrows, 128), 1)
    encode(3, [scale[y] * (jnp.where(wide < 127, up_z(field[y]), 0.0) - jnp.where(wide > 0, down_z(field[y]), 0.0))
               for y in range(Y)])
    field = arrived(1)
    encode(1, field)
    outside = []
    for side in range(2):
        quarter = [edges[2 * q + side] for q in range(4)]
        outside.append(jnp.concatenate([jnp.where(upper, quarter[q], pltpu.roll(quarter[q + 1], 4, 0)) for q in (0, 2)], axis=0))
    field = [outside[0]] + field + [outside[1]]
    encode(4, [scale[y] * (field[y + 2] - field[y]) for y in range(Y)])
    drain(0)
    drain(1)
    for at in range(4):
        landed(inb.at[at], tsend.at[at])
    landed(inx, tsend.at[4])


def store(disp_in, coef_in, disp_out, coef_out, sems):
    copies = [pltpu.make_async_copy(disp_in, disp_out, sems.at[0]), pltpu.make_async_copy(coef_in, coef_out, sems.at[1])]
    for copy in copies:
        copy.start()
    for copy in copies:
        copy.wait()


def fused(mesh, u_now, u_prev, force, stiffness, broken, flags):
    ns, ng = mesh.shape["slab"], mesh.shape["grp"]
    _, X, Y, Z = u_now.shape
    xe, pairs, half = X + 2 * HALO, X // 2 + HALO, X // 2
    zrows = Z // ns
    ez = jnp.asarray(np.kron(np.eye(Z // 4), np.ones((1, 4))), jnp.float32)
    gth, gtl = split_table(wavelet_table(X * ns).T)
    gt = jnp.asarray(np.block([[gth, gtl], [gth, np.zeros_like(gtl)]]), jnp.bfloat16)

    def vm(*shape):
        return pltpu.VMEM(shape, jnp.float32)

    def ext(n):
        return vm(n, xe, Y, Z)

    def stage(n):
        return vm(2, n, half, Y, Z)

    def land(n):
        return vm(2, n, pairs, Y, Z)

    dma = pltpu.SemaphoreType.DMA
    shapes = (u_now.shape, (6, Y * zrows, X * ns))
    operands = [pltpu.with_memory_space_constraint(v, pltpu.HBM)
                for v in (u_now, u_prev, force, stiffness, broken, flags, ez, gt)]
    results = pl.pallas_call(
        lambda *refs: kernel(ns, ng, *refs),
        name="lattice",
        out_shape=tuple(vm(*shape) for shape in shapes),
        in_specs=[pl.BlockSpec(memory_space=pltpu.MemorySpace.HBM)] * 8,
        out_specs=(pl.BlockSpec(memory_space=pltpu.VMEM),) * 2,
        scratch_shapes=[
            vm(*u_now.shape), vm(*u_now.shape), vm(*u_now.shape), vm(*stiffness.shape),
            pltpu.VMEM(broken.shape, broken.dtype), pltpu.VMEM(flags.shape, flags.dtype),
            vm(*ez.shape), pltpu.VMEM(gt.shape, gt.dtype), pltpu.SemaphoreType.DMA((8,)),
            ext(7), ext(7), stage(7), land(7),
            ext(3), ext(3), stage(3), land(3),
            ext(6), ext(6), stage(3), land(3), vm(2, 2, 3, 1, Y, Z),
            ext(3), ext(3), vm(Y, zrows, X * ns), ext(3), ext(3), ext(5), ext(5),
            pltpu.SemaphoreType.REGULAR((4,)), vm(2, ns * ng, 1, 128), vm(5, Y * X, Z), vm(4, ns, zrows, 128), vm(4, ns, zrows, 128), vm(ns, 8, 128), vm(ns, 8, 128), vm(6, Y * zrows, X * ns),
            vm(2, 2, 4, Y, Z), vm(2, 2, 4, Y, Z), dma((4,)), dma((4,)), dma((4,)), dma((4,)),
            dma((4,)), dma((4,)), dma((4,)), dma((4,)), dma((8,)), dma((8,)), dma((4,)), dma((4,)), dma((2,)), dma((2,)), dma((4,)), dma((4,)),
            dma((2,)), dma((2,)), dma((5,)), dma((5,)),
        ],
        compiler_params=pltpu.CompilerParams(collective_id=0, has_side_effects=True, vmem_limit_bytes=24 << 20),
    )(*operands)
    disp, coef = pl.pallas_call(
        store,
        name="store",
        out_shape=tuple(jax.ShapeDtypeStruct(shape, jnp.float32) for shape in shapes),
        in_specs=[pl.BlockSpec(memory_space=pltpu.VMEM)] * 2,
        out_specs=(pl.BlockSpec(memory_space=pltpu.MemorySpace.HBM),) * 2,
        scratch_shapes=[dma((2,))],
        compiler_params=pltpu.CompilerParams(vmem_limit_bytes=1 << 20),
    )(*[pltpu.with_memory_space_constraint(v, pltpu.VMEM) for v in results])
    return disp, coef.reshape(6, Y, zrows, X * ns)


def fits(mesh, shape):
    ns, ng = mesh.shape["slab"], mesh.shape["grp"]
    x, y, z = shape[1] // ns, shape[2] // ng, shape[3]
    return y == 8 and z == 128 and x * y == 128 and x * ns == 128 and z % (8 * ns) == 0


def entry(mesh, *args):
    ns, ng = mesh.shape["slab"], mesh.shape["grp"]
    _, x, y, z = args[0].shape
    if fits(mesh, (3, x * ns, y * ng, z)):
        return fused(mesh, *args)
    return body(*args)


def solution(mesh):
    return jax.shard_map(
        lambda *args: entry(mesh, *args),
        mesh=mesh,
        in_specs=(
            P(None, "slab", "grp", None),
            P(None, "slab", "grp", None),
            P(None, "slab", "grp", None),
            P("slab", "grp", None),
            P("slab", "grp", None),
            P("slab", "grp", None),
        ),
        out_specs=(P(None, "slab", "grp", None), P(None, "grp", "slab", None)),
        check_vma=False,
    )
```

```python
import jax
import jax.numpy as jnp
import numpy as np
from jax import lax
from jax.experimental import pallas as pl
from jax.experimental.pallas import tpu as pltpu
from jax.sharding import PartitionSpec as P

STEPS = 2
ITERS = 2
LEVELS = 3


SPRING_NORMAL = 1.0
SPRING_SHEAR = 0.4
MASS_TERM = 1.0
CRACK_CUT = 0.9


def with_halo(block, sides, width):
    for axis, dim in sides:
        count = lax.axis_size(axis)
        forward = [(i, i + 1) for i in range(count - 1)]
        backward = [(target, source) for source, target in forward]
        low = lax.ppermute(
            lax.slice_in_dim(block, block.shape[dim] - width, None, axis=dim), axis, forward
        )
        high = lax.ppermute(lax.slice_in_dim(block, 0, width, axis=dim), axis, backward)
        block = jnp.concatenate([low, block, high], axis=dim)
    return block


def cosine_table():
    freq = np.arange(4)[:, None]
    place = np.arange(4)[None, :]
    factor = np.where(freq == 0, 0.5, np.sqrt(0.5))
    return factor * np.cos(np.pi * (2 * place + 1) * freq / 8.0)


def block_table(count):
    return jnp.asarray(np.kron(np.eye(count // 4), cosine_table()), jnp.float32)


def spread(mask):
    values = mask.astype(jnp.float32)
    size_a, size_b, size_c = values.shape
    wide = jnp.broadcast_to(values[:, None, :, None, :, None], (size_a, 4, size_b, 4, size_c, 4))
    return wide.reshape(size_a * 4, size_b * 4, size_c * 4)


def sides(padded, axis_index):
    leading = padded.ndim - 3

    def cut(offset):
        index_list = [slice(None)] * leading + [slice(1, -1)] * 3
        length = padded.shape[leading + axis_index]
        index_list[leading + axis_index] = slice(1 + offset, length - 1 + offset)
        return padded[tuple(index_list)]

    return (cut(1), cut(-1))


def springs(field, weight, field_pad, weight_pad):
    result = MASS_TERM * field
    for axis_index in range(3):
        upper_v, lower_v = sides(field_pad, axis_index)
        upper_w, lower_w = sides(weight_pad, axis_index)
        k_upper = 0.5 * (weight + upper_w)
        k_lower = 0.5 * (weight + lower_w)
        change = k_upper * (field - upper_v) + k_lower * (field - lower_v)
        coupling = jnp.array(
            [SPRING_NORMAL if comp == axis_index else SPRING_SHEAR for comp in range(3)],
            jnp.float32,
        ).reshape(3, 1, 1, 1)
        result = result + coupling * change
    return result


def faces(field):
    padded = with_halo(field, (("slab", 1), ("grp", 2)), 1)
    return jnp.pad(padded, ((0, 0), (0, 0), (0, 0), (1, 1)))


def stresses(carry, field_pad):
    rows_out = []
    for axis_index in range(3):
        upper_v, lower_v = sides(field_pad, axis_index)
        rows_out.append(SPRING_NORMAL * carry * 0.5 * (upper_v[axis_index] - lower_v[axis_index]))
    return jnp.stack(rows_out)


def paired_sum(residual, image):
    return lax.psum((jnp.sum(residual * residual), jnp.sum(residual * image)), ("slab", "grp"))


def lift(signal):
    even = signal[..., 0::2]
    odd = signal[..., 1::2]
    detail = odd - 0.5 * (even + jnp.roll(even, -1, axis=-1))
    approx = even + 0.25 * (jnp.roll(detail, 1, axis=-1) + detail)
    return (approx, detail)


def wavelet(signal):
    pieces = []
    approx = signal
    for level_index in range(LEVELS):
        approx, detail = lift(approx)
        pieces.insert(0, detail)
    return jnp.concatenate([approx] + pieces, axis=-1)


def body(u_now, u_prev, force, stiffness, broken, flags):
    weight = stiffness * (1.0 - CRACK_CUT * spread(broken))
    carry = spread(flags) * weight
    weight_pad = with_halo(weight, (("slab", 0), ("grp", 1)), 1)
    weight_pad = jnp.pad(weight_pad, ((0, 0), (0, 0), (1, 1)))

    def operate(field):
        return springs(field, weight, faces(field), weight_pad)

    for step_index in range(STEPS):
        rhs = MASS_TERM * (2.0 * u_now - u_prev) + force
        guess = u_now
        residual = rhs - operate(guess)
        image = operate(residual)
        norm_now, product = paired_sum(residual, image)
        alpha = norm_now / product
        direction, along = (residual, image)
        for turn_index in range(ITERS):
            guess = guess + alpha * direction
            residual = residual - alpha * along
            if turn_index + 1 < ITERS:
                image = operate(residual)
                norm_next, product = paired_sum(residual, image)
                ratio = norm_next / norm_now
                alpha = norm_next / (product - ratio * norm_next / alpha)
                direction = residual + ratio * direction
                along = image + ratio * along
                norm_now = norm_next
        u_prev = u_now
        u_now = guess
    stress = stresses(carry, faces(u_now))
    fields = jnp.concatenate([u_now, stress], axis=0)
    table_x = block_table(fields.shape[1])
    table_y = block_table(fields.shape[2])
    table_z = block_table(fields.shape[3])
    blockc = jnp.einsum("ax,hxyz->hayz", table_x, fields, precision=lax.Precision.HIGHEST)
    blockc = jnp.einsum("by,hxyz->hxbz", table_y, blockc, precision=lax.Precision.HIGHEST)
    blockc = jnp.einsum("hxyz,cz->hxyc", blockc, table_z, precision=lax.Precision.HIGHEST)
    moved = jnp.transpose(blockc, (0, 2, 3, 1))
    shipped = lax.all_to_all(moved, "slab", split_axis=2, concat_axis=3, tiled=True)
    coeffs = wavelet(shipped)
    return (u_now, coeffs)


MESH = pl.DeviceIdType.MESH
HALO = 4
REACH = 3
SHEAR_REST = SPRING_NORMAL - SPRING_SHEAR
WIDE_R, WIDE_A, WIDE_C, WIDE_K = 20, 16, 16, 20


def wavelet_table(count):
    table = np.kron(np.eye(count // 4), cosine_table())
    pieces = []
    approx = table
    for level_index in range(LEVELS):
        even, odd = approx[0::2], approx[1::2]
        detail = odd - 0.5 * (even + np.roll(even, -1, axis=0))
        approx = even + 0.25 * (np.roll(detail, 1, axis=0) + detail)
        pieces.insert(0, detail)
    return np.concatenate([approx] + pieces, axis=0)


def split_table(table):
    high = table.astype(jnp.bfloat16).astype(np.float64)
    return high, (table - high).astype(jnp.bfloat16).astype(np.float64)


def sub_index():
    return lax.broadcasted_iota(jnp.int32, (8, 128), 0)


def lane_index():
    return lax.broadcasted_iota(jnp.int32, (8, 128), 1)


def up_y(a, b):
    ra, rb = pltpu.roll(a, 7, 0), pltpu.roll(b, 7, 0)
    last = sub_index() == 7
    return jnp.where(last, rb, ra), jnp.where(last, ra, rb)


def down_y(a, b):
    ra, rb = pltpu.roll(a, 1, 0), pltpu.roll(b, 1, 0)
    first = sub_index() == 0
    return jnp.where(first, rb, ra), jnp.where(first, ra, rb)


def up_z(v):
    return pltpu.roll(v, 127, 1)


def down_z(v):
    return pltpu.roll(v, 1, 1)


def total(v):
    return jnp.sum(jnp.sum(v, axis=0, keepdims=True), axis=1, keepdims=True)


def kernel(ns, ng, u_in, p_in, f_in, k_in, br_in, fl_in, ez_in, gt_in,
           disp_ref, coef_ref,
           u_ref, p_ref, f_ref, k_ref, br_ref, fl_ref, ez_ref, gt_ref, isem,
           e1a, e1b, s1, h1, e2a, e2b, s2, h2, rqa, rqb, s3, h3, k3,
           u1a, u1b, scale, dga, dgb, kca, kcb, known, gath, rows, outb, inb, outx, inx, work,
           ctake, cland, csend, crecv, send4, recv4, send0, recv0, send1, recv1, send2, recv2, send3, recv3, sendq, recvq, sendk, recvk, asend, arecv, tsend, trecv):
    X, Y, Z = u_ref.shape[1:]
    si, gi = lax.axis_index("slab"), lax.axis_index("grp")
    me = si * ng + gi
    count = ns * ng
    barrier = pltpu.get_barrier_semaphore()

    def mirrored(place, mask, length):
        bit, result = 1, 0
        while bit < length:
            here = place // bit % 2
            result = result + bit * (1 - here if mask // bit % 2 else here)
            bit *= 2
        return result

    others = []
    for k in sorted(range(ns), key=lambda k: -min(k, ns - k)):
        for g in range(ng):
            if k or g:
                others.append((lax.rem(si + k, ns), lax.rem(gi + g, ng)))

    sub, lane = sub_index(), lane_index()
    upper = sub < 4

    steps = [(-1, 0), (1, 0), (0, -1), (0, 1), (-1, -1), (-1, 1), (1, -1), (1, 1)]

    def inside(ds, dg):
        ok = None
        if ds:
            ok = (si >= -ds) if ds < 0 else (si <= ns - 1 - ds)
        if dg:
            more = (gi >= -dg) if dg < 0 else (gi <= ng - 1 - dg)
            ok = more if ok is None else jnp.logical_and(ok, more)
        return ok

    def around(reach):
        return [(ds, dg) for ds in (-reach, 0, reach) for dg in (-reach, 0, reach)
                if (ds or dg) and abs(ds) < ns and abs(dg) < ng]

    def greet(sem, reach):
        for ds, dg in around(reach):
            @pl.when(inside(ds, dg))
            def _():
                pl.semaphore_signal(sem, inc=1, device_id=(si + ds, gi + dg), device_id_type=MESH)

    def meet(sem, reach):
        pl.semaphore_wait(sem, sum(jnp.where(inside(ds, dg), 1, 0) for ds, dg in around(reach)))

    rounds = []
    while (rounds[-1] * 2 if rounds else 1) < max(ns, ng):
        rounds.append(rounds[-1] * 2 if rounds else 1)

    greet(barrier, 1)
    fetched = []
    for at, (source, target) in enumerate((
        (br_in, br_ref), (fl_in, fl_ref), (ez_in, ez_ref), (k_in, k_ref), (u_in, u_ref), (p_in, p_ref),
        (f_in, f_ref), (gt_in, gt_ref),
    )):
        fetch = pltpu.make_async_copy(source, target, isem.at[at])
        fetch.start()
        fetched.append(fetch)

    def copies(ea, dst_a, stage, land, send, recv, low=0, high=None, ways=8, reach=REACH, depth=None):
        depth = reach if depth is None else depth
        half = X // 2
        edge = HALO // 2
        made = []
        chans = pl.ds(low, (ea.shape[0] if high is None else high) - low)
        for at, (ds, dg) in enumerate(steps[:ways]):
            if dg == 0:
                if ds < 0:
                    source = ea.at[chans, pl.ds(HALO + depth - reach, reach)]
                    target = dst_a.at[chans, pl.ds(HALO + X + depth - reach, reach)]
                else:
                    source = ea.at[chans, pl.ds(HALO + X - depth, reach)]
                    target = dst_a.at[chans, pl.ds(HALO - depth, reach)]
            else:
                side = 0 if dg < 0 else 1
                if ds == 0:
                    source, target = stage.at[side, chans], land.at[side, chans, pl.ds(edge, half)]
                elif ds < 0:
                    source = stage.at[side, chans, pl.ds(0, 1)]
                    target = land.at[side, chans, pl.ds(edge + half, 1)]
                else:
                    source = stage.at[side, chans, pl.ds(half - 1, 1)]
                    target = land.at[side, chans, pl.ds(edge - 1, 1)]
            made.append((ds, dg, pltpu.make_async_remote_copy(
                src_ref=source, dst_ref=target, send_sem=send.at[at], recv_sem=recv.at[at ^ 1 if at < 4 else 11 - at],
                device_id=(si + ds, gi + dg), device_id_type=MESH)))
        return made

    def begin(made):
        for ds, dg, copy in made:
            @pl.when(inside(ds, dg))
            def _():
                copy.start()

    def finish_recv(made, recv):
        for at, (ds, dg) in enumerate(steps[:len(made)]):
            back = made[at ^ 1 if at < 4 else 11 - at][2]

            @pl.when(inside(ds, dg))
            def _():
                back.wait_recv()

    def finish_send(made):
        for ds, dg, copy in made:
            @pl.when(inside(ds, dg))
            def _():
                copy.wait_send()

    def blank(dst_a, land):
        zero_a = jnp.zeros((dst_a.shape[0], HALO) + dst_a.shape[2:], jnp.float32)
        half, edge = X // 2, HALO // 2
        zero_l = jnp.zeros((land.shape[1], edge, 8, 128), jnp.float32)

        @pl.when(si == 0)
        def _():
            dst_a[:, pl.ds(0, HALO)] = zero_a
            for side in range(2):
                land[side, :, pl.ds(0, edge)] = zero_l

        @pl.when(si == ns - 1)
        def _():
            dst_a[:, pl.ds(HALO + X, HALO)] = zero_a
            for side in range(2):
                land[side, :, pl.ds(edge + half, edge)] = zero_l

        for side, edge_here in ((0, gi == ng - 1), (1, gi == 0)):
            @pl.when(edge_here)
            def _(side=side):
                land[side] = jnp.zeros(land.shape[1:], jnp.float32)

    def pack(stage, ch, pair, even, odd):
        stage[0, ch, pair] = jnp.where(upper, even, pltpu.roll(odd, 4, 0))
        stage[1, ch, pair] = jnp.where(upper, pltpu.roll(even, 4, 0), odd)

    def unpack(land, ch, pair):
        high, low = land[0, ch, pair], land[1, ch, pair]
        return (jnp.where(upper, high, pltpu.roll(low, 4, 0)),
                jnp.where(upper, pltpu.roll(high, 4, 0), low))

    def spread_rows(mask):
        wide = jnp.dot(mask.astype(jnp.float32), ez_ref[...], preferred_element_type=jnp.float32)
        return jnp.where(upper, jnp.broadcast_to(wide[0:1], (8, 128)), jnp.broadcast_to(wide[1:2], (8, 128)))

    for at in range(4):
        fetched[at].wait()
    for bx in range(X // 4):
        cut = 1.0 - CRACK_CUT * spread_rows(br_ref[bx])
        flag = spread_rows(fl_ref[bx])
        for at in range(4):
            x = bx * 4 + at
            w = k_ref[x] * cut
            e1a[6, HALO + x] = w
            rows[3, pl.ds(x, 8, stride=X), :] = (SPRING_NORMAL * 0.5) * (flag * w)

    def own(i, _):
        for c in range(3):
            tiles = []
            for o in range(2):
                x = 2 * i + o
                u = u_ref[c, x]
                f = f_ref[c, x]
                rhs = MASS_TERM * (2.0 * u - p_ref[c, x]) + f
                e1a[c, HALO + x] = u
                e1a[3 + c, HALO + x] = rhs
                e2a[c, HALO + x] = f
                tiles.append((u, rhs, f))
            pack(s1, c, i, tiles[0][0], tiles[1][0])
            pack(s1, 3 + c, i, tiles[0][1], tiles[1][1])
            pack(s2, c, i, tiles[0][2], tiles[1][2])
        pack(s1, 6, i, e1a[6, HALO + 2 * i], e1a[6, HALO + 2 * i + 1])
        return 0

    for at in range(4, 7):
        fetched[at].wait()
    lax.fori_loop(0, X // 2, own, 0)
    blank(e1a, h1)
    blank(e2a, h2)
    blank(rqa, h3)

    zrows = Z // ns

    def turn_out(value, out):
        turned = value.T
        for j in range(ns):
            out[j] = turned[j * zrows:(j + 1) * zrows]

    def spread_out(source, target, at):
        for m in reversed(range(1, ns)):
            to = mirrored(si, m, ns)
            pltpu.make_async_remote_copy(
                src_ref=source.at[to], dst_ref=target.at[si], send_sem=tsend.at[at], recv_sem=trecv.at[at],
                device_id=(to, gi), device_id_type=MESH).start()

    def landed(target, sem):
        block = target.at[pl.ds(0, ns - 1)]
        pltpu.make_async_copy(block, block, sem).wait()

    def regroup(pieces):
        lanes = lax.broadcasted_iota(jnp.int32, pieces[0].shape, 1)
        gap = ns // 2
        while gap:
            keep = (lanes // (X * gap)) % 2 == 0
            mixed = list(pieces)
            for j in range(ns):
                if (j // gap) % 2 == 0:
                    a, b = pieces[j], pieces[j + gap]
                    mixed[j] = jnp.where(keep, a, pltpu.roll(b, X * gap, 1))
                    mixed[j + gap] = jnp.where(keep, pltpu.roll(a, 128 - X * gap, 1), b)
            pieces = mixed
            gap //= 2
        return pieces

    def wedge_copies():
        made = []
        for at, (ds, dg) in enumerate(steps[4:]):
            side, end = (0 if dg < 0 else 1), (0 if ds < 0 else 1)
            pair = HALO // 2 + X // 2 if ds < 0 else HALO // 2 - 1
            made.append((ds, dg, pltpu.make_async_remote_copy(
                src_ref=k3.at[side, end], dst_ref=h3.at[side, :, pl.ds(pair, 1)],
                send_sem=sendk.at[at], recv_sem=recvk.at[3 - at],
                device_id=(si + ds, gi + dg), device_id_type=MESH)))
        return made

    def corner_copies():
        made = []
        for at, (ds, dg) in enumerate(steps[4:]):
            side, end = (0 if dg < 0 else 1), (0 if ds < 0 else 1)
            made.append((ds, dg, pltpu.make_async_remote_copy(
                src_ref=ctake.at[side, end], dst_ref=cland.at[side, 1 - end],
                send_sem=csend.at[at], recv_sem=crecv.at[3 - at],
                device_id=(si + ds, gi + dg), device_id_type=MESH)))
        return made

    def corner_rows(side, end):
        dx1, dx2 = (0, 4) if end == 0 else (4, 0)
        dy1, dy2 = (0, 1) if side == 0 else (3, 2)
        return dx1 + dy1, dx1 + dy2, dx2 + dy1

    def any_row(places):
        found = sub == places[0]
        for place in places[1:]:
            found = jnp.logical_or(found, sub == place)
        return found

    corner_sets = ((0, 1, (3, 4)), (2, 6, (5,)))
    for side in range(2):
        for end in range(2):
            places = corner_rows(side, end)
            first_here, second_here = any_row(places), any_row([(v + 2) % 8 for v in places])
            for at, (ch_a, ch_b, right) in enumerate(corner_sets):
                tiles = [s1[side, ch, end * (X // 2 - 1)] for ch in (ch_a, ch_b) + right]
                tile = pltpu.roll(tiles[2], 5, 0)
                if len(right) == 2:
                    tile = jnp.where(sub == (places[0] + 5) % 8, tile, pltpu.roll(tiles[3], 3 if side else 7, 0))
                tile = jnp.where(first_here, tiles[0], jnp.where(second_here, pltpu.roll(tiles[1], 2, 0), tile))
                ctake[side, end, at] = tile

    def corner_unpack(made):
        for at, (ds, dg) in enumerate(steps[4:]):
            side, end = (0 if dg > 0 else 1), (1 if ds > 0 else 0)
            pair = HALO // 2 + X // 2 if ds > 0 else HALO // 2 - 1
            back = made[3 - at][2]

            @pl.when(inside(ds, dg))
            def _():
                back.wait_recv()
                for at, (ch_a, ch_b, right) in enumerate(corner_sets):
                    tile = cland[side, end, at]
                    h1[side, ch_a, pair] = tile
                    h1[side, ch_b, pair] = pltpu.roll(tile, 6, 0)
                    h1[side, right[0], pair] = pltpu.roll(tile, 3, 0)
                    if len(right) == 2:
                        h1[side, right[1], pair] = pltpu.roll(tile, 5 if side else 1, 0)

    corners = corner_copies()
    zeroth = copies(e1a, e1a, s1, h1, send0, recv0, 6, 7, 4)
    first = copies(e1a, e1a, s1, h1, send1, recv1, 0, 3, 4)
    rest = copies(e1a, e1a, s1, h1, send4, recv4, 3, 6, 4, REACH - 1)
    second = copies(e2a, e2a, s2, h2, send2, recv2, reach=REACH - 1)
    third = copies(rqa, rqa, s3, h3, send3, recv3, 0, 3, 4, 1, REACH)
    outer = copies(rqa, rqa, s3, h3, sendq, recvq, 3, 6, 2, REACH - 1, REACH)
    wedges = wedge_copies()
    meet(barrier, 1)
    begin(zeroth)
    begin(corners)
    begin(first)
    begin(rest)
    greet(known.at[0], rounds[0])
    turn_out(rows[3], outb.at[3])
    inb[3, si] = outb[3, si]
    for at in range(len(rounds) - 2):
        meet(known.at[at], rounds[at])
        greet(known.at[at + 1], rounds[at + 1])
    finish_recv(zeroth, recv0)
    corner_unpack(corners)
    meet(known.at[len(rounds) - 2], rounds[-2])
    greet(known.at[len(rounds) - 1], rounds[-1])

    def open0(i, _):
        e1b[6, 2 * i], e1b[6, 2 * i + 1] = unpack(h1, 6, i)
        return 0

    def open1(i, _):
        for ch in range(6):
            e1b[ch, 2 * i], e1b[ch, 2 * i + 1] = unpack(h1, ch, i)
        return 0

    lax.fori_loop(0, (X + 2 * HALO) // 2, open0, 0)

    def link(w, other):
        return jnp.where(jnp.minimum(w, other) > 0.0, (0.5 * SPRING_SHEAR) * (w + other), 0.0)

    not_last, not_first = lane < 127, lane > 0

    def over_rows(low, high, width, body, carried=0):
        width = max(v for v in range(1, width + 1) if (high - low) % v == 0)

        def chunk(i, state):
            return body([low + i * width + o for o in range(width)], state)

        return lax.fori_loop(0, (high - low) // width, chunk, carried)

    def all_coefficients(rows_here, _):
        for x in rows_here:
            coefficients(x)
        return 0

    def coefficients(x):
        wa, wb = e1a[6, x], e1b[6, x]
        ya, yb = up_y(wa, wb)
        da, db = down_y(wa, wb)
        for w, wu, wd, yu, yd, dg, kc in (
            (wa, e1a[6, x + 1], e1a[6, x - 1], ya, da, dga, kca),
            (wb, e1b[6, x + 1], e1b[6, x - 1], yb, db, dgb, kcb),
        ):
            zu = jnp.where(not_last, up_z(w), 0.0)
            zd = jnp.where(not_first, down_z(w), 0.0)
            kc[0, x] = link(w, wu)
            kc[1, x] = link(w, yu)
            kc[2, x] = link(w, yd)
            kc[3, x] = link(w, zu)
            kc[4, x] = link(w, zd)
            sx = w + 0.5 * (wu + wd)
            sy = w + 0.5 * (yu + yd)
            sz = w + 0.5 * (zu + zd)
            every = MASS_TERM + SPRING_SHEAR * (sx + sy + sz)
            dg[0, x] = every + SHEAR_REST * sx
            dg[1, x] = every + SHEAR_REST * sy
            dg[2, x] = every + SHEAR_REST * sz

    kca[0, HALO - REACH] = link(e1a[6, HALO - REACH], e1a[6, HALO - REACH + 1])
    kcb[0, HALO - REACH] = link(e1b[6, HALO - REACH], e1b[6, HALO - REACH + 1])
    over_rows(HALO - 2, HALO + X + 2, WIDE_K, all_coefficients)
    finish_recv(first, recv1)
    finish_recv(rest, recv4)
    begin(second)
    lax.fori_loop(0, (X + 2 * HALO) // 2, open1, 0)

    def operate(x, va, vb, base, both=True):
        result = []
        coef = [[kc[j, x] for j in range(5)] + [kc[0, x - 1]] for kc in (kca, kcb)]
        for c in range(3):
            a, b = va[base + c, x], vb[base + c, x]
            ua, ub = up_y(a, b)
            la, lb = down_y(a, b)
            pair = []
            halves = ((a, va, ua, la, coef[0], dga), (b, vb, ub, lb, coef[1], dgb))
            for v, ref, u, l, k, dg in halves if both else halves[:1]:
                parts = (
                    k[0] * ref[base + c, x + 1] + k[5] * ref[base + c, x - 1],
                    k[1] * u + k[2] * l,
                    k[3] * up_z(v) + k[4] * down_z(v),
                )
                shear = parts[(c + 1) % 3] + parts[(c + 2) % 3]
                pair.append(dg[c, x] * v - (shear + (SPRING_NORMAL / SPRING_SHEAR) * parts[c]))
            result.append(pair)
        return result

    def solve(step, va, vb, rhs_of, ship_halo=None):
        def residual(rows_here, _):
            for x in rows_here:
                image = operate(x, va, vb, 0)
                for c in range(3):
                    ra, rb = rhs_of(c, x)
                    rqa[c, x] = ra - image[c][0]
                    rqb[c, x] = rb - image[c][1]
            return 0

        over_rows(HALO - 2, HALO + X + 2, WIDE_R, residual)

        def put(x, image):
            for c in range(3):
                rqa[3 + c, x] = image[c][0]
                rqb[3 + c, x] = image[c][1]

        def apply(rows_here, sums):
            rr, rq = sums
            for x in rows_here:
                image = operate(x, rqa, rqb, 0)
                for c in range(3):
                    r = rqa[c, x]
                    rr, rq = rr + r * r, rq + r * image[c][0]
                put(x, image)
            return rr, rq

        zero = jnp.zeros((8, 128), jnp.float32)
        images = [operate(x, rqa, rqb, 0) for x in (HALO - 1, HALO + X)]
        put(HALO - 1, images[0])
        put(HALO + X, images[1])
        rr, rq = over_rows(HALO, HALO + X, WIDE_A, apply, (zero, zero))
        if ship_halo is not None:
            ship_halo()
        rr, rq = total(rr), total(rq)
        mu = jnp.where(rr > 0.0, rq / jnp.where(rr > 0.0, rr, 1.0), 0.0)

        def centred(rows_here, sums):
            ww, wr, mix, wt = sums
            for x in rows_here:
                image = operate(x, rqa, rqb, 3, False)
                for c in range(3):
                    r, q, s = rqa[c, x], rqa[3 + c, x], image[c][0]
                    w, t = q - mu * r, s - mu * q
                    ww, wr, mix, wt = ww + w * w, wr + w * r, mix + (r * t + w * q), wt + w * t
            return ww, wr, mix, wt

        sums = over_rows(HALO, HALO + X, WIDE_C, centred, (zero,) * 4)
        ww, wr, mix, wt = [total(v) for v in sums]
        one = lax.broadcasted_iota(jnp.int32, (1, 128), 1)
        row = jnp.zeros((1, 128), jnp.float32)
        for at, value in enumerate((rr, rq, mu, ww, wr, mix, wt)):
            row = jnp.where(one == at, value, row)
        gath[step, me] = row

        if step == 0:
            meet(known.at[len(rounds) - 1], rounds[-1])
        for other in others:
            pltpu.make_async_remote_copy(
                src_ref=gath.at[step, me], dst_ref=gath.at[step, me], send_sem=asend.at[step], recv_sem=arecv.at[step],
                device_id=other, device_id_type=MESH).start()

    def collect(step):
        block = gath.at[step, pl.ds(0, count - 1)]
        pltpu.make_async_copy(block, block, arecv.at[step]).wait()
        table = gath[step].reshape(count, 128)
        rr, rq, mu, ww, wr, mix, wt = [table[:, at:at + 1] for at in range(7)]

        def down(v):
            return jnp.sum(v, axis=0, keepdims=True)

        norm = down(rr)
        alpha = norm / down(rq)
        rest = 1.0 - alpha * mu
        after = down(alpha * alpha * ww - 2.0 * alpha * rest * wr + rest * rest * rr)
        curved = down(rest * rest * rq - alpha * rest * mix + alpha * alpha * wt)
        ratio = after / norm
        beta = after / (curved - ratio * after / alpha)
        return jnp.broadcast_to(alpha + beta * (1.0 + ratio), (8, 128)), jnp.broadcast_to(-beta * alpha, (8, 128))

    def drain(step):
        block = gath.at[step, pl.ds(0, count - 1)]
        pltpu.make_async_copy(block, block, asend.at[step]).wait()

    def joined(c, x, near, far):
        r, q = rqa[c, x], rqa[3 + c, x]
        return jnp.where(sub == 3, pltpu.roll(r, near, 0), jnp.where(sub == 4, pltpu.roll(r, far, 0), q))

    def split(c, x, tile, row, near, far):
        r = rqb[c, x]
        rqb[c, x] = jnp.where(sub == row, pltpu.roll(tile, near, 0), jnp.where(sub == 7 - row, pltpu.roll(tile, far, 0), r))
        rqb[3 + c, x] = tile

    def ship_halo():
        def pack3(i, _):
            x = HALO + 2 * i
            for c in range(3):
                pack(s3, c, i, joined(c, x, 1, 7), joined(c, x + 1, 1, 7))
            return 0

        lax.fori_loop(0, X // 2, pack3, 0)
        for end, x in ((0, HALO), (1, HALO + X - 2)):
            for c in range(3):
                even, odd = [joined(c, x + o, 2, 6) if o == end else joined(c, x + o, 3, 5) for o in range(2)]
                k3[0, end, c, 0] = jnp.where(upper, even, pltpu.roll(odd, 4, 0))
                k3[1, end, c, 0] = jnp.where(upper, pltpu.roll(even, 4, 0), odd)
        begin(third)
        begin(wedges)
        begin(outer)

    solve(0, e1a, e1b, lambda c, x: (e1a[3 + c, x], e1b[3 + c, x]), ship_halo)
    spread_out(outb.at[3], inb.at[3], 3)
    finish_recv(second, recv2)

    def open2(i, _):
        for ch in range(3):
            e2b[ch, 2 * i], e2b[ch, 2 * i + 1] = unpack(h2, ch, i)
        return 0

    lax.fori_loop(0, (X + 2 * HALO) // 2, open2, 0)
    finish_recv(third, recv3)
    for at, (ds, dg) in enumerate(steps[4:]):
        back = wedges[3 - at][2]

        @pl.when(inside(ds, dg))
        def _():
            back.wait_recv()

    def open3(i, _):
        for c in range(3):
            even, odd = unpack(h3, c, i)
            split(c, 2 * i, even, 2, 7, 1)
            split(c, 2 * i + 1, odd, 2, 7, 1)
        return 0

    lax.fori_loop(HALO // 2, (HALO + X) // 2, open3, 0)
    for pair, one in ((HALO // 2 - 1, 1), ((HALO + X) // 2, 0)):
        for c in range(3):
            for o, tile in enumerate(unpack(h3, c, pair)):
                if o == one:
                    split(c, 2 * pair + o, tile, 1, 6, 2)
                else:
                    split(c, 2 * pair + o, tile, 0, 5, 3)
    finish_recv(outer, recvq)
    c0, c1 = collect(0)

    def step1(x, both=True):
        for c in range(3):
            u1a[c, x] = e1a[c, x] + (c0 * rqa[c, x] + c1 * rqa[3 + c, x])
            u1b[c, x] = e1b[c, x] + (c0 * rqb[c, x] + c1 * rqb[3 + c, x]) if both else jnp.zeros((8, 128), jnp.float32)

    for x in range(HALO - REACH + 1, HALO + X + REACH - 1):
        step1(x)
    step1(HALO - REACH, False)
    step1(HALO + X + REACH - 1, False)
    finish_send(zeroth)
    finish_send(corners)
    finish_send(rest)
    finish_send(first)
    finish_send(second)
    finish_send(third)
    finish_send(outer)
    finish_send(wedges)

    def rhs2(c, x):
        return (MASS_TERM * (2.0 * u1a[c, x] - e1a[c, x]) + e2a[c, x],
                MASS_TERM * (2.0 * u1b[c, x] - e1b[c, x]) + e2b[c, x])

    def early(at, ref, ch):
        for x in range(X):
            rows[at, pl.ds(x, 8, stride=X), :] = ref[ch, HALO + x]
        turn_out(rows[at], outb.at[at])
        spread_out(outb.at[at], inb.at[at], at)
        inb[at, si] = outb[at, si]

    early(2, u1a, 2)
    solve(1, u1a, u1b, rhs2)
    early(4, rqa, 2)
    early(5, rqa, 5)
    landed(inb.at[3], trecv.at[3])
    for y, piece in enumerate(regroup([inb[3, j] for j in range(ns)])):
        scale[y] = piece
    c0, c1 = collect(1)

    def step2(ra, rb, c, x):
        return ra[c, x] + (c0 * rb[c, x] + c1 * rb[3 + c, x])

    def halves(v):
        high = v.astype(jnp.bfloat16)
        return high, (v - high.astype(jnp.float32)).astype(jnp.bfloat16)

    def finish(c):
        for x in range(X):
            v = step2(u1a, rqa, c, HALO + x)
            disp_ref[c, x] = v
            rows[c, pl.ds(x, 8, stride=X), :] = v
        turned = turn_out(rows[c], outb.at[c])
        spread_out(outb.at[c], inb.at[c], c)
        inb[c, si] = outb[c, si]

    def joint(ref, j, low, high):
        return jnp.concatenate([
            ref[2, j, at:at + 8] + (c0 * ref[4, j, at:at + 8] + c1 * ref[5, j, at:at + 8])
            for at in range(low, high, 8)], axis=0)

    def finish_edges():
        for x in range(X):
            rows[6, pl.ds(x, 8, stride=X), :] = step2(u1b, rqb, 1, HALO + x)
        sides_y = rows[6].T
        zero = jnp.zeros((8, 128), jnp.float32)
        for j in range(ns):
            low, high = sides_y[zrows * j:zrows * j + 8], sides_y[zrows * j + 8:zrows * j + 16]
            tile = jnp.where(lane < 32, pltpu.roll(low, 16, 1),
                             jnp.where(lane < 64, pltpu.roll(pltpu.roll(low, 4, 0), 48, 1),
                                       jnp.where(lane < 96, pltpu.roll(high, 80, 1),
                                                 pltpu.roll(pltpu.roll(high, 4, 0), 112, 1))))
            before = pltpu.roll(joint(outb, j - 1, zrows - 8, zrows), 5, 0) if j else zero
            after = pltpu.roll(joint(outb, j + 1, 0, 8), 5, 0) if j + 1 < ns else zero
            outx[j] = jnp.where(sub == 4, before, jnp.where(sub == 5, after, tile))
        spread_out(outx, inx, 6)
        inx[si] = outx[si]

    finish(0)
    finish_edges()
    finish(1)
    for x in range(X):
        disp_ref[2, x] = step2(u1a, rqa, 2, HALO + x)
    fetched[7].wait()

    c1t, c3t = float(np.sqrt(0.5) * np.cos(np.pi / 8)), float(np.sqrt(0.5) * np.cos(3 * np.pi / 8))

    def cosine(v0, v1, v2, v3):
        s03, s12, d03, d12 = v0 + v3, v1 + v2, v0 - v3, v1 - v2
        return [0.5 * (s03 + s12), c1t * d03 + c3t * d12, 0.5 * (s03 - s12), c3t * d03 - c1t * d12]

    def encode(ch, fields):
        for b in range(Y // 4):
            for k, v in enumerate(cosine(*fields[4 * b:4 * b + 4])):
                work[ch, (4 * b + k) * zrows:(4 * b + k + 1) * zrows] = v
        parts = []
        for p in range(Y * zrows // 32):
            parts += cosine(*[work[ch, pl.ds(32 * p + n, 8, stride=4), :] for n in range(4)])
        high, low = halves(jnp.concatenate(parts, axis=0))
        done = jnp.dot(jnp.concatenate([high, low], axis=1), gt_ref[...], preferred_element_type=jnp.float32)
        done = done[:, 0:128] + done[:, 128:256]
        for p in range(Y * zrows // 32):
            for n in range(4):
                coef_ref[ch, pl.ds(32 * p + n, 8, stride=4), :] = done[(4 * p + n) * 8:(4 * p + n + 1) * 8]

    def arrived(c):
        landed(inb.at[c], trecv.at[c])
        return regroup([inb[c, j] for j in range(ns)])

    for at in (2, 4, 5):
        landed(inb.at[at], trecv.at[at])
    along = regroup([joint(inb, j, 0, zrows) for j in range(ns)])
    encode(2, along)
    field = arrived(0)
    encode(0, field)
    wide = lax.broadcasted_iota(jnp.int32, (zrows, 128), 1)
    encode(3, [scale[y] * (jnp.where(wide < 127, up_z(field[y]), 0.0) - jnp.where(wide > 0, down_z(field[y]), 0.0))
               for y in range(Y)])
    landed(inx, trecv.at[6])
    edges = regroup([inx[j] for j in range(ns)])
    stress = []
    for y in range(Y):
        low, high = along[y][0:8], along[y][8:16]
        ul, uh, dl, dh = pltpu.roll(low, 7, 0), pltpu.roll(high, 7, 0), pltpu.roll(low, 1, 0), pltpu.roll(high, 1, 0)
        first, last = sub == 0, sub == 7
        low = jnp.where(last, uh, ul) - jnp.where(first, pltpu.roll(edges[y], 4, 0), dl)
        high = jnp.where(last, pltpu.roll(edges[y], 2, 0), uh) - jnp.where(first, dl, dh)
        stress.append(scale[y] * jnp.concatenate([low, high], axis=0))
    encode(5, stress)
    field = arrived(1)
    encode(1, field)
    outside = []
    for side in range(2):
        quarter = [edges[2 * q + side] for q in range(4)]
        outside.append(jnp.concatenate([jnp.where(upper, quarter[q], pltpu.roll(quarter[q + 1], 4, 0)) for q in (0, 2)], axis=0))
    field = [outside[0]] + field + [outside[1]]
    encode(4, [scale[y] * (field[y + 2] - field[y]) for y in range(Y)])
    drain(0)
    drain(1)
    for at in range(6):
        landed(inb.at[at], tsend.at[at])
    landed(inx, tsend.at[6])


def store(disp_in, coef_in, disp_out, coef_out, sems):
    copies = [pltpu.make_async_copy(disp_in, disp_out, sems.at[0]), pltpu.make_async_copy(coef_in, coef_out, sems.at[1])]
    for copy in copies:
        copy.start()
    for copy in copies:
        copy.wait()


def fused(mesh, u_now, u_prev, force, stiffness, broken, flags):
    ns, ng = mesh.shape["slab"], mesh.shape["grp"]
    _, X, Y, Z = u_now.shape
    xe, pairs, half = X + 2 * HALO, X // 2 + HALO, X // 2
    zrows = Z // ns
    ez = jnp.asarray(np.kron(np.eye(Z // 4), np.ones((1, 4))), jnp.float32)
    gth, gtl = split_table(wavelet_table(X * ns).T)
    gt = jnp.asarray(np.block([[gth, gtl], [gth, np.zeros_like(gtl)]]), jnp.bfloat16)

    def vm(*shape):
        return pltpu.VMEM(shape, jnp.float32)

    def ext(n):
        return vm(n, xe, Y, Z)

    def stage(n):
        return vm(2, n, half, Y, Z)

    def land(n):
        return vm(2, n, pairs, Y, Z)

    dma = pltpu.SemaphoreType.DMA
    shapes = (u_now.shape, (6, Y * zrows, X * ns))
    operands = [pltpu.with_memory_space_constraint(v, pltpu.HBM)
                for v in (u_now, u_prev, force, stiffness, broken, flags, ez, gt)]
    results = pl.pallas_call(
        lambda *refs: kernel(ns, ng, *refs),
        name="lattice",
        out_shape=tuple(vm(*shape) for shape in shapes),
        in_specs=[pl.BlockSpec(memory_space=pltpu.MemorySpace.HBM)] * 8,
        out_specs=(pl.BlockSpec(memory_space=pltpu.VMEM),) * 2,
        scratch_shapes=[
            vm(*u_now.shape), vm(*u_now.shape), vm(*u_now.shape), vm(*stiffness.shape),
            pltpu.VMEM(broken.shape, broken.dtype), pltpu.VMEM(flags.shape, flags.dtype),
            vm(*ez.shape), pltpu.VMEM(gt.shape, gt.dtype), pltpu.SemaphoreType.DMA((8,)),
            ext(7), ext(7), stage(7), land(7),
            ext(3), ext(3), stage(3), land(3),
            ext(6), ext(6), stage(3), land(3), vm(2, 2, 3, 1, Y, Z),
            ext(3), ext(3), vm(Y, zrows, X * ns), ext(3), ext(3), ext(5), ext(5),
            pltpu.SemaphoreType.REGULAR((4,)), vm(2, ns * ng, 1, 128), vm(7, Y * X, Z), vm(6, ns, zrows, 128), vm(6, ns, zrows, 128), vm(ns, 8, 128), vm(ns, 8, 128), vm(6, Y * zrows, X * ns),
            vm(2, 2, 2, Y, Z), vm(2, 2, 2, Y, Z), dma((4,)), dma((4,)), dma((4,)), dma((4,)),
            dma((4,)), dma((4,)), dma((4,)), dma((4,)), dma((8,)), dma((8,)), dma((4,)), dma((4,)), dma((2,)), dma((2,)), dma((4,)), dma((4,)),
            dma((2,)), dma((2,)), dma((7,)), dma((7,)),
        ],
        compiler_params=pltpu.CompilerParams(collective_id=0, has_side_effects=True, vmem_limit_bytes=24 << 20),
    )(*operands)
    disp, coef = pl.pallas_call(
        store,
        name="store",
        out_shape=tuple(jax.ShapeDtypeStruct(shape, jnp.float32) for shape in shapes),
        in_specs=[pl.BlockSpec(memory_space=pltpu.VMEM)] * 2,
        out_specs=(pl.BlockSpec(memory_space=pltpu.MemorySpace.HBM),) * 2,
        scratch_shapes=[dma((2,))],
        compiler_params=pltpu.CompilerParams(vmem_limit_bytes=1 << 20),
    )(*[pltpu.with_memory_space_constraint(v, pltpu.VMEM) for v in results])
    return disp, coef.reshape(6, Y, zrows, X * ns)


def fits(mesh, shape):
    ns, ng = mesh.shape["slab"], mesh.shape["grp"]
    x, y, z = shape[1] // ns, shape[2] // ng, shape[3]
    return y == 8 and z == 128 and x * y == 128 and x * ns == 128 and z % (8 * ns) == 0


def entry(mesh, *args):
    ns, ng = mesh.shape["slab"], mesh.shape["grp"]
    _, x, y, z = args[0].shape
    if fits(mesh, (3, x * ns, y * ng, z)):
        return fused(mesh, *args)
    return body(*args)


def solution(mesh):
    return jax.shard_map(
        lambda *args: entry(mesh, *args),
        mesh=mesh,
        in_specs=(
            P(None, "slab", "grp", None),
            P(None, "slab", "grp", None),
            P(None, "slab", "grp", None),
            P("slab", "grp", None),
            P("slab", "grp", None),
            P("slab", "grp", None),
        ),
        out_specs=(P(None, "slab", "grp", None), P(None, "grp", "slab", None)),
        check_vma=False,
    )
```

```python
import jax
import jax.numpy as jnp
import numpy as np
from jax import lax
from jax.experimental import pallas as pl
from jax.experimental.pallas import tpu as pltpu
from jax.sharding import PartitionSpec as P

STEPS = 2
ITERS = 2
LEVELS = 3


SPRING_NORMAL = 1.0
SPRING_SHEAR = 0.4
MASS_TERM = 1.0
CRACK_CUT = 0.9


def with_halo(block, sides, width):
    for axis, dim in sides:
        count = lax.axis_size(axis)
        forward = [(i, i + 1) for i in range(count - 1)]
        backward = [(target, source) for source, target in forward]
        low = lax.ppermute(
            lax.slice_in_dim(block, block.shape[dim] - width, None, axis=dim), axis, forward
        )
        high = lax.ppermute(lax.slice_in_dim(block, 0, width, axis=dim), axis, backward)
        block = jnp.concatenate([low, block, high], axis=dim)
    return block


def cosine_table():
    freq = np.arange(4)[:, None]
    place = np.arange(4)[None, :]
    factor = np.where(freq == 0, 0.5, np.sqrt(0.5))
    return factor * np.cos(np.pi * (2 * place + 1) * freq / 8.0)


def block_table(count):
    return jnp.asarray(np.kron(np.eye(count // 4), cosine_table()), jnp.float32)


def spread(mask):
    values = mask.astype(jnp.float32)
    size_a, size_b, size_c = values.shape
    wide = jnp.broadcast_to(values[:, None, :, None, :, None], (size_a, 4, size_b, 4, size_c, 4))
    return wide.reshape(size_a * 4, size_b * 4, size_c * 4)


def sides(padded, axis_index):
    leading = padded.ndim - 3

    def cut(offset):
        index_list = [slice(None)] * leading + [slice(1, -1)] * 3
        length = padded.shape[leading + axis_index]
        index_list[leading + axis_index] = slice(1 + offset, length - 1 + offset)
        return padded[tuple(index_list)]

    return (cut(1), cut(-1))


def springs(field, weight, field_pad, weight_pad):
    result = MASS_TERM * field
    for axis_index in range(3):
        upper_v, lower_v = sides(field_pad, axis_index)
        upper_w, lower_w = sides(weight_pad, axis_index)
        k_upper = 0.5 * (weight + upper_w)
        k_lower = 0.5 * (weight + lower_w)
        change = k_upper * (field - upper_v) + k_lower * (field - lower_v)
        coupling = jnp.array(
            [SPRING_NORMAL if comp == axis_index else SPRING_SHEAR for comp in range(3)],
            jnp.float32,
        ).reshape(3, 1, 1, 1)
        result = result + coupling * change
    return result


def faces(field):
    padded = with_halo(field, (("slab", 1), ("grp", 2)), 1)
    return jnp.pad(padded, ((0, 0), (0, 0), (0, 0), (1, 1)))


def stresses(carry, field_pad):
    rows_out = []
    for axis_index in range(3):
        upper_v, lower_v = sides(field_pad, axis_index)
        rows_out.append(SPRING_NORMAL * carry * 0.5 * (upper_v[axis_index] - lower_v[axis_index]))
    return jnp.stack(rows_out)


def paired_sum(residual, image):
    return lax.psum((jnp.sum(residual * residual), jnp.sum(residual * image)), ("slab", "grp"))


def lift(signal):
    even = signal[..., 0::2]
    odd = signal[..., 1::2]
    detail = odd - 0.5 * (even + jnp.roll(even, -1, axis=-1))
    approx = even + 0.25 * (jnp.roll(detail, 1, axis=-1) + detail)
    return (approx, detail)


def wavelet(signal):
    pieces = []
    approx = signal
    for level_index in range(LEVELS):
        approx, detail = lift(approx)
        pieces.insert(0, detail)
    return jnp.concatenate([approx] + pieces, axis=-1)


def body(u_now, u_prev, force, stiffness, broken, flags):
    weight = stiffness * (1.0 - CRACK_CUT * spread(broken))
    carry = spread(flags) * weight
    weight_pad = with_halo(weight, (("slab", 0), ("grp", 1)), 1)
    weight_pad = jnp.pad(weight_pad, ((0, 0), (0, 0), (1, 1)))

    def operate(field):
        return springs(field, weight, faces(field), weight_pad)

    for step_index in range(STEPS):
        rhs = MASS_TERM * (2.0 * u_now - u_prev) + force
        guess = u_now
        residual = rhs - operate(guess)
        image = operate(residual)
        norm_now, product = paired_sum(residual, image)
        alpha = norm_now / product
        direction, along = (residual, image)
        for turn_index in range(ITERS):
            guess = guess + alpha * direction
            residual = residual - alpha * along
            if turn_index + 1 < ITERS:
                image = operate(residual)
                norm_next, product = paired_sum(residual, image)
                ratio = norm_next / norm_now
                alpha = norm_next / (product - ratio * norm_next / alpha)
                direction = residual + ratio * direction
                along = image + ratio * along
                norm_now = norm_next
        u_prev = u_now
        u_now = guess
    stress = stresses(carry, faces(u_now))
    fields = jnp.concatenate([u_now, stress], axis=0)
    table_x = block_table(fields.shape[1])
    table_y = block_table(fields.shape[2])
    table_z = block_table(fields.shape[3])
    blockc = jnp.einsum("ax,hxyz->hayz", table_x, fields, precision=lax.Precision.HIGHEST)
    blockc = jnp.einsum("by,hxyz->hxbz", table_y, blockc, precision=lax.Precision.HIGHEST)
    blockc = jnp.einsum("hxyz,cz->hxyc", blockc, table_z, precision=lax.Precision.HIGHEST)
    moved = jnp.transpose(blockc, (0, 2, 3, 1))
    shipped = lax.all_to_all(moved, "slab", split_axis=2, concat_axis=3, tiled=True)
    coeffs = wavelet(shipped)
    return (u_now, coeffs)


MESH = pl.DeviceIdType.MESH
HALO = 4
REACH = 3
SHEAR_REST = SPRING_NORMAL - SPRING_SHEAR
WIDE_R, WIDE_A, WIDE_C, WIDE_K = 20, 16, 16, 20


def wavelet_table(count):
    table = np.kron(np.eye(count // 4), cosine_table())
    pieces = []
    approx = table
    for level_index in range(LEVELS):
        even, odd = approx[0::2], approx[1::2]
        detail = odd - 0.5 * (even + np.roll(even, -1, axis=0))
        approx = even + 0.25 * (np.roll(detail, 1, axis=0) + detail)
        pieces.insert(0, detail)
    return np.concatenate([approx] + pieces, axis=0)


def split_table(table):
    high = table.astype(jnp.bfloat16).astype(np.float64)
    return high, (table - high).astype(jnp.bfloat16).astype(np.float64)


def sub_index():
    return lax.broadcasted_iota(jnp.int32, (8, 128), 0)


def lane_index():
    return lax.broadcasted_iota(jnp.int32, (8, 128), 1)


def up_y(a, b):
    ra, rb = pltpu.roll(a, 7, 0), pltpu.roll(b, 7, 0)
    last = sub_index() == 7
    return jnp.where(last, rb, ra), jnp.where(last, ra, rb)


def down_y(a, b):
    ra, rb = pltpu.roll(a, 1, 0), pltpu.roll(b, 1, 0)
    first = sub_index() == 0
    return jnp.where(first, rb, ra), jnp.where(first, ra, rb)


def up_z(v):
    return pltpu.roll(v, 127, 1)


def down_z(v):
    return pltpu.roll(v, 1, 1)


def total(v):
    return jnp.sum(jnp.sum(v, axis=0, keepdims=True), axis=1, keepdims=True)


def kernel(ns, ng, u_in, p_in, f_in, k_in, br_in, fl_in, ez_in, gt_in,
           disp_ref, coef_ref,
           u_ref, p_ref, f_ref, k_ref, br_ref, fl_ref, ez_ref, gt_ref, isem,
           e1a, e1b, s1, h1, e2a, e2b, s2, h2, rqa, rqb, s3, h3, k3, ends,
           u1a, u1b, scale, dga, dgb, kca, kcb, known, gath, rows, outb, inb, outx, inx, work,
           ctake, cland, csend, crecv, send4, recv4, send0, recv0, send1, recv1, send2, recv2, send3, recv3, sendq, recvq, sendk, recvk, sendu, recvu, sendw, recvw, ftake, fland, sendf, recvf, asend, arecv, tsend, trecv):
    X, Y, Z = u_ref.shape[1:]
    si, gi = lax.axis_index("slab"), lax.axis_index("grp")
    me = si * ng + gi
    count = ns * ng
    barrier = pltpu.get_barrier_semaphore()

    def mirrored(place, mask, length):
        bit, result = 1, 0
        while bit < length:
            here = place // bit % 2
            result = result + bit * (1 - here if mask // bit % 2 else here)
            bit *= 2
        return result

    others = []
    for k in sorted(range(ns), key=lambda k: -min(k, ns - k)):
        for g in range(ng):
            if k or g:
                others.append((lax.rem(si + k, ns), lax.rem(gi + g, ng)))

    sub, lane = sub_index(), lane_index()
    upper = sub < 4

    steps = [(-1, 0), (1, 0), (0, -1), (0, 1), (-1, -1), (-1, 1), (1, -1), (1, 1)]

    def inside(ds, dg):
        ok = None
        if ds:
            ok = (si >= -ds) if ds < 0 else (si <= ns - 1 - ds)
        if dg:
            more = (gi >= -dg) if dg < 0 else (gi <= ng - 1 - dg)
            ok = more if ok is None else jnp.logical_and(ok, more)
        return ok

    def around(reach):
        return [(ds, dg) for ds in (-reach, 0, reach) for dg in (-reach, 0, reach)
                if (ds or dg) and abs(ds) < ns and abs(dg) < ng]

    def greet(sem, reach):
        for ds, dg in around(reach):
            @pl.when(inside(ds, dg))
            def _():
                pl.semaphore_signal(sem, inc=1, device_id=(si + ds, gi + dg), device_id_type=MESH)

    def meet(sem, reach):
        pl.semaphore_wait(sem, sum(jnp.where(inside(ds, dg), 1, 0) for ds, dg in around(reach)))

    rounds = []
    while (rounds[-1] * 2 if rounds else 1) < max(ns, ng):
        rounds.append(rounds[-1] * 2 if rounds else 1)

    greet(barrier, 1)
    fetched = []
    for at, (source, target) in enumerate((
        (br_in, br_ref), (fl_in, fl_ref), (ez_in, ez_ref), (k_in, k_ref), (u_in, u_ref), (p_in, p_ref),
        (f_in, f_ref), (gt_in, gt_ref),
    )):
        fetch = pltpu.make_async_copy(source, target, isem.at[at])
        fetch.start()
        fetched.append(fetch)

    def copies(ea, dst_a, stage, land, send, recv, low=0, high=None, ways=8, reach=REACH, depth=None, ends=None):
        depth = reach if depth is None else depth
        half = X // 2
        edge = HALO // 2
        made = []
        chans = pl.ds(low, (ea.shape[0] if high is None else high) - low)
        for at, (ds, dg) in enumerate(steps[:ways]):
            if dg == 0:
                if ends is not None:
                    source = ends.at[0 if ds < 0 else 1]
                    target = dst_a.at[chans, pl.ds(HALO + X if ds < 0 else HALO - depth, reach)]
                elif ds < 0:
                    source = ea.at[chans, pl.ds(HALO + depth - reach, reach)]
                    target = dst_a.at[chans, pl.ds(HALO + X + depth - reach, reach)]
                else:
                    source = ea.at[chans, pl.ds(HALO + X - depth, reach)]
                    target = dst_a.at[chans, pl.ds(HALO - depth, reach)]
            else:
                side = 0 if dg < 0 else 1
                if ds == 0:
                    source, target = stage.at[side, chans], land.at[side, chans, pl.ds(edge, half)]
                elif ds < 0:
                    source = stage.at[side, chans, pl.ds(0, 1)]
                    target = land.at[side, chans, pl.ds(edge + half, 1)]
                else:
                    source = stage.at[side, chans, pl.ds(half - 1, 1)]
                    target = land.at[side, chans, pl.ds(edge - 1, 1)]
            made.append((ds, dg, pltpu.make_async_remote_copy(
                src_ref=source, dst_ref=target, send_sem=send.at[at], recv_sem=recv.at[at ^ 1 if at < 4 else 11 - at],
                device_id=(si + ds, gi + dg), device_id_type=MESH)))
        return made

    def begin(made):
        for ds, dg, copy in made:
            @pl.when(inside(ds, dg))
            def _():
                copy.start()

    def finish_recv(made, recv):
        for at, (ds, dg) in enumerate(steps[:len(made)]):
            back = made[at ^ 1 if at < 4 else 11 - at][2]

            @pl.when(inside(ds, dg))
            def _():
                back.wait_recv()

    def finish_send(made):
        for ds, dg, copy in made:
            @pl.when(inside(ds, dg))
            def _():
                copy.wait_send()

    def blank(dst_a, land):
        zero_a = jnp.zeros((dst_a.shape[0], HALO) + dst_a.shape[2:], jnp.float32)
        half, edge = X // 2, HALO // 2
        zero_l = jnp.zeros((land.shape[1], edge, 8, 128), jnp.float32)

        @pl.when(si == 0)
        def _():
            dst_a[:, pl.ds(0, HALO)] = zero_a
            for side in range(2):
                land[side, :, pl.ds(0, edge)] = zero_l

        @pl.when(si == ns - 1)
        def _():
            dst_a[:, pl.ds(HALO + X, HALO)] = zero_a
            for side in range(2):
                land[side, :, pl.ds(edge + half, edge)] = zero_l

        for side, edge_here in ((0, gi == ng - 1), (1, gi == 0)):
            @pl.when(edge_here)
            def _(side=side):
                land[side] = jnp.zeros(land.shape[1:], jnp.float32)

    def pack(stage, ch, pair, even, odd):
        stage[0, ch, pair] = jnp.where(upper, even, pltpu.roll(odd, 4, 0))
        stage[1, ch, pair] = jnp.where(upper, pltpu.roll(even, 4, 0), odd)

    def unpack(land, ch, pair):
        high, low = land[0, ch, pair], land[1, ch, pair]
        return (jnp.where(upper, high, pltpu.roll(low, 4, 0)),
                jnp.where(upper, pltpu.roll(high, 4, 0), low))

    def spread_rows(mask):
        wide = jnp.dot(mask.astype(jnp.float32), ez_ref[...], preferred_element_type=jnp.float32)
        return jnp.where(upper, jnp.broadcast_to(wide[0:1], (8, 128)), jnp.broadcast_to(wide[1:2], (8, 128)))

    for at in range(4):
        fetched[at].wait()
    for bx in range(X // 4):
        cut = 1.0 - CRACK_CUT * spread_rows(br_ref[bx])
        flag = spread_rows(fl_ref[bx])
        for at in range(4):
            x = bx * 4 + at
            w = k_ref[x] * cut
            e1a[6, HALO + x] = w
            rows[3, pl.ds(x, 8, stride=X), :] = (SPRING_NORMAL * 0.5) * (flag * w)

    def own(i, _):
        for c in range(3):
            tiles = []
            for o in range(2):
                x = 2 * i + o
                u = u_ref[c, x]
                f = f_ref[c, x]
                rhs = MASS_TERM * (2.0 * u - p_ref[c, x]) + f
                e1a[c, HALO + x] = u
                e1a[3 + c, HALO + x] = rhs
                e2a[c, HALO + x] = f
                tiles.append((u, rhs, f))
            pack(s1, c, i, tiles[0][0], tiles[1][0])
            pack(s1, 3 + c, i, tiles[0][1], tiles[1][1])
            pack(s2, c, i, tiles[0][2], tiles[1][2])
        pack(s1, 6, i, e1a[6, HALO + 2 * i], e1a[6, HALO + 2 * i + 1])
        return 0

    for at in range(4, 7):
        fetched[at].wait()
    lax.fori_loop(0, X // 2, own, 0)
    blank(e1a, h1)
    blank(e2a, h2)
    blank(rqa, h3)

    zrows = Z // ns

    def turn_out(value, out):
        turned = value.T
        for j in range(ns):
            out[j] = turned[j * zrows:(j + 1) * zrows]

    def spread_out(source, target, at):
        for m in reversed(range(1, ns)):
            to = mirrored(si, m, ns)
            pltpu.make_async_remote_copy(
                src_ref=source.at[to], dst_ref=target.at[si], send_sem=tsend.at[at], recv_sem=trecv.at[at],
                device_id=(to, gi), device_id_type=MESH).start()

    def landed(target, sem):
        block = target.at[pl.ds(0, ns - 1)]
        pltpu.make_async_copy(block, block, sem).wait()

    def regroup(pieces):
        lanes = lax.broadcasted_iota(jnp.int32, pieces[0].shape, 1)
        gap = ns // 2
        while gap:
            keep = (lanes // (X * gap)) % 2 == 0
            mixed = list(pieces)
            for j in range(ns):
                if (j // gap) % 2 == 0:
                    a, b = pieces[j], pieces[j + gap]
                    mixed[j] = jnp.where(keep, a, pltpu.roll(b, X * gap, 1))
                    mixed[j + gap] = jnp.where(keep, pltpu.roll(a, 128 - X * gap, 1), b)
            pieces = mixed
            gap //= 2
        return pieces

    not_last, not_first = lane < 127, lane > 0

    def inner_ends():
        for end, x in ((0, HALO + 1), (1, HALO + X - 2)):
            w = e1a[6, x]
            along = (0.5 * (w + e1a[6, x + 1]), 0.5 * (w + e1a[6, x - 1]),
                     jnp.where(sub < 7, 0.5 * (w + pltpu.roll(w, 7, 0)), 0.0),
                     jnp.where(sub > 0, 0.5 * (w + pltpu.roll(w, 1, 0)), 0.0),
                     0.5 * (w + jnp.where(not_last, up_z(w), 0.0)), 0.5 * (w + jnp.where(not_first, down_z(w), 0.0)))
            for c in range(3):
                v = e1a[c, x]
                parts = (along[0] * (v - e1a[c, x + 1]) + along[1] * (v - e1a[c, x - 1]),
                         along[2] * (v - pltpu.roll(v, 7, 0)) + along[3] * (v - pltpu.roll(v, 1, 0)),
                         along[4] * (v - jnp.where(not_last, up_z(v), 0.0))
                         + along[5] * (v - jnp.where(not_first, down_z(v), 0.0)))
                image = MASS_TERM * v + (SPRING_SHEAR * (parts[0] + parts[1] + parts[2]) + SHEAR_REST * parts[c])
                ends[end, c, 1 - end] = e1a[3 + c, x] - image
                ends[end, c, end] = e1a[3 + c, x - 1 + 2 * end]

    def outer_residual(x):
        wa, wb = e1a[6, x], e1b[6, x]
        above = jnp.where(sub == 7, 0.5 * (wa + up_y(wa, wb)[0]), 0.0)
        below = jnp.where(sub == 0, 0.5 * (wa + down_y(wa, wb)[0]), 0.0)
        for c in range(3):
            a, b = e1a[c, x], e1b[c, x]
            change = above * (a - up_y(a, b)[0]) + below * (a - down_y(a, b)[0])
            rqa[c, x] = e1a[3 + c, x] - (SPRING_NORMAL if c == 1 else SPRING_SHEAR) * change
            rqb[c, x] = jnp.zeros((8, 128), jnp.float32)

    def tip_copies():
        made = []
        for at, (ds, dg) in enumerate(steps[4:]):
            side, end = (0 if dg < 0 else 1), (0 if ds < 0 else 1)
            made.append((ds, dg, pltpu.make_async_remote_copy(
                src_ref=ftake.at[side, end], dst_ref=fland.at[side, 1 - end],
                send_sem=sendf.at[at], recv_sem=recvf.at[3 - at],
                device_id=(si + ds, gi + dg), device_id_type=MESH)))
        return made

    def tip_unpack(made):
        for at, (ds, dg) in enumerate(steps[4:]):
            side, end = (0 if dg > 0 else 1), (1 if ds > 0 else 0)
            pair = HALO // 2 + X // 2 if ds > 0 else HALO // 2 - 1
            back = made[3 - at][2]

            @pl.when(inside(ds, dg))
            def _():
                back.wait_recv()
                tile = fland[side, end]
                for c in range(3):
                    h2[side, c, pair] = pltpu.roll(tile, 8 - 2 * c, 0) if c else tile

    def wedge_copies():
        made = []
        for at, (ds, dg) in enumerate(steps[4:]):
            side, end = (0 if dg < 0 else 1), (0 if ds < 0 else 1)
            pair = HALO // 2 + X // 2 if ds < 0 else HALO // 2 - 1
            made.append((ds, dg, pltpu.make_async_remote_copy(
                src_ref=k3.at[side, end], dst_ref=h3.at[side, :, pl.ds(pair, 1)],
                send_sem=sendk.at[at], recv_sem=recvk.at[3 - at],
                device_id=(si + ds, gi + dg), device_id_type=MESH)))
        return made

    def corner_copies():
        made = []
        for at, (ds, dg) in enumerate(steps[4:]):
            side, end = (0 if dg < 0 else 1), (0 if ds < 0 else 1)
            made.append((ds, dg, pltpu.make_async_remote_copy(
                src_ref=ctake.at[side, end], dst_ref=cland.at[side, 1 - end],
                send_sem=csend.at[at], recv_sem=crecv.at[3 - at],
                device_id=(si + ds, gi + dg), device_id_type=MESH)))
        return made

    def corner_rows(side, end):
        dx1, dx2 = (0, 4) if end == 0 else (4, 0)
        dy1, dy2 = (0, 1) if side == 0 else (3, 2)
        return dx1 + dy1, dx1 + dy2, dx2 + dy1

    def any_row(places):
        found = sub == places[0]
        for place in places[1:]:
            found = jnp.logical_or(found, sub == place)
        return found

    corner_sets = ((0, 1, (3, 4)), (2, 6, (5,)))
    for side in range(2):
        for end in range(2):
            places = corner_rows(side, end)
            first_here, second_here = any_row(places), any_row([(v + 2) % 8 for v in places])
            for at, (ch_a, ch_b, right) in enumerate(corner_sets):
                tiles = [s1[side, ch, end * (X // 2 - 1)] for ch in (ch_a, ch_b) + right]
                tile = pltpu.roll(tiles[2], 5, 0)
                if len(right) == 2:
                    tile = jnp.where(sub == (places[0] + 5) % 8, tile, pltpu.roll(tiles[3], 3 if side else 7, 0))
                tile = jnp.where(first_here, tiles[0], jnp.where(second_here, pltpu.roll(tiles[1], 2, 0), tile))
                ctake[side, end, at] = tile
            near = [s2[side, c, end * (X // 2 - 1)] for c in range(3)]
            ftake[side, end] = jnp.where(sub == places[0], near[0], jnp.where(
                sub == (places[0] + 2) % 8, pltpu.roll(near[1], 2, 0), pltpu.roll(near[2], 4, 0)))

    def corner_unpack(made):
        for at, (ds, dg) in enumerate(steps[4:]):
            side, end = (0 if dg > 0 else 1), (1 if ds > 0 else 0)
            pair = HALO // 2 + X // 2 if ds > 0 else HALO // 2 - 1
            back = made[3 - at][2]

            @pl.when(inside(ds, dg))
            def _():
                back.wait_recv()
                for at, (ch_a, ch_b, right) in enumerate(corner_sets):
                    tile = cland[side, end, at]
                    h1[side, ch_a, pair] = tile
                    h1[side, ch_b, pair] = pltpu.roll(tile, 6, 0)
                    h1[side, right[0], pair] = pltpu.roll(tile, 3, 0)
                    if len(right) == 2:
                        h1[side, right[1], pair] = pltpu.roll(tile, 5 if side else 1, 0)

    corners = corner_copies()
    zeroth = copies(e1a, e1a, s1, h1, send0, recv0, 6, 7, 4, REACH - 1)
    first = copies(e1a, e1a, s1, h1, send1, recv1, 0, 3, 4, REACH - 1)
    rest = copies(e1a, e1a, s1, h1, send4, recv4, 3, 6, 4, REACH - 1, None, ends)
    late = (copies(e1a, e1a, s1, h1, sendu, recvu, 0, 3, 2, 1, REACH),
            copies(e1a, e1a, s1, h1, sendw, recvw, 6, 7, 2, 1, REACH))
    second = copies(e2a, e2a, s2, h2, send2, recv2, 0, 3, 4, REACH - 1)
    tips = tip_copies()
    third = copies(rqa, rqa, s3, h3, send3, recv3, 0, 3, 4, 1, REACH)
    outer = copies(rqa, rqa, s3, h3, sendq, recvq, 3, 6, 2, REACH - 1, REACH)
    wedges = wedge_copies()
    meet(barrier, 1)
    begin(zeroth)
    begin(corners)
    begin(first)
    inner_ends()
    begin(rest)
    greet(known.at[0], rounds[0])
    turn_out(rows[3], outb.at[3])
    inb[3, si] = outb[3, si]
    for at in range(len(rounds) - 2):
        meet(known.at[at], rounds[at])
        greet(known.at[at + 1], rounds[at + 1])
    finish_recv(zeroth, recv0)
    corner_unpack(corners)
    meet(known.at[len(rounds) - 2], rounds[-2])
    greet(known.at[len(rounds) - 1], rounds[-1])

    def open0(i, _):
        e1b[6, 2 * i], e1b[6, 2 * i + 1] = unpack(h1, 6, i)
        return 0

    def open1(i, _):
        for ch in range(6):
            e1b[ch, 2 * i], e1b[ch, 2 * i + 1] = unpack(h1, ch, i)
        return 0

    lax.fori_loop(0, (X + 2 * HALO) // 2, open0, 0)

    def link(w, other):
        return jnp.where(jnp.minimum(w, other) > 0.0, (0.5 * SPRING_SHEAR) * (w + other), 0.0)


    def over_rows(low, high, width, body, carried=0):
        width = max(v for v in range(1, width + 1) if (high - low) % v == 0)

        def chunk(i, state):
            return body([low + i * width + o for o in range(width)], state)

        return lax.fori_loop(0, (high - low) // width, chunk, carried)

    def all_coefficients(rows_here, _):
        for x in rows_here:
            coefficients(x)
        return 0

    def coefficients(x):
        wa, wb = e1a[6, x], e1b[6, x]
        ya, yb = up_y(wa, wb)
        da, db = down_y(wa, wb)
        for w, wu, wd, yu, yd, dg, kc in (
            (wa, e1a[6, x + 1], e1a[6, x - 1], ya, da, dga, kca),
            (wb, e1b[6, x + 1], e1b[6, x - 1], yb, db, dgb, kcb),
        ):
            zu = jnp.where(not_last, up_z(w), 0.0)
            zd = jnp.where(not_first, down_z(w), 0.0)
            kc[0, x] = link(w, wu)
            kc[1, x] = link(w, yu)
            kc[2, x] = link(w, yd)
            kc[3, x] = link(w, zu)
            kc[4, x] = link(w, zd)
            sx = w + 0.5 * (wu + wd)
            sy = w + 0.5 * (yu + yd)
            sz = w + 0.5 * (zu + zd)
            every = MASS_TERM + SPRING_SHEAR * (sx + sy + sz)
            dg[0, x] = every + SHEAR_REST * sx
            dg[1, x] = every + SHEAR_REST * sy
            dg[2, x] = every + SHEAR_REST * sz

    def edge_link(x):
        kca[0, x] = link(e1a[6, x], e1a[6, x + 1])
        kcb[0, x] = link(e1b[6, x], e1b[6, x + 1])

    edge_link(HALO - 2)
    over_rows(HALO - 1, HALO + X + 1, WIDE_K, all_coefficients)
    finish_recv(first, recv1)
    finish_recv(rest, recv4)
    begin(second)
    begin(tips)
    for made in late:
        begin(made)
    lax.fori_loop(0, (X + 2 * HALO) // 2, open1, 0)

    def operate(x, va, vb, base, both=True):
        result = []
        coef = [[kc[j, x] for j in range(5)] + [kc[0, x - 1]] for kc in (kca, kcb)]
        for c in range(3):
            a, b = va[base + c, x], vb[base + c, x]
            ua, ub = up_y(a, b)
            la, lb = down_y(a, b)
            pair = []
            halves = ((a, va, ua, la, coef[0], dga), (b, vb, ub, lb, coef[1], dgb))
            for v, ref, u, l, k, dg in halves if both else halves[:1]:
                parts = (
                    k[0] * ref[base + c, x + 1] + k[5] * ref[base + c, x - 1],
                    k[1] * u + k[2] * l,
                    k[3] * up_z(v) + k[4] * down_z(v),
                )
                shear = parts[(c + 1) % 3] + parts[(c + 2) % 3]
                pair.append(dg[c, x] * v - (shear + (SPRING_NORMAL / SPRING_SHEAR) * parts[c]))
            result.append(pair)
        return result

    def solve(step, va, vb, rhs_of, reach, ship_halo=None):
        def residual(rows_here, _):
            for x in rows_here:
                image = operate(x, va, vb, 0)
                for c in range(3):
                    ra, rb = rhs_of(c, x)
                    rqa[c, x] = ra - image[c][0]
                    rqb[c, x] = rb - image[c][1]
            return 0

        over_rows(HALO - reach, HALO + X + reach, WIDE_R, residual)

        def put(x, image):
            for c in range(3):
                rqa[3 + c, x] = image[c][0]
                rqb[3 + c, x] = image[c][1]

        def apply(rows_here, sums):
            rr, rq = sums
            for x in rows_here:
                image = operate(x, rqa, rqb, 0)
                for c in range(3):
                    r = rqa[c, x]
                    rr, rq = rr + r * r, rq + r * image[c][0]
                put(x, image)
            return rr, rq

        zero = jnp.zeros((8, 128), jnp.float32)
        images = [operate(x, rqa, rqb, 0) for x in (HALO - 1, HALO + X)]
        put(HALO - 1, images[0])
        put(HALO + X, images[1])
        rr, rq = over_rows(HALO, HALO + X, WIDE_A, apply, (zero, zero))
        if ship_halo is not None:
            ship_halo()
        rr, rq = total(rr), total(rq)
        mu = jnp.where(rr > 0.0, rq / jnp.where(rr > 0.0, rr, 1.0), 0.0)

        def centred(rows_here, sums):
            ww, wr, mix, wt = sums
            for x in rows_here:
                image = operate(x, rqa, rqb, 3, False)
                for c in range(3):
                    r, q, s = rqa[c, x], rqa[3 + c, x], image[c][0]
                    w, t = q - mu * r, s - mu * q
                    ww, wr, mix, wt = ww + w * w, wr + w * r, mix + (r * t + w * q), wt + w * t
            return ww, wr, mix, wt

        sums = over_rows(HALO, HALO + X, WIDE_C, centred, (zero,) * 4)
        ww, wr, mix, wt = [total(v) for v in sums]
        one = lax.broadcasted_iota(jnp.int32, (1, 128), 1)
        row = jnp.zeros((1, 128), jnp.float32)
        for at, value in enumerate((rr, rq, mu, ww, wr, mix, wt)):
            row = jnp.where(one == at, value, row)
        gath[step, me] = row

        if step == 0:
            meet(known.at[len(rounds) - 1], rounds[-1])
        for other in others:
            pltpu.make_async_remote_copy(
                src_ref=gath.at[step, me], dst_ref=gath.at[step, me], send_sem=asend.at[step], recv_sem=arecv.at[step],
                device_id=other, device_id_type=MESH).start()

    def collect(step):
        block = gath.at[step, pl.ds(0, count - 1)]
        pltpu.make_async_copy(block, block, arecv.at[step]).wait()
        table = gath[step].reshape(count, 128)
        rr, rq, mu, ww, wr, mix, wt = [table[:, at:at + 1] for at in range(7)]

        def down(v):
            return jnp.sum(v, axis=0, keepdims=True)

        norm = down(rr)
        alpha = norm / down(rq)
        rest = 1.0 - alpha * mu
        after = down(alpha * alpha * ww - 2.0 * alpha * rest * wr + rest * rest * rr)
        curved = down(rest * rest * rq - alpha * rest * mix + alpha * alpha * wt)
        ratio = after / norm
        beta = after / (curved - ratio * after / alpha)
        return jnp.broadcast_to(alpha + beta * (1.0 + ratio), (8, 128)), jnp.broadcast_to(-beta * alpha, (8, 128))

    def drain(step):
        block = gath.at[step, pl.ds(0, count - 1)]
        pltpu.make_async_copy(block, block, asend.at[step]).wait()

    def joined(c, x, near, far):
        r, q = rqa[c, x], rqa[3 + c, x]
        return jnp.where(sub == 3, pltpu.roll(r, near, 0), jnp.where(sub == 4, pltpu.roll(r, far, 0), q))

    def split(c, x, tile, row, near, far):
        r = rqb[c, x]
        rqb[c, x] = jnp.where(sub == row, pltpu.roll(tile, near, 0), jnp.where(sub == 7 - row, pltpu.roll(tile, far, 0), r))
        rqb[3 + c, x] = tile

    def ship_halo():
        def pack3(i, _):
            x = HALO + 2 * i
            for c in range(3):
                pack(s3, c, i, joined(c, x, 1, 7), joined(c, x + 1, 1, 7))
            return 0

        lax.fori_loop(0, X // 2, pack3, 0)
        for end, x in ((0, HALO), (1, HALO + X - 2)):
            for c in range(3):
                even, odd = [joined(c, x + o, 2, 6) if o == end else joined(c, x + o, 3, 5) for o in range(2)]
                k3[0, end, c, 0] = jnp.where(upper, even, pltpu.roll(odd, 4, 0))
                k3[1, end, c, 0] = jnp.where(upper, pltpu.roll(even, 4, 0), odd)
        begin(third)
        begin(wedges)
        begin(outer)

    outer_residual(HALO - 2)
    outer_residual(HALO + X + 1)
    solve(0, e1a, e1b, lambda c, x: (e1a[3 + c, x], e1b[3 + c, x]), 1, ship_halo)
    spread_out(outb.at[3], inb.at[3], 3)
    finish_recv(second, recv2)
    tip_unpack(tips)
    for made, recv in zip(late, (recvu, recvw)):
        finish_recv(made, recv)
    edge_link(HALO - REACH)
    coefficients(HALO - 2)
    coefficients(HALO + X + 1)

    def open2(i, _):
        for ch in range(3):
            e2b[ch, 2 * i], e2b[ch, 2 * i + 1] = unpack(h2, ch, i)
        return 0

    lax.fori_loop(0, (X + 2 * HALO) // 2, open2, 0)
    finish_recv(third, recv3)
    for at, (ds, dg) in enumerate(steps[4:]):
        back = wedges[3 - at][2]

        @pl.when(inside(ds, dg))
        def _():
            back.wait_recv()

    def open3(i, _):
        for c in range(3):
            even, odd = unpack(h3, c, i)
            split(c, 2 * i, even, 2, 7, 1)
            split(c, 2 * i + 1, odd, 2, 7, 1)
        return 0

    lax.fori_loop(HALO // 2, (HALO + X) // 2, open3, 0)
    for pair, one in ((HALO // 2 - 1, 1), ((HALO + X) // 2, 0)):
        for c in range(3):
            for o, tile in enumerate(unpack(h3, c, pair)):
                if o == one:
                    split(c, 2 * pair + o, tile, 1, 6, 2)
                else:
                    split(c, 2 * pair + o, tile, 0, 5, 3)
    finish_recv(outer, recvq)
    c0, c1 = collect(0)

    def step1(x, both=True):
        for c in range(3):
            u1a[c, x] = e1a[c, x] + (c0 * rqa[c, x] + c1 * rqa[3 + c, x])
            u1b[c, x] = e1b[c, x] + (c0 * rqb[c, x] + c1 * rqb[3 + c, x]) if both else jnp.zeros((8, 128), jnp.float32)

    for x in range(HALO - REACH + 1, HALO + X + REACH - 1):
        step1(x)
    step1(HALO - REACH, False)
    step1(HALO + X + REACH - 1, False)
    finish_send(zeroth)
    finish_send(corners)
    finish_send(rest)
    finish_send(first)
    finish_send(second)
    finish_send(tips)
    for made in late:
        finish_send(made)
    finish_send(third)
    finish_send(outer)
    finish_send(wedges)

    def rhs2(c, x):
        return (MASS_TERM * (2.0 * u1a[c, x] - e1a[c, x]) + e2a[c, x],
                MASS_TERM * (2.0 * u1b[c, x] - e1b[c, x]) + e2b[c, x])

    def early(at, ref, ch):
        for x in range(X):
            rows[at, pl.ds(x, 8, stride=X), :] = ref[ch, HALO + x]
        turn_out(rows[at], outb.at[at])
        spread_out(outb.at[at], inb.at[at], at)
        inb[at, si] = outb[at, si]

    early(2, u1a, 2)
    solve(1, u1a, u1b, rhs2, 2)
    early(4, rqa, 2)
    early(5, rqa, 5)
    c0, c1 = collect(1)

    def step2(ra, rb, c, x):
        return ra[c, x] + (c0 * rb[c, x] + c1 * rb[3 + c, x])

    def halves(v):
        high = v.astype(jnp.bfloat16)
        return high, (v - high.astype(jnp.float32)).astype(jnp.bfloat16)

    def finish(c):
        for x in range(X):
            v = step2(u1a, rqa, c, HALO + x)
            disp_ref[c, x] = v
            rows[c, pl.ds(x, 8, stride=X), :] = v
        turned = turn_out(rows[c], outb.at[c])
        spread_out(outb.at[c], inb.at[c], c)
        inb[c, si] = outb[c, si]

    def joint(ref, j, low, high):
        return jnp.concatenate([
            ref[2, j, at:at + 8] + (c0 * ref[4, j, at:at + 8] + c1 * ref[5, j, at:at + 8])
            for at in range(low, high, 8)], axis=0)

    def finish_edges():
        for x in range(X):
            rows[6, pl.ds(x, 8, stride=X), :] = step2(u1b, rqb, 1, HALO + x)
        sides_y = rows[6].T
        zero = jnp.zeros((8, 128), jnp.float32)
        for j in range(ns):
            low, high = sides_y[zrows * j:zrows * j + 8], sides_y[zrows * j + 8:zrows * j + 16]
            tile = jnp.where(lane < 32, pltpu.roll(low, 16, 1),
                             jnp.where(lane < 64, pltpu.roll(pltpu.roll(low, 4, 0), 48, 1),
                                       jnp.where(lane < 96, pltpu.roll(high, 80, 1),
                                                 pltpu.roll(pltpu.roll(high, 4, 0), 112, 1))))
            before = pltpu.roll(joint(outb, j - 1, zrows - 8, zrows), 5, 0) if j else zero
            after = pltpu.roll(joint(outb, j + 1, 0, 8), 5, 0) if j + 1 < ns else zero
            outx[j] = jnp.where(sub == 4, before, jnp.where(sub == 5, after, tile))
        spread_out(outx, inx, 6)
        inx[si] = outx[si]

    finish(0)
    finish_edges()
    finish(1)
    for x in range(X):
        disp_ref[2, x] = step2(u1a, rqa, 2, HALO + x)
    fetched[7].wait()

    c1t, c3t = float(np.sqrt(0.5) * np.cos(np.pi / 8)), float(np.sqrt(0.5) * np.cos(3 * np.pi / 8))

    def cosine(v0, v1, v2, v3):
        s03, s12, d03, d12 = v0 + v3, v1 + v2, v0 - v3, v1 - v2
        return [0.5 * (s03 + s12), c1t * d03 + c3t * d12, 0.5 * (s03 - s12), c3t * d03 - c1t * d12]

    def encode(ch, fields):
        for b in range(Y // 4):
            for k, v in enumerate(cosine(*fields[4 * b:4 * b + 4])):
                work[ch, (4 * b + k) * zrows:(4 * b + k + 1) * zrows] = v
        parts = []
        for p in range(Y * zrows // 32):
            parts += cosine(*[work[ch, pl.ds(32 * p + n, 8, stride=4), :] for n in range(4)])
        high, low = halves(jnp.concatenate(parts, axis=0))
        done = jnp.dot(jnp.concatenate([high, low], axis=1), gt_ref[...], preferred_element_type=jnp.float32)
        done = done[:, 0:128] + done[:, 128:256]
        for p in range(Y * zrows // 32):
            for n in range(4):
                coef_ref[ch, pl.ds(32 * p + n, 8, stride=4), :] = done[(4 * p + n) * 8:(4 * p + n + 1) * 8]

    def arrived(c):
        landed(inb.at[c], trecv.at[c])
        return regroup([inb[c, j] for j in range(ns)])

    for at in (2, 4, 5):
        landed(inb.at[at], trecv.at[at])
    along = regroup([joint(inb, j, 0, zrows) for j in range(ns)])
    encode(2, along)
    landed(inb.at[3], trecv.at[3])
    for y, piece in enumerate(regroup([inb[3, j] for j in range(ns)])):
        scale[y] = piece
    field = arrived(0)
    encode(0, field)
    wide = lax.broadcasted_iota(jnp.int32, (zrows, 128), 1)
    encode(3, [scale[y] * (jnp.where(wide < 127, up_z(field[y]), 0.0) - jnp.where(wide > 0, down_z(field[y]), 0.0))
               for y in range(Y)])
    landed(inx, trecv.at[6])
    edges = regroup([inx[j] for j in range(ns)])
    stress = []
    for y in range(Y):
        low, high = along[y][0:8], along[y][8:16]
        ul, uh, dl, dh = pltpu.roll(low, 7, 0), pltpu.roll(high, 7, 0), pltpu.roll(low, 1, 0), pltpu.roll(high, 1, 0)
        first, last = sub == 0, sub == 7
        low = jnp.where(last, uh, ul) - jnp.where(first, pltpu.roll(edges[y], 4, 0), dl)
        high = jnp.where(last, pltpu.roll(edges[y], 2, 0), uh) - jnp.where(first, dl, dh)
        stress.append(scale[y] * jnp.concatenate([low, high], axis=0))
    encode(5, stress)
    field = arrived(1)
    encode(1, field)
    outside = []
    for side in range(2):
        quarter = [edges[2 * q + side] for q in range(4)]
        outside.append(jnp.concatenate([jnp.where(upper, quarter[q], pltpu.roll(quarter[q + 1], 4, 0)) for q in (0, 2)], axis=0))
    field = [outside[0]] + field + [outside[1]]
    encode(4, [scale[y] * (field[y + 2] - field[y]) for y in range(Y)])
    drain(0)
    drain(1)
    for at in range(6):
        landed(inb.at[at], tsend.at[at])
    landed(inx, tsend.at[6])


def store(disp_in, coef_in, disp_out, coef_out, sems):
    copies = [pltpu.make_async_copy(disp_in, disp_out, sems.at[0]), pltpu.make_async_copy(coef_in, coef_out, sems.at[1])]
    for copy in copies:
        copy.start()
    for copy in copies:
        copy.wait()


def fused(mesh, u_now, u_prev, force, stiffness, broken, flags):
    ns, ng = mesh.shape["slab"], mesh.shape["grp"]
    _, X, Y, Z = u_now.shape
    xe, pairs, half = X + 2 * HALO, X // 2 + HALO, X // 2
    zrows = Z // ns
    ez = jnp.asarray(np.kron(np.eye(Z // 4), np.ones((1, 4))), jnp.float32)
    gth, gtl = split_table(wavelet_table(X * ns).T)
    gt = jnp.asarray(np.block([[gth, gtl], [gth, np.zeros_like(gtl)]]), jnp.bfloat16)

    def vm(*shape):
        return pltpu.VMEM(shape, jnp.float32)

    def ext(n):
        return vm(n, xe, Y, Z)

    def stage(n):
        return vm(2, n, half, Y, Z)

    def land(n):
        return vm(2, n, pairs, Y, Z)

    dma = pltpu.SemaphoreType.DMA
    shapes = (u_now.shape, (6, Y * zrows, X * ns))
    operands = [pltpu.with_memory_space_constraint(v, pltpu.HBM)
                for v in (u_now, u_prev, force, stiffness, broken, flags, ez, gt)]
    results = pl.pallas_call(
        lambda *refs: kernel(ns, ng, *refs),
        name="lattice",
        out_shape=tuple(vm(*shape) for shape in shapes),
        in_specs=[pl.BlockSpec(memory_space=pltpu.MemorySpace.HBM)] * 8,
        out_specs=(pl.BlockSpec(memory_space=pltpu.VMEM),) * 2,
        scratch_shapes=[
            vm(*u_now.shape), vm(*u_now.shape), vm(*u_now.shape), vm(*stiffness.shape),
            pltpu.VMEM(broken.shape, broken.dtype), pltpu.VMEM(flags.shape, flags.dtype),
            vm(*ez.shape), pltpu.VMEM(gt.shape, gt.dtype), pltpu.SemaphoreType.DMA((8,)),
            ext(7), ext(7), stage(7), land(7),
            ext(3), ext(3), stage(3), land(3),
            ext(6), ext(6), stage(3), land(3), vm(2, 2, 3, 1, Y, Z), vm(2, 3, 2, Y, Z),
            ext(3), ext(3), vm(Y, zrows, X * ns), ext(3), ext(3), ext(5), ext(5),
            pltpu.SemaphoreType.REGULAR((4,)), vm(2, ns * ng, 1, 128), vm(7, Y * X, Z), vm(6, ns, zrows, 128), vm(6, ns, zrows, 128), vm(ns, 8, 128), vm(ns, 8, 128), vm(6, Y * zrows, X * ns),
            vm(2, 2, 2, Y, Z), vm(2, 2, 2, Y, Z), dma((4,)), dma((4,)), dma((4,)), dma((4,)),
            dma((4,)), dma((4,)), dma((4,)), dma((4,)), dma((4,)), dma((4,)), dma((4,)), dma((4,)), dma((2,)), dma((2,)), dma((4,)), dma((4,)),
            dma((2,)), dma((2,)), dma((2,)), dma((2,)), vm(2, 2, Y, Z), vm(2, 2, Y, Z), dma((4,)), dma((4,)),
            dma((2,)), dma((2,)), dma((7,)), dma((7,)),
        ],
        compiler_params=pltpu.CompilerParams(collective_id=0, has_side_effects=True, vmem_limit_bytes=24 << 20),
    )(*operands)
    disp, coef = pl.pallas_call(
        store,
        name="store",
        out_shape=tuple(jax.ShapeDtypeStruct(shape, jnp.float32) for shape in shapes),
        in_specs=[pl.BlockSpec(memory_space=pltpu.VMEM)] * 2,
        out_specs=(pl.BlockSpec(memory_space=pltpu.MemorySpace.HBM),) * 2,
        scratch_shapes=[dma((2,))],
        compiler_params=pltpu.CompilerParams(vmem_limit_bytes=1 << 20),
    )(*[pltpu.with_memory_space_constraint(v, pltpu.VMEM) for v in results])
    return disp, coef.reshape(6, Y, zrows, X * ns)


def fits(mesh, shape):
    ns, ng = mesh.shape["slab"], mesh.shape["grp"]
    x, y, z = shape[1] // ns, shape[2] // ng, shape[3]
    return y == 8 and z == 128 and x * y == 128 and x * ns == 128 and z % (8 * ns) == 0


def entry(mesh, *args):
    ns, ng = mesh.shape["slab"], mesh.shape["grp"]
    _, x, y, z = args[0].shape
    if fits(mesh, (3, x * ns, y * ng, z)):
        return fused(mesh, *args)
    return body(*args)


def solution(mesh):
    return jax.shard_map(
        lambda *args: entry(mesh, *args),
        mesh=mesh,
        in_specs=(
            P(None, "slab", "grp", None),
            P(None, "slab", "grp", None),
            P(None, "slab", "grp", None),
            P("slab", "grp", None),
            P("slab", "grp", None),
            P("slab", "grp", None),
        ),
        out_specs=(P(None, "slab", "grp", None), P(None, "grp", "slab", None)),
        check_vma=False,
    )
```

```python
import jax
import jax.numpy as jnp
import numpy as np
from jax import lax
from jax.experimental import pallas as pl
from jax.experimental.pallas import tpu as pltpu
from jax.sharding import PartitionSpec as P

STEPS = 2
ITERS = 2
LEVELS = 3


SPRING_NORMAL = 1.0
SPRING_SHEAR = 0.4
MASS_TERM = 1.0
CRACK_CUT = 0.9


def with_halo(block, sides, width):
    for axis, dim in sides:
        count = lax.axis_size(axis)
        forward = [(i, i + 1) for i in range(count - 1)]
        backward = [(target, source) for source, target in forward]
        low = lax.ppermute(
            lax.slice_in_dim(block, block.shape[dim] - width, None, axis=dim), axis, forward
        )
        high = lax.ppermute(lax.slice_in_dim(block, 0, width, axis=dim), axis, backward)
        block = jnp.concatenate([low, block, high], axis=dim)
    return block


def cosine_table():
    freq = np.arange(4)[:, None]
    place = np.arange(4)[None, :]
    factor = np.where(freq == 0, 0.5, np.sqrt(0.5))
    return factor * np.cos(np.pi * (2 * place + 1) * freq / 8.0)


def block_table(count):
    return jnp.asarray(np.kron(np.eye(count // 4), cosine_table()), jnp.float32)


def spread(mask):
    values = mask.astype(jnp.float32)
    size_a, size_b, size_c = values.shape
    wide = jnp.broadcast_to(values[:, None, :, None, :, None], (size_a, 4, size_b, 4, size_c, 4))
    return wide.reshape(size_a * 4, size_b * 4, size_c * 4)


def sides(padded, axis_index):
    leading = padded.ndim - 3

    def cut(offset):
        index_list = [slice(None)] * leading + [slice(1, -1)] * 3
        length = padded.shape[leading + axis_index]
        index_list[leading + axis_index] = slice(1 + offset, length - 1 + offset)
        return padded[tuple(index_list)]

    return (cut(1), cut(-1))


def springs(field, weight, field_pad, weight_pad):
    result = MASS_TERM * field
    for axis_index in range(3):
        upper_v, lower_v = sides(field_pad, axis_index)
        upper_w, lower_w = sides(weight_pad, axis_index)
        k_upper = 0.5 * (weight + upper_w)
        k_lower = 0.5 * (weight + lower_w)
        change = k_upper * (field - upper_v) + k_lower * (field - lower_v)
        coupling = jnp.array(
            [SPRING_NORMAL if comp == axis_index else SPRING_SHEAR for comp in range(3)],
            jnp.float32,
        ).reshape(3, 1, 1, 1)
        result = result + coupling * change
    return result


def faces(field):
    padded = with_halo(field, (("slab", 1), ("grp", 2)), 1)
    return jnp.pad(padded, ((0, 0), (0, 0), (0, 0), (1, 1)))


def stresses(carry, field_pad):
    rows_out = []
    for axis_index in range(3):
        upper_v, lower_v = sides(field_pad, axis_index)
        rows_out.append(SPRING_NORMAL * carry * 0.5 * (upper_v[axis_index] - lower_v[axis_index]))
    return jnp.stack(rows_out)


def paired_sum(residual, image):
    return lax.psum((jnp.sum(residual * residual), jnp.sum(residual * image)), ("slab", "grp"))


def lift(signal):
    even = signal[..., 0::2]
    odd = signal[..., 1::2]
    detail = odd - 0.5 * (even + jnp.roll(even, -1, axis=-1))
    approx = even + 0.25 * (jnp.roll(detail, 1, axis=-1) + detail)
    return (approx, detail)


def wavelet(signal):
    pieces = []
    approx = signal
    for level_index in range(LEVELS):
        approx, detail = lift(approx)
        pieces.insert(0, detail)
    return jnp.concatenate([approx] + pieces, axis=-1)


def body(u_now, u_prev, force, stiffness, broken, flags):
    weight = stiffness * (1.0 - CRACK_CUT * spread(broken))
    carry = spread(flags) * weight
    weight_pad = with_halo(weight, (("slab", 0), ("grp", 1)), 1)
    weight_pad = jnp.pad(weight_pad, ((0, 0), (0, 0), (1, 1)))

    def operate(field):
        return springs(field, weight, faces(field), weight_pad)

    for step_index in range(STEPS):
        rhs = MASS_TERM * (2.0 * u_now - u_prev) + force
        guess = u_now
        residual = rhs - operate(guess)
        image = operate(residual)
        norm_now, product = paired_sum(residual, image)
        alpha = norm_now / product
        direction, along = (residual, image)
        for turn_index in range(ITERS):
            guess = guess + alpha * direction
            residual = residual - alpha * along
            if turn_index + 1 < ITERS:
                image = operate(residual)
                norm_next, product = paired_sum(residual, image)
                ratio = norm_next / norm_now
                alpha = norm_next / (product - ratio * norm_next / alpha)
                direction = residual + ratio * direction
                along = image + ratio * along
                norm_now = norm_next
        u_prev = u_now
        u_now = guess
    stress = stresses(carry, faces(u_now))
    fields = jnp.concatenate([u_now, stress], axis=0)
    table_x = block_table(fields.shape[1])
    table_y = block_table(fields.shape[2])
    table_z = block_table(fields.shape[3])
    blockc = jnp.einsum("ax,hxyz->hayz", table_x, fields, precision=lax.Precision.HIGHEST)
    blockc = jnp.einsum("by,hxyz->hxbz", table_y, blockc, precision=lax.Precision.HIGHEST)
    blockc = jnp.einsum("hxyz,cz->hxyc", blockc, table_z, precision=lax.Precision.HIGHEST)
    moved = jnp.transpose(blockc, (0, 2, 3, 1))
    shipped = lax.all_to_all(moved, "slab", split_axis=2, concat_axis=3, tiled=True)
    coeffs = wavelet(shipped)
    return (u_now, coeffs)


MESH = pl.DeviceIdType.MESH
HALO = 4
REACH = 3
SHEAR_REST = SPRING_NORMAL - SPRING_SHEAR
WIDE_R, WIDE_A, WIDE_C, WIDE_K = 20, 16, 16, 20


def wavelet_table(count):
    table = np.kron(np.eye(count // 4), cosine_table())
    pieces = []
    approx = table
    for level_index in range(LEVELS):
        even, odd = approx[0::2], approx[1::2]
        detail = odd - 0.5 * (even + np.roll(even, -1, axis=0))
        approx = even + 0.25 * (np.roll(detail, 1, axis=0) + detail)
        pieces.insert(0, detail)
    return np.concatenate([approx] + pieces, axis=0)


def split_table(table):
    high = table.astype(jnp.bfloat16).astype(np.float64)
    return high, (table - high).astype(jnp.bfloat16).astype(np.float64)


def sub_index():
    return lax.broadcasted_iota(jnp.int32, (8, 128), 0)


def lane_index():
    return lax.broadcasted_iota(jnp.int32, (8, 128), 1)


def up_y(a, b):
    ra, rb = pltpu.roll(a, 7, 0), pltpu.roll(b, 7, 0)
    last = sub_index() == 7
    return jnp.where(last, rb, ra), jnp.where(last, ra, rb)


def down_y(a, b):
    ra, rb = pltpu.roll(a, 1, 0), pltpu.roll(b, 1, 0)
    first = sub_index() == 0
    return jnp.where(first, rb, ra), jnp.where(first, ra, rb)


def up_z(v):
    return pltpu.roll(v, 127, 1)


def down_z(v):
    return pltpu.roll(v, 1, 1)


def total(v):
    return jnp.sum(jnp.sum(v, axis=0, keepdims=True), axis=1, keepdims=True)


def kernel(ns, ng, u_in, p_in, f_in, k_in, br_in, fl_in, ez_in, gt_in,
           disp_ref, coef_ref,
           u_ref, p_ref, f_ref, k_ref, br_ref, fl_ref, ez_ref, gt_ref, isem,
           e1a, e1b, s1, h1, e2a, e2b, s2, h2, rqa, rqb, s3, h3, k3, ends,
           u1a, u1b, scale, dga, dgb, kca, kcb, known, gath, rows, outb, inb, outx, inx, work,
           ctake, cland, csend, crecv, send4, recv4, send0, recv0, send1, recv1, send2, recv2, send3, recv3, sendq, recvq, sendk, recvk, sendu, recvu, sendw, recvw, ftake, fland, sendf, recvf, asend, arecv, tsend, trecv):
    X, Y, Z = u_ref.shape[1:]
    si, gi = lax.axis_index("slab"), lax.axis_index("grp")
    me = si * ng + gi
    count = ns * ng
    barrier = pltpu.get_barrier_semaphore()

    def mirrored(place, mask, length):
        bit, result = 1, 0
        while bit < length:
            here = place // bit % 2
            result = result + bit * (1 - here if mask // bit % 2 else here)
            bit *= 2
        return result

    others = []
    for k in sorted(range(ns), key=lambda k: -min(k, ns - k)):
        for g in range(ng):
            if k or g:
                others.append((lax.rem(si + k, ns), lax.rem(gi + g, ng)))

    sub, lane = sub_index(), lane_index()
    upper = sub < 4

    steps = [(-1, 0), (1, 0), (0, -1), (0, 1), (-1, -1), (-1, 1), (1, -1), (1, 1)]

    def inside(ds, dg):
        ok = None
        if ds:
            ok = (si >= -ds) if ds < 0 else (si <= ns - 1 - ds)
        if dg:
            more = (gi >= -dg) if dg < 0 else (gi <= ng - 1 - dg)
            ok = more if ok is None else jnp.logical_and(ok, more)
        return ok

    def around(reach):
        return [(ds, dg) for ds in (-reach, 0, reach) for dg in (-reach, 0, reach)
                if (ds or dg) and abs(ds) < ns and abs(dg) < ng]

    def greet(sem, reach):
        for ds, dg in around(reach):
            @pl.when(inside(ds, dg))
            def _():
                pl.semaphore_signal(sem, inc=1, device_id=(si + ds, gi + dg), device_id_type=MESH)

    def meet(sem, reach):
        pl.semaphore_wait(sem, sum(jnp.where(inside(ds, dg), 1, 0) for ds, dg in around(reach)))

    rounds = []
    while (rounds[-1] * 2 if rounds else 1) < max(ns, ng):
        rounds.append(rounds[-1] * 2 if rounds else 1)

    greet(barrier, 1)
    fetched = []
    for at, (source, target) in enumerate((
        (br_in, br_ref), (fl_in, fl_ref), (ez_in, ez_ref), (k_in, k_ref), (u_in, u_ref), (p_in, p_ref),
        (f_in, f_ref), (gt_in, gt_ref),
    )):
        fetch = pltpu.make_async_copy(source, target, isem.at[at])
        fetch.start()
        fetched.append(fetch)

    def copies(ea, dst_a, stage, land, send, recv, low=0, high=None, ways=8, reach=REACH, depth=None, ends=None):
        depth = reach if depth is None else depth
        half = X // 2
        edge = HALO // 2
        made = []
        chans = pl.ds(low, (ea.shape[0] if high is None else high) - low)
        for at, (ds, dg) in enumerate(steps[:ways]):
            if dg == 0:
                if ends is not None:
                    source = ends.at[0 if ds < 0 else 1]
                    target = dst_a.at[chans, pl.ds(HALO + X if ds < 0 else HALO - depth, reach)]
                elif ds < 0:
                    source = ea.at[chans, pl.ds(HALO + depth - reach, reach)]
                    target = dst_a.at[chans, pl.ds(HALO + X + depth - reach, reach)]
                else:
                    source = ea.at[chans, pl.ds(HALO + X - depth, reach)]
                    target = dst_a.at[chans, pl.ds(HALO - depth, reach)]
            else:
                side = 0 if dg < 0 else 1
                if ds == 0:
                    source, target = stage.at[side, chans], land.at[side, chans, pl.ds(edge, half)]
                elif ds < 0:
                    source = stage.at[side, chans, pl.ds(0, 1)]
                    target = land.at[side, chans, pl.ds(edge + half, 1)]
                else:
                    source = stage.at[side, chans, pl.ds(half - 1, 1)]
                    target = land.at[side, chans, pl.ds(edge - 1, 1)]
            made.append((ds, dg, pltpu.make_async_remote_copy(
                src_ref=source, dst_ref=target, send_sem=send.at[at], recv_sem=recv.at[at ^ 1 if at < 4 else 11 - at],
                device_id=(si + ds, gi + dg), device_id_type=MESH)))
        return made

    def begin(made):
        for ds, dg, copy in made:
            @pl.when(inside(ds, dg))
            def _():
                copy.start()

    def finish_recv(made, recv):
        for at, (ds, dg) in enumerate(steps[:len(made)]):
            back = made[at ^ 1 if at < 4 else 11 - at][2]

            @pl.when(inside(ds, dg))
            def _():
                back.wait_recv()

    def finish_send(made):
        for ds, dg, copy in made:
            @pl.when(inside(ds, dg))
            def _():
                copy.wait_send()

    def blank(dst_a, land):
        zero_a = jnp.zeros((dst_a.shape[0], HALO) + dst_a.shape[2:], jnp.float32)
        half, edge = X // 2, HALO // 2
        zero_l = jnp.zeros((land.shape[1], edge, 8, 128), jnp.float32)

        @pl.when(si == 0)
        def _():
            dst_a[:, pl.ds(0, HALO)] = zero_a
            for side in range(2):
                land[side, :, pl.ds(0, edge)] = zero_l

        @pl.when(si == ns - 1)
        def _():
            dst_a[:, pl.ds(HALO + X, HALO)] = zero_a
            for side in range(2):
                land[side, :, pl.ds(edge + half, edge)] = zero_l

        for side, edge_here in ((0, gi == ng - 1), (1, gi == 0)):
            @pl.when(edge_here)
            def _(side=side):
                land[side] = jnp.zeros(land.shape[1:], jnp.float32)

    def pack(stage, ch, pair, even, odd):
        stage[0, ch, pair] = jnp.where(upper, even, pltpu.roll(odd, 4, 0))
        stage[1, ch, pair] = jnp.where(upper, pltpu.roll(even, 4, 0), odd)

    def unpack(land, ch, pair):
        high, low = land[0, ch, pair], land[1, ch, pair]
        return (jnp.where(upper, high, pltpu.roll(low, 4, 0)),
                jnp.where(upper, pltpu.roll(high, 4, 0), low))

    def spread_rows(mask):
        wide = jnp.dot(mask.astype(jnp.float32), ez_ref[...], preferred_element_type=jnp.float32)
        return jnp.where(upper, jnp.broadcast_to(wide[0:1], (8, 128)), jnp.broadcast_to(wide[1:2], (8, 128)))

    for at in range(4):
        fetched[at].wait()
    for bx in range(X // 4):
        cut = 1.0 - CRACK_CUT * spread_rows(br_ref[bx])
        flag = spread_rows(fl_ref[bx])
        for at in range(4):
            x = bx * 4 + at
            w = k_ref[x] * cut
            e1a[6, HALO + x] = w
            rows[3, pl.ds(x, 8, stride=X), :] = (SPRING_NORMAL * 0.5) * (flag * w)

    def own(i, _):
        for c in range(3):
            tiles = []
            for o in range(2):
                x = 2 * i + o
                u = u_ref[c, x]
                f = f_ref[c, x]
                rhs = MASS_TERM * (2.0 * u - p_ref[c, x]) + f
                e1a[c, HALO + x] = u
                e1a[3 + c, HALO + x] = rhs
                e2a[c, HALO + x] = f
                tiles.append((u, rhs, f))
            pack(s1, c, i, tiles[0][0], tiles[1][0])
            pack(s1, 3 + c, i, tiles[0][1], tiles[1][1])
            pack(s2, c, i, tiles[0][2], tiles[1][2])
        pack(s1, 6, i, e1a[6, HALO + 2 * i], e1a[6, HALO + 2 * i + 1])
        return 0

    for at in range(4, 7):
        fetched[at].wait()
    lax.fori_loop(0, X // 2, own, 0)
    blank(e1a, h1)
    blank(e2a, h2)
    blank(rqa, h3)

    zrows = Z // ns

    def turn_out(value, out):
        turned = value.T
        for j in range(ns):
            out[j] = turned[j * zrows:(j + 1) * zrows]

    def spread_out(source, target, at):
        for m in reversed(range(1, ns)):
            to = mirrored(si, m, ns)
            pltpu.make_async_remote_copy(
                src_ref=source.at[to], dst_ref=target.at[si], send_sem=tsend.at[at], recv_sem=trecv.at[at],
                device_id=(to, gi), device_id_type=MESH).start()

    def landed(target, sem):
        block = target.at[pl.ds(0, ns - 1)]
        pltpu.make_async_copy(block, block, sem).wait()

    def regroup(pieces):
        lanes = lax.broadcasted_iota(jnp.int32, pieces[0].shape, 1)
        gap = ns // 2
        while gap:
            keep = (lanes // (X * gap)) % 2 == 0
            mixed = list(pieces)
            for j in range(ns):
                if (j // gap) % 2 == 0:
                    a, b = pieces[j], pieces[j + gap]
                    mixed[j] = jnp.where(keep, a, pltpu.roll(b, X * gap, 1))
                    mixed[j + gap] = jnp.where(keep, pltpu.roll(a, 128 - X * gap, 1), b)
            pieces = mixed
            gap //= 2
        return pieces

    not_last, not_first = lane < 127, lane > 0

    def inner_ends():
        for end, x in ((0, HALO + 1), (1, HALO + X - 2)):
            w = e1a[6, x]
            along = (0.5 * (w + e1a[6, x + 1]), 0.5 * (w + e1a[6, x - 1]),
                     jnp.where(sub < 7, 0.5 * (w + pltpu.roll(w, 7, 0)), 0.0),
                     jnp.where(sub > 0, 0.5 * (w + pltpu.roll(w, 1, 0)), 0.0),
                     0.5 * (w + jnp.where(not_last, up_z(w), 0.0)), 0.5 * (w + jnp.where(not_first, down_z(w), 0.0)))
            for c in range(3):
                v = e1a[c, x]
                parts = (along[0] * (v - e1a[c, x + 1]) + along[1] * (v - e1a[c, x - 1]),
                         along[2] * (v - pltpu.roll(v, 7, 0)) + along[3] * (v - pltpu.roll(v, 1, 0)),
                         along[4] * (v - jnp.where(not_last, up_z(v), 0.0))
                         + along[5] * (v - jnp.where(not_first, down_z(v), 0.0)))
                image = MASS_TERM * v + (SPRING_SHEAR * (parts[0] + parts[1] + parts[2]) + SHEAR_REST * parts[c])
                ends[end, c, 1 - end] = e1a[3 + c, x] - image
                ends[end, c, end] = e1a[3 + c, x - 1 + 2 * end]

    def outer_residual(x):
        wa, wb = e1a[6, x], e1b[6, x]
        above = jnp.where(sub == 7, 0.5 * (wa + up_y(wa, wb)[0]), 0.0)
        below = jnp.where(sub == 0, 0.5 * (wa + down_y(wa, wb)[0]), 0.0)
        for c in range(3):
            a, b = e1a[c, x], e1b[c, x]
            change = above * (a - up_y(a, b)[0]) + below * (a - down_y(a, b)[0])
            rqa[c, x] = e1a[3 + c, x] - (SPRING_NORMAL if c == 1 else SPRING_SHEAR) * change
            rqb[c, x] = jnp.zeros((8, 128), jnp.float32)

    def tip_copies():
        made = []
        for at, (ds, dg) in enumerate(steps[4:]):
            side, end = (0 if dg < 0 else 1), (0 if ds < 0 else 1)
            made.append((ds, dg, pltpu.make_async_remote_copy(
                src_ref=ftake.at[side, end], dst_ref=fland.at[side, 1 - end],
                send_sem=sendf.at[at], recv_sem=recvf.at[3 - at],
                device_id=(si + ds, gi + dg), device_id_type=MESH)))
        return made

    def tip_unpack(made):
        for at, (ds, dg) in enumerate(steps[4:]):
            side, end = (0 if dg > 0 else 1), (1 if ds > 0 else 0)
            pair = HALO // 2 + X // 2 if ds > 0 else HALO // 2 - 1
            back = made[3 - at][2]

            @pl.when(inside(ds, dg))
            def _():
                back.wait_recv()
                tile = fland[side, end]
                for c in range(3):
                    h2[side, c, pair] = pltpu.roll(tile, 8 - 2 * c, 0) if c else tile

    def wedge_copies():
        made = []
        for at, (ds, dg) in enumerate(steps[4:]):
            side, end = (0 if dg < 0 else 1), (0 if ds < 0 else 1)
            pair = HALO // 2 + X // 2 if ds < 0 else HALO // 2 - 1
            made.append((ds, dg, pltpu.make_async_remote_copy(
                src_ref=k3.at[side, end], dst_ref=h3.at[side, :, pl.ds(pair, 1)],
                send_sem=sendk.at[at], recv_sem=recvk.at[3 - at],
                device_id=(si + ds, gi + dg), device_id_type=MESH)))
        return made

    def corner_copies():
        made = []
        for at, (ds, dg) in enumerate(steps[4:]):
            side, end = (0 if dg < 0 else 1), (0 if ds < 0 else 1)
            made.append((ds, dg, pltpu.make_async_remote_copy(
                src_ref=ctake.at[side, end], dst_ref=cland.at[side, 1 - end],
                send_sem=csend.at[at], recv_sem=crecv.at[3 - at],
                device_id=(si + ds, gi + dg), device_id_type=MESH)))
        return made

    def corner_rows(side, end):
        dx1, dx2 = (0, 4) if end == 0 else (4, 0)
        dy1, dy2 = (0, 1) if side == 0 else (3, 2)
        return dx1 + dy1, dx1 + dy2, dx2 + dy1

    def any_row(places):
        found = sub == places[0]
        for place in places[1:]:
            found = jnp.logical_or(found, sub == place)
        return found

    corner_sets = ((0, 1, (3, 4)), (2, 6, (5,)))
    for side in range(2):
        for end in range(2):
            places = corner_rows(side, end)
            first_here, second_here = any_row(places), any_row([(v + 2) % 8 for v in places])
            for at, (ch_a, ch_b, right) in enumerate(corner_sets):
                tiles = [s1[side, ch, end * (X // 2 - 1)] for ch in (ch_a, ch_b) + right]
                tile = pltpu.roll(tiles[2], 5, 0)
                if len(right) == 2:
                    tile = jnp.where(sub == (places[0] + 5) % 8, tile, pltpu.roll(tiles[3], 3 if side else 7, 0))
                tile = jnp.where(first_here, tiles[0], jnp.where(second_here, pltpu.roll(tiles[1], 2, 0), tile))
                ctake[side, end, at] = tile
            near = [s2[side, c, end * (X // 2 - 1)] for c in range(3)]
            ftake[side, end] = jnp.where(sub == places[0], near[0], jnp.where(
                sub == (places[0] + 2) % 8, pltpu.roll(near[1], 2, 0), pltpu.roll(near[2], 4, 0)))

    def corner_unpack(made):
        for at, (ds, dg) in enumerate(steps[4:]):
            side, end = (0 if dg > 0 else 1), (1 if ds > 0 else 0)
            pair = HALO // 2 + X // 2 if ds > 0 else HALO // 2 - 1
            back = made[3 - at][2]

            @pl.when(inside(ds, dg))
            def _():
                back.wait_recv()
                for at, (ch_a, ch_b, right) in enumerate(corner_sets):
                    tile = cland[side, end, at]
                    h1[side, ch_a, pair] = tile
                    h1[side, ch_b, pair] = pltpu.roll(tile, 6, 0)
                    h1[side, right[0], pair] = pltpu.roll(tile, 3, 0)
                    if len(right) == 2:
                        h1[side, right[1], pair] = pltpu.roll(tile, 5 if side else 1, 0)

    corners = corner_copies()
    zeroth = copies(e1a, e1a, s1, h1, send0, recv0, 6, 7, 4, REACH - 1)
    first = copies(e1a, e1a, s1, h1, send1, recv1, 0, 3, 4, REACH - 1)
    rest = copies(e1a, e1a, s1, h1, send4, recv4, 3, 6, 4, REACH - 1, None, ends)
    late = (copies(e1a, e1a, s1, h1, sendu, recvu, 0, 3, 2, 1, REACH),
            copies(e1a, e1a, s1, h1, sendw, recvw, 6, 7, 2, 1, REACH))
    second = copies(e2a, e2a, s2, h2, send2, recv2, 0, 3, 4, REACH - 1)
    tips = tip_copies()
    third = copies(rqa, rqa, s3, h3, send3, recv3, 0, 3, 4, 1, REACH)
    outer = copies(rqa, rqa, s3, h3, sendq, recvq, 3, 6, 2, REACH - 1, REACH)
    wedges = wedge_copies()
    meet(barrier, 1)
    begin(zeroth)
    begin(corners)
    begin(first)
    inner_ends()
    begin(rest)
    greet(known.at[0], rounds[0])
    turn_out(rows[3], outb.at[3])
    inb[3, si] = outb[3, si]
    for at in range(len(rounds) - 2):
        meet(known.at[at], rounds[at])
        greet(known.at[at + 1], rounds[at + 1])
    finish_recv(zeroth, recv0)
    corner_unpack(corners)
    meet(known.at[len(rounds) - 2], rounds[-2])
    greet(known.at[len(rounds) - 1], rounds[-1])
    begin(second)
    begin(tips)
    for made in late:
        begin(made)

    def open0(i, _):
        e1b[6, 2 * i], e1b[6, 2 * i + 1] = unpack(h1, 6, i)
        return 0

    def open1(i, _):
        for ch in range(6):
            e1b[ch, 2 * i], e1b[ch, 2 * i + 1] = unpack(h1, ch, i)
        return 0

    lax.fori_loop(0, (X + 2 * HALO) // 2, open0, 0)

    def link(w, other):
        return jnp.where(jnp.minimum(w, other) > 0.0, (0.5 * SPRING_SHEAR) * (w + other), 0.0)


    def over_rows(low, high, width, body, carried=0):
        width = max(v for v in range(1, width + 1) if (high - low) % v == 0)

        def chunk(i, state):
            return body([low + i * width + o for o in range(width)], state)

        return lax.fori_loop(0, (high - low) // width, chunk, carried)

    def all_coefficients(rows_here, _):
        for x in rows_here:
            coefficients(x)
        return 0

    def coefficients(x):
        wa, wb = e1a[6, x], e1b[6, x]
        ya, yb = up_y(wa, wb)
        da, db = down_y(wa, wb)
        for w, wu, wd, yu, yd, dg, kc in (
            (wa, e1a[6, x + 1], e1a[6, x - 1], ya, da, dga, kca),
            (wb, e1b[6, x + 1], e1b[6, x - 1], yb, db, dgb, kcb),
        ):
            zu = jnp.where(not_last, up_z(w), 0.0)
            zd = jnp.where(not_first, down_z(w), 0.0)
            kc[0, x] = link(w, wu)
            kc[1, x] = link(w, yu)
            kc[2, x] = link(w, yd)
            kc[3, x] = link(w, zu)
            kc[4, x] = link(w, zd)
            sx = w + 0.5 * (wu + wd)
            sy = w + 0.5 * (yu + yd)
            sz = w + 0.5 * (zu + zd)
            every = MASS_TERM + SPRING_SHEAR * (sx + sy + sz)
            dg[0, x] = every + SHEAR_REST * sx
            dg[1, x] = every + SHEAR_REST * sy
            dg[2, x] = every + SHEAR_REST * sz

    def edge_link(x):
        kca[0, x] = link(e1a[6, x], e1a[6, x + 1])
        kcb[0, x] = link(e1b[6, x], e1b[6, x + 1])

    edge_link(HALO - 2)
    over_rows(HALO - 1, HALO + X + 1, WIDE_K, all_coefficients)
    finish_recv(first, recv1)
    finish_recv(rest, recv4)
    lax.fori_loop(0, (X + 2 * HALO) // 2, open1, 0)

    def operate(x, va, vb, base, both=True):
        result = []
        coef = [[kc[j, x] for j in range(5)] + [kc[0, x - 1]] for kc in (kca, kcb)]
        for c in range(3):
            a, b = va[base + c, x], vb[base + c, x]
            ua, ub = up_y(a, b)
            la, lb = down_y(a, b)
            pair = []
            halves = ((a, va, ua, la, coef[0], dga), (b, vb, ub, lb, coef[1], dgb))
            for v, ref, u, l, k, dg in halves if both else halves[:1]:
                parts = (
                    k[0] * ref[base + c, x + 1] + k[5] * ref[base + c, x - 1],
                    k[1] * u + k[2] * l,
                    k[3] * up_z(v) + k[4] * down_z(v),
                )
                shear = parts[(c + 1) % 3] + parts[(c + 2) % 3]
                pair.append(dg[c, x] * v - (shear + (SPRING_NORMAL / SPRING_SHEAR) * parts[c]))
            result.append(pair)
        return result

    def solve(step, va, vb, rhs_of, reach, ship_halo=None):
        def residual(rows_here, _):
            for x in rows_here:
                image = operate(x, va, vb, 0)
                for c in range(3):
                    ra, rb = rhs_of(c, x)
                    rqa[c, x] = ra - image[c][0]
                    rqb[c, x] = rb - image[c][1]
            return 0

        over_rows(HALO - reach, HALO + X + reach, WIDE_R, residual)

        def put(x, image):
            for c in range(3):
                rqa[3 + c, x] = image[c][0]
                rqb[3 + c, x] = image[c][1]

        def apply(rows_here, sums):
            rr, rq = sums
            for x in rows_here:
                image = operate(x, rqa, rqb, 0)
                for c in range(3):
                    r = rqa[c, x]
                    rr, rq = rr + r * r, rq + r * image[c][0]
                put(x, image)
            return rr, rq

        zero = jnp.zeros((8, 128), jnp.float32)
        images = [operate(x, rqa, rqb, 0) for x in (HALO - 1, HALO + X)]
        put(HALO - 1, images[0])
        put(HALO + X, images[1])
        rr, rq = over_rows(HALO, HALO + X, WIDE_A, apply, (zero, zero))
        if ship_halo is not None:
            ship_halo()
        rr, rq = total(rr), total(rq)
        mu = jnp.where(rr > 0.0, rq / jnp.where(rr > 0.0, rr, 1.0), 0.0)

        def centred(rows_here, sums):
            ww, wr, mix, wt = sums
            for x in rows_here:
                image = operate(x, rqa, rqb, 3, False)
                for c in range(3):
                    r, q, s = rqa[c, x], rqa[3 + c, x], image[c][0]
                    w, t = q - mu * r, s - mu * q
                    ww, wr, mix, wt = ww + w * w, wr + w * r, mix + (r * t + w * q), wt + w * t
            return ww, wr, mix, wt

        sums = over_rows(HALO, HALO + X, WIDE_C, centred, (zero,) * 4)
        ww, wr, mix, wt = [total(v) for v in sums]
        one = lax.broadcasted_iota(jnp.int32, (1, 128), 1)
        row = jnp.zeros((1, 128), jnp.float32)
        for at, value in enumerate((rr, rq, mu, ww, wr, mix, wt)):
            row = jnp.where(one == at, value, row)
        gath[step, me] = row

        if step == 0:
            meet(known.at[len(rounds) - 1], rounds[-1])
        for other in others:
            pltpu.make_async_remote_copy(
                src_ref=gath.at[step, me], dst_ref=gath.at[step, me], send_sem=asend.at[step], recv_sem=arecv.at[step],
                device_id=other, device_id_type=MESH).start()

    def collect(step):
        block = gath.at[step, pl.ds(0, count - 1)]
        pltpu.make_async_copy(block, block, arecv.at[step]).wait()
        table = gath[step].reshape(count, 128)
        rr, rq, mu, ww, wr, mix, wt = [table[:, at:at + 1] for at in range(7)]

        def down(v):
            return jnp.sum(v, axis=0, keepdims=True)

        norm = down(rr)
        alpha = norm / down(rq)
        rest = 1.0 - alpha * mu
        after = down(alpha * alpha * ww - 2.0 * alpha * rest * wr + rest * rest * rr)
        curved = down(rest * rest * rq - alpha * rest * mix + alpha * alpha * wt)
        ratio = after / norm
        beta = after / (curved - ratio * after / alpha)
        return jnp.broadcast_to(alpha + beta * (1.0 + ratio), (8, 128)), jnp.broadcast_to(-beta * alpha, (8, 128))

    def drain(step):
        block = gath.at[step, pl.ds(0, count - 1)]
        pltpu.make_async_copy(block, block, asend.at[step]).wait()

    def joined(c, x, near, far):
        r, q = rqa[c, x], rqa[3 + c, x]
        return jnp.where(sub == 3, pltpu.roll(r, near, 0), jnp.where(sub == 4, pltpu.roll(r, far, 0), q))

    def split(c, x, tile, row, near, far):
        r = rqb[c, x]
        rqb[c, x] = jnp.where(sub == row, pltpu.roll(tile, near, 0), jnp.where(sub == 7 - row, pltpu.roll(tile, far, 0), r))
        rqb[3 + c, x] = tile

    def ship_halo():
        def pack3(i, _):
            x = HALO + 2 * i
            for c in range(3):
                pack(s3, c, i, joined(c, x, 1, 7), joined(c, x + 1, 1, 7))
            return 0

        lax.fori_loop(0, X // 2, pack3, 0)
        for end, x in ((0, HALO), (1, HALO + X - 2)):
            for c in range(3):
                even, odd = [joined(c, x + o, 2, 6) if o == end else joined(c, x + o, 3, 5) for o in range(2)]
                k3[0, end, c, 0] = jnp.where(upper, even, pltpu.roll(odd, 4, 0))
                k3[1, end, c, 0] = jnp.where(upper, pltpu.roll(even, 4, 0), odd)
        begin(third)
        begin(wedges)
        begin(outer)

    outer_residual(HALO - 2)
    outer_residual(HALO + X + 1)
    solve(0, e1a, e1b, lambda c, x: (e1a[3 + c, x], e1b[3 + c, x]), 1, ship_halo)
    spread_out(outb.at[3], inb.at[3], 3)
    finish_recv(second, recv2)
    tip_unpack(tips)
    for made, recv in zip(late, (recvu, recvw)):
        finish_recv(made, recv)
    edge_link(HALO - REACH)
    coefficients(HALO - 2)
    coefficients(HALO + X + 1)

    def open2(i, _):
        for ch in range(3):
            e2b[ch, 2 * i], e2b[ch, 2 * i + 1] = unpack(h2, ch, i)
        return 0

    lax.fori_loop(0, (X + 2 * HALO) // 2, open2, 0)
    finish_recv(third, recv3)
    for at, (ds, dg) in enumerate(steps[4:]):
        back = wedges[3 - at][2]

        @pl.when(inside(ds, dg))
        def _():
            back.wait_recv()

    def open3(i, _):
        for c in range(3):
            even, odd = unpack(h3, c, i)
            split(c, 2 * i, even, 2, 7, 1)
            split(c, 2 * i + 1, odd, 2, 7, 1)
        return 0

    lax.fori_loop(HALO // 2, (HALO + X) // 2, open3, 0)
    for pair, one in ((HALO // 2 - 1, 1), ((HALO + X) // 2, 0)):
        for c in range(3):
            for o, tile in enumerate(unpack(h3, c, pair)):
                if o == one:
                    split(c, 2 * pair + o, tile, 1, 6, 2)
                else:
                    split(c, 2 * pair + o, tile, 0, 5, 3)
    finish_recv(outer, recvq)
    c0, c1 = collect(0)

    def step1(x, both=True):
        for c in range(3):
            u1a[c, x] = e1a[c, x] + (c0 * rqa[c, x] + c1 * rqa[3 + c, x])
            u1b[c, x] = e1b[c, x] + (c0 * rqb[c, x] + c1 * rqb[3 + c, x]) if both else jnp.zeros((8, 128), jnp.float32)

    for x in range(HALO - REACH + 1, HALO + X + REACH - 1):
        step1(x)
    step1(HALO - REACH, False)
    step1(HALO + X + REACH - 1, False)
    finish_send(zeroth)
    finish_send(corners)
    finish_send(rest)
    finish_send(first)
    finish_send(second)
    finish_send(tips)
    for made in late:
        finish_send(made)
    finish_send(third)
    finish_send(outer)
    finish_send(wedges)

    def rhs2(c, x):
        return (MASS_TERM * (2.0 * u1a[c, x] - e1a[c, x]) + e2a[c, x],
                MASS_TERM * (2.0 * u1b[c, x] - e1b[c, x]) + e2b[c, x])

    def early(at, ref, ch):
        for x in range(X):
            rows[at, pl.ds(x, 8, stride=X), :] = ref[ch, HALO + x]
        turn_out(rows[at], outb.at[at])
        spread_out(outb.at[at], inb.at[at], at)
        inb[at, si] = outb[at, si]

    early(2, u1a, 2)
    solve(1, u1a, u1b, rhs2, 2)
    early(4, rqa, 2)
    early(5, rqa, 5)
    c0, c1 = collect(1)

    def step2(ra, rb, c, x):
        return ra[c, x] + (c0 * rb[c, x] + c1 * rb[3 + c, x])

    def halves(v):
        high = v.astype(jnp.bfloat16)
        return high, (v - high.astype(jnp.float32)).astype(jnp.bfloat16)

    def finish(c):
        for x in range(X):
            v = step2(u1a, rqa, c, HALO + x)
            disp_ref[c, x] = v
            rows[c, pl.ds(x, 8, stride=X), :] = v
        turned = turn_out(rows[c], outb.at[c])
        spread_out(outb.at[c], inb.at[c], c)
        inb[c, si] = outb[c, si]

    def joint(ref, j, low, high):
        return jnp.concatenate([
            ref[2, j, at:at + 8] + (c0 * ref[4, j, at:at + 8] + c1 * ref[5, j, at:at + 8])
            for at in range(low, high, 8)], axis=0)

    def finish_edges():
        for x in range(X):
            rows[6, pl.ds(x, 8, stride=X), :] = step2(u1b, rqb, 1, HALO + x)
        sides_y = rows[6].T
        zero = jnp.zeros((8, 128), jnp.float32)
        for j in range(ns):
            low, high = sides_y[zrows * j:zrows * j + 8], sides_y[zrows * j + 8:zrows * j + 16]
            tile = jnp.where(lane < 32, pltpu.roll(low, 16, 1),
                             jnp.where(lane < 64, pltpu.roll(pltpu.roll(low, 4, 0), 48, 1),
                                       jnp.where(lane < 96, pltpu.roll(high, 80, 1),
                                                 pltpu.roll(pltpu.roll(high, 4, 0), 112, 1))))
            before = pltpu.roll(joint(outb, j - 1, zrows - 8, zrows), 5, 0) if j else zero
            after = pltpu.roll(joint(outb, j + 1, 0, 8), 5, 0) if j + 1 < ns else zero
            outx[j] = jnp.where(sub == 4, before, jnp.where(sub == 5, after, tile))
        spread_out(outx, inx, 6)
        inx[si] = outx[si]

    finish(0)
    finish_edges()
    finish(1)
    for x in range(X):
        disp_ref[2, x] = step2(u1a, rqa, 2, HALO + x)
    fetched[7].wait()

    c1t, c3t = float(np.sqrt(0.5) * np.cos(np.pi / 8)), float(np.sqrt(0.5) * np.cos(3 * np.pi / 8))

    def cosine(v0, v1, v2, v3):
        s03, s12, d03, d12 = v0 + v3, v1 + v2, v0 - v3, v1 - v2
        return [0.5 * (s03 + s12), c1t * d03 + c3t * d12, 0.5 * (s03 - s12), c3t * d03 - c1t * d12]

    def encode(ch, fields):
        for b in range(Y // 4):
            for k, v in enumerate(cosine(*fields[4 * b:4 * b + 4])):
                work[ch, (4 * b + k) * zrows:(4 * b + k + 1) * zrows] = v
        parts = []
        for p in range(Y * zrows // 32):
            parts += cosine(*[work[ch, pl.ds(32 * p + n, 8, stride=4), :] for n in range(4)])
        high, low = halves(jnp.concatenate(parts, axis=0))
        done = jnp.dot(jnp.concatenate([high, low], axis=1), gt_ref[...], preferred_element_type=jnp.float32)
        done = done[:, 0:128] + done[:, 128:256]
        for p in range(Y * zrows // 32):
            for n in range(4):
                coef_ref[ch, pl.ds(32 * p + n, 8, stride=4), :] = done[(4 * p + n) * 8:(4 * p + n + 1) * 8]

    def arrived(c):
        landed(inb.at[c], trecv.at[c])
        return regroup([inb[c, j] for j in range(ns)])

    for at in (2, 4, 5):
        landed(inb.at[at], trecv.at[at])
    along = regroup([joint(inb, j, 0, zrows) for j in range(ns)])
    encode(2, along)
    landed(inb.at[3], trecv.at[3])
    for y, piece in enumerate(regroup([inb[3, j] for j in range(ns)])):
        scale[y] = piece
    field = arrived(0)
    encode(0, field)
    wide = lax.broadcasted_iota(jnp.int32, (zrows, 128), 1)
    encode(3, [scale[y] * (jnp.where(wide < 127, up_z(field[y]), 0.0) - jnp.where(wide > 0, down_z(field[y]), 0.0))
               for y in range(Y)])
    landed(inx, trecv.at[6])
    edges = regroup([inx[j] for j in range(ns)])
    stress = []
    for y in range(Y):
        low, high = along[y][0:8], along[y][8:16]
        ul, uh, dl, dh = pltpu.roll(low, 7, 0), pltpu.roll(high, 7, 0), pltpu.roll(low, 1, 0), pltpu.roll(high, 1, 0)
        first, last = sub == 0, sub == 7
        low = jnp.where(last, uh, ul) - jnp.where(first, pltpu.roll(edges[y], 4, 0), dl)
        high = jnp.where(last, pltpu.roll(edges[y], 2, 0), uh) - jnp.where(first, dl, dh)
        stress.append(scale[y] * jnp.concatenate([low, high], axis=0))
    encode(5, stress)
    field = arrived(1)
    encode(1, field)
    outside = []
    for side in range(2):
        quarter = [edges[2 * q + side] for q in range(4)]
        outside.append(jnp.concatenate([jnp.where(upper, quarter[q], pltpu.roll(quarter[q + 1], 4, 0)) for q in (0, 2)], axis=0))
    field = [outside[0]] + field + [outside[1]]
    encode(4, [scale[y] * (field[y + 2] - field[y]) for y in range(Y)])
    drain(0)
    drain(1)
    for at in range(6):
        landed(inb.at[at], tsend.at[at])
    landed(inx, tsend.at[6])


def store(disp_in, coef_in, disp_out, coef_out, sems):
    copies = [pltpu.make_async_copy(disp_in, disp_out, sems.at[0]), pltpu.make_async_copy(coef_in, coef_out, sems.at[1])]
    for copy in copies:
        copy.start()
    for copy in copies:
        copy.wait()


def fused(mesh, u_now, u_prev, force, stiffness, broken, flags):
    ns, ng = mesh.shape["slab"], mesh.shape["grp"]
    _, X, Y, Z = u_now.shape
    xe, pairs, half = X + 2 * HALO, X // 2 + HALO, X // 2
    zrows = Z // ns
    ez = jnp.asarray(np.kron(np.eye(Z // 4), np.ones((1, 4))), jnp.float32)
    gth, gtl = split_table(wavelet_table(X * ns).T)
    gt = jnp.asarray(np.block([[gth, gtl], [gth, np.zeros_like(gtl)]]), jnp.bfloat16)

    def vm(*shape):
        return pltpu.VMEM(shape, jnp.float32)

    def ext(n):
        return vm(n, xe, Y, Z)

    def stage(n):
        return vm(2, n, half, Y, Z)

    def land(n):
        return vm(2, n, pairs, Y, Z)

    dma = pltpu.SemaphoreType.DMA
    shapes = (u_now.shape, (6, Y * zrows, X * ns))
    operands = [pltpu.with_memory_space_constraint(v, pltpu.HBM)
                for v in (u_now, u_prev, force, stiffness, broken, flags, ez, gt)]
    results = pl.pallas_call(
        lambda *refs: kernel(ns, ng, *refs),
        name="lattice",
        out_shape=tuple(vm(*shape) for shape in shapes),
        in_specs=[pl.BlockSpec(memory_space=pltpu.MemorySpace.HBM)] * 8,
        out_specs=(pl.BlockSpec(memory_space=pltpu.VMEM),) * 2,
        scratch_shapes=[
            vm(*u_now.shape), vm(*u_now.shape), vm(*u_now.shape), vm(*stiffness.shape),
            pltpu.VMEM(broken.shape, broken.dtype), pltpu.VMEM(flags.shape, flags.dtype),
            vm(*ez.shape), pltpu.VMEM(gt.shape, gt.dtype), pltpu.SemaphoreType.DMA((8,)),
            ext(7), ext(7), stage(7), land(7),
            ext(3), ext(3), stage(3), land(3),
            ext(6), ext(6), stage(3), land(3), vm(2, 2, 3, 1, Y, Z), vm(2, 3, 2, Y, Z),
            ext(3), ext(3), vm(Y, zrows, X * ns), ext(3), ext(3), ext(5), ext(5),
            pltpu.SemaphoreType.REGULAR((4,)), vm(2, ns * ng, 1, 128), vm(7, Y * X, Z), vm(6, ns, zrows, 128), vm(6, ns, zrows, 128), vm(ns, 8, 128), vm(ns, 8, 128), vm(6, Y * zrows, X * ns),
            vm(2, 2, 2, Y, Z), vm(2, 2, 2, Y, Z), dma((4,)), dma((4,)), dma((4,)), dma((4,)),
            dma((4,)), dma((4,)), dma((4,)), dma((4,)), dma((4,)), dma((4,)), dma((4,)), dma((4,)), dma((2,)), dma((2,)), dma((4,)), dma((4,)),
            dma((2,)), dma((2,)), dma((2,)), dma((2,)), vm(2, 2, Y, Z), vm(2, 2, Y, Z), dma((4,)), dma((4,)),
            dma((2,)), dma((2,)), dma((7,)), dma((7,)),
        ],
        compiler_params=pltpu.CompilerParams(collective_id=0, has_side_effects=True, vmem_limit_bytes=24 << 20),
    )(*operands)
    disp, coef = pl.pallas_call(
        store,
        name="store",
        out_shape=tuple(jax.ShapeDtypeStruct(shape, jnp.float32) for shape in shapes),
        in_specs=[pl.BlockSpec(memory_space=pltpu.VMEM)] * 2,
        out_specs=(pl.BlockSpec(memory_space=pltpu.MemorySpace.HBM),) * 2,
        scratch_shapes=[dma((2,))],
        compiler_params=pltpu.CompilerParams(vmem_limit_bytes=1 << 20),
    )(*[pltpu.with_memory_space_constraint(v, pltpu.VMEM) for v in results])
    return disp, coef.reshape(6, Y, zrows, X * ns)


def fits(mesh, shape):
    ns, ng = mesh.shape["slab"], mesh.shape["grp"]
    x, y, z = shape[1] // ns, shape[2] // ng, shape[3]
    return y == 8 and z == 128 and x * y == 128 and x * ns == 128 and z % (8 * ns) == 0


def entry(mesh, *args):
    ns, ng = mesh.shape["slab"], mesh.shape["grp"]
    _, x, y, z = args[0].shape
    if fits(mesh, (3, x * ns, y * ng, z)):
        return fused(mesh, *args)
    return body(*args)


def solution(mesh):
    return jax.shard_map(
        lambda *args: entry(mesh, *args),
        mesh=mesh,
        in_specs=(
            P(None, "slab", "grp", None),
            P(None, "slab", "grp", None),
            P(None, "slab", "grp", None),
            P("slab", "grp", None),
            P("slab", "grp", None),
            P("slab", "grp", None),
        ),
        out_specs=(P(None, "slab", "grp", None), P(None, "grp", "slab", None)),
        check_vma=False,
    )
```

```python
import jax
import jax.numpy as jnp
import numpy as np
from jax import lax
from jax.experimental import pallas as pl
from jax.experimental.pallas import tpu as pltpu
from jax.sharding import PartitionSpec as P

STEPS = 2
ITERS = 2
LEVELS = 3


SPRING_NORMAL = 1.0
SPRING_SHEAR = 0.4
MASS_TERM = 1.0
CRACK_CUT = 0.9


def with_halo(block, sides, width):
    for axis, dim in sides:
        count = lax.axis_size(axis)
        forward = [(i, i + 1) for i in range(count - 1)]
        backward = [(target, source) for source, target in forward]
        low = lax.ppermute(
            lax.slice_in_dim(block, block.shape[dim] - width, None, axis=dim), axis, forward
        )
        high = lax.ppermute(lax.slice_in_dim(block, 0, width, axis=dim), axis, backward)
        block = jnp.concatenate([low, block, high], axis=dim)
    return block


def cosine_table():
    freq = np.arange(4)[:, None]
    place = np.arange(4)[None, :]
    factor = np.where(freq == 0, 0.5, np.sqrt(0.5))
    return factor * np.cos(np.pi * (2 * place + 1) * freq / 8.0)


def block_table(count):
    return jnp.asarray(np.kron(np.eye(count // 4), cosine_table()), jnp.float32)


def spread(mask):
    values = mask.astype(jnp.float32)
    size_a, size_b, size_c = values.shape
    wide = jnp.broadcast_to(values[:, None, :, None, :, None], (size_a, 4, size_b, 4, size_c, 4))
    return wide.reshape(size_a * 4, size_b * 4, size_c * 4)


def sides(padded, axis_index):
    leading = padded.ndim - 3

    def cut(offset):
        index_list = [slice(None)] * leading + [slice(1, -1)] * 3
        length = padded.shape[leading + axis_index]
        index_list[leading + axis_index] = slice(1 + offset, length - 1 + offset)
        return padded[tuple(index_list)]

    return (cut(1), cut(-1))


def springs(field, weight, field_pad, weight_pad):
    result = MASS_TERM * field
    for axis_index in range(3):
        upper_v, lower_v = sides(field_pad, axis_index)
        upper_w, lower_w = sides(weight_pad, axis_index)
        k_upper = 0.5 * (weight + upper_w)
        k_lower = 0.5 * (weight + lower_w)
        change = k_upper * (field - upper_v) + k_lower * (field - lower_v)
        coupling = jnp.array(
            [SPRING_NORMAL if comp == axis_index else SPRING_SHEAR for comp in range(3)],
            jnp.float32,
        ).reshape(3, 1, 1, 1)
        result = result + coupling * change
    return result


def faces(field):
    padded = with_halo(field, (("slab", 1), ("grp", 2)), 1)
    return jnp.pad(padded, ((0, 0), (0, 0), (0, 0), (1, 1)))


def stresses(carry, field_pad):
    rows_out = []
    for axis_index in range(3):
        upper_v, lower_v = sides(field_pad, axis_index)
        rows_out.append(SPRING_NORMAL * carry * 0.5 * (upper_v[axis_index] - lower_v[axis_index]))
    return jnp.stack(rows_out)


def paired_sum(residual, image):
    return lax.psum((jnp.sum(residual * residual), jnp.sum(residual * image)), ("slab", "grp"))


def lift(signal):
    even = signal[..., 0::2]
    odd = signal[..., 1::2]
    detail = odd - 0.5 * (even + jnp.roll(even, -1, axis=-1))
    approx = even + 0.25 * (jnp.roll(detail, 1, axis=-1) + detail)
    return (approx, detail)


def wavelet(signal):
    pieces = []
    approx = signal
    for level_index in range(LEVELS):
        approx, detail = lift(approx)
        pieces.insert(0, detail)
    return jnp.concatenate([approx] + pieces, axis=-1)


def body(u_now, u_prev, force, stiffness, broken, flags):
    weight = stiffness * (1.0 - CRACK_CUT * spread(broken))
    carry = spread(flags) * weight
    weight_pad = with_halo(weight, (("slab", 0), ("grp", 1)), 1)
    weight_pad = jnp.pad(weight_pad, ((0, 0), (0, 0), (1, 1)))

    def operate(field):
        return springs(field, weight, faces(field), weight_pad)

    for step_index in range(STEPS):
        rhs = MASS_TERM * (2.0 * u_now - u_prev) + force
        guess = u_now
        residual = rhs - operate(guess)
        image = operate(residual)
        norm_now, product = paired_sum(residual, image)
        alpha = norm_now / product
        direction, along = (residual, image)
        for turn_index in range(ITERS):
            guess = guess + alpha * direction
            residual = residual - alpha * along
            if turn_index + 1 < ITERS:
                image = operate(residual)
                norm_next, product = paired_sum(residual, image)
                ratio = norm_next / norm_now
                alpha = norm_next / (product - ratio * norm_next / alpha)
                direction = residual + ratio * direction
                along = image + ratio * along
                norm_now = norm_next
        u_prev = u_now
        u_now = guess
    stress = stresses(carry, faces(u_now))
    fields = jnp.concatenate([u_now, stress], axis=0)
    table_x = block_table(fields.shape[1])
    table_y = block_table(fields.shape[2])
    table_z = block_table(fields.shape[3])
    blockc = jnp.einsum("ax,hxyz->hayz", table_x, fields, precision=lax.Precision.HIGHEST)
    blockc = jnp.einsum("by,hxyz->hxbz", table_y, blockc, precision=lax.Precision.HIGHEST)
    blockc = jnp.einsum("hxyz,cz->hxyc", blockc, table_z, precision=lax.Precision.HIGHEST)
    moved = jnp.transpose(blockc, (0, 2, 3, 1))
    shipped = lax.all_to_all(moved, "slab", split_axis=2, concat_axis=3, tiled=True)
    coeffs = wavelet(shipped)
    return (u_now, coeffs)


MESH = pl.DeviceIdType.MESH
HALO = 4
REACH = 3
SHEAR_REST = SPRING_NORMAL - SPRING_SHEAR
WIDE_R, WIDE_A, WIDE_C, WIDE_K = 20, 16, 16, 20


def wavelet_table(count):
    table = np.kron(np.eye(count // 4), cosine_table())
    pieces = []
    approx = table
    for level_index in range(LEVELS):
        even, odd = approx[0::2], approx[1::2]
        detail = odd - 0.5 * (even + np.roll(even, -1, axis=0))
        approx = even + 0.25 * (np.roll(detail, 1, axis=0) + detail)
        pieces.insert(0, detail)
    return np.concatenate([approx] + pieces, axis=0)


def split_table(table):
    high = table.astype(jnp.bfloat16).astype(np.float64)
    return high, (table - high).astype(jnp.bfloat16).astype(np.float64)


def sub_index():
    return lax.broadcasted_iota(jnp.int32, (8, 128), 0)


def lane_index():
    return lax.broadcasted_iota(jnp.int32, (8, 128), 1)


def up_y(a, b):
    ra, rb = pltpu.roll(a, 7, 0), pltpu.roll(b, 7, 0)
    last = sub_index() == 7
    return jnp.where(last, rb, ra), jnp.where(last, ra, rb)


def down_y(a, b):
    ra, rb = pltpu.roll(a, 1, 0), pltpu.roll(b, 1, 0)
    first = sub_index() == 0
    return jnp.where(first, rb, ra), jnp.where(first, ra, rb)


def up_z(v):
    return pltpu.roll(v, 127, 1)


def down_z(v):
    return pltpu.roll(v, 1, 1)


def total(v):
    return jnp.sum(jnp.sum(v, axis=0, keepdims=True), axis=1, keepdims=True)


def kernel(ns, ng, u_in, p_in, f_in, k_in, br_in, fl_in, ez_in, gt_in,
           disp_ref, coef_ref,
           u_ref, p_ref, f_ref, k_ref, br_ref, fl_ref, ez_ref, gt_ref, isem,
           e1a, e1b, s1, h1, e2a, e2b, s2, h2, rqa, rqb, s3, h3, k3, ends,
           u1a, u1b, sa, sb, scale, dga, dgb, kca, kcb, known, gath, rows, outb, inb, outx, inx, work,
           blanks, sends, ctake, cland, crecv, recv0, recv1, recv2, recv3, recvk, ftake, fland, recvf, asend, arecv, tsend, trecv):
    X, Y, Z = u_ref.shape[1:]
    si, gi = lax.axis_index("slab"), lax.axis_index("grp")
    me = si * ng + gi
    count = ns * ng
    barrier = pltpu.get_barrier_semaphore()

    def mirrored(place, mask, length):
        bit, result = 1, 0
        while bit < length:
            here = place // bit % 2
            result = result + bit * (1 - here if mask // bit % 2 else here)
            bit *= 2
        return result

    others = []
    for k in sorted(range(ns), key=lambda k: -min(k, ns - k)):
        for g in range(ng):
            if k or g:
                others.append((lax.rem(si + k, ns), lax.rem(gi + g, ng)))

    sub, lane = sub_index(), lane_index()
    upper = sub < 4

    steps = [(-1, 0), (1, 0), (0, -1), (0, 1), (-1, -1), (-1, 1), (1, -1), (1, 1)]

    def inside(ds, dg):
        ok = None
        if ds:
            ok = (si >= -ds) if ds < 0 else (si <= ns - 1 - ds)
        if dg:
            more = (gi >= -dg) if dg < 0 else (gi <= ng - 1 - dg)
            ok = more if ok is None else jnp.logical_and(ok, more)
        return ok

    def around(reach):
        return [(ds, dg) for ds in (-reach, 0, reach) for dg in (-reach, 0, reach)
                if (ds or dg) and abs(ds) < ns and abs(dg) < ng]

    def greet(sem, reach):
        for ds, dg in around(reach):
            @pl.when(inside(ds, dg))
            def _():
                pl.semaphore_signal(sem, inc=1, device_id=(si + ds, gi + dg), device_id_type=MESH)

    def meet(sem, reach):
        pl.semaphore_wait(sem, sum(jnp.where(inside(ds, dg), 1, 0) for ds, dg in around(reach)))

    rounds = []
    while (rounds[-1] * 2 if rounds else 1) < max(ns, ng):
        rounds.append(rounds[-1] * 2 if rounds else 1)

    greet(barrier, 1)
    fetched = []
    for at, (source, target) in enumerate((
        (br_in, br_ref), (fl_in, fl_ref), (ez_in, ez_ref), (k_in, k_ref), (u_in, u_ref), (p_in, p_ref),
        (f_in, f_ref), (gt_in, gt_ref),
    )):
        fetch = pltpu.make_async_copy(source, target, isem.at[min(at, 4) if at < 7 else 5])
        fetch.start()
        fetched.append(fetch)

    def copies(ea, dst_a, stage, land, recv, low=0, high=None, ways=4, reach=REACH, depth=None, ends=None):
        depth = reach if depth is None else depth
        half = X // 2
        edge = HALO // 2
        made = []
        chans = pl.ds(low, (ea.shape[0] if high is None else high) - low)
        for at, (ds, dg) in enumerate(steps[:ways]):
            if dg == 0:
                if ends is not None:
                    source = ends.at[0 if ds < 0 else 1]
                    target = dst_a.at[chans, pl.ds(HALO + X if ds < 0 else HALO - depth, reach)]
                elif ds < 0:
                    source = ea.at[chans, pl.ds(HALO + depth - reach, reach)]
                    target = dst_a.at[chans, pl.ds(HALO + X + depth - reach, reach)]
                else:
                    source = ea.at[chans, pl.ds(HALO + X - depth, reach)]
                    target = dst_a.at[chans, pl.ds(HALO - depth, reach)]
            else:
                side = 0 if dg < 0 else 1
                source, target = stage.at[side, chans], land.at[side, chans, pl.ds(edge, half)]
            made.append((ds, dg, pltpu.make_async_remote_copy(
                src_ref=source, dst_ref=target, send_sem=sends.at[at], recv_sem=recv.at[at ^ 1],
                device_id=(si + ds, gi + dg), device_id_type=MESH)))
        return made

    def begin(made):
        for ds, dg, copy in made:
            @pl.when(inside(ds, dg))
            def _():
                copy.start()

    def take(tiles, sem):
        block = blanks.at[pl.ds(0, tiles)]
        pltpu.make_async_copy(block, block, sem).wait()

    def finish_recv(recv, slab_tiles, grp_tiles):
        for at, (ds, dg) in enumerate(steps[:4]):
            @pl.when(inside(ds, dg))
            def _():
                if (slab_tiles if ds else grp_tiles):
                    take(slab_tiles if ds else grp_tiles, recv.at[at])

    def finish_send(slab_tiles, grp_tiles, corner_tiles):
        for at, (ds, dg) in enumerate(steps):
            @pl.when(inside(ds, dg))
            def _():
                take(corner_tiles if ds and dg else slab_tiles if ds else grp_tiles, sends.at[at])

    def blank(dst_a, land):
        zero_a = jnp.zeros((dst_a.shape[0], HALO) + dst_a.shape[2:], jnp.float32)
        half, edge = X // 2, HALO // 2
        zero_l = jnp.zeros((land.shape[1], edge, 8, 128), jnp.float32)

        @pl.when(si == 0)
        def _():
            dst_a[:, pl.ds(0, HALO)] = zero_a
            for side in range(2):
                land[side, :, pl.ds(0, edge)] = zero_l

        @pl.when(si == ns - 1)
        def _():
            dst_a[:, pl.ds(HALO + X, HALO)] = zero_a
            for side in range(2):
                land[side, :, pl.ds(edge + half, edge)] = zero_l

        for side, edge_here in ((0, gi == ng - 1), (1, gi == 0)):
            @pl.when(edge_here)
            def _(side=side):
                land[side] = jnp.zeros(land.shape[1:], jnp.float32)

    def pack(stage, ch, pair, even, odd):
        stage[0, ch, pair] = jnp.where(upper, even, pltpu.roll(odd, 4, 0))
        stage[1, ch, pair] = jnp.where(upper, pltpu.roll(even, 4, 0), odd)

    def unpack(land, ch, pair):
        high, low = land[0, ch, pair], land[1, ch, pair]
        return (jnp.where(upper, high, pltpu.roll(low, 4, 0)),
                jnp.where(upper, pltpu.roll(high, 4, 0), low))

    def spread_rows(mask):
        wide = jnp.dot(mask.astype(jnp.float32), ez_ref[...], preferred_element_type=jnp.float32)
        return jnp.where(upper, jnp.broadcast_to(wide[0:1], (8, 128)), jnp.broadcast_to(wide[1:2], (8, 128)))

    for at in range(4):
        fetched[at].wait()
    for bx in range(X // 4):
        cut = 1.0 - CRACK_CUT * spread_rows(br_ref[bx])
        flag = spread_rows(fl_ref[bx])
        for at in range(4):
            x = bx * 4 + at
            w = k_ref[x] * cut
            e1a[6, HALO + x] = w
            rows[3, pl.ds(x, 8, stride=X), :] = (SPRING_NORMAL * 0.5) * (flag * w)

    def own(i, _):
        for c in range(3):
            tiles = []
            for o in range(2):
                x = 2 * i + o
                u = u_ref[c, x]
                f = f_ref[c, x]
                rhs = MASS_TERM * (2.0 * u - p_ref[c, x]) + f
                e1a[c, HALO + x] = u
                e1a[3 + c, HALO + x] = rhs
                e2a[c, HALO + x] = f
                tiles.append((u, rhs, f))
            pack(s1, c, i, tiles[0][0], tiles[1][0])
            pack(s1, 3 + c, i, tiles[0][1], tiles[1][1])
            pack(s2, c, i, tiles[0][2], tiles[1][2])
        pack(s1, 6, i, e1a[6, HALO + 2 * i], e1a[6, HALO + 2 * i + 1])
        return 0

    take(9 * X, isem.at[4])
    lax.fori_loop(0, X // 2, own, 0)
    blank(e1a, h1)
    blank(e2a, h2)
    blank(rqa, h3)
    for ch in range(6):
        for x in (HALO - REACH, HALO + X + REACH - 1):
            rqb[ch, x] = jnp.zeros((8, 128), jnp.float32)

    zrows = Z // ns

    def turn_out(value, out):
        turned = value.T
        for j in range(ns):
            out[j] = turned[j * zrows:(j + 1) * zrows]

    def spread_out(source, target, at):
        for m in reversed(range(1, ns)):
            to = mirrored(si, m, ns)
            pltpu.make_async_remote_copy(
                src_ref=source.at[to], dst_ref=target.at[si], send_sem=tsend.at[0 if at < 6 else 1], recv_sem=trecv.at[at],
                device_id=(to, gi), device_id_type=MESH).start()

    def landed(target, sem):
        block = target.at[pl.ds(0, ns - 1)]
        pltpu.make_async_copy(block, block, sem).wait()

    def regroup(pieces):
        lanes = lax.broadcasted_iota(jnp.int32, pieces[0].shape, 1)
        gap = ns // 2
        while gap:
            keep = (lanes // (X * gap)) % 2 == 0
            mixed = list(pieces)
            for j in range(ns):
                if (j // gap) % 2 == 0:
                    a, b = pieces[j], pieces[j + gap]
                    mixed[j] = jnp.where(keep, a, pltpu.roll(b, X * gap, 1))
                    mixed[j + gap] = jnp.where(keep, pltpu.roll(a, 128 - X * gap, 1), b)
            pieces = mixed
            gap //= 2
        return pieces

    not_last, not_first = lane < 127, lane > 0

    def inner_ends():
        for end, x in ((0, HALO + 1), (1, HALO + X - 2)):
            w = e1a[6, x]
            along = (0.5 * (w + e1a[6, x + 1]), 0.5 * (w + e1a[6, x - 1]),
                     jnp.where(sub < 7, 0.5 * (w + pltpu.roll(w, 7, 0)), 0.0),
                     jnp.where(sub > 0, 0.5 * (w + pltpu.roll(w, 1, 0)), 0.0),
                     0.5 * (w + jnp.where(not_last, up_z(w), 0.0)), 0.5 * (w + jnp.where(not_first, down_z(w), 0.0)))
            for c in range(3):
                v = e1a[c, x]
                parts = (along[0] * (v - e1a[c, x + 1]) + along[1] * (v - e1a[c, x - 1]),
                         along[2] * (v - pltpu.roll(v, 7, 0)) + along[3] * (v - pltpu.roll(v, 1, 0)),
                         along[4] * (v - jnp.where(not_last, up_z(v), 0.0))
                         + along[5] * (v - jnp.where(not_first, down_z(v), 0.0)))
                image = MASS_TERM * v + (SPRING_SHEAR * (parts[0] + parts[1] + parts[2]) + SHEAR_REST * parts[c])
                ends[end, c, 1 - end] = e1a[3 + c, x] - image
                ends[end, c, end] = e1a[3 + c, x - 1 + 2 * end]

    def outer_residual(x):
        wa, wb = e1a[6, x], e1b[6, x]
        above = jnp.where(sub == 7, 0.5 * (wa + up_y(wa, wb)[0]), 0.0)
        below = jnp.where(sub == 0, 0.5 * (wa + down_y(wa, wb)[0]), 0.0)
        for c in range(3):
            a, b = e1a[c, x], e1b[c, x]
            change = above * (a - up_y(a, b)[0]) + below * (a - down_y(a, b)[0])
            rqa[c, x] = e1a[3 + c, x] - (SPRING_NORMAL if c == 1 else SPRING_SHEAR) * change
            rqb[c, x] = jnp.zeros((8, 128), jnp.float32)

    def tip_copies():
        made = []
        for at, (ds, dg) in enumerate(steps[4:]):
            side, end = (0 if dg < 0 else 1), (0 if ds < 0 else 1)
            made.append((ds, dg, pltpu.make_async_remote_copy(
                src_ref=ftake.at[side, end], dst_ref=fland.at[side, 1 - end],
                send_sem=sends.at[4 + at], recv_sem=recvf.at[3 - at],
                device_id=(si + ds, gi + dg), device_id_type=MESH)))
        return made

    def tip_unpack(made):
        for at, (ds, dg) in enumerate(steps[4:]):
            side, end = (0 if dg > 0 else 1), (1 if ds > 0 else 0)
            pair = HALO // 2 + X // 2 if ds > 0 else HALO // 2 - 1
            back = made[3 - at][2]

            @pl.when(inside(ds, dg))
            def _():
                back.wait_recv()
                tile = fland[side, end]
                for c in range(3):
                    h2[side, c, pair] = pltpu.roll(tile, 8 - 2 * c, 0) if c else tile

    def wedge_copies():
        made = []
        for at, (ds, dg) in enumerate(steps[4:]):
            side, end = (0 if dg < 0 else 1), (0 if ds < 0 else 1)
            pair = HALO // 2 + X // 2 if ds < 0 else HALO // 2 - 1
            made.append((ds, dg, pltpu.make_async_remote_copy(
                src_ref=k3.at[side, end], dst_ref=h3.at[side, :, pl.ds(pair, 1)],
                send_sem=sends.at[4 + at], recv_sem=recvk.at[3 - at],
                device_id=(si + ds, gi + dg), device_id_type=MESH)))
        return made

    def corner_copies():
        made = []
        for at, (ds, dg) in enumerate(steps[4:]):
            side, end = (0 if dg < 0 else 1), (0 if ds < 0 else 1)
            made.append((ds, dg, pltpu.make_async_remote_copy(
                src_ref=ctake.at[side, end], dst_ref=cland.at[side, 1 - end],
                send_sem=sends.at[4 + at], recv_sem=crecv.at[3 - at],
                device_id=(si + ds, gi + dg), device_id_type=MESH)))
        return made

    def corner_rows(side, end):
        dx1, dx2 = (0, 4) if end == 0 else (4, 0)
        dy1, dy2 = (0, 1) if side == 0 else (3, 2)
        return dx1 + dy1, dx1 + dy2, dx2 + dy1

    def any_row(places):
        found = sub == places[0]
        for place in places[1:]:
            found = jnp.logical_or(found, sub == place)
        return found

    corner_sets = ((0, 1, (3, 4)), (2, 6, (5,)))
    for side in range(2):
        for end in range(2):
            places = corner_rows(side, end)
            first_here, second_here = any_row(places), any_row([(v + 2) % 8 for v in places])
            for at, (ch_a, ch_b, right) in enumerate(corner_sets):
                tiles = [s1[side, ch, end * (X // 2 - 1)] for ch in (ch_a, ch_b) + right]
                tile = pltpu.roll(tiles[2], 5, 0)
                if len(right) == 2:
                    tile = jnp.where(sub == (places[0] + 5) % 8, tile, pltpu.roll(tiles[3], 3 if side else 7, 0))
                tile = jnp.where(first_here, tiles[0], jnp.where(second_here, pltpu.roll(tiles[1], 2, 0), tile))
                ctake[side, end, at] = tile
            near = [s2[side, c, end * (X // 2 - 1)] for c in range(3)]
            ftake[side, end] = jnp.where(sub == places[0], near[0], jnp.where(
                sub == (places[0] + 2) % 8, pltpu.roll(near[1], 2, 0), pltpu.roll(near[2], 4, 0)))

    def corner_unpack(made):
        for at, (ds, dg) in enumerate(steps[4:]):
            side, end = (0 if dg > 0 else 1), (1 if ds > 0 else 0)
            pair = HALO // 2 + X // 2 if ds > 0 else HALO // 2 - 1
            back = made[3 - at][2]

            @pl.when(inside(ds, dg))
            def _():
                back.wait_recv()
                for at, (ch_a, ch_b, right) in enumerate(corner_sets):
                    tile = cland[side, end, at]
                    h1[side, ch_a, pair] = tile
                    h1[side, ch_b, pair] = pltpu.roll(tile, 6, 0)
                    h1[side, right[0], pair] = pltpu.roll(tile, 3, 0)
                    if len(right) == 2:
                        h1[side, right[1], pair] = pltpu.roll(tile, 5 if side else 1, 0)

    corners = corner_copies()
    zeroth = copies(e1a, e1a, s1, h1, recv0, 6, 7, 4, REACH - 1)
    first = copies(e1a, e1a, s1, h1, recv1, 0, 3, 4, REACH - 1)
    rest = copies(e1a, e1a, s1, h1, recv1, 3, 6, 4, REACH - 1, None, ends)
    late = (copies(e1a, e1a, s1, h1, recv2, 0, 3, 2, 1, REACH),
            copies(e1a, e1a, s1, h1, recv2, 6, 7, 2, 1, REACH))
    second = copies(e2a, e2a, s2, h2, recv2, 0, 3, 4, REACH - 1)
    tips = tip_copies()
    third = copies(rqa, rqa, s3, h3, recv3, 0, 3, 4, 1, REACH)
    outer = copies(rqa, rqa, s3, h3, recv3, 3, 6, 2, REACH - 1, REACH)
    wedges = wedge_copies()
    meet(barrier, 1)
    begin(zeroth)
    begin(corners)
    begin(first)
    inner_ends()
    begin(rest)
    greet(known.at[0], rounds[0])
    turn_out(rows[3], outb.at[3])
    inb[3, si] = outb[3, si]
    for at in range(len(rounds) - 2):
        meet(known.at[at], rounds[at])
        greet(known.at[at + 1], rounds[at + 1])
    finish_recv(recv0, REACH - 1, X // 2)
    corner_unpack(corners)
    meet(known.at[len(rounds) - 2], rounds[-2])
    greet(known.at[len(rounds) - 1], rounds[-1])
    begin(second)
    begin(tips)
    for made in late:
        begin(made)

    def open0(i, _):
        e1b[6, 2 * i], e1b[6, 2 * i + 1] = unpack(h1, 6, i)
        return 0

    def open1(i, _):
        for ch in range(6):
            e1b[ch, 2 * i], e1b[ch, 2 * i + 1] = unpack(h1, ch, i)
        return 0

    lax.fori_loop(0, (X + 2 * HALO) // 2, open0, 0)

    def link(w, other):
        return jnp.where(jnp.minimum(w, other) > 0.0, (0.5 * SPRING_SHEAR) * (w + other), 0.0)


    def over_rows(low, high, width, body, carried=0):
        width = max(v for v in range(1, width + 1) if (high - low) % v == 0)

        def chunk(i, state):
            return body([low + i * width + o for o in range(width)], state)

        return lax.fori_loop(0, (high - low) // width, chunk, carried)

    def all_coefficients(rows_here, _):
        for x in rows_here:
            coefficients(x)
        return 0

    def coefficients(x):
        wa, wb = e1a[6, x], e1b[6, x]
        ya, yb = up_y(wa, wb)
        da, db = down_y(wa, wb)
        for w, wu, wd, yu, yd, dg, kc in (
            (wa, e1a[6, x + 1], e1a[6, x - 1], ya, da, dga, kca),
            (wb, e1b[6, x + 1], e1b[6, x - 1], yb, db, dgb, kcb),
        ):
            zu = jnp.where(not_last, up_z(w), 0.0)
            zd = jnp.where(not_first, down_z(w), 0.0)
            kc[0, x] = link(w, wu)
            kc[1, x] = link(w, yu)
            kc[2, x] = link(w, yd)
            kc[3, x] = link(w, zu)
            kc[4, x] = link(w, zd)
            sx = w + 0.5 * (wu + wd)
            sy = w + 0.5 * (yu + yd)
            sz = w + 0.5 * (zu + zd)
            every = MASS_TERM + SPRING_SHEAR * (sx + sy + sz)
            dg[0, x] = every + SHEAR_REST * sx
            dg[1, x] = every + SHEAR_REST * sy
            dg[2, x] = every + SHEAR_REST * sz

    def edge_link(x):
        kca[0, x] = link(e1a[6, x], e1a[6, x + 1])
        kcb[0, x] = link(e1b[6, x], e1b[6, x + 1])

    edge_link(HALO - 2)
    over_rows(HALO - 1, HALO + X + 1, WIDE_K, all_coefficients)
    finish_recv(recv1, 6 * (REACH - 1), 3 * X)
    lax.fori_loop(0, (X + 2 * HALO) // 2, open1, 0)

    def operate(x, va, vb, base, chosen=slice(0, 2)):
        result = []
        coef = [[kc[j, x] for j in range(5)] + [kc[0, x - 1]] for kc in (kca, kcb)]
        for c in range(3):
            a, b = va[base + c, x], vb[base + c, x]
            ua, ub = up_y(a, b)
            la, lb = down_y(a, b)
            pair = []
            halves = ((a, va, ua, la, coef[0], dga), (b, vb, ub, lb, coef[1], dgb))
            for v, ref, u, l, k, dg in halves[chosen]:
                parts = (
                    k[0] * ref[base + c, x + 1] + k[5] * ref[base + c, x - 1],
                    k[1] * u + k[2] * l,
                    k[3] * up_z(v) + k[4] * down_z(v),
                )
                shear = parts[(c + 1) % 3] + parts[(c + 2) % 3]
                pair.append(dg[c, x] * v - (shear + (SPRING_NORMAL / SPRING_SHEAR) * parts[c]))
            result.append(pair)
        return result

    only_a, only_b = slice(0, 1), slice(1, 2)

    def residual(rows_here, _):
        for x in rows_here:
            image = operate(x, e1a, e1b, 0)
            for c in range(3):
                rqa[c, x] = e1a[3 + c, x] - image[c][0]
                rqb[c, x] = e1b[3 + c, x] - image[c][1]
        return 0

    def solve(step, ship_halo=None):
        def put(x, image):
            for c in range(3):
                rqa[3 + c, x] = image[c][0]
                rqb[3 + c, x] = image[c][1]

        def apply(rows_here, sums):
            rr, rq = sums
            for x in rows_here:
                image = operate(x, rqa, rqb, 0)
                for c in range(3):
                    r = rqa[c, x]
                    rr, rq = rr + r * r, rq + r * image[c][0]
                put(x, image)
            return rr, rq

        zero = jnp.zeros((8, 128), jnp.float32)
        images = [operate(x, rqa, rqb, 0) for x in (HALO - 1, HALO + X)]
        put(HALO - 1, images[0])
        put(HALO + X, images[1])
        rr, rq = over_rows(HALO, HALO + X, WIDE_A, apply, (zero, zero))
        if ship_halo is not None:
            ship_halo()
        rr, rq = total(rr), total(rq)
        mu = jnp.where(rr > 0.0, rq / jnp.where(rr > 0.0, rr, 1.0), 0.0)

        def centred(rows_here, sums):
            ww, wr, mix, wt = sums
            for x in rows_here:
                image = operate(x, rqa, rqb, 3, only_a)
                for c in range(3):
                    r, q, s = rqa[c, x], rqa[3 + c, x], image[c][0]
                    if step == 0:
                        sa[c, x] = s
                    w, t = q - mu * r, s - mu * q
                    ww, wr, mix, wt = ww + w * w, wr + w * r, mix + (r * t + w * q), wt + w * t
            return ww, wr, mix, wt

        sums = over_rows(HALO, HALO + X, WIDE_C, centred, (zero,) * 4)
        ww, wr, mix, wt = [total(v) for v in sums]
        one = lax.broadcasted_iota(jnp.int32, (1, 128), 1)
        row = jnp.zeros((1, 128), jnp.float32)
        for at, value in enumerate((rr, rq, mu, ww, wr, mix, wt)):
            row = jnp.where(one == at, value, row)
        gath[step, me] = row

        if step == 0:
            meet(known.at[len(rounds) - 1], rounds[-1])
        for other in others:
            pltpu.make_async_remote_copy(
                src_ref=gath.at[step, me], dst_ref=gath.at[step, me], send_sem=asend, recv_sem=arecv.at[step],
                device_id=other, device_id_type=MESH).start()

    def collect(step):
        block = gath.at[step, pl.ds(0, count - 1)]
        pltpu.make_async_copy(block, block, arecv.at[step]).wait()
        table = gath[step].reshape(count, 128)
        rr, rq, mu, ww, wr, mix, wt = [table[:, at:at + 1] for at in range(7)]

        def down(v):
            return jnp.sum(v, axis=0, keepdims=True)

        norm = down(rr)
        alpha = norm / down(rq)
        rest = 1.0 - alpha * mu
        after = down(alpha * alpha * ww - 2.0 * alpha * rest * wr + rest * rest * rr)
        curved = down(rest * rest * rq - alpha * rest * mix + alpha * alpha * wt)
        ratio = after / norm
        beta = after / (curved - ratio * after / alpha)
        return jnp.broadcast_to(alpha + beta * (1.0 + ratio), (8, 128)), jnp.broadcast_to(-beta * alpha, (8, 128))

    def drain():
        block = gath.at[:, pl.ds(0, count - 1)]
        pltpu.make_async_copy(block, block, asend).wait()

    def joined(c, x, near, far):
        r, q = rqa[c, x], rqa[3 + c, x]
        return jnp.where(sub == 3, pltpu.roll(r, near, 0), jnp.where(sub == 4, pltpu.roll(r, far, 0), q))

    def split(c, x, tile, row, near, far):
        r = rqb[c, x]
        rqb[c, x] = jnp.where(sub == row, pltpu.roll(tile, near, 0), jnp.where(sub == 7 - row, pltpu.roll(tile, far, 0), r))
        rqb[3 + c, x] = tile

    def ship_halo():
        def pack3(i, _):
            x = HALO + 2 * i
            for c in range(3):
                pack(s3, c, i, joined(c, x, 1, 7), joined(c, x + 1, 1, 7))
            return 0

        lax.fori_loop(0, X // 2, pack3, 0)
        for end, x in ((0, HALO), (1, HALO + X - 2)):
            for c in range(3):
                even, odd = [joined(c, x + o, 2, 6) if o == end else joined(c, x + o, 3, 5) for o in range(2)]
                k3[0, end, c, 0] = jnp.where(upper, even, pltpu.roll(odd, 4, 0))
                k3[1, end, c, 0] = jnp.where(upper, pltpu.roll(even, 4, 0), odd)
        begin(third)
        begin(wedges)
        begin(outer)

    outer_residual(HALO - 2)
    outer_residual(HALO + X + 1)
    over_rows(HALO - 1, HALO + X + 1, WIDE_R, residual)
    solve(0, ship_halo)
    spread_out(outb.at[3], inb.at[3], 3)
    finish_recv(recv2, 3 * (REACH - 1) + 4, 3 * X // 2)
    tip_unpack(tips)
    edge_link(HALO - REACH)
    coefficients(HALO - 2)
    coefficients(HALO + X + 1)

    def open2(i, _):
        for ch in range(3):
            e2b[ch, 2 * i], e2b[ch, 2 * i + 1] = unpack(h2, ch, i)
        return 0

    lax.fori_loop(0, (X + 2 * HALO) // 2, open2, 0)
    finish_recv(recv3, 3 + 3 * (REACH - 1), 3 * X // 2)
    for at, (ds, dg) in enumerate(steps[4:]):
        back = wedges[3 - at][2]

        @pl.when(inside(ds, dg))
        def _():
            back.wait_recv()

    def open3(i, _):
        for c in range(3):
            even, odd = unpack(h3, c, i)
            split(c, 2 * i, even, 2, 7, 1)
            split(c, 2 * i + 1, odd, 2, 7, 1)
        return 0

    lax.fori_loop(HALO // 2, (HALO + X) // 2, open3, 0)
    for pair, one in ((HALO // 2 - 1, 1), ((HALO + X) // 2, 0)):
        for c in range(3):
            for o, tile in enumerate(unpack(h3, c, pair)):
                if o == one:
                    split(c, 2 * pair + o, tile, 1, 6, 2)
                else:
                    split(c, 2 * pair + o, tile, 0, 5, 3)
    finish_send(13 * (REACH - 1) + 7, 13 * X // 2, 6)
    for x in range(HALO - 1, HALO + X + 1):
        image = operate(x, rqa, rqb, 3, only_b)
        for c in range(3):
            sb[c, x] = image[c][0]
            e2a[c, x] = MASS_TERM * e1a[c, x] + e2a[c, x] - e1a[3 + c, x] + rqa[c, x]
            e2b[c, x] = MASS_TERM * e1b[c, x] + e2b[c, x] - e1b[3 + c, x] + rqb[c, x]
    for x in (HALO - 2, HALO + X + 1):
        image = operate(x, e1a, e1b, 0, only_a)
        for c in range(3):
            e2a[c, x] = MASS_TERM * e1a[c, x] + e2a[c, x] - image[c][0]
    for x in (HALO - 2, HALO - 1, HALO + X, HALO + X + 1):
        image = operate(x, rqa, rqb, 3, only_a)
        for c in range(3):
            sa[c, x] = image[c][0]
    c0, c1 = collect(0)

    def step1(x, base, rq, g, s, u1, comps):
        for c in range(3):
            r, q = rq[c, x], rq[3 + c, x]
            grown = c0 * r + c1 * q
            if c in comps:
                u1[c, x] = base[c, x] + grown
            rq[c, x] = g[c, x] + (2.0 * MASS_TERM) * grown - (c0 * q + c1 * s[c, x])

    for x in range(HALO - 2, HALO + X + 2):
        own_row = HALO <= x < HALO + X
        step1(x, e1a, rqa, e2a, sa, u1a, (0, 1, 2) if own_row else ())
        if HALO - 1 <= x <= HALO + X:
            step1(x, e1b, rqb, e2b, sb, u1b, (1,) if own_row else ())

    def early(at, ref, ch):
        for x in range(X):
            rows[at, pl.ds(x, 8, stride=X), :] = ref[ch, HALO + x]
        turn_out(rows[at], outb.at[at])
        spread_out(outb.at[at], inb.at[at], at)
        inb[at, si] = outb[at, si]

    solve(1)
    early(2, u1a, 2)
    early(4, rqa, 2)
    early(5, rqa, 5)
    c0, c1 = collect(1)

    def step2(ra, rb, c, x):
        return ra[c, x] + (c0 * rb[c, x] + c1 * rb[3 + c, x])

    def halves(v):
        high = v.astype(jnp.bfloat16)
        return high, (v - high.astype(jnp.float32)).astype(jnp.bfloat16)

    def finish(c):
        for x in range(X):
            v = step2(u1a, rqa, c, HALO + x)
            disp_ref[c, x] = v
            rows[c, pl.ds(x, 8, stride=X), :] = v
        turned = turn_out(rows[c], outb.at[c])
        spread_out(outb.at[c], inb.at[c], c)
        inb[c, si] = outb[c, si]

    def joint(ref, j, low, high):
        return jnp.concatenate([
            ref[2, j, at:at + 8] + (c0 * ref[4, j, at:at + 8] + c1 * ref[5, j, at:at + 8])
            for at in range(low, high, 8)], axis=0)

    def finish_edges():
        for x in range(X):
            rows[6, pl.ds(x, 8, stride=X), :] = step2(u1b, rqb, 1, HALO + x)
        sides_y = rows[6].T
        zero = jnp.zeros((8, 128), jnp.float32)
        for j in range(ns):
            low, high = sides_y[zrows * j:zrows * j + 8], sides_y[zrows * j + 8:zrows * j + 16]
            tile = jnp.where(lane < 32, pltpu.roll(low, 16, 1),
                             jnp.where(lane < 64, pltpu.roll(pltpu.roll(low, 4, 0), 48, 1),
                                       jnp.where(lane < 96, pltpu.roll(high, 80, 1),
                                                 pltpu.roll(pltpu.roll(high, 4, 0), 112, 1))))
            before = pltpu.roll(joint(outb, j - 1, zrows - 8, zrows), 5, 0) if j else zero
            after = pltpu.roll(joint(outb, j + 1, 0, 8), 5, 0) if j + 1 < ns else zero
            outx[j] = jnp.where(sub == 4, before, jnp.where(sub == 5, after, tile))
        spread_out(outx.at[:, pl.ds(0, 6)], inx.at[:, pl.ds(0, 6)], 6)
        inx[si] = outx[si]

    finish(0)
    finish_edges()
    finish(1)
    for x in range(X):
        disp_ref[2, x] = step2(u1a, rqa, 2, HALO + x)
    fetched[7].wait()

    c1t, c3t = float(np.sqrt(0.5) * np.cos(np.pi / 8)), float(np.sqrt(0.5) * np.cos(3 * np.pi / 8))

    def cosine(v0, v1, v2, v3):
        s03, s12, d03, d12 = v0 + v3, v1 + v2, v0 - v3, v1 - v2
        return [0.5 * (s03 + s12), c1t * d03 + c3t * d12, 0.5 * (s03 - s12), c3t * d03 - c1t * d12]

    def encode(ch, fields):
        for b in range(Y // 4):
            for k, v in enumerate(cosine(*fields[4 * b:4 * b + 4])):
                work[ch, (4 * b + k) * zrows:(4 * b + k + 1) * zrows] = v
        parts = []
        for p in range(Y * zrows // 32):
            parts += cosine(*[work[ch, pl.ds(32 * p + n, 8, stride=4), :] for n in range(4)])
        high, low = halves(jnp.concatenate(parts, axis=0))
        done = jnp.dot(jnp.concatenate([high, low], axis=1), gt_ref[...], preferred_element_type=jnp.float32)
        done = done[:, 0:128] + done[:, 128:256]
        for p in range(Y * zrows // 32):
            for n in range(4):
                coef_ref[ch, pl.ds(32 * p + n, 8, stride=4), :] = done[(4 * p + n) * 8:(4 * p + n + 1) * 8]

    def arrived(c):
        landed(inb.at[c], trecv.at[c])
        return regroup([inb[c, j] for j in range(ns)])

    for at in (2, 4, 5):
        landed(inb.at[at], trecv.at[at])
    along = regroup([joint(inb, j, 0, zrows) for j in range(ns)])
    encode(2, along)
    landed(inb.at[3], trecv.at[3])
    for y, piece in enumerate(regroup([inb[3, j] for j in range(ns)])):
        scale[y] = piece
    field = arrived(0)
    encode(0, field)
    wide = lax.broadcasted_iota(jnp.int32, (zrows, 128), 1)
    encode(3, [scale[y] * (jnp.where(wide < 127, up_z(field[y]), 0.0) - jnp.where(wide > 0, down_z(field[y]), 0.0))
               for y in range(Y)])
    landed(inx.at[:, pl.ds(0, 6)], trecv.at[6])
    edges = regroup([inx[j] for j in range(ns)])
    stress = []
    for y in range(Y):
        low, high = along[y][0:8], along[y][8:16]
        ul, uh, dl, dh = pltpu.roll(low, 7, 0), pltpu.roll(high, 7, 0), pltpu.roll(low, 1, 0), pltpu.roll(high, 1, 0)
        first, last = sub == 0, sub == 7
        low = jnp.where(last, uh, ul) - jnp.where(first, pltpu.roll(edges[y], 4, 0), dl)
        high = jnp.where(last, pltpu.roll(edges[y], 2, 0), uh) - jnp.where(first, dl, dh)
        stress.append(scale[y] * jnp.concatenate([low, high], axis=0))
    encode(5, stress)
    field = arrived(1)
    encode(1, field)
    outside = []
    for side in range(2):
        quarter = [edges[2 * q + side] for q in range(4)]
        outside.append(jnp.concatenate([jnp.where(upper, quarter[q], pltpu.roll(quarter[q + 1], 4, 0)) for q in (0, 2)], axis=0))
    field = [outside[0]] + field + [outside[1]]
    encode(4, [scale[y] * (field[y + 2] - field[y]) for y in range(Y)])
    drain()
    block = inb.at[:, pl.ds(0, ns - 1)]
    pltpu.make_async_copy(block, block, tsend.at[0]).wait()
    landed(inx.at[:, pl.ds(0, 6)], tsend.at[1])


def store(disp_in, coef_in, disp_out, coef_out, sems):
    copies = [pltpu.make_async_copy(disp_in, disp_out, sems.at[0]), pltpu.make_async_copy(coef_in, coef_out, sems.at[1])]
    for copy in copies:
        copy.start()
    for copy in copies:
        copy.wait()


def fused(mesh, u_now, u_prev, force, stiffness, broken, flags):
    ns, ng = mesh.shape["slab"], mesh.shape["grp"]
    _, X, Y, Z = u_now.shape
    xe, pairs, half = X + 2 * HALO, X // 2 + HALO, X // 2
    zrows = Z // ns
    ez = jnp.asarray(np.kron(np.eye(Z // 4), np.ones((1, 4))), jnp.float32)
    gth, gtl = split_table(wavelet_table(X * ns).T)
    gt = jnp.asarray(np.block([[gth, gtl], [gth, np.zeros_like(gtl)]]), jnp.bfloat16)

    def vm(*shape):
        return pltpu.VMEM(shape, jnp.float32)

    def ext(n):
        return vm(n, xe, Y, Z)

    def stage(n):
        return vm(2, n, half, Y, Z)

    def land(n):
        return vm(2, n, pairs, Y, Z)

    dma = pltpu.SemaphoreType.DMA
    shapes = (u_now.shape, (6, Y * zrows, X * ns))
    operands = [pltpu.with_memory_space_constraint(v, pltpu.HBM)
                for v in (u_now, u_prev, force, stiffness, broken, flags, ez, gt)]
    results = pl.pallas_call(
        lambda *refs: kernel(ns, ng, *refs),
        name="lattice",
        out_shape=tuple(vm(*shape) for shape in shapes),
        in_specs=[pl.BlockSpec(memory_space=pltpu.MemorySpace.HBM)] * 8,
        out_specs=(pl.BlockSpec(memory_space=pltpu.VMEM),) * 2,
        scratch_shapes=[
            vm(*u_now.shape), vm(*u_now.shape), vm(*u_now.shape), vm(*stiffness.shape),
            pltpu.VMEM(broken.shape, broken.dtype), pltpu.VMEM(flags.shape, flags.dtype),
            vm(*ez.shape), pltpu.VMEM(gt.shape, gt.dtype), pltpu.SemaphoreType.DMA((6,)),
            ext(7), ext(7), stage(7), land(7),
            ext(3), ext(3), stage(3), land(3),
            ext(6), ext(6), stage(3), land(3), vm(2, 2, 3, 1, Y, Z), vm(2, 3, 2, Y, Z),
            ext(3), ext(3), ext(3), ext(3), vm(Y, zrows, X * ns), ext(3), ext(3), ext(5), ext(5),
            pltpu.SemaphoreType.REGULAR((3,)), vm(2, ns * ng, 1, 128), vm(7, Y * X, Z), vm(6, ns, zrows, 128), vm(6, ns, zrows, 128), vm(ns, 8, 128), vm(ns, 8, 128), vm(6, Y * zrows, X * ns),
            vm(max(9 * X, 13 * X // 2), Y, Z), dma((8,)), vm(2, 2, 2, Y, Z), vm(2, 2, 2, Y, Z), dma((4,)),
            dma((4,)), dma((4,)), dma((4,)), dma((4,)), dma((4,)), vm(2, 2, Y, Z), vm(2, 2, Y, Z), dma((4,)),
            dma, dma((2,)), dma((2,)), dma((7,)),
        ],
        compiler_params=pltpu.CompilerParams(collective_id=0, has_side_effects=True, vmem_limit_bytes=24 << 20),
    )(*operands)
    disp, coef = pl.pallas_call(
        store,
        name="store",
        out_shape=tuple(jax.ShapeDtypeStruct(shape, jnp.float32) for shape in shapes),
        in_specs=[pl.BlockSpec(memory_space=pltpu.VMEM)] * 2,
        out_specs=(pl.BlockSpec(memory_space=pltpu.MemorySpace.HBM),) * 2,
        scratch_shapes=[dma((2,))],
        compiler_params=pltpu.CompilerParams(vmem_limit_bytes=1 << 20),
    )(*[pltpu.with_memory_space_constraint(v, pltpu.VMEM) for v in results])
    return disp, coef.reshape(6, Y, zrows, X * ns)


def fits(mesh, shape):
    ns, ng = mesh.shape["slab"], mesh.shape["grp"]
    x, y, z = shape[1] // ns, shape[2] // ng, shape[3]
    return y == 8 and z == 128 and x * y == 128 and x * ns == 128 and z % (8 * ns) == 0


def entry(mesh, *args):
    ns, ng = mesh.shape["slab"], mesh.shape["grp"]
    _, x, y, z = args[0].shape
    if fits(mesh, (3, x * ns, y * ng, z)):
        return fused(mesh, *args)
    return body(*args)


def solution(mesh):
    return jax.shard_map(
        lambda *args: entry(mesh, *args),
        mesh=mesh,
        in_specs=(
            P(None, "slab", "grp", None),
            P(None, "slab", "grp", None),
            P(None, "slab", "grp", None),
            P("slab", "grp", None),
            P("slab", "grp", None),
            P("slab", "grp", None),
        ),
        out_specs=(P(None, "slab", "grp", None), P(None, "grp", "slab", None)),
        check_vma=False,
    )
```

```python
import jax
import jax.numpy as jnp
import numpy as np
from jax import lax
from jax.experimental import pallas as pl
from jax.experimental.pallas import tpu as pltpu
from jax.sharding import PartitionSpec as P

STEPS = 2
ITERS = 2
LEVELS = 3


SPRING_NORMAL = 1.0
SPRING_SHEAR = 0.4
MASS_TERM = 1.0
CRACK_CUT = 0.9


def with_halo(block, sides, width):
    for axis, dim in sides:
        count = lax.axis_size(axis)
        forward = [(i, i + 1) for i in range(count - 1)]
        backward = [(target, source) for source, target in forward]
        low = lax.ppermute(
            lax.slice_in_dim(block, block.shape[dim] - width, None, axis=dim), axis, forward
        )
        high = lax.ppermute(lax.slice_in_dim(block, 0, width, axis=dim), axis, backward)
        block = jnp.concatenate([low, block, high], axis=dim)
    return block


def cosine_table():
    freq = np.arange(4)[:, None]
    place = np.arange(4)[None, :]
    factor = np.where(freq == 0, 0.5, np.sqrt(0.5))
    return factor * np.cos(np.pi * (2 * place + 1) * freq / 8.0)


def block_table(count):
    return jnp.asarray(np.kron(np.eye(count // 4), cosine_table()), jnp.float32)


def spread(mask):
    values = mask.astype(jnp.float32)
    size_a, size_b, size_c = values.shape
    wide = jnp.broadcast_to(values[:, None, :, None, :, None], (size_a, 4, size_b, 4, size_c, 4))
    return wide.reshape(size_a * 4, size_b * 4, size_c * 4)


def sides(padded, axis_index):
    leading = padded.ndim - 3

    def cut(offset):
        index_list = [slice(None)] * leading + [slice(1, -1)] * 3
        length = padded.shape[leading + axis_index]
        index_list[leading + axis_index] = slice(1 + offset, length - 1 + offset)
        return padded[tuple(index_list)]

    return (cut(1), cut(-1))


def springs(field, weight, field_pad, weight_pad):
    result = MASS_TERM * field
    for axis_index in range(3):
        upper_v, lower_v = sides(field_pad, axis_index)
        upper_w, lower_w = sides(weight_pad, axis_index)
        k_upper = 0.5 * (weight + upper_w)
        k_lower = 0.5 * (weight + lower_w)
        change = k_upper * (field - upper_v) + k_lower * (field - lower_v)
        coupling = jnp.array(
            [SPRING_NORMAL if comp == axis_index else SPRING_SHEAR for comp in range(3)],
            jnp.float32,
        ).reshape(3, 1, 1, 1)
        result = result + coupling * change
    return result


def faces(field):
    padded = with_halo(field, (("slab", 1), ("grp", 2)), 1)
    return jnp.pad(padded, ((0, 0), (0, 0), (0, 0), (1, 1)))


def stresses(carry, field_pad):
    rows_out = []
    for axis_index in range(3):
        upper_v, lower_v = sides(field_pad, axis_index)
        rows_out.append(SPRING_NORMAL * carry * 0.5 * (upper_v[axis_index] - lower_v[axis_index]))
    return jnp.stack(rows_out)


def paired_sum(residual, image):
    return lax.psum((jnp.sum(residual * residual), jnp.sum(residual * image)), ("slab", "grp"))


def lift(signal):
    even = signal[..., 0::2]
    odd = signal[..., 1::2]
    detail = odd - 0.5 * (even + jnp.roll(even, -1, axis=-1))
    approx = even + 0.25 * (jnp.roll(detail, 1, axis=-1) + detail)
    return (approx, detail)


def wavelet(signal):
    pieces = []
    approx = signal
    for level_index in range(LEVELS):
        approx, detail = lift(approx)
        pieces.insert(0, detail)
    return jnp.concatenate([approx] + pieces, axis=-1)


def body(u_now, u_prev, force, stiffness, broken, flags):
    weight = stiffness * (1.0 - CRACK_CUT * spread(broken))
    carry = spread(flags) * weight
    weight_pad = with_halo(weight, (("slab", 0), ("grp", 1)), 1)
    weight_pad = jnp.pad(weight_pad, ((0, 0), (0, 0), (1, 1)))

    def operate(field):
        return springs(field, weight, faces(field), weight_pad)

    for step_index in range(STEPS):
        rhs = MASS_TERM * (2.0 * u_now - u_prev) + force
        guess = u_now
        residual = rhs - operate(guess)
        image = operate(residual)
        norm_now, product = paired_sum(residual, image)
        alpha = norm_now / product
        direction, along = (residual, image)
        for turn_index in range(ITERS):
            guess = guess + alpha * direction
            residual = residual - alpha * along
            if turn_index + 1 < ITERS:
                image = operate(residual)
                norm_next, product = paired_sum(residual, image)
                ratio = norm_next / norm_now
                alpha = norm_next / (product - ratio * norm_next / alpha)
                direction = residual + ratio * direction
                along = image + ratio * along
                norm_now = norm_next
        u_prev = u_now
        u_now = guess
    stress = stresses(carry, faces(u_now))
    fields = jnp.concatenate([u_now, stress], axis=0)
    table_x = block_table(fields.shape[1])
    table_y = block_table(fields.shape[2])
    table_z = block_table(fields.shape[3])
    blockc = jnp.einsum("ax,hxyz->hayz", table_x, fields, precision=lax.Precision.HIGHEST)
    blockc = jnp.einsum("by,hxyz->hxbz", table_y, blockc, precision=lax.Precision.HIGHEST)
    blockc = jnp.einsum("hxyz,cz->hxyc", blockc, table_z, precision=lax.Precision.HIGHEST)
    moved = jnp.transpose(blockc, (0, 2, 3, 1))
    shipped = lax.all_to_all(moved, "slab", split_axis=2, concat_axis=3, tiled=True)
    coeffs = wavelet(shipped)
    return (u_now, coeffs)


MESH = pl.DeviceIdType.MESH
HALO = 4
REACH = 3
SHEAR_REST = SPRING_NORMAL - SPRING_SHEAR
WIDE_R, WIDE_A, WIDE_C, WIDE_K = 20, 16, 16, 20


def wavelet_table(count):
    table = np.kron(np.eye(count // 4), cosine_table())
    pieces = []
    approx = table
    for level_index in range(LEVELS):
        even, odd = approx[0::2], approx[1::2]
        detail = odd - 0.5 * (even + np.roll(even, -1, axis=0))
        approx = even + 0.25 * (np.roll(detail, 1, axis=0) + detail)
        pieces.insert(0, detail)
    return np.concatenate([approx] + pieces, axis=0)


def split_table(table):
    high = table.astype(jnp.bfloat16).astype(np.float64)
    return high, (table - high).astype(jnp.bfloat16).astype(np.float64)


def sub_index():
    return lax.broadcasted_iota(jnp.int32, (8, 128), 0)


def lane_index():
    return lax.broadcasted_iota(jnp.int32, (8, 128), 1)


def up_y(a, b):
    ra, rb = pltpu.roll(a, 7, 0), pltpu.roll(b, 7, 0)
    last = sub_index() == 7
    return jnp.where(last, rb, ra), jnp.where(last, ra, rb)


def down_y(a, b):
    ra, rb = pltpu.roll(a, 1, 0), pltpu.roll(b, 1, 0)
    first = sub_index() == 0
    return jnp.where(first, rb, ra), jnp.where(first, ra, rb)


def up_z(v):
    return pltpu.roll(v, 127, 1)


def down_z(v):
    return pltpu.roll(v, 1, 1)


def total(v):
    return jnp.sum(jnp.sum(v, axis=0, keepdims=True), axis=1, keepdims=True)


def kernel(ns, ng, u_in, p_in, f_in, k_in, br_in, fl_in, ez_in, gt_in,
           disp_ref, coef_ref,
           u_ref, p_ref, f_ref, k_ref, br_ref, fl_ref, ez_ref, gt_ref, isem,
           e1a, e1b, s1, h1, e2a, e2b, s2, h2, rqa, rqb, s3, h3, k3, ends,
           u1a, u1b, sa, sb, scale, dga, dgb, kca, kcb, known, gath, rows, outb, inb, outx, inx, work,
           blanks, sends, ctake, cland, crecv, recv0, recv1, recv2, recv3, recvk, ftake, fland, recvf, asend, arecv, tsend, trecv):
    X, Y, Z = u_ref.shape[1:]
    si, gi = lax.axis_index("slab"), lax.axis_index("grp")
    me = si * ng + gi
    count = ns * ng
    barrier = pltpu.get_barrier_semaphore()

    def mirrored(place, mask, length):
        bit, result = 1, 0
        while bit < length:
            here = place // bit % 2
            result = result + bit * (1 - here if mask // bit % 2 else here)
            bit *= 2
        return result

    others = []
    for k in sorted(range(ns), key=lambda k: -min(k, ns - k)):
        for g in range(ng):
            if k or g:
                others.append((lax.rem(si + k, ns), lax.rem(gi + g, ng)))

    sub, lane = sub_index(), lane_index()
    upper = sub < 4

    steps = [(-1, 0), (1, 0), (0, -1), (0, 1), (-1, -1), (-1, 1), (1, -1), (1, 1)]

    def inside(ds, dg):
        ok = None
        if ds:
            ok = (si >= -ds) if ds < 0 else (si <= ns - 1 - ds)
        if dg:
            more = (gi >= -dg) if dg < 0 else (gi <= ng - 1 - dg)
            ok = more if ok is None else jnp.logical_and(ok, more)
        return ok

    def around(reach):
        return [(ds, dg) for ds in (-reach, 0, reach) for dg in (-reach, 0, reach)
                if (ds or dg) and abs(ds) < ns and abs(dg) < ng]

    def greet(sem, reach):
        for ds, dg in around(reach):
            @pl.when(inside(ds, dg))
            def _():
                pl.semaphore_signal(sem, inc=1, device_id=(si + ds, gi + dg), device_id_type=MESH)

    def meet(sem, reach):
        pl.semaphore_wait(sem, sum(jnp.where(inside(ds, dg), 1, 0) for ds, dg in around(reach)))

    rounds = []
    while (rounds[-1] * 2 if rounds else 1) < max(ns, ng):
        rounds.append(rounds[-1] * 2 if rounds else 1)

    greet(barrier, 1)
    fetched = []
    for at, (source, target) in enumerate((
        (br_in, br_ref), (fl_in, fl_ref), (ez_in, ez_ref), (k_in, k_ref), (u_in, u_ref), (p_in, p_ref),
        (f_in, f_ref), (gt_in, gt_ref),
    )):
        fetch = pltpu.make_async_copy(source, target, isem.at[min(at, 4) if at < 7 else 5])
        fetch.start()
        fetched.append(fetch)

    def copies(ea, dst_a, stage, land, recv, low=0, high=None, ways=4, reach=REACH, depth=None, ends=None):
        depth = reach if depth is None else depth
        half = X // 2
        edge = HALO // 2
        made = []
        chans = pl.ds(low, (ea.shape[0] if high is None else high) - low)
        for at, (ds, dg) in enumerate(steps[:ways]):
            if dg == 0:
                if ends is not None:
                    source = ends.at[0 if ds < 0 else 1]
                    target = dst_a.at[chans, pl.ds(HALO + X if ds < 0 else HALO - depth, reach)]
                elif ds < 0:
                    source = ea.at[chans, pl.ds(HALO + depth - reach, reach)]
                    target = dst_a.at[chans, pl.ds(HALO + X + depth - reach, reach)]
                else:
                    source = ea.at[chans, pl.ds(HALO + X - depth, reach)]
                    target = dst_a.at[chans, pl.ds(HALO - depth, reach)]
            else:
                side = 0 if dg < 0 else 1
                source, target = stage.at[side, chans], land.at[side, chans, pl.ds(edge, half)]
            made.append((ds, dg, pltpu.make_async_remote_copy(
                src_ref=source, dst_ref=target, send_sem=sends.at[at], recv_sem=recv.at[at ^ 1],
                device_id=(si + ds, gi + dg), device_id_type=MESH)))
        return made

    def begin(made):
        for ds, dg, copy in made:
            @pl.when(inside(ds, dg))
            def _():
                copy.start()

    def take(tiles, sem):
        block = blanks.at[pl.ds(0, tiles)]
        pltpu.make_async_copy(block, block, sem).wait()

    def finish_recv(recv, slab_tiles, grp_tiles):
        for at, (ds, dg) in enumerate(steps[:4]):
            @pl.when(inside(ds, dg))
            def _():
                if (slab_tiles if ds else grp_tiles):
                    take(slab_tiles if ds else grp_tiles, recv.at[at])

    def finish_send(slab_tiles, grp_tiles, corner_tiles):
        for at, (ds, dg) in enumerate(steps):
            @pl.when(inside(ds, dg))
            def _():
                take(corner_tiles if ds and dg else slab_tiles if ds else grp_tiles, sends.at[at])

    def blank(dst_a, land):
        zero_a = jnp.zeros((dst_a.shape[0], HALO) + dst_a.shape[2:], jnp.float32)
        half, edge = X // 2, HALO // 2
        zero_l = jnp.zeros((land.shape[1], edge, 8, 128), jnp.float32)

        @pl.when(si == 0)
        def _():
            dst_a[:, pl.ds(0, HALO)] = zero_a
            for side in range(2):
                land[side, :, pl.ds(0, edge)] = zero_l

        @pl.when(si == ns - 1)
        def _():
            dst_a[:, pl.ds(HALO + X, HALO)] = zero_a
            for side in range(2):
                land[side, :, pl.ds(edge + half, edge)] = zero_l

        for side, edge_here in ((0, gi == ng - 1), (1, gi == 0)):
            @pl.when(edge_here)
            def _(side=side):
                land[side] = jnp.zeros(land.shape[1:], jnp.float32)

    def pack(stage, ch, pair, even, odd):
        stage[0, ch, pair] = jnp.where(upper, even, pltpu.roll(odd, 4, 0))
        stage[1, ch, pair] = jnp.where(upper, pltpu.roll(even, 4, 0), odd)

    def unpack(land, ch, pair):
        high, low = land[0, ch, pair], land[1, ch, pair]
        return (jnp.where(upper, high, pltpu.roll(low, 4, 0)),
                jnp.where(upper, pltpu.roll(high, 4, 0), low))

    def spread_rows(mask):
        wide = jnp.dot(mask.astype(jnp.float32), ez_ref[...], preferred_element_type=jnp.float32)
        return jnp.where(upper, jnp.broadcast_to(wide[0:1], (8, 128)), jnp.broadcast_to(wide[1:2], (8, 128)))

    for at in range(4):
        fetched[at].wait()
    for bx in range(X // 4):
        cut = 1.0 - CRACK_CUT * spread_rows(br_ref[bx])
        flag = spread_rows(fl_ref[bx])
        for at in range(4):
            x = bx * 4 + at
            w = k_ref[x] * cut
            e1a[6, HALO + x] = w
            rows[3, pl.ds(x, 8, stride=X), :] = (SPRING_NORMAL * 0.5) * (flag * w)

    def own(i, _):
        for c in range(3):
            tiles = []
            for o in range(2):
                x = 2 * i + o
                u = u_ref[c, x]
                f = f_ref[c, x]
                rhs = MASS_TERM * (2.0 * u - p_ref[c, x]) + f
                e1a[c, HALO + x] = u
                e1a[3 + c, HALO + x] = rhs
                e2a[c, HALO + x] = f
                tiles.append((u, rhs, f))
            pack(s1, c, i, tiles[0][0], tiles[1][0])
            pack(s1, 3 + c, i, tiles[0][1], tiles[1][1])
            pack(s2, c, i, tiles[0][2], tiles[1][2])
        pack(s1, 6, i, e1a[6, HALO + 2 * i], e1a[6, HALO + 2 * i + 1])
        return 0

    take(9 * X, isem.at[4])
    lax.fori_loop(0, X // 2, own, 0)
    blank(e1a, h1)
    blank(e2a, h2)
    blank(rqa, h3)
    for ch in range(6):
        for x in (HALO - REACH, HALO + X + REACH - 1):
            rqb[ch, x] = jnp.zeros((8, 128), jnp.float32)

    zrows = Z // ns

    def turn_out(value, out):
        turned = value.T
        for j in range(ns):
            out[j] = turned[j * zrows:(j + 1) * zrows]

    def spread_out(source, target, at):
        for m in range(1, ns):
            to = lax.rem(si + m, ns)
            pltpu.make_async_remote_copy(
                src_ref=source.at[to], dst_ref=target.at[si], send_sem=tsend.at[0 if at < 6 else 1], recv_sem=trecv.at[at],
                device_id=(to, gi), device_id_type=MESH).start()

    def landed(target, sem):
        block = target.at[pl.ds(0, ns - 1)]
        pltpu.make_async_copy(block, block, sem).wait()

    def regroup(pieces):
        lanes = lax.broadcasted_iota(jnp.int32, pieces[0].shape, 1)
        gap = ns // 2
        while gap:
            keep = (lanes // (X * gap)) % 2 == 0
            mixed = list(pieces)
            for j in range(ns):
                if (j // gap) % 2 == 0:
                    a, b = pieces[j], pieces[j + gap]
                    mixed[j] = jnp.where(keep, a, pltpu.roll(b, X * gap, 1))
                    mixed[j + gap] = jnp.where(keep, pltpu.roll(a, 128 - X * gap, 1), b)
            pieces = mixed
            gap //= 2
        return pieces

    not_last, not_first = lane < 127, lane > 0

    def inner_ends():
        for end, x in ((0, HALO + 1), (1, HALO + X - 2)):
            w = e1a[6, x]
            along = (0.5 * (w + e1a[6, x + 1]), 0.5 * (w + e1a[6, x - 1]),
                     jnp.where(sub < 7, 0.5 * (w + pltpu.roll(w, 7, 0)), 0.0),
                     jnp.where(sub > 0, 0.5 * (w + pltpu.roll(w, 1, 0)), 0.0),
                     0.5 * (w + jnp.where(not_last, up_z(w), 0.0)), 0.5 * (w + jnp.where(not_first, down_z(w), 0.0)))
            for c in range(3):
                v = e1a[c, x]
                parts = (along[0] * (v - e1a[c, x + 1]) + along[1] * (v - e1a[c, x - 1]),
                         along[2] * (v - pltpu.roll(v, 7, 0)) + along[3] * (v - pltpu.roll(v, 1, 0)),
                         along[4] * (v - jnp.where(not_last, up_z(v), 0.0))
                         + along[5] * (v - jnp.where(not_first, down_z(v), 0.0)))
                image = MASS_TERM * v + (SPRING_SHEAR * (parts[0] + parts[1] + parts[2]) + SHEAR_REST * parts[c])
                ends[end, c, 1 - end] = e1a[3 + c, x] - image
                ends[end, c, end] = e1a[3 + c, x - 1 + 2 * end]

    def outer_residual(x):
        wa, wb = e1a[6, x], e1b[6, x]
        above = jnp.where(sub == 7, 0.5 * (wa + up_y(wa, wb)[0]), 0.0)
        below = jnp.where(sub == 0, 0.5 * (wa + down_y(wa, wb)[0]), 0.0)
        for c in range(3):
            a, b = e1a[c, x], e1b[c, x]
            change = above * (a - up_y(a, b)[0]) + below * (a - down_y(a, b)[0])
            rqa[c, x] = e1a[3 + c, x] - (SPRING_NORMAL if c == 1 else SPRING_SHEAR) * change
            rqb[c, x] = jnp.zeros((8, 128), jnp.float32)

    def tip_copies():
        made = []
        for at, (ds, dg) in enumerate(steps[4:]):
            side, end = (0 if dg < 0 else 1), (0 if ds < 0 else 1)
            made.append((ds, dg, pltpu.make_async_remote_copy(
                src_ref=ftake.at[side, end], dst_ref=fland.at[side, 1 - end],
                send_sem=sends.at[4 + at], recv_sem=recvf.at[3 - at],
                device_id=(si + ds, gi + dg), device_id_type=MESH)))
        return made

    def tip_unpack(made):
        for at, (ds, dg) in enumerate(steps[4:]):
            side, end = (0 if dg > 0 else 1), (1 if ds > 0 else 0)
            pair = HALO // 2 + X // 2 if ds > 0 else HALO // 2 - 1
            back = made[3 - at][2]

            @pl.when(inside(ds, dg))
            def _():
                back.wait_recv()
                tile = fland[side, end]
                for c in range(3):
                    h2[side, c, pair] = pltpu.roll(tile, 8 - 2 * c, 0) if c else tile

    def wedge_copies():
        made = []
        for at, (ds, dg) in enumerate(steps[4:]):
            side, end = (0 if dg < 0 else 1), (0 if ds < 0 else 1)
            pair = HALO // 2 + X // 2 if ds < 0 else HALO // 2 - 1
            made.append((ds, dg, pltpu.make_async_remote_copy(
                src_ref=k3.at[side, end], dst_ref=h3.at[side, :, pl.ds(pair, 1)],
                send_sem=sends.at[4 + at], recv_sem=recvk.at[3 - at],
                device_id=(si + ds, gi + dg), device_id_type=MESH)))
        return made

    def corner_copies():
        made = []
        for at, (ds, dg) in enumerate(steps[4:]):
            side, end = (0 if dg < 0 else 1), (0 if ds < 0 else 1)
            made.append((ds, dg, pltpu.make_async_remote_copy(
                src_ref=ctake.at[side, end], dst_ref=cland.at[side, 1 - end],
                send_sem=sends.at[4 + at], recv_sem=crecv.at[3 - at],
                device_id=(si + ds, gi + dg), device_id_type=MESH)))
        return made

    def corner_rows(side, end):
        dx1, dx2 = (0, 4) if end == 0 else (4, 0)
        dy1, dy2 = (0, 1) if side == 0 else (3, 2)
        return dx1 + dy1, dx1 + dy2, dx2 + dy1

    def any_row(places):
        found = sub == places[0]
        for place in places[1:]:
            found = jnp.logical_or(found, sub == place)
        return found

    corner_sets = ((0, 1, (3, 4)), (2, 6, (5,)))
    for side in range(2):
        for end in range(2):
            places = corner_rows(side, end)
            first_here, second_here = any_row(places), any_row([(v + 2) % 8 for v in places])
            for at, (ch_a, ch_b, right) in enumerate(corner_sets):
                tiles = [s1[side, ch, end * (X // 2 - 1)] for ch in (ch_a, ch_b) + right]
                tile = pltpu.roll(tiles[2], 5, 0)
                if len(right) == 2:
                    tile = jnp.where(sub == (places[0] + 5) % 8, tile, pltpu.roll(tiles[3], 3 if side else 7, 0))
                tile = jnp.where(first_here, tiles[0], jnp.where(second_here, pltpu.roll(tiles[1], 2, 0), tile))
                ctake[side, end, at] = tile
            near = [s2[side, c, end * (X // 2 - 1)] for c in range(3)]
            ftake[side, end] = jnp.where(sub == places[0], near[0], jnp.where(
                sub == (places[0] + 2) % 8, pltpu.roll(near[1], 2, 0), pltpu.roll(near[2], 4, 0)))

    def corner_unpack(made):
        for at, (ds, dg) in enumerate(steps[4:]):
            side, end = (0 if dg > 0 else 1), (1 if ds > 0 else 0)
            pair = HALO // 2 + X // 2 if ds > 0 else HALO // 2 - 1
            back = made[3 - at][2]

            @pl.when(inside(ds, dg))
            def _():
                back.wait_recv()
                for at, (ch_a, ch_b, right) in enumerate(corner_sets):
                    tile = cland[side, end, at]
                    h1[side, ch_a, pair] = tile
                    h1[side, ch_b, pair] = pltpu.roll(tile, 6, 0)
                    h1[side, right[0], pair] = pltpu.roll(tile, 3, 0)
                    if len(right) == 2:
                        h1[side, right[1], pair] = pltpu.roll(tile, 5 if side else 1, 0)

    corners = corner_copies()
    zeroth = copies(e1a, e1a, s1, h1, recv0, 6, 7, 4, REACH - 1)
    first = copies(e1a, e1a, s1, h1, recv1, 0, 3, 4, REACH - 1)
    rest = copies(e1a, e1a, s1, h1, recv1, 3, 6, 4, REACH - 1, None, ends)
    late = (copies(e1a, e1a, s1, h1, recv2, 0, 3, 2, 1, REACH),
            copies(e1a, e1a, s1, h1, recv2, 6, 7, 2, 1, REACH))
    second = copies(e2a, e2a, s2, h2, recv2, 0, 3, 4, REACH - 1)
    tips = tip_copies()
    third = copies(rqa, rqa, s3, h3, recv3, 0, 3, 4, 1, REACH)
    outer = copies(rqa, rqa, s3, h3, recv3, 3, 6, 2, REACH - 1, REACH)
    wedges = wedge_copies()
    meet(barrier, 1)
    begin(zeroth)
    begin(corners)
    begin(first)
    inner_ends()
    begin(rest)
    greet(known.at[0], rounds[0])
    turn_out(rows[3], outb.at[3])
    inb[3, si] = outb[3, si]
    for at in range(len(rounds) - 2):
        meet(known.at[at], rounds[at])
        greet(known.at[at + 1], rounds[at + 1])
    finish_recv(recv0, REACH - 1, X // 2)
    corner_unpack(corners)
    meet(known.at[len(rounds) - 2], rounds[-2])
    greet(known.at[len(rounds) - 1], rounds[-1])
    begin(second)
    begin(tips)
    for made in late:
        begin(made)

    def open0(i, _):
        e1b[6, 2 * i], e1b[6, 2 * i + 1] = unpack(h1, 6, i)
        return 0

    def open1(i, _):
        for ch in range(6):
            e1b[ch, 2 * i], e1b[ch, 2 * i + 1] = unpack(h1, ch, i)
        return 0

    lax.fori_loop(0, (X + 2 * HALO) // 2, open0, 0)

    def link(w, other):
        return jnp.where(jnp.minimum(w, other) > 0.0, (0.5 * SPRING_SHEAR) * (w + other), 0.0)


    def over_rows(low, high, width, body, carried=0):
        width = max(v for v in range(1, width + 1) if (high - low) % v == 0)

        def chunk(i, state):
            return body([low + i * width + o for o in range(width)], state)

        return lax.fori_loop(0, (high - low) // width, chunk, carried)

    def all_coefficients(rows_here, _):
        for x in rows_here:
            coefficients(x)
        return 0

    def coefficients(x):
        wa, wb = e1a[6, x], e1b[6, x]
        ya, yb = up_y(wa, wb)
        da, db = down_y(wa, wb)
        for w, wu, wd, yu, yd, dg, kc in (
            (wa, e1a[6, x + 1], e1a[6, x - 1], ya, da, dga, kca),
            (wb, e1b[6, x + 1], e1b[6, x - 1], yb, db, dgb, kcb),
        ):
            zu = jnp.where(not_last, up_z(w), 0.0)
            zd = jnp.where(not_first, down_z(w), 0.0)
            kc[0, x] = link(w, wu)
            kc[1, x] = link(w, yu)
            kc[2, x] = link(w, yd)
            kc[3, x] = link(w, zu)
            kc[4, x] = link(w, zd)
            sx = w + 0.5 * (wu + wd)
            sy = w + 0.5 * (yu + yd)
            sz = w + 0.5 * (zu + zd)
            every = MASS_TERM + SPRING_SHEAR * (sx + sy + sz)
            dg[0, x] = every + SHEAR_REST * sx
            dg[1, x] = every + SHEAR_REST * sy
            dg[2, x] = every + SHEAR_REST * sz

    def edge_link(x):
        kca[0, x] = link(e1a[6, x], e1a[6, x + 1])
        kcb[0, x] = link(e1b[6, x], e1b[6, x + 1])

    edge_link(HALO - 2)
    over_rows(HALO - 1, HALO + X + 1, WIDE_K, all_coefficients)
    finish_recv(recv1, 6 * (REACH - 1), 3 * X)
    lax.fori_loop(0, (X + 2 * HALO) // 2, open1, 0)

    def operate(x, va, vb, base, chosen=slice(0, 2)):
        result = []
        coef = [[kc[j, x] for j in range(5)] + [kc[0, x - 1]] for kc in (kca, kcb)]
        for c in range(3):
            a, b = va[base + c, x], vb[base + c, x]
            ua, ub = up_y(a, b)
            la, lb = down_y(a, b)
            pair = []
            halves = ((a, va, ua, la, coef[0], dga), (b, vb, ub, lb, coef[1], dgb))
            for v, ref, u, l, k, dg in halves[chosen]:
                parts = (
                    k[0] * ref[base + c, x + 1] + k[5] * ref[base + c, x - 1],
                    k[1] * u + k[2] * l,
                    k[3] * up_z(v) + k[4] * down_z(v),
                )
                shear = parts[(c + 1) % 3] + parts[(c + 2) % 3]
                pair.append(dg[c, x] * v - (shear + (SPRING_NORMAL / SPRING_SHEAR) * parts[c]))
            result.append(pair)
        return result

    only_a, only_b = slice(0, 1), slice(1, 2)

    def residual(rows_here, _):
        for x in rows_here:
            image = operate(x, e1a, e1b, 0)
            for c in range(3):
                rqa[c, x] = e1a[3 + c, x] - image[c][0]
                rqb[c, x] = e1b[3 + c, x] - image[c][1]
        return 0

    def solve(step, ship_halo=None):
        def put(x, image):
            for c in range(3):
                rqa[3 + c, x] = image[c][0]
                rqb[3 + c, x] = image[c][1]

        def apply(rows_here, sums):
            rr, rq = sums
            for x in rows_here:
                image = operate(x, rqa, rqb, 0)
                for c in range(3):
                    r = rqa[c, x]
                    rr, rq = rr + r * r, rq + r * image[c][0]
                put(x, image)
            return rr, rq

        zero = jnp.zeros((8, 128), jnp.float32)
        images = [operate(x, rqa, rqb, 0) for x in (HALO - 1, HALO + X)]
        put(HALO - 1, images[0])
        put(HALO + X, images[1])
        rr, rq = over_rows(HALO, HALO + X, WIDE_A, apply, (zero, zero))
        if ship_halo is not None:
            ship_halo()
        rr, rq = total(rr), total(rq)
        mu = jnp.where(rr > 0.0, rq / jnp.where(rr > 0.0, rr, 1.0), 0.0)

        def centred(rows_here, sums):
            ww, wr, mix, wt = sums
            for x in rows_here:
                image = operate(x, rqa, rqb, 3, only_a)
                for c in range(3):
                    r, q, s = rqa[c, x], rqa[3 + c, x], image[c][0]
                    if step == 0:
                        sa[c, x] = s
                    w, t = q - mu * r, s - mu * q
                    ww, wr, mix, wt = ww + w * w, wr + w * r, mix + (r * t + w * q), wt + w * t
            return ww, wr, mix, wt

        sums = over_rows(HALO, HALO + X, WIDE_C, centred, (zero,) * 4)
        ww, wr, mix, wt = [total(v) for v in sums]
        one = lax.broadcasted_iota(jnp.int32, (1, 128), 1)
        row = jnp.zeros((1, 128), jnp.float32)
        for at, value in enumerate((rr, rq, mu, ww, wr, mix, wt)):
            row = jnp.where(one == at, value, row)
        gath[step, me] = row

        if step == 0:
            meet(known.at[len(rounds) - 1], rounds[-1])
        for other in others:
            pltpu.make_async_remote_copy(
                src_ref=gath.at[step, me], dst_ref=gath.at[step, me], send_sem=asend, recv_sem=arecv.at[step],
                device_id=other, device_id_type=MESH).start()

    def collect(step):
        block = gath.at[step, pl.ds(0, count - 1)]
        pltpu.make_async_copy(block, block, arecv.at[step]).wait()
        table = gath[step].reshape(count, 128)
        rr, rq, mu, ww, wr, mix, wt = [table[:, at:at + 1] for at in range(7)]

        def down(v):
            return jnp.sum(v, axis=0, keepdims=True)

        norm = down(rr)
        alpha = norm / down(rq)
        rest = 1.0 - alpha * mu
        after = down(alpha * alpha * ww - 2.0 * alpha * rest * wr + rest * rest * rr)
        curved = down(rest * rest * rq - alpha * rest * mix + alpha * alpha * wt)
        ratio = after / norm
        beta = after / (curved - ratio * after / alpha)
        return jnp.broadcast_to(alpha + beta * (1.0 + ratio), (8, 128)), jnp.broadcast_to(-beta * alpha, (8, 128))

    def drain():
        block = gath.at[:, pl.ds(0, count - 1)]
        pltpu.make_async_copy(block, block, asend).wait()

    def joined(c, x, near, far):
        r, q = rqa[c, x], rqa[3 + c, x]
        return jnp.where(sub == 3, pltpu.roll(r, near, 0), jnp.where(sub == 4, pltpu.roll(r, far, 0), q))

    def split(c, x, tile, row, near, far):
        r = rqb[c, x]
        rqb[c, x] = jnp.where(sub == row, pltpu.roll(tile, near, 0), jnp.where(sub == 7 - row, pltpu.roll(tile, far, 0), r))
        rqb[3 + c, x] = tile

    def ship_halo():
        def pack3(i, _):
            x = HALO + 2 * i
            for c in range(3):
                pack(s3, c, i, joined(c, x, 1, 7), joined(c, x + 1, 1, 7))
            return 0

        lax.fori_loop(0, X // 2, pack3, 0)
        for end, x in ((0, HALO), (1, HALO + X - 2)):
            for c in range(3):
                even, odd = [joined(c, x + o, 2, 6) if o == end else joined(c, x + o, 3, 5) for o in range(2)]
                k3[0, end, c, 0] = jnp.where(upper, even, pltpu.roll(odd, 4, 0))
                k3[1, end, c, 0] = jnp.where(upper, pltpu.roll(even, 4, 0), odd)
        begin(third)
        begin(wedges)
        begin(outer)

    outer_residual(HALO - 2)
    outer_residual(HALO + X + 1)
    over_rows(HALO - 1, HALO + X + 1, WIDE_R, residual)
    solve(0, ship_halo)
    finish_recv(recv2, 3 * (REACH - 1) + 4, 3 * X // 2)
    tip_unpack(tips)
    edge_link(HALO - REACH)
    coefficients(HALO - 2)
    coefficients(HALO + X + 1)

    def open2(i, _):
        for ch in range(3):
            e2b[ch, 2 * i], e2b[ch, 2 * i + 1] = unpack(h2, ch, i)
        return 0

    lax.fori_loop(0, (X + 2 * HALO) // 2, open2, 0)
    finish_recv(recv3, 3 + 3 * (REACH - 1), 3 * X // 2)
    for at, (ds, dg) in enumerate(steps[4:]):
        back = wedges[3 - at][2]

        @pl.when(inside(ds, dg))
        def _():
            back.wait_recv()

    def open3(i, _):
        for c in range(3):
            even, odd = unpack(h3, c, i)
            split(c, 2 * i, even, 2, 7, 1)
            split(c, 2 * i + 1, odd, 2, 7, 1)
        return 0

    lax.fori_loop(HALO // 2, (HALO + X) // 2, open3, 0)
    for pair, one in ((HALO // 2 - 1, 1), ((HALO + X) // 2, 0)):
        for c in range(3):
            for o, tile in enumerate(unpack(h3, c, pair)):
                if o == one:
                    split(c, 2 * pair + o, tile, 1, 6, 2)
                else:
                    split(c, 2 * pair + o, tile, 0, 5, 3)
    finish_send(13 * (REACH - 1) + 7, 13 * X // 2, 6)
    spread_out(outb.at[3], inb.at[3], 3)
    for x in range(HALO - 1, HALO + X + 1):
        image = operate(x, rqa, rqb, 3, only_b)
        for c in range(3):
            sb[c, x] = image[c][0]
            e2a[c, x] = MASS_TERM * e1a[c, x] + e2a[c, x] - e1a[3 + c, x] + rqa[c, x]
            e2b[c, x] = MASS_TERM * e1b[c, x] + e2b[c, x] - e1b[3 + c, x] + rqb[c, x]
    for x in (HALO - 2, HALO + X + 1):
        image = operate(x, e1a, e1b, 0, only_a)
        for c in range(3):
            e2a[c, x] = MASS_TERM * e1a[c, x] + e2a[c, x] - image[c][0]
    for x in (HALO - 2, HALO - 1, HALO + X, HALO + X + 1):
        image = operate(x, rqa, rqb, 3, only_a)
        for c in range(3):
            sa[c, x] = image[c][0]
    c0, c1 = collect(0)

    def step1(x, base, rq, g, s, u1, comps):
        for c in range(3):
            r, q = rq[c, x], rq[3 + c, x]
            grown = c0 * r + c1 * q
            if c in comps:
                u1[c, x] = base[c, x] + grown
            rq[c, x] = g[c, x] + (2.0 * MASS_TERM) * grown - (c0 * q + c1 * s[c, x])

    for x in range(HALO - 2, HALO + X + 2):
        own_row = HALO <= x < HALO + X
        step1(x, e1a, rqa, e2a, sa, u1a, (0, 1, 2) if own_row else ())
        if HALO - 1 <= x <= HALO + X:
            step1(x, e1b, rqb, e2b, sb, u1b, (1,) if own_row else ())

    def early(at, ref, ch):
        for x in range(X):
            rows[at, pl.ds(x, 8, stride=X), :] = ref[ch, HALO + x]
        turn_out(rows[at], outb.at[at])
        spread_out(outb.at[at], inb.at[at], at)
        inb[at, si] = outb[at, si]

    solve(1)
    early(2, u1a, 2)
    early(4, rqa, 2)
    early(5, rqa, 5)
    c0, c1 = collect(1)

    def step2(ra, rb, c, x):
        return ra[c, x] + (c0 * rb[c, x] + c1 * rb[3 + c, x])

    def halves(v):
        high = v.astype(jnp.bfloat16)
        return high, (v - high.astype(jnp.float32)).astype(jnp.bfloat16)

    def finish(c):
        for x in range(X):
            v = step2(u1a, rqa, c, HALO + x)
            disp_ref[c, x] = v
            rows[c, pl.ds(x, 8, stride=X), :] = v
        turned = turn_out(rows[c], outb.at[c])
        spread_out(outb.at[c], inb.at[c], c)
        inb[c, si] = outb[c, si]

    def joint(ref, j, low, high):
        return jnp.concatenate([
            ref[2, j, at:at + 8] + (c0 * ref[4, j, at:at + 8] + c1 * ref[5, j, at:at + 8])
            for at in range(low, high, 8)], axis=0)

    def finish_edges():
        for x in range(X):
            rows[6, pl.ds(x, 8, stride=X), :] = step2(u1b, rqb, 1, HALO + x)
        sides_y = rows[6].T
        zero = jnp.zeros((8, 128), jnp.float32)
        for j in range(ns):
            low, high = sides_y[zrows * j:zrows * j + 8], sides_y[zrows * j + 8:zrows * j + 16]
            tile = jnp.where(lane < 32, pltpu.roll(low, 16, 1),
                             jnp.where(lane < 64, pltpu.roll(pltpu.roll(low, 4, 0), 48, 1),
                                       jnp.where(lane < 96, pltpu.roll(high, 80, 1),
                                                 pltpu.roll(pltpu.roll(high, 4, 0), 112, 1))))
            before = pltpu.roll(joint(outb, j - 1, zrows - 8, zrows), 5, 0) if j else zero
            after = pltpu.roll(joint(outb, j + 1, 0, 8), 5, 0) if j + 1 < ns else zero
            outx[j] = jnp.where(sub == 4, before, jnp.where(sub == 5, after, tile))
        spread_out(outx.at[:, pl.ds(0, 6)], inx.at[:, pl.ds(0, 6)], 6)
        inx[si] = outx[si]

    finish(0)
    finish_edges()
    finish(1)
    for x in range(X):
        disp_ref[2, x] = step2(u1a, rqa, 2, HALO + x)
    fetched[7].wait()

    c1t, c3t = float(np.sqrt(0.5) * np.cos(np.pi / 8)), float(np.sqrt(0.5) * np.cos(3 * np.pi / 8))

    def cosine(v0, v1, v2, v3):
        s03, s12, d03, d12 = v0 + v3, v1 + v2, v0 - v3, v1 - v2
        return [0.5 * (s03 + s12), c1t * d03 + c3t * d12, 0.5 * (s03 - s12), c3t * d03 - c1t * d12]

    def encode(ch, fields):
        for b in range(Y // 4):
            for k, v in enumerate(cosine(*fields[4 * b:4 * b + 4])):
                work[ch, (4 * b + k) * zrows:(4 * b + k + 1) * zrows] = v
        parts = []
        for p in range(Y * zrows // 32):
            parts += cosine(*[work[ch, pl.ds(32 * p + n, 8, stride=4), :] for n in range(4)])
        high, low = halves(jnp.concatenate(parts, axis=0))
        done = jnp.dot(jnp.concatenate([high, low], axis=1), gt_ref[...], preferred_element_type=jnp.float32)
        done = done[:, 0:128] + done[:, 128:256]
        for p in range(Y * zrows // 32):
            for n in range(4):
                coef_ref[ch, pl.ds(32 * p + n, 8, stride=4), :] = done[(4 * p + n) * 8:(4 * p + n + 1) * 8]

    def arrived(c):
        landed(inb.at[c], trecv.at[c])
        return regroup([inb[c, j] for j in range(ns)])

    for at in (2, 4, 5):
        landed(inb.at[at], trecv.at[at])
    along = regroup([joint(inb, j, 0, zrows) for j in range(ns)])
    encode(2, along)
    landed(inb.at[3], trecv.at[3])
    for y, piece in enumerate(regroup([inb[3, j] for j in range(ns)])):
        scale[y] = piece
    field = arrived(0)
    encode(0, field)
    wide = lax.broadcasted_iota(jnp.int32, (zrows, 128), 1)
    encode(3, [scale[y] * (jnp.where(wide < 127, up_z(field[y]), 0.0) - jnp.where(wide > 0, down_z(field[y]), 0.0))
               for y in range(Y)])
    landed(inx.at[:, pl.ds(0, 6)], trecv.at[6])
    edges = regroup([inx[j] for j in range(ns)])
    stress = []
    for y in range(Y):
        low, high = along[y][0:8], along[y][8:16]
        ul, uh, dl, dh = pltpu.roll(low, 7, 0), pltpu.roll(high, 7, 0), pltpu.roll(low, 1, 0), pltpu.roll(high, 1, 0)
        first, last = sub == 0, sub == 7
        low = jnp.where(last, uh, ul) - jnp.where(first, pltpu.roll(edges[y], 4, 0), dl)
        high = jnp.where(last, pltpu.roll(edges[y], 2, 0), uh) - jnp.where(first, dl, dh)
        stress.append(scale[y] * jnp.concatenate([low, high], axis=0))
    encode(5, stress)
    field = arrived(1)
    encode(1, field)
    outside = []
    for side in range(2):
        quarter = [edges[2 * q + side] for q in range(4)]
        outside.append(jnp.concatenate([jnp.where(upper, quarter[q], pltpu.roll(quarter[q + 1], 4, 0)) for q in (0, 2)], axis=0))
    field = [outside[0]] + field + [outside[1]]
    encode(4, [scale[y] * (field[y + 2] - field[y]) for y in range(Y)])
    drain()
    block = inb.at[:, pl.ds(0, ns - 1)]
    pltpu.make_async_copy(block, block, tsend.at[0]).wait()
    landed(inx.at[:, pl.ds(0, 6)], tsend.at[1])


def store(disp_in, coef_in, disp_out, coef_out, sems):
    copies = [pltpu.make_async_copy(disp_in, disp_out, sems.at[0]), pltpu.make_async_copy(coef_in, coef_out, sems.at[1])]
    for copy in copies:
        copy.start()
    for copy in copies:
        copy.wait()


def fused(mesh, u_now, u_prev, force, stiffness, broken, flags):
    ns, ng = mesh.shape["slab"], mesh.shape["grp"]
    _, X, Y, Z = u_now.shape
    xe, pairs, half = X + 2 * HALO, X // 2 + HALO, X // 2
    zrows = Z // ns
    ez = jnp.asarray(np.kron(np.eye(Z // 4), np.ones((1, 4))), jnp.float32)
    gth, gtl = split_table(wavelet_table(X * ns).T)
    gt = jnp.asarray(np.block([[gth, gtl], [gth, np.zeros_like(gtl)]]), jnp.bfloat16)

    def vm(*shape):
        return pltpu.VMEM(shape, jnp.float32)

    def ext(n):
        return vm(n, xe, Y, Z)

    def stage(n):
        return vm(2, n, half, Y, Z)

    def land(n):
        return vm(2, n, pairs, Y, Z)

    dma = pltpu.SemaphoreType.DMA
    shapes = (u_now.shape, (6, Y * zrows, X * ns))
    operands = [pltpu.with_memory_space_constraint(v, pltpu.HBM)
                for v in (u_now, u_prev, force, stiffness, broken, flags, ez, gt)]
    results = pl.pallas_call(
        lambda *refs: kernel(ns, ng, *refs),
        name="lattice",
        out_shape=tuple(vm(*shape) for shape in shapes),
        in_specs=[pl.BlockSpec(memory_space=pltpu.MemorySpace.HBM)] * 8,
        out_specs=(pl.BlockSpec(memory_space=pltpu.VMEM),) * 2,
        scratch_shapes=[
            vm(*u_now.shape), vm(*u_now.shape), vm(*u_now.shape), vm(*stiffness.shape),
            pltpu.VMEM(broken.shape, broken.dtype), pltpu.VMEM(flags.shape, flags.dtype),
            vm(*ez.shape), pltpu.VMEM(gt.shape, gt.dtype), pltpu.SemaphoreType.DMA((6,)),
            ext(7), ext(7), stage(7), land(7),
            ext(3), ext(3), stage(3), land(3),
            ext(6), ext(6), stage(3), land(3), vm(2, 2, 3, 1, Y, Z), vm(2, 3, 2, Y, Z),
            ext(3), ext(3), ext(3), ext(3), vm(Y, zrows, X * ns), ext(3), ext(3), ext(5), ext(5),
            pltpu.SemaphoreType.REGULAR((3,)), vm(2, ns * ng, 1, 128), vm(7, Y * X, Z), vm(6, ns, zrows, 128), vm(6, ns, zrows, 128), vm(ns, 8, 128), vm(ns, 8, 128), vm(6, Y * zrows, X * ns),
            vm(max(9 * X, 13 * X // 2), Y, Z), dma((8,)), vm(2, 2, 2, Y, Z), vm(2, 2, 2, Y, Z), dma((4,)),
            dma((4,)), dma((4,)), dma((4,)), dma((4,)), dma((4,)), vm(2, 2, Y, Z), vm(2, 2, Y, Z), dma((4,)),
            dma, dma((2,)), dma((2,)), dma((7,)),
        ],
        compiler_params=pltpu.CompilerParams(collective_id=0, has_side_effects=True, vmem_limit_bytes=24 << 20),
    )(*operands)
    disp, coef = pl.pallas_call(
        store,
        name="store",
        out_shape=tuple(jax.ShapeDtypeStruct(shape, jnp.float32) for shape in shapes),
        in_specs=[pl.BlockSpec(memory_space=pltpu.VMEM)] * 2,
        out_specs=(pl.BlockSpec(memory_space=pltpu.MemorySpace.HBM),) * 2,
        scratch_shapes=[dma((2,))],
        compiler_params=pltpu.CompilerParams(vmem_limit_bytes=1 << 20),
    )(*[pltpu.with_memory_space_constraint(v, pltpu.VMEM) for v in results])
    return disp, coef.reshape(6, Y, zrows, X * ns)


def fits(mesh, shape):
    ns, ng = mesh.shape["slab"], mesh.shape["grp"]
    x, y, z = shape[1] // ns, shape[2] // ng, shape[3]
    return y == 8 and z == 128 and x * y == 128 and x * ns == 128 and z % (8 * ns) == 0


def entry(mesh, *args):
    ns, ng = mesh.shape["slab"], mesh.shape["grp"]
    _, x, y, z = args[0].shape
    if fits(mesh, (3, x * ns, y * ng, z)):
        return fused(mesh, *args)
    return body(*args)


def solution(mesh):
    return jax.shard_map(
        lambda *args: entry(mesh, *args),
        mesh=mesh,
        in_specs=(
            P(None, "slab", "grp", None),
            P(None, "slab", "grp", None),
            P(None, "slab", "grp", None),
            P("slab", "grp", None),
            P("slab", "grp", None),
            P("slab", "grp", None),
        ),
        out_specs=(P(None, "slab", "grp", None), P(None, "grp", "slab", None)),
        check_vma=False,
    )
```

```python
import jax
import jax.numpy as jnp
import numpy as np
from jax import lax
from jax.experimental import pallas as pl
from jax.experimental.pallas import tpu as pltpu
from jax.sharding import PartitionSpec as P

STEPS = 2
ITERS = 2
LEVELS = 3


SPRING_NORMAL = 1.0
SPRING_SHEAR = 0.4
MASS_TERM = 1.0
CRACK_CUT = 0.9


def with_halo(block, sides, width):
    for axis, dim in sides:
        count = lax.axis_size(axis)
        forward = [(i, i + 1) for i in range(count - 1)]
        backward = [(target, source) for source, target in forward]
        low = lax.ppermute(
            lax.slice_in_dim(block, block.shape[dim] - width, None, axis=dim), axis, forward
        )
        high = lax.ppermute(lax.slice_in_dim(block, 0, width, axis=dim), axis, backward)
        block = jnp.concatenate([low, block, high], axis=dim)
    return block


def cosine_table():
    freq = np.arange(4)[:, None]
    place = np.arange(4)[None, :]
    factor = np.where(freq == 0, 0.5, np.sqrt(0.5))
    return factor * np.cos(np.pi * (2 * place + 1) * freq / 8.0)


def block_table(count):
    return jnp.asarray(np.kron(np.eye(count // 4), cosine_table()), jnp.float32)


def spread(mask):
    values = mask.astype(jnp.float32)
    size_a, size_b, size_c = values.shape
    wide = jnp.broadcast_to(values[:, None, :, None, :, None], (size_a, 4, size_b, 4, size_c, 4))
    return wide.reshape(size_a * 4, size_b * 4, size_c * 4)


def sides(padded, axis_index):
    leading = padded.ndim - 3

    def cut(offset):
        index_list = [slice(None)] * leading + [slice(1, -1)] * 3
        length = padded.shape[leading + axis_index]
        index_list[leading + axis_index] = slice(1 + offset, length - 1 + offset)
        return padded[tuple(index_list)]

    return (cut(1), cut(-1))


def springs(field, weight, field_pad, weight_pad):
    result = MASS_TERM * field
    for axis_index in range(3):
        upper_v, lower_v = sides(field_pad, axis_index)
        upper_w, lower_w = sides(weight_pad, axis_index)
        k_upper = 0.5 * (weight + upper_w)
        k_lower = 0.5 * (weight + lower_w)
        change = k_upper * (field - upper_v) + k_lower * (field - lower_v)
        coupling = jnp.array(
            [SPRING_NORMAL if comp == axis_index else SPRING_SHEAR for comp in range(3)],
            jnp.float32,
        ).reshape(3, 1, 1, 1)
        result = result + coupling * change
    return result


def faces(field):
    padded = with_halo(field, (("slab", 1), ("grp", 2)), 1)
    return jnp.pad(padded, ((0, 0), (0, 0), (0, 0), (1, 1)))


def stresses(carry, field_pad):
    rows_out = []
    for axis_index in range(3):
        upper_v, lower_v = sides(field_pad, axis_index)
        rows_out.append(SPRING_NORMAL * carry * 0.5 * (upper_v[axis_index] - lower_v[axis_index]))
    return jnp.stack(rows_out)


def paired_sum(residual, image):
    return lax.psum((jnp.sum(residual * residual), jnp.sum(residual * image)), ("slab", "grp"))


def lift(signal):
    even = signal[..., 0::2]
    odd = signal[..., 1::2]
    detail = odd - 0.5 * (even + jnp.roll(even, -1, axis=-1))
    approx = even + 0.25 * (jnp.roll(detail, 1, axis=-1) + detail)
    return (approx, detail)


def wavelet(signal):
    pieces = []
    approx = signal
    for level_index in range(LEVELS):
        approx, detail = lift(approx)
        pieces.insert(0, detail)
    return jnp.concatenate([approx] + pieces, axis=-1)


def body(u_now, u_prev, force, stiffness, broken, flags):
    weight = stiffness * (1.0 - CRACK_CUT * spread(broken))
    carry = spread(flags) * weight
    weight_pad = with_halo(weight, (("slab", 0), ("grp", 1)), 1)
    weight_pad = jnp.pad(weight_pad, ((0, 0), (0, 0), (1, 1)))

    def operate(field):
        return springs(field, weight, faces(field), weight_pad)

    for step_index in range(STEPS):
        rhs = MASS_TERM * (2.0 * u_now - u_prev) + force
        guess = u_now
        residual = rhs - operate(guess)
        image = operate(residual)
        norm_now, product = paired_sum(residual, image)
        alpha = norm_now / product
        direction, along = (residual, image)
        for turn_index in range(ITERS):
            guess = guess + alpha * direction
            residual = residual - alpha * along
            if turn_index + 1 < ITERS:
                image = operate(residual)
                norm_next, product = paired_sum(residual, image)
                ratio = norm_next / norm_now
                alpha = norm_next / (product - ratio * norm_next / alpha)
                direction = residual + ratio * direction
                along = image + ratio * along
                norm_now = norm_next
        u_prev = u_now
        u_now = guess
    stress = stresses(carry, faces(u_now))
    fields = jnp.concatenate([u_now, stress], axis=0)
    table_x = block_table(fields.shape[1])
    table_y = block_table(fields.shape[2])
    table_z = block_table(fields.shape[3])
    blockc = jnp.einsum("ax,hxyz->hayz", table_x, fields, precision=lax.Precision.HIGHEST)
    blockc = jnp.einsum("by,hxyz->hxbz", table_y, blockc, precision=lax.Precision.HIGHEST)
    blockc = jnp.einsum("hxyz,cz->hxyc", blockc, table_z, precision=lax.Precision.HIGHEST)
    moved = jnp.transpose(blockc, (0, 2, 3, 1))
    shipped = lax.all_to_all(moved, "slab", split_axis=2, concat_axis=3, tiled=True)
    coeffs = wavelet(shipped)
    return (u_now, coeffs)


MESH = pl.DeviceIdType.MESH
HALO = 4
REACH = 3
SHEAR_REST = SPRING_NORMAL - SPRING_SHEAR
WIDE_R, WIDE_A, WIDE_C, WIDE_K = 20, 16, 16, 20


def wavelet_table(count):
    table = np.kron(np.eye(count // 4), cosine_table())
    pieces = []
    approx = table
    for level_index in range(LEVELS):
        even, odd = approx[0::2], approx[1::2]
        detail = odd - 0.5 * (even + np.roll(even, -1, axis=0))
        approx = even + 0.25 * (np.roll(detail, 1, axis=0) + detail)
        pieces.insert(0, detail)
    return np.concatenate([approx] + pieces, axis=0)


def split_table(table):
    high = table.astype(jnp.bfloat16).astype(np.float64)
    return high, (table - high).astype(jnp.bfloat16).astype(np.float64)


def sub_index():
    return lax.broadcasted_iota(jnp.int32, (8, 128), 0)


def lane_index():
    return lax.broadcasted_iota(jnp.int32, (8, 128), 1)


def up_y(a, b):
    ra, rb = pltpu.roll(a, 7, 0), pltpu.roll(b, 7, 0)
    last = sub_index() == 7
    return jnp.where(last, rb, ra), jnp.where(last, ra, rb)


def down_y(a, b):
    ra, rb = pltpu.roll(a, 1, 0), pltpu.roll(b, 1, 0)
    first = sub_index() == 0
    return jnp.where(first, rb, ra), jnp.where(first, ra, rb)


def up_z(v):
    return pltpu.roll(v, 127, 1)


def down_z(v):
    return pltpu.roll(v, 1, 1)


def total(v):
    return jnp.sum(jnp.sum(v, axis=0, keepdims=True), axis=1, keepdims=True)


def kernel(ns, ng, u_in, p_in, f_in, k_in, br_in, fl_in, ez_in, gt_in,
           disp_ref, coef_ref,
           u_ref, p_ref, f_ref, k_ref, br_ref, fl_ref, ez_ref, gt_ref, isem,
           e1a, e1b, s1, h1, e2a, e2b, s2, h2, rqa, rqb, s3, h3, k3, ends,
           u1a, u1b, sa, sb, scale, dga, dgb, kca, kcb, known, gath, rows, outb, inb, outx, inx, work,
           blanks, sends, ctake, cland, crecv, recv0, recv1, recv2, recv3, recvk, ftake, fland, recvf, asend, arecv, tsend, trecv):
    X, Y, Z = u_ref.shape[1:]
    si, gi = lax.axis_index("slab"), lax.axis_index("grp")
    me = si * ng + gi
    count = ns * ng
    barrier = pltpu.get_barrier_semaphore()

    def mirrored(place, mask, length):
        bit, result = 1, 0
        while bit < length:
            here = place // bit % 2
            result = result + bit * (1 - here if mask // bit % 2 else here)
            bit *= 2
        return result

    others = []
    for k in sorted(range(ns), key=lambda k: -min(k, ns - k)):
        for g in range(ng):
            if k or g:
                others.append((lax.rem(si + k, ns), lax.rem(gi + g, ng)))

    sub, lane = sub_index(), lane_index()
    upper = sub < 4

    steps = [(-1, 0), (1, 0), (0, -1), (0, 1), (-1, -1), (-1, 1), (1, -1), (1, 1)]

    def inside(ds, dg):
        ok = None
        if ds:
            ok = (si >= -ds) if ds < 0 else (si <= ns - 1 - ds)
        if dg:
            more = (gi >= -dg) if dg < 0 else (gi <= ng - 1 - dg)
            ok = more if ok is None else jnp.logical_and(ok, more)
        return ok

    def around(reach):
        return [(ds, dg) for ds in (-reach, 0, reach) for dg in (-reach, 0, reach)
                if (ds or dg) and abs(ds) < ns and abs(dg) < ng]

    def greet(sem, reach):
        for ds, dg in around(reach):
            @pl.when(inside(ds, dg))
            def _():
                pl.semaphore_signal(sem, inc=1, device_id=(si + ds, gi + dg), device_id_type=MESH)

    def meet(sem, reach):
        pl.semaphore_wait(sem, sum(jnp.where(inside(ds, dg), 1, 0) for ds, dg in around(reach)))

    rounds = []
    while (rounds[-1] * 2 if rounds else 1) < max(ns, ng):
        rounds.append(rounds[-1] * 2 if rounds else 1)

    greet(barrier, 1)
    fetched = []
    for at, (source, target) in enumerate((
        (br_in, br_ref), (fl_in, fl_ref), (ez_in, ez_ref), (k_in, k_ref), (u_in, u_ref), (p_in, p_ref),
        (f_in, f_ref), (gt_in, gt_ref),
    )):
        fetch = pltpu.make_async_copy(source, target, isem.at[min(at, 4) if at < 7 else 5])
        fetch.start()
        fetched.append(fetch)

    def copies(ea, dst_a, stage, land, recv, low=0, high=None, ways=4, reach=REACH, depth=None, ends=None):
        depth = reach if depth is None else depth
        half = X // 2
        edge = HALO // 2
        made = []
        chans = pl.ds(low, (ea.shape[0] if high is None else high) - low)
        for at, (ds, dg) in enumerate(steps[:ways]):
            if dg == 0:
                if ends is not None:
                    source = ends.at[0 if ds < 0 else 1]
                    target = dst_a.at[chans, pl.ds(HALO + X if ds < 0 else HALO - depth, reach)]
                elif ds < 0:
                    source = ea.at[chans, pl.ds(HALO + depth - reach, reach)]
                    target = dst_a.at[chans, pl.ds(HALO + X + depth - reach, reach)]
                else:
                    source = ea.at[chans, pl.ds(HALO + X - depth, reach)]
                    target = dst_a.at[chans, pl.ds(HALO - depth, reach)]
            else:
                side = 0 if dg < 0 else 1
                source, target = stage.at[side, chans], land.at[side, chans, pl.ds(edge, half)]
            made.append((ds, dg, pltpu.make_async_remote_copy(
                src_ref=source, dst_ref=target, send_sem=sends.at[at], recv_sem=recv.at[at ^ 1],
                device_id=(si + ds, gi + dg), device_id_type=MESH)))
        return made

    def begin(made):
        for ds, dg, copy in made:
            @pl.when(inside(ds, dg))
            def _():
                copy.start()

    def take(tiles, sem):
        block = blanks.at[pl.ds(0, tiles)]
        pltpu.make_async_copy(block, block, sem).wait()

    def finish_recv(recv, slab_tiles, grp_tiles):
        for at, (ds, dg) in enumerate(steps[:4]):
            @pl.when(inside(ds, dg))
            def _():
                if (slab_tiles if ds else grp_tiles):
                    take(slab_tiles if ds else grp_tiles, recv.at[at])

    def finish_send(slab_tiles, grp_tiles, corner_tiles):
        for at, (ds, dg) in enumerate(steps):
            @pl.when(inside(ds, dg))
            def _():
                take(corner_tiles if ds and dg else slab_tiles if ds else grp_tiles, sends.at[at])

    def blank(dst_a, land):
        zero_a = jnp.zeros((dst_a.shape[0], HALO) + dst_a.shape[2:], jnp.float32)
        half, edge = X // 2, HALO // 2
        zero_l = jnp.zeros((land.shape[1], edge, 8, 128), jnp.float32)

        @pl.when(si == 0)
        def _():
            dst_a[:, pl.ds(0, HALO)] = zero_a
            for side in range(2):
                land[side, :, pl.ds(0, edge)] = zero_l

        @pl.when(si == ns - 1)
        def _():
            dst_a[:, pl.ds(HALO + X, HALO)] = zero_a
            for side in range(2):
                land[side, :, pl.ds(edge + half, edge)] = zero_l

        for side, edge_here in ((0, gi == ng - 1), (1, gi == 0)):
            @pl.when(edge_here)
            def _(side=side):
                land[side] = jnp.zeros(land.shape[1:], jnp.float32)

    def pack(stage, ch, pair, even, odd):
        stage[0, ch, pair] = jnp.where(upper, even, pltpu.roll(odd, 4, 0))
        stage[1, ch, pair] = jnp.where(upper, pltpu.roll(even, 4, 0), odd)

    def unpack(land, ch, pair):
        high, low = land[0, ch, pair], land[1, ch, pair]
        return (jnp.where(upper, high, pltpu.roll(low, 4, 0)),
                jnp.where(upper, pltpu.roll(high, 4, 0), low))

    def spread_rows(mask):
        wide = jnp.dot(mask.astype(jnp.float32), ez_ref[...], preferred_element_type=jnp.float32)
        return jnp.where(upper, jnp.broadcast_to(wide[0:1], (8, 128)), jnp.broadcast_to(wide[1:2], (8, 128)))

    for at in range(4):
        fetched[at].wait()
    for bx in range(X // 4):
        cut = 1.0 - CRACK_CUT * spread_rows(br_ref[bx])
        flag = spread_rows(fl_ref[bx])
        for at in range(4):
            x = bx * 4 + at
            w = k_ref[x] * cut
            e1a[6, HALO + x] = w
            rows[3, pl.ds(x, 8, stride=X), :] = (SPRING_NORMAL * 0.5) * (flag * w)

    def own(i, _):
        for c in range(3):
            tiles = []
            for o in range(2):
                x = 2 * i + o
                u = u_ref[c, x]
                f = f_ref[c, x]
                rhs = MASS_TERM * (2.0 * u - p_ref[c, x]) + f
                e1a[c, HALO + x] = u
                e1a[3 + c, HALO + x] = rhs
                e2a[c, HALO + x] = f
                tiles.append((u, rhs, f))
            pack(s1, c, i, tiles[0][0], tiles[1][0])
            pack(s1, 3 + c, i, tiles[0][1], tiles[1][1])
            pack(s2, c, i, tiles[0][2], tiles[1][2])
        pack(s1, 6, i, e1a[6, HALO + 2 * i], e1a[6, HALO + 2 * i + 1])
        return 0

    take(9 * X, isem.at[4])
    lax.fori_loop(0, X // 2, own, 0)
    blank(e1a, h1)
    blank(e2a, h2)
    blank(rqa, h3)
    for ch in range(6):
        for x in (HALO - REACH, HALO + X + REACH - 1):
            rqb[ch, x] = jnp.zeros((8, 128), jnp.float32)

    zrows = Z // ns

    def turn_out(value, out):
        turned = value.T
        for j in range(ns):
            out[j] = turned[j * zrows:(j + 1) * zrows]

    def spread_out(source, target, at):
        for m in range(1, ns):
            to = lax.rem(si + m, ns)
            pltpu.make_async_remote_copy(
                src_ref=source.at[to], dst_ref=target.at[si], send_sem=tsend.at[0 if at < 6 else 1], recv_sem=trecv.at[at],
                device_id=(to, gi), device_id_type=MESH).start()

    def landed(target, sem):
        block = target.at[pl.ds(0, ns - 1)]
        pltpu.make_async_copy(block, block, sem).wait()

    def regroup(pieces):
        lanes = lax.broadcasted_iota(jnp.int32, pieces[0].shape, 1)
        gap = ns // 2
        while gap:
            keep = (lanes // (X * gap)) % 2 == 0
            mixed = list(pieces)
            for j in range(ns):
                if (j // gap) % 2 == 0:
                    a, b = pieces[j], pieces[j + gap]
                    mixed[j] = jnp.where(keep, a, pltpu.roll(b, X * gap, 1))
                    mixed[j + gap] = jnp.where(keep, pltpu.roll(a, 128 - X * gap, 1), b)
            pieces = mixed
            gap //= 2
        return pieces

    not_last, not_first = lane < 127, lane > 0

    def inner_ends():
        for end, x in ((0, HALO + 1), (1, HALO + X - 2)):
            w = e1a[6, x]
            along = (0.5 * (w + e1a[6, x + 1]), 0.5 * (w + e1a[6, x - 1]),
                     jnp.where(sub < 7, 0.5 * (w + pltpu.roll(w, 7, 0)), 0.0),
                     jnp.where(sub > 0, 0.5 * (w + pltpu.roll(w, 1, 0)), 0.0),
                     0.5 * (w + jnp.where(not_last, up_z(w), 0.0)), 0.5 * (w + jnp.where(not_first, down_z(w), 0.0)))
            for c in range(3):
                v = e1a[c, x]
                parts = (along[0] * (v - e1a[c, x + 1]) + along[1] * (v - e1a[c, x - 1]),
                         along[2] * (v - pltpu.roll(v, 7, 0)) + along[3] * (v - pltpu.roll(v, 1, 0)),
                         along[4] * (v - jnp.where(not_last, up_z(v), 0.0))
                         + along[5] * (v - jnp.where(not_first, down_z(v), 0.0)))
                image = MASS_TERM * v + (SPRING_SHEAR * (parts[0] + parts[1] + parts[2]) + SHEAR_REST * parts[c])
                ends[end, c, 1 - end] = e1a[3 + c, x] - image
                ends[end, c, end] = e1a[3 + c, x - 1 + 2 * end]

    def outer_residual(x):
        wa, wb = e1a[6, x], e1b[6, x]
        above = jnp.where(sub == 7, 0.5 * (wa + up_y(wa, wb)[0]), 0.0)
        below = jnp.where(sub == 0, 0.5 * (wa + down_y(wa, wb)[0]), 0.0)
        for c in range(3):
            a, b = e1a[c, x], e1b[c, x]
            change = above * (a - up_y(a, b)[0]) + below * (a - down_y(a, b)[0])
            rqa[c, x] = e1a[3 + c, x] - (SPRING_NORMAL if c == 1 else SPRING_SHEAR) * change
            rqb[c, x] = jnp.zeros((8, 128), jnp.float32)

    def tip_copies():
        made = []
        for at, (ds, dg) in enumerate(steps[4:]):
            side, end = (0 if dg < 0 else 1), (0 if ds < 0 else 1)
            made.append((ds, dg, pltpu.make_async_remote_copy(
                src_ref=ftake.at[side, end], dst_ref=fland.at[side, 1 - end],
                send_sem=sends.at[4 + at], recv_sem=recvf.at[3 - at],
                device_id=(si + ds, gi + dg), device_id_type=MESH)))
        return made

    def tip_unpack(made):
        for at, (ds, dg) in enumerate(steps[4:]):
            side, end = (0 if dg > 0 else 1), (1 if ds > 0 else 0)
            pair = HALO // 2 + X // 2 if ds > 0 else HALO // 2 - 1
            back = made[3 - at][2]

            @pl.when(inside(ds, dg))
            def _():
                back.wait_recv()
                tile = fland[side, end]
                for c in range(3):
                    h2[side, c, pair] = pltpu.roll(tile, 8 - 2 * c, 0) if c else tile

    def wedge_copies():
        made = []
        for at, (ds, dg) in enumerate(steps[4:]):
            side, end = (0 if dg < 0 else 1), (0 if ds < 0 else 1)
            pair = HALO // 2 + X // 2 if ds < 0 else HALO // 2 - 1
            made.append((ds, dg, pltpu.make_async_remote_copy(
                src_ref=k3.at[side, end], dst_ref=h3.at[side, :, pl.ds(pair, 1)],
                send_sem=sends.at[4 + at], recv_sem=recvk.at[3 - at],
                device_id=(si + ds, gi + dg), device_id_type=MESH)))
        return made

    def corner_copies():
        made = []
        for at, (ds, dg) in enumerate(steps[4:]):
            side, end = (0 if dg < 0 else 1), (0 if ds < 0 else 1)
            made.append((ds, dg, pltpu.make_async_remote_copy(
                src_ref=ctake.at[side, end], dst_ref=cland.at[side, 1 - end],
                send_sem=sends.at[4 + at], recv_sem=crecv.at[3 - at],
                device_id=(si + ds, gi + dg), device_id_type=MESH)))
        return made

    def corner_rows(side, end):
        dx1, dx2 = (0, 4) if end == 0 else (4, 0)
        dy1, dy2 = (0, 1) if side == 0 else (3, 2)
        return dx1 + dy1, dx1 + dy2, dx2 + dy1

    def any_row(places):
        found = sub == places[0]
        for place in places[1:]:
            found = jnp.logical_or(found, sub == place)
        return found

    corner_sets = ((0, 1, (3, 4)), (2, 6, (5,)))
    for side in range(2):
        for end in range(2):
            places = corner_rows(side, end)
            first_here, second_here = any_row(places), any_row([(v + 2) % 8 for v in places])
            for at, (ch_a, ch_b, right) in enumerate(corner_sets):
                tiles = [s1[side, ch, end * (X // 2 - 1)] for ch in (ch_a, ch_b) + right]
                tile = pltpu.roll(tiles[2], 5, 0)
                if len(right) == 2:
                    tile = jnp.where(sub == (places[0] + 5) % 8, tile, pltpu.roll(tiles[3], 3 if side else 7, 0))
                tile = jnp.where(first_here, tiles[0], jnp.where(second_here, pltpu.roll(tiles[1], 2, 0), tile))
                ctake[side, end, at] = tile
            near = [s2[side, c, end * (X // 2 - 1)] for c in range(3)]
            ftake[side, end] = jnp.where(sub == places[0], near[0], jnp.where(
                sub == (places[0] + 2) % 8, pltpu.roll(near[1], 2, 0), pltpu.roll(near[2], 4, 0)))

    def corner_unpack(made):
        for at, (ds, dg) in enumerate(steps[4:]):
            side, end = (0 if dg > 0 else 1), (1 if ds > 0 else 0)
            pair = HALO // 2 + X // 2 if ds > 0 else HALO // 2 - 1
            back = made[3 - at][2]

            @pl.when(inside(ds, dg))
            def _():
                back.wait_recv()
                for at, (ch_a, ch_b, right) in enumerate(corner_sets):
                    tile = cland[side, end, at]
                    h1[side, ch_a, pair] = tile
                    h1[side, ch_b, pair] = pltpu.roll(tile, 6, 0)
                    h1[side, right[0], pair] = pltpu.roll(tile, 3, 0)
                    if len(right) == 2:
                        h1[side, right[1], pair] = pltpu.roll(tile, 5 if side else 1, 0)

    corners = corner_copies()
    zeroth = copies(e1a, e1a, s1, h1, recv0, 6, 7, 4, REACH - 1)
    first = copies(e1a, e1a, s1, h1, recv1, 0, 3, 4, REACH - 1)
    rest = copies(e1a, e1a, s1, h1, recv1, 3, 6, 4, REACH - 1, None, ends)
    late = (copies(e1a, e1a, s1, h1, recv2, 0, 3, 2, 1, REACH),
            copies(e1a, e1a, s1, h1, recv2, 6, 7, 2, 1, REACH))
    second = copies(e2a, e2a, s2, h2, recv2, 0, 3, 4, REACH - 1)
    tips = tip_copies()
    third = copies(rqa, rqa, s3, h3, recv3, 0, 3, 4, 1, REACH)
    outer = copies(rqa, rqa, s3, h3, recv3, 3, 6, 2, REACH - 1, REACH)
    wedges = wedge_copies()
    meet(barrier, 1)
    begin(zeroth)
    begin(corners)
    begin(first)
    inner_ends()
    begin(rest)
    greet(known.at[0], rounds[0])
    turn_out(rows[3], outb.at[3])
    inb[3, si] = outb[3, si]
    for at in range(len(rounds) - 2):
        meet(known.at[at], rounds[at])
        greet(known.at[at + 1], rounds[at + 1])
    finish_recv(recv0, REACH - 1, X // 2)
    corner_unpack(corners)
    meet(known.at[len(rounds) - 2], rounds[-2])
    greet(known.at[len(rounds) - 1], rounds[-1])
    begin(second)
    begin(tips)
    for made in late:
        begin(made)

    def open0(i, _):
        e1b[6, 2 * i], e1b[6, 2 * i + 1] = unpack(h1, 6, i)
        return 0

    def open1(i, _):
        for ch in range(6):
            e1b[ch, 2 * i], e1b[ch, 2 * i + 1] = unpack(h1, ch, i)
        return 0

    lax.fori_loop(0, (X + 2 * HALO) // 2, open0, 0)

    def link(w, other):
        return jnp.where(jnp.minimum(w, other) > 0.0, (0.5 * SPRING_SHEAR) * (w + other), 0.0)


    def over_rows(low, high, width, body, carried=0):
        width = max(v for v in range(1, width + 1) if (high - low) % v == 0)

        def chunk(i, state):
            return body([low + i * width + o for o in range(width)], state)

        return lax.fori_loop(0, (high - low) // width, chunk, carried)

    def all_coefficients(rows_here, _):
        for x in rows_here:
            coefficients(x)
        return 0

    def coefficients(x):
        wa, wb = e1a[6, x], e1b[6, x]
        ya, yb = up_y(wa, wb)
        da, db = down_y(wa, wb)
        for w, wu, wd, yu, yd, dg, kc in (
            (wa, e1a[6, x + 1], e1a[6, x - 1], ya, da, dga, kca),
            (wb, e1b[6, x + 1], e1b[6, x - 1], yb, db, dgb, kcb),
        ):
            zu = jnp.where(not_last, up_z(w), 0.0)
            zd = jnp.where(not_first, down_z(w), 0.0)
            kc[0, x] = link(w, wu)
            kc[1, x] = link(w, yu)
            kc[2, x] = link(w, yd)
            kc[3, x] = link(w, zu)
            kc[4, x] = link(w, zd)
            sx = w + 0.5 * (wu + wd)
            sy = w + 0.5 * (yu + yd)
            sz = w + 0.5 * (zu + zd)
            every = MASS_TERM + SPRING_SHEAR * (sx + sy + sz)
            dg[0, x] = every + SHEAR_REST * sx
            dg[1, x] = every + SHEAR_REST * sy
            dg[2, x] = every + SHEAR_REST * sz

    def edge_link(x):
        kca[0, x] = link(e1a[6, x], e1a[6, x + 1])
        kcb[0, x] = link(e1b[6, x], e1b[6, x + 1])

    edge_link(HALO - 2)
    over_rows(HALO - 1, HALO + X + 1, WIDE_K, all_coefficients)
    finish_recv(recv1, 6 * (REACH - 1), 3 * X)
    lax.fori_loop(0, (X + 2 * HALO) // 2, open1, 0)

    def operate(x, va, vb, base, chosen=slice(0, 2)):
        result = []
        coef = [[kc[j, x] for j in range(5)] + [kc[0, x - 1]] for kc in (kca, kcb)]
        for c in range(3):
            a, b = va[base + c, x], vb[base + c, x]
            ua, ub = up_y(a, b)
            la, lb = down_y(a, b)
            pair = []
            halves = ((a, va, ua, la, coef[0], dga), (b, vb, ub, lb, coef[1], dgb))
            for v, ref, u, l, k, dg in halves[chosen]:
                parts = (
                    k[0] * ref[base + c, x + 1] + k[5] * ref[base + c, x - 1],
                    k[1] * u + k[2] * l,
                    k[3] * up_z(v) + k[4] * down_z(v),
                )
                shear = parts[(c + 1) % 3] + parts[(c + 2) % 3]
                pair.append(dg[c, x] * v - (shear + (SPRING_NORMAL / SPRING_SHEAR) * parts[c]))
            result.append(pair)
        return result

    only_a, only_b = slice(0, 1), slice(1, 2)

    def residual(rows_here, _):
        for x in rows_here:
            image = operate(x, e1a, e1b, 0)
            for c in range(3):
                rqa[c, x] = e1a[3 + c, x] - image[c][0]
                rqb[c, x] = e1b[3 + c, x] - image[c][1]
        return 0

    def solve(step, ship_halo=None):
        def put(x, image):
            for c in range(3):
                rqa[3 + c, x] = image[c][0]
                rqb[3 + c, x] = image[c][1]

        def apply(rows_here, sums):
            rr, rq = sums
            for x in rows_here:
                image = operate(x, rqa, rqb, 0)
                for c in range(3):
                    r = rqa[c, x]
                    rr, rq = rr + r * r, rq + r * image[c][0]
                put(x, image)
            return rr, rq

        zero = jnp.zeros((8, 128), jnp.float32)
        images = [operate(x, rqa, rqb, 0) for x in (HALO - 1, HALO + X)]
        put(HALO - 1, images[0])
        put(HALO + X, images[1])
        rr, rq = over_rows(HALO, HALO + X, WIDE_A, apply, (zero, zero))
        if ship_halo is not None:
            ship_halo()
        rr, rq = total(rr), total(rq)
        mu = jnp.where(rr > 0.0, rq / jnp.where(rr > 0.0, rr, 1.0), 0.0)

        def centred(rows_here, sums):
            ww, wr, mix, wt = sums
            for x in rows_here:
                image = operate(x, rqa, rqb, 3, only_a)
                for c in range(3):
                    r, q, s = rqa[c, x], rqa[3 + c, x], image[c][0]
                    if step == 0:
                        sa[c, x] = s
                    w, t = q - mu * r, s - mu * q
                    ww, wr, mix, wt = ww + w * w, wr + w * r, mix + (r * t + w * q), wt + w * t
            return ww, wr, mix, wt

        sums = over_rows(HALO, HALO + X, WIDE_C, centred, (zero,) * 4)
        ww, wr, mix, wt = [total(v) for v in sums]
        one = lax.broadcasted_iota(jnp.int32, (1, 128), 1)
        row = jnp.zeros((1, 128), jnp.float32)
        for at, value in enumerate((rr, rq, mu, ww, wr, mix, wt)):
            row = jnp.where(one == at, value, row)
        gath[step, me] = row

        if step == 0:
            meet(known.at[len(rounds) - 1], rounds[-1])
        for other in others:
            pltpu.make_async_remote_copy(
                src_ref=gath.at[step, me], dst_ref=gath.at[step, me], send_sem=asend, recv_sem=arecv.at[step],
                device_id=other, device_id_type=MESH).start()

    def collect(step):
        block = gath.at[step, pl.ds(0, count - 1)]
        pltpu.make_async_copy(block, block, arecv.at[step]).wait()
        table = gath[step].reshape(count, 128)
        rr, rq, mu, ww, wr, mix, wt = [table[:, at:at + 1] for at in range(7)]

        def down(v):
            return jnp.sum(v, axis=0, keepdims=True)

        norm = down(rr)
        alpha = norm / down(rq)
        rest = 1.0 - alpha * mu
        after = down(alpha * alpha * ww - 2.0 * alpha * rest * wr + rest * rest * rr)
        curved = down(rest * rest * rq - alpha * rest * mix + alpha * alpha * wt)
        ratio = after / norm
        beta = after / (curved - ratio * after / alpha)
        return jnp.broadcast_to(alpha + beta * (1.0 + ratio), (8, 128)), jnp.broadcast_to(-beta * alpha, (8, 128))

    def drain():
        block = gath.at[:, pl.ds(0, count - 1)]
        pltpu.make_async_copy(block, block, asend).wait()

    def joined(c, x, near, far):
        r, q = rqa[c, x], rqa[3 + c, x]
        return jnp.where(sub == 3, pltpu.roll(r, near, 0), jnp.where(sub == 4, pltpu.roll(r, far, 0), q))

    def split(c, x, tile, row, near, far):
        r = rqb[c, x]
        rqb[c, x] = jnp.where(sub == row, pltpu.roll(tile, near, 0), jnp.where(sub == 7 - row, pltpu.roll(tile, far, 0), r))
        rqb[3 + c, x] = tile

    def ship_halo():
        def pack3(i, _):
            x = HALO + 2 * i
            for c in range(3):
                pack(s3, c, i, joined(c, x, 1, 7), joined(c, x + 1, 1, 7))
            return 0

        lax.fori_loop(0, X // 2, pack3, 0)
        for end, x in ((0, HALO), (1, HALO + X - 2)):
            for c in range(3):
                even, odd = [joined(c, x + o, 2, 6) if o == end else joined(c, x + o, 3, 5) for o in range(2)]
                k3[0, end, c, 0] = jnp.where(upper, even, pltpu.roll(odd, 4, 0))
                k3[1, end, c, 0] = jnp.where(upper, pltpu.roll(even, 4, 0), odd)
        begin(wedges)
        begin(outer)
        begin(third)

    outer_residual(HALO - 2)
    outer_residual(HALO + X + 1)
    over_rows(HALO - 1, HALO + X + 1, WIDE_R, residual)
    solve(0, ship_halo)
    finish_recv(recv2, 3 * (REACH - 1) + 4, 3 * X // 2)
    tip_unpack(tips)
    edge_link(HALO - REACH)
    coefficients(HALO - 2)
    coefficients(HALO + X + 1)

    def open2(i, _):
        for ch in range(3):
            e2b[ch, 2 * i], e2b[ch, 2 * i + 1] = unpack(h2, ch, i)
        return 0

    lax.fori_loop(0, (X + 2 * HALO) // 2, open2, 0)
    finish_recv(recv3, 3 + 3 * (REACH - 1), 3 * X // 2)
    for at, (ds, dg) in enumerate(steps[4:]):
        back = wedges[3 - at][2]

        @pl.when(inside(ds, dg))
        def _():
            back.wait_recv()

    def open3(i, _):
        for c in range(3):
            even, odd = unpack(h3, c, i)
            split(c, 2 * i, even, 2, 7, 1)
            split(c, 2 * i + 1, odd, 2, 7, 1)
        return 0

    lax.fori_loop(HALO // 2, (HALO + X) // 2, open3, 0)
    for pair, one in ((HALO // 2 - 1, 1), ((HALO + X) // 2, 0)):
        for c in range(3):
            for o, tile in enumerate(unpack(h3, c, pair)):
                if o == one:
                    split(c, 2 * pair + o, tile, 1, 6, 2)
                else:
                    split(c, 2 * pair + o, tile, 0, 5, 3)
    finish_send(13 * (REACH - 1) + 7, 13 * X // 2, 6)
    spread_out(outb.at[3], inb.at[3], 3)
    for x in range(HALO - 1, HALO + X + 1):
        image = operate(x, rqa, rqb, 3, only_b)
        for c in range(3):
            sb[c, x] = image[c][0]
            e2a[c, x] = MASS_TERM * e1a[c, x] + e2a[c, x] - e1a[3 + c, x] + rqa[c, x]
            e2b[c, x] = MASS_TERM * e1b[c, x] + e2b[c, x] - e1b[3 + c, x] + rqb[c, x]
    for x in (HALO - 2, HALO + X + 1):
        image = operate(x, e1a, e1b, 0, only_a)
        for c in range(3):
            e2a[c, x] = MASS_TERM * e1a[c, x] + e2a[c, x] - image[c][0]
    for x in (HALO - 2, HALO - 1, HALO + X, HALO + X + 1):
        image = operate(x, rqa, rqb, 3, only_a)
        for c in range(3):
            sa[c, x] = image[c][0]
    c0, c1 = collect(0)

    def step1(x, base, rq, g, s, u1, comps):
        for c in range(3):
            r, q = rq[c, x], rq[3 + c, x]
            grown = c0 * r + c1 * q
            if c in comps:
                u1[c, x] = base[c, x] + grown
            rq[c, x] = g[c, x] + (2.0 * MASS_TERM) * grown - (c0 * q + c1 * s[c, x])

    for x in range(HALO - 2, HALO + X + 2):
        own_row = HALO <= x < HALO + X
        step1(x, e1a, rqa, e2a, sa, u1a, (0, 1, 2) if own_row else ())
        if HALO - 1 <= x <= HALO + X:
            step1(x, e1b, rqb, e2b, sb, u1b, (1,) if own_row else ())

    def early(at, ref, ch):
        for x in range(X):
            rows[at, pl.ds(x, 8, stride=X), :] = ref[ch, HALO + x]
        turn_out(rows[at], outb.at[at])
        spread_out(outb.at[at], inb.at[at], at)
        inb[at, si] = outb[at, si]

    solve(1)
    early(2, u1a, 2)
    early(4, rqa, 2)
    early(5, rqa, 5)
    c0, c1 = collect(1)

    def step2(ra, rb, c, x):
        return ra[c, x] + (c0 * rb[c, x] + c1 * rb[3 + c, x])

    def halves(v):
        high = v.astype(jnp.bfloat16)
        return high, (v - high.astype(jnp.float32)).astype(jnp.bfloat16)

    def finish(c):
        for x in range(X):
            v = step2(u1a, rqa, c, HALO + x)
            disp_ref[c, x] = v
            rows[c, pl.ds(x, 8, stride=X), :] = v
        turned = turn_out(rows[c], outb.at[c])
        spread_out(outb.at[c], inb.at[c], c)
        inb[c, si] = outb[c, si]

    def joint(ref, j, low, high):
        return jnp.concatenate([
            ref[2, j, at:at + 8] + (c0 * ref[4, j, at:at + 8] + c1 * ref[5, j, at:at + 8])
            for at in range(low, high, 8)], axis=0)

    def finish_edges():
        for x in range(X):
            rows[6, pl.ds(x, 8, stride=X), :] = step2(u1b, rqb, 1, HALO + x)
        sides_y = rows[6].T
        zero = jnp.zeros((8, 128), jnp.float32)
        for j in range(ns):
            low, high = sides_y[zrows * j:zrows * j + 8], sides_y[zrows * j + 8:zrows * j + 16]
            tile = jnp.where(lane < 32, pltpu.roll(low, 16, 1),
                             jnp.where(lane < 64, pltpu.roll(pltpu.roll(low, 4, 0), 48, 1),
                                       jnp.where(lane < 96, pltpu.roll(high, 80, 1),
                                                 pltpu.roll(pltpu.roll(high, 4, 0), 112, 1))))
            before = pltpu.roll(joint(outb, j - 1, zrows - 8, zrows), 5, 0) if j else zero
            after = pltpu.roll(joint(outb, j + 1, 0, 8), 5, 0) if j + 1 < ns else zero
            outx[j] = jnp.where(sub == 4, before, jnp.where(sub == 5, after, tile))
        spread_out(outx.at[:, pl.ds(0, 6)], inx.at[:, pl.ds(0, 6)], 6)
        inx[si] = outx[si]

    finish(0)
    finish_edges()
    finish(1)
    for x in range(X):
        disp_ref[2, x] = step2(u1a, rqa, 2, HALO + x)
    fetched[7].wait()

    c1t, c3t = float(np.sqrt(0.5) * np.cos(np.pi / 8)), float(np.sqrt(0.5) * np.cos(3 * np.pi / 8))

    def cosine(v0, v1, v2, v3):
        s03, s12, d03, d12 = v0 + v3, v1 + v2, v0 - v3, v1 - v2
        return [0.5 * (s03 + s12), c1t * d03 + c3t * d12, 0.5 * (s03 - s12), c3t * d03 - c1t * d12]

    def encode(ch, fields):
        for b in range(Y // 4):
            for k, v in enumerate(cosine(*fields[4 * b:4 * b + 4])):
                work[ch, (4 * b + k) * zrows:(4 * b + k + 1) * zrows] = v
        parts = []
        for p in range(Y * zrows // 32):
            parts += cosine(*[work[ch, pl.ds(32 * p + n, 8, stride=4), :] for n in range(4)])
        high, low = halves(jnp.concatenate(parts, axis=0))
        done = jnp.dot(jnp.concatenate([high, low], axis=1), gt_ref[...], preferred_element_type=jnp.float32)
        done = done[:, 0:128] + done[:, 128:256]
        for p in range(Y * zrows // 32):
            for n in range(4):
                coef_ref[ch, pl.ds(32 * p + n, 8, stride=4), :] = done[(4 * p + n) * 8:(4 * p + n + 1) * 8]

    def arrived(c):
        landed(inb.at[c], trecv.at[c])
        return regroup([inb[c, j] for j in range(ns)])

    for at in (2, 4, 5):
        landed(inb.at[at], trecv.at[at])
    along = regroup([joint(inb, j, 0, zrows) for j in range(ns)])
    encode(2, along)
    landed(inb.at[3], trecv.at[3])
    for y, piece in enumerate(regroup([inb[3, j] for j in range(ns)])):
        scale[y] = piece
    field = arrived(0)
    encode(0, field)
    wide = lax.broadcasted_iota(jnp.int32, (zrows, 128), 1)
    encode(3, [scale[y] * (jnp.where(wide < 127, up_z(field[y]), 0.0) - jnp.where(wide > 0, down_z(field[y]), 0.0))
               for y in range(Y)])
    landed(inx.at[:, pl.ds(0, 6)], trecv.at[6])
    edges = regroup([inx[j] for j in range(ns)])
    stress = []
    for y in range(Y):
        low, high = along[y][0:8], along[y][8:16]
        ul, uh, dl, dh = pltpu.roll(low, 7, 0), pltpu.roll(high, 7, 0), pltpu.roll(low, 1, 0), pltpu.roll(high, 1, 0)
        first, last = sub == 0, sub == 7
        low = jnp.where(last, uh, ul) - jnp.where(first, pltpu.roll(edges[y], 4, 0), dl)
        high = jnp.where(last, pltpu.roll(edges[y], 2, 0), uh) - jnp.where(first, dl, dh)
        stress.append(scale[y] * jnp.concatenate([low, high], axis=0))
    encode(5, stress)
    field = arrived(1)
    encode(1, field)
    outside = []
    for side in range(2):
        quarter = [edges[2 * q + side] for q in range(4)]
        outside.append(jnp.concatenate([jnp.where(upper, quarter[q], pltpu.roll(quarter[q + 1], 4, 0)) for q in (0, 2)], axis=0))
    field = [outside[0]] + field + [outside[1]]
    encode(4, [scale[y] * (field[y + 2] - field[y]) for y in range(Y)])
    drain()
    block = inb.at[:, pl.ds(0, ns - 1)]
    pltpu.make_async_copy(block, block, tsend.at[0]).wait()
    landed(inx.at[:, pl.ds(0, 6)], tsend.at[1])


def store(disp_in, coef_in, disp_out, coef_out, sems):
    copies = [pltpu.make_async_copy(disp_in, disp_out, sems.at[0]), pltpu.make_async_copy(coef_in, coef_out, sems.at[1])]
    for copy in copies:
        copy.start()
    for copy in copies:
        copy.wait()


def fused(mesh, u_now, u_prev, force, stiffness, broken, flags):
    ns, ng = mesh.shape["slab"], mesh.shape["grp"]
    _, X, Y, Z = u_now.shape
    xe, pairs, half = X + 2 * HALO, X // 2 + HALO, X // 2
    zrows = Z // ns
    ez = jnp.asarray(np.kron(np.eye(Z // 4), np.ones((1, 4))), jnp.float32)
    gth, gtl = split_table(wavelet_table(X * ns).T)
    gt = jnp.asarray(np.block([[gth, gtl], [gth, np.zeros_like(gtl)]]), jnp.bfloat16)

    def vm(*shape):
        return pltpu.VMEM(shape, jnp.float32)

    def ext(n):
        return vm(n, xe, Y, Z)

    def stage(n):
        return vm(2, n, half, Y, Z)

    def land(n):
        return vm(2, n, pairs, Y, Z)

    dma = pltpu.SemaphoreType.DMA
    shapes = (u_now.shape, (6, Y * zrows, X * ns))
    operands = [pltpu.with_memory_space_constraint(v, pltpu.HBM)
                for v in (u_now, u_prev, force, stiffness, broken, flags, ez, gt)]
    results = pl.pallas_call(
        lambda *refs: kernel(ns, ng, *refs),
        name="lattice",
        out_shape=tuple(vm(*shape) for shape in shapes),
        in_specs=[pl.BlockSpec(memory_space=pltpu.MemorySpace.HBM)] * 8,
        out_specs=(pl.BlockSpec(memory_space=pltpu.VMEM),) * 2,
        scratch_shapes=[
            vm(*u_now.shape), vm(*u_now.shape), vm(*u_now.shape), vm(*stiffness.shape),
            pltpu.VMEM(broken.shape, broken.dtype), pltpu.VMEM(flags.shape, flags.dtype),
            vm(*ez.shape), pltpu.VMEM(gt.shape, gt.dtype), pltpu.SemaphoreType.DMA((6,)),
            ext(7), ext(7), stage(7), land(7),
            ext(3), ext(3), stage(3), land(3),
            ext(6), ext(6), stage(3), land(3), vm(2, 2, 3, 1, Y, Z), vm(2, 3, 2, Y, Z),
            ext(3), ext(3), ext(3), ext(3), vm(Y, zrows, X * ns), ext(3), ext(3), ext(5), ext(5),
            pltpu.SemaphoreType.REGULAR((3,)), vm(2, ns * ng, 1, 128), vm(7, Y * X, Z), vm(6, ns, zrows, 128), vm(6, ns, zrows, 128), vm(ns, 8, 128), vm(ns, 8, 128), vm(6, Y * zrows, X * ns),
            vm(max(9 * X, 13 * X // 2), Y, Z), dma((8,)), vm(2, 2, 2, Y, Z), vm(2, 2, 2, Y, Z), dma((4,)),
            dma((4,)), dma((4,)), dma((4,)), dma((4,)), dma((4,)), vm(2, 2, Y, Z), vm(2, 2, Y, Z), dma((4,)),
            dma, dma((2,)), dma((2,)), dma((7,)),
        ],
        compiler_params=pltpu.CompilerParams(collective_id=0, has_side_effects=True, vmem_limit_bytes=24 << 20),
    )(*operands)
    disp, coef = pl.pallas_call(
        store,
        name="store",
        out_shape=tuple(jax.ShapeDtypeStruct(shape, jnp.float32) for shape in shapes),
        in_specs=[pl.BlockSpec(memory_space=pltpu.VMEM)] * 2,
        out_specs=(pl.BlockSpec(memory_space=pltpu.MemorySpace.HBM),) * 2,
        scratch_shapes=[dma((2,))],
        compiler_params=pltpu.CompilerParams(vmem_limit_bytes=1 << 20),
    )(*[pltpu.with_memory_space_constraint(v, pltpu.VMEM) for v in results])
    return disp, coef.reshape(6, Y, zrows, X * ns)


def fits(mesh, shape):
    ns, ng = mesh.shape["slab"], mesh.shape["grp"]
    x, y, z = shape[1] // ns, shape[2] // ng, shape[3]
    return y == 8 and z == 128 and x * y == 128 and x * ns == 128 and z % (8 * ns) == 0


def entry(mesh, *args):
    ns, ng = mesh.shape["slab"], mesh.shape["grp"]
    _, x, y, z = args[0].shape
    if fits(mesh, (3, x * ns, y * ng, z)):
        return fused(mesh, *args)
    return body(*args)


def solution(mesh):
    return jax.shard_map(
        lambda *args: entry(mesh, *args),
        mesh=mesh,
        in_specs=(
            P(None, "slab", "grp", None),
            P(None, "slab", "grp", None),
            P(None, "slab", "grp", None),
            P("slab", "grp", None),
            P("slab", "grp", None),
            P("slab", "grp", None),
        ),
        out_specs=(P(None, "slab", "grp", None), P(None, "grp", "slab", None)),
        check_vma=False,
    )
```

```python
import jax
import jax.numpy as jnp
import numpy as np
from jax import lax
from jax.experimental import pallas as pl
from jax.experimental.pallas import tpu as pltpu
from jax.sharding import PartitionSpec as P

STEPS = 2
ITERS = 2
LEVELS = 3


SPRING_NORMAL = 1.0
SPRING_SHEAR = 0.4
MASS_TERM = 1.0
CRACK_CUT = 0.9


def with_halo(block, sides, width):
    for axis, dim in sides:
        count = lax.axis_size(axis)
        forward = [(i, i + 1) for i in range(count - 1)]
        backward = [(target, source) for source, target in forward]
        low = lax.ppermute(
            lax.slice_in_dim(block, block.shape[dim] - width, None, axis=dim), axis, forward
        )
        high = lax.ppermute(lax.slice_in_dim(block, 0, width, axis=dim), axis, backward)
        block = jnp.concatenate([low, block, high], axis=dim)
    return block


def cosine_table():
    freq = np.arange(4)[:, None]
    place = np.arange(4)[None, :]
    factor = np.where(freq == 0, 0.5, np.sqrt(0.5))
    return factor * np.cos(np.pi * (2 * place + 1) * freq / 8.0)


def block_table(count):
    return jnp.asarray(np.kron(np.eye(count // 4), cosine_table()), jnp.float32)


def spread(mask):
    values = mask.astype(jnp.float32)
    size_a, size_b, size_c = values.shape
    wide = jnp.broadcast_to(values[:, None, :, None, :, None], (size_a, 4, size_b, 4, size_c, 4))
    return wide.reshape(size_a * 4, size_b * 4, size_c * 4)


def sides(padded, axis_index):
    leading = padded.ndim - 3

    def cut(offset):
        index_list = [slice(None)] * leading + [slice(1, -1)] * 3
        length = padded.shape[leading + axis_index]
        index_list[leading + axis_index] = slice(1 + offset, length - 1 + offset)
        return padded[tuple(index_list)]

    return (cut(1), cut(-1))


def springs(field, weight, field_pad, weight_pad):
    result = MASS_TERM * field
    for axis_index in range(3):
        upper_v, lower_v = sides(field_pad, axis_index)
        upper_w, lower_w = sides(weight_pad, axis_index)
        k_upper = 0.5 * (weight + upper_w)
        k_lower = 0.5 * (weight + lower_w)
        change = k_upper * (field - upper_v) + k_lower * (field - lower_v)
        coupling = jnp.array(
            [SPRING_NORMAL if comp == axis_index else SPRING_SHEAR for comp in range(3)],
            jnp.float32,
        ).reshape(3, 1, 1, 1)
        result = result + coupling * change
    return result


def faces(field):
    padded = with_halo(field, (("slab", 1), ("grp", 2)), 1)
    return jnp.pad(padded, ((0, 0), (0, 0), (0, 0), (1, 1)))


def stresses(carry, field_pad):
    rows_out = []
    for axis_index in range(3):
        upper_v, lower_v = sides(field_pad, axis_index)
        rows_out.append(SPRING_NORMAL * carry * 0.5 * (upper_v[axis_index] - lower_v[axis_index]))
    return jnp.stack(rows_out)


def paired_sum(residual, image):
    return lax.psum((jnp.sum(residual * residual), jnp.sum(residual * image)), ("slab", "grp"))


def lift(signal):
    even = signal[..., 0::2]
    odd = signal[..., 1::2]
    detail = odd - 0.5 * (even + jnp.roll(even, -1, axis=-1))
    approx = even + 0.25 * (jnp.roll(detail, 1, axis=-1) + detail)
    return (approx, detail)


def wavelet(signal):
    pieces = []
    approx = signal
    for level_index in range(LEVELS):
        approx, detail = lift(approx)
        pieces.insert(0, detail)
    return jnp.concatenate([approx] + pieces, axis=-1)


def body(u_now, u_prev, force, stiffness, broken, flags):
    weight = stiffness * (1.0 - CRACK_CUT * spread(broken))
    carry = spread(flags) * weight
    weight_pad = with_halo(weight, (("slab", 0), ("grp", 1)), 1)
    weight_pad = jnp.pad(weight_pad, ((0, 0), (0, 0), (1, 1)))

    def operate(field):
        return springs(field, weight, faces(field), weight_pad)

    for step_index in range(STEPS):
        rhs = MASS_TERM * (2.0 * u_now - u_prev) + force
        guess = u_now
        residual = rhs - operate(guess)
        image = operate(residual)
        norm_now, product = paired_sum(residual, image)
        alpha = norm_now / product
        direction, along = (residual, image)
        for turn_index in range(ITERS):
            guess = guess + alpha * direction
            residual = residual - alpha * along
            if turn_index + 1 < ITERS:
                image = operate(residual)
                norm_next, product = paired_sum(residual, image)
                ratio = norm_next / norm_now
                alpha = norm_next / (product - ratio * norm_next / alpha)
                direction = residual + ratio * direction
                along = image + ratio * along
                norm_now = norm_next
        u_prev = u_now
        u_now = guess
    stress = stresses(carry, faces(u_now))
    fields = jnp.concatenate([u_now, stress], axis=0)
    table_x = block_table(fields.shape[1])
    table_y = block_table(fields.shape[2])
    table_z = block_table(fields.shape[3])
    blockc = jnp.einsum("ax,hxyz->hayz", table_x, fields, precision=lax.Precision.HIGHEST)
    blockc = jnp.einsum("by,hxyz->hxbz", table_y, blockc, precision=lax.Precision.HIGHEST)
    blockc = jnp.einsum("hxyz,cz->hxyc", blockc, table_z, precision=lax.Precision.HIGHEST)
    moved = jnp.transpose(blockc, (0, 2, 3, 1))
    shipped = lax.all_to_all(moved, "slab", split_axis=2, concat_axis=3, tiled=True)
    coeffs = wavelet(shipped)
    return (u_now, coeffs)


MESH = pl.DeviceIdType.MESH
HALO = 4
REACH = 3
SHEAR_REST = SPRING_NORMAL - SPRING_SHEAR
WIDE_R, WIDE_A, WIDE_C, WIDE_K = 20, 16, 16, 20


def wavelet_table(count):
    table = np.kron(np.eye(count // 4), cosine_table())
    pieces = []
    approx = table
    for level_index in range(LEVELS):
        even, odd = approx[0::2], approx[1::2]
        detail = odd - 0.5 * (even + np.roll(even, -1, axis=0))
        approx = even + 0.25 * (np.roll(detail, 1, axis=0) + detail)
        pieces.insert(0, detail)
    return np.concatenate([approx] + pieces, axis=0)


def split_table(table):
    high = table.astype(jnp.bfloat16).astype(np.float64)
    return high, (table - high).astype(jnp.bfloat16).astype(np.float64)


def sub_index():
    return lax.broadcasted_iota(jnp.int32, (8, 128), 0)


def lane_index():
    return lax.broadcasted_iota(jnp.int32, (8, 128), 1)


def up_y(a, b):
    ra, rb = pltpu.roll(a, 7, 0), pltpu.roll(b, 7, 0)
    last = sub_index() == 7
    return jnp.where(last, rb, ra), jnp.where(last, ra, rb)


def down_y(a, b):
    ra, rb = pltpu.roll(a, 1, 0), pltpu.roll(b, 1, 0)
    first = sub_index() == 0
    return jnp.where(first, rb, ra), jnp.where(first, ra, rb)


def up_z(v):
    return pltpu.roll(v, 127, 1)


def down_z(v):
    return pltpu.roll(v, 1, 1)


def total(v):
    return jnp.sum(jnp.sum(v, axis=0, keepdims=True), axis=1, keepdims=True)


def kernel(ns, ng, u_in, p_in, f_in, k_in, br_in, fl_in, ez_in, gt_in,
           disp_ref, coef_ref,
           u_ref, p_ref, f_ref, k_ref, br_ref, fl_ref, ez_ref, gt_ref, isem,
           e1a, e1b, s1, h1, e2a, e2b, s2, h2, rqa, rqb, s3, h3, k3, ends,
           u1a, u1b, sa, sb, scale, dga, dgb, kca, kcb, known, gath, rows, outb, inb, outx, inx, work,
           blanks, sends, ctake, cland, crecv, recv0, recv1, recv2, recv3, recvk, ftake, fland, recvf, asend, arecv, tsend, trecv):
    X, Y, Z = u_ref.shape[1:]
    si, gi = lax.axis_index("slab"), lax.axis_index("grp")
    me = si * ng + gi
    count = ns * ng
    barrier = pltpu.get_barrier_semaphore()

    def mirrored(place, mask, length):
        bit, result = 1, 0
        while bit < length:
            here = place // bit % 2
            result = result + bit * (1 - here if mask // bit % 2 else here)
            bit *= 2
        return result

    others = []
    for k in sorted(range(ns), key=lambda k: -min(k, ns - k)):
        for g in range(ng):
            if k or g:
                others.append((lax.rem(si + k, ns), lax.rem(gi + g, ng)))

    sub, lane = sub_index(), lane_index()
    upper = sub < 4

    steps = [(-1, 0), (1, 0), (0, -1), (0, 1), (-1, -1), (-1, 1), (1, -1), (1, 1)]

    def inside(ds, dg):
        ok = None
        if ds:
            ok = (si >= -ds) if ds < 0 else (si <= ns - 1 - ds)
        if dg:
            more = (gi >= -dg) if dg < 0 else (gi <= ng - 1 - dg)
            ok = more if ok is None else jnp.logical_and(ok, more)
        return ok

    def around(reach):
        return [(ds, dg) for ds in (-reach, 0, reach) for dg in (-reach, 0, reach)
                if (ds or dg) and abs(ds) < ns and abs(dg) < ng]

    def greet(sem, reach):
        for ds, dg in around(reach):
            @pl.when(inside(ds, dg))
            def _():
                pl.semaphore_signal(sem, inc=1, device_id=(si + ds, gi + dg), device_id_type=MESH)

    def meet(sem, reach):
        pl.semaphore_wait(sem, sum(jnp.where(inside(ds, dg), 1, 0) for ds, dg in around(reach)))

    rounds = []
    while (rounds[-1] * 2 if rounds else 1) < max(ns, ng):
        rounds.append(rounds[-1] * 2 if rounds else 1)

    greet(barrier, 1)
    fetched = []
    for at, (source, target) in enumerate((
        (br_in, br_ref), (fl_in, fl_ref), (ez_in, ez_ref), (k_in, k_ref), (u_in, u_ref), (p_in, p_ref),
        (f_in, f_ref), (gt_in, gt_ref),
    )):
        fetch = pltpu.make_async_copy(source, target, isem.at[min(at, 4) if at < 7 else 5])
        fetch.start()
        fetched.append(fetch)

    def copies(ea, dst_a, stage, land, recv, low=0, high=None, ways=4, reach=REACH, depth=None, ends=None):
        depth = reach if depth is None else depth
        half = X // 2
        edge = HALO // 2
        made = []
        chans = pl.ds(low, (ea.shape[0] if high is None else high) - low)
        for at, (ds, dg) in enumerate(steps[:ways]):
            if dg == 0:
                if ends is not None:
                    source = ends.at[0 if ds < 0 else 1]
                    target = dst_a.at[chans, pl.ds(HALO + X if ds < 0 else HALO - depth, reach)]
                elif ds < 0:
                    source = ea.at[chans, pl.ds(HALO + depth - reach, reach)]
                    target = dst_a.at[chans, pl.ds(HALO + X + depth - reach, reach)]
                else:
                    source = ea.at[chans, pl.ds(HALO + X - depth, reach)]
                    target = dst_a.at[chans, pl.ds(HALO - depth, reach)]
            else:
                side = 0 if dg < 0 else 1
                source, target = stage.at[side, chans], land.at[side, chans, pl.ds(edge, half)]
            made.append((ds, dg, pltpu.make_async_remote_copy(
                src_ref=source, dst_ref=target, send_sem=sends.at[at], recv_sem=recv.at[at ^ 1],
                device_id=(si + ds, gi + dg), device_id_type=MESH)))
        return made

    def begin(made):
        for ds, dg, copy in made:
            @pl.when(inside(ds, dg))
            def _():
                copy.start()

    def take(tiles, sem):
        block = blanks.at[pl.ds(0, tiles)]
        pltpu.make_async_copy(block, block, sem).wait()

    def finish_recv(recv, slab_tiles, grp_tiles):
        for at, (ds, dg) in enumerate(steps[:4]):
            @pl.when(inside(ds, dg))
            def _():
                if (slab_tiles if ds else grp_tiles):
                    take(slab_tiles if ds else grp_tiles, recv.at[at])

    def finish_send(slab_tiles, grp_tiles, corner_tiles):
        for at, (ds, dg) in enumerate(steps):
            @pl.when(inside(ds, dg))
            def _():
                take(corner_tiles if ds and dg else slab_tiles if ds else grp_tiles, sends.at[at])

    def blank(dst_a, land):
        zero_a = jnp.zeros((dst_a.shape[0], HALO) + dst_a.shape[2:], jnp.float32)
        half, edge = X // 2, HALO // 2
        zero_l = jnp.zeros((land.shape[1], edge, 8, 128), jnp.float32)

        @pl.when(si == 0)
        def _():
            dst_a[:, pl.ds(0, HALO)] = zero_a
            for side in range(2):
                land[side, :, pl.ds(0, edge)] = zero_l

        @pl.when(si == ns - 1)
        def _():
            dst_a[:, pl.ds(HALO + X, HALO)] = zero_a
            for side in range(2):
                land[side, :, pl.ds(edge + half, edge)] = zero_l

        for side, edge_here in ((0, gi == ng - 1), (1, gi == 0)):
            @pl.when(edge_here)
            def _(side=side):
                land[side] = jnp.zeros(land.shape[1:], jnp.float32)

    def pack(stage, ch, pair, even, odd):
        stage[0, ch, pair] = jnp.where(upper, even, pltpu.roll(odd, 4, 0))
        stage[1, ch, pair] = jnp.where(upper, pltpu.roll(even, 4, 0), odd)

    def unpack(land, ch, pair):
        high, low = land[0, ch, pair], land[1, ch, pair]
        return (jnp.where(upper, high, pltpu.roll(low, 4, 0)),
                jnp.where(upper, pltpu.roll(high, 4, 0), low))

    def spread_rows(mask):
        wide = jnp.dot(mask.astype(jnp.float32), ez_ref[...], preferred_element_type=jnp.float32)
        return jnp.where(upper, jnp.broadcast_to(wide[0:1], (8, 128)), jnp.broadcast_to(wide[1:2], (8, 128)))

    for at in range(4):
        fetched[at].wait()
    for bx in range(X // 4):
        cut = 1.0 - CRACK_CUT * spread_rows(br_ref[bx])
        flag = spread_rows(fl_ref[bx])
        for at in range(4):
            x = bx * 4 + at
            w = k_ref[x] * cut
            e1a[6, HALO + x] = w
            rows[3, pl.ds(x, 8, stride=X), :] = (SPRING_NORMAL * 0.5) * (flag * w)

    def own(i, _):
        for c in range(3):
            tiles = []
            for o in range(2):
                x = 2 * i + o
                u = u_ref[c, x]
                f = f_ref[c, x]
                rhs = MASS_TERM * (2.0 * u - p_ref[c, x]) + f
                e1a[c, HALO + x] = u
                e1a[3 + c, HALO + x] = rhs
                e2a[c, HALO + x] = f
                tiles.append((u, rhs, f))
            pack(s1, c, i, tiles[0][0], tiles[1][0])
            pack(s1, 3 + c, i, tiles[0][1], tiles[1][1])
            pack(s2, c, i, tiles[0][2], tiles[1][2])
        pack(s1, 6, i, e1a[6, HALO + 2 * i], e1a[6, HALO + 2 * i + 1])
        return 0

    take(9 * X, isem.at[4])
    lax.fori_loop(0, X // 2, own, 0)
    zrows = Z // ns

    def turn_out(value, out):
        turned = value.T
        for j in range(ns):
            out[j] = turned[j * zrows:(j + 1) * zrows]

    def spread_out(source, target, at):
        for m in range(1, ns):
            to = lax.rem(si + m, ns)
            pltpu.make_async_remote_copy(
                src_ref=source.at[to], dst_ref=target.at[si], send_sem=tsend.at[0 if at < 6 else 1], recv_sem=trecv.at[at],
                device_id=(to, gi), device_id_type=MESH).start()

    def landed(target, sem):
        block = target.at[pl.ds(0, ns - 1)]
        pltpu.make_async_copy(block, block, sem).wait()

    def regroup(pieces):
        lanes = lax.broadcasted_iota(jnp.int32, pieces[0].shape, 1)
        gap = ns // 2
        while gap:
            keep = (lanes // (X * gap)) % 2 == 0
            mixed = list(pieces)
            for j in range(ns):
                if (j // gap) % 2 == 0:
                    a, b = pieces[j], pieces[j + gap]
                    mixed[j] = jnp.where(keep, a, pltpu.roll(b, X * gap, 1))
                    mixed[j + gap] = jnp.where(keep, pltpu.roll(a, 128 - X * gap, 1), b)
            pieces = mixed
            gap //= 2
        return pieces

    not_last, not_first = lane < 127, lane > 0

    def inner_ends():
        for end, x in ((0, HALO + 1), (1, HALO + X - 2)):
            w = e1a[6, x]
            along = (0.5 * (w + e1a[6, x + 1]), 0.5 * (w + e1a[6, x - 1]),
                     jnp.where(sub < 7, 0.5 * (w + pltpu.roll(w, 7, 0)), 0.0),
                     jnp.where(sub > 0, 0.5 * (w + pltpu.roll(w, 1, 0)), 0.0),
                     0.5 * (w + jnp.where(not_last, up_z(w), 0.0)), 0.5 * (w + jnp.where(not_first, down_z(w), 0.0)))
            for c in range(3):
                v = e1a[c, x]
                parts = (along[0] * (v - e1a[c, x + 1]) + along[1] * (v - e1a[c, x - 1]),
                         along[2] * (v - pltpu.roll(v, 7, 0)) + along[3] * (v - pltpu.roll(v, 1, 0)),
                         along[4] * (v - jnp.where(not_last, up_z(v), 0.0))
                         + along[5] * (v - jnp.where(not_first, down_z(v), 0.0)))
                image = MASS_TERM * v + (SPRING_SHEAR * (parts[0] + parts[1] + parts[2]) + SHEAR_REST * parts[c])
                ends[end, c, 1 - end] = e1a[3 + c, x] - image
                ends[end, c, end] = e1a[3 + c, x - 1 + 2 * end]

    def outer_residual(x):
        wa, wb = e1a[6, x], e1b[6, x]
        above = jnp.where(sub == 7, 0.5 * (wa + up_y(wa, wb)[0]), 0.0)
        below = jnp.where(sub == 0, 0.5 * (wa + down_y(wa, wb)[0]), 0.0)
        for c in range(3):
            a, b = e1a[c, x], e1b[c, x]
            change = above * (a - up_y(a, b)[0]) + below * (a - down_y(a, b)[0])
            rqa[c, x] = e1a[3 + c, x] - (SPRING_NORMAL if c == 1 else SPRING_SHEAR) * change
            rqb[c, x] = jnp.zeros((8, 128), jnp.float32)

    def tip_copies():
        made = []
        for at, (ds, dg) in enumerate(steps[4:]):
            side, end = (0 if dg < 0 else 1), (0 if ds < 0 else 1)
            made.append((ds, dg, pltpu.make_async_remote_copy(
                src_ref=ftake.at[side, end], dst_ref=fland.at[side, 1 - end],
                send_sem=sends.at[4 + at], recv_sem=recvf.at[3 - at],
                device_id=(si + ds, gi + dg), device_id_type=MESH)))
        return made

    def tip_unpack(made):
        for at, (ds, dg) in enumerate(steps[4:]):
            side, end = (0 if dg > 0 else 1), (1 if ds > 0 else 0)
            pair = HALO // 2 + X // 2 if ds > 0 else HALO // 2 - 1
            back = made[3 - at][2]

            @pl.when(inside(ds, dg))
            def _():
                back.wait_recv()
                tile = fland[side, end]
                for c in range(3):
                    h2[side, c, pair] = pltpu.roll(tile, 8 - 2 * c, 0) if c else tile

    def wedge_copies():
        made = []
        for at, (ds, dg) in enumerate(steps[4:]):
            side, end = (0 if dg < 0 else 1), (0 if ds < 0 else 1)
            pair = HALO // 2 + X // 2 if ds < 0 else HALO // 2 - 1
            made.append((ds, dg, pltpu.make_async_remote_copy(
                src_ref=k3.at[side, end], dst_ref=h3.at[side, :, pl.ds(pair, 1)],
                send_sem=sends.at[4 + at], recv_sem=recvk.at[3 - at],
                device_id=(si + ds, gi + dg), device_id_type=MESH)))
        return made

    def corner_copies():
        made = []
        for at, (ds, dg) in enumerate(steps[4:]):
            side, end = (0 if dg < 0 else 1), (0 if ds < 0 else 1)
            made.append((ds, dg, pltpu.make_async_remote_copy(
                src_ref=ctake.at[side, end], dst_ref=cland.at[side, 1 - end],
                send_sem=sends.at[4 + at], recv_sem=crecv.at[3 - at],
                device_id=(si + ds, gi + dg), device_id_type=MESH)))
        return made

    def corner_rows(side, end):
        dx1, dx2 = (0, 4) if end == 0 else (4, 0)
        dy1, dy2 = (0, 1) if side == 0 else (3, 2)
        return dx1 + dy1, dx1 + dy2, dx2 + dy1

    def any_row(places):
        found = sub == places[0]
        for place in places[1:]:
            found = jnp.logical_or(found, sub == place)
        return found

    corner_sets = ((0, 1, (3, 4)), (2, 6, (5,)))
    for side in range(2):
        for end in range(2):
            places = corner_rows(side, end)
            first_here, second_here = any_row(places), any_row([(v + 2) % 8 for v in places])
            for at, (ch_a, ch_b, right) in enumerate(corner_sets):
                tiles = [s1[side, ch, end * (X // 2 - 1)] for ch in (ch_a, ch_b) + right]
                tile = pltpu.roll(tiles[2], 5, 0)
                if len(right) == 2:
                    tile = jnp.where(sub == (places[0] + 5) % 8, tile, pltpu.roll(tiles[3], 3 if side else 7, 0))
                tile = jnp.where(first_here, tiles[0], jnp.where(second_here, pltpu.roll(tiles[1], 2, 0), tile))
                ctake[side, end, at] = tile
            near = [s2[side, c, end * (X // 2 - 1)] for c in range(3)]
            ftake[side, end] = jnp.where(sub == places[0], near[0], jnp.where(
                sub == (places[0] + 2) % 8, pltpu.roll(near[1], 2, 0), pltpu.roll(near[2], 4, 0)))

    def corner_unpack(made):
        for at, (ds, dg) in enumerate(steps[4:]):
            side, end = (0 if dg > 0 else 1), (1 if ds > 0 else 0)
            pair = HALO // 2 + X // 2 if ds > 0 else HALO // 2 - 1
            back = made[3 - at][2]

            @pl.when(inside(ds, dg))
            def _():
                back.wait_recv()
                for at, (ch_a, ch_b, right) in enumerate(corner_sets):
                    tile = cland[side, end, at]
                    h1[side, ch_a, pair] = tile
                    h1[side, ch_b, pair] = pltpu.roll(tile, 6, 0)
                    h1[side, right[0], pair] = pltpu.roll(tile, 3, 0)
                    if len(right) == 2:
                        h1[side, right[1], pair] = pltpu.roll(tile, 5 if side else 1, 0)

    corners = corner_copies()
    zeroth = copies(e1a, e1a, s1, h1, recv0, 6, 7, 4, REACH - 1)
    first = copies(e1a, e1a, s1, h1, recv1, 0, 3, 4, REACH - 1)
    rest = copies(e1a, e1a, s1, h1, recv1, 3, 6, 4, REACH - 1, None, ends)
    late = (copies(e1a, e1a, s1, h1, recv2, 0, 3, 2, 1, REACH),
            copies(e1a, e1a, s1, h1, recv2, 6, 7, 2, 1, REACH))
    second = copies(e2a, e2a, s2, h2, recv2, 0, 3, 4, REACH - 1)
    tips = tip_copies()
    third = copies(rqa, rqa, s3, h3, recv3, 0, 3, 4, 1, REACH)
    outer = copies(rqa, rqa, s3, h3, recv3, 3, 6, 2, REACH - 1, REACH)
    wedges = wedge_copies()
    meet(barrier, 1)
    begin(zeroth)
    begin(corners)
    begin(first)
    inner_ends()
    begin(rest)
    greet(known.at[0], rounds[0])
    blank(e1a, h1)
    blank(e2a, h2)
    blank(rqa, h3)
    for ch in range(6):
        for x in (HALO - REACH, HALO + X + REACH - 1):
            rqb[ch, x] = jnp.zeros((8, 128), jnp.float32)

    turn_out(rows[3], outb.at[3])
    inb[3, si] = outb[3, si]
    for at in range(len(rounds) - 2):
        meet(known.at[at], rounds[at])
        greet(known.at[at + 1], rounds[at + 1])
    finish_recv(recv0, REACH - 1, X // 2)
    corner_unpack(corners)
    meet(known.at[len(rounds) - 2], rounds[-2])
    greet(known.at[len(rounds) - 1], rounds[-1])
    begin(second)
    begin(tips)
    for made in late:
        begin(made)

    def open0(i, _):
        e1b[6, 2 * i], e1b[6, 2 * i + 1] = unpack(h1, 6, i)
        return 0

    def open1(i, _):
        for ch in range(6):
            e1b[ch, 2 * i], e1b[ch, 2 * i + 1] = unpack(h1, ch, i)
        return 0

    lax.fori_loop(0, (X + 2 * HALO) // 2, open0, 0)

    def link(w, other):
        return jnp.where(jnp.minimum(w, other) > 0.0, (0.5 * SPRING_SHEAR) * (w + other), 0.0)


    def over_rows(low, high, width, body, carried=0):
        width = max(v for v in range(1, width + 1) if (high - low) % v == 0)

        def chunk(i, state):
            return body([low + i * width + o for o in range(width)], state)

        return lax.fori_loop(0, (high - low) // width, chunk, carried)

    def all_coefficients(rows_here, _):
        for x in rows_here:
            coefficients(x)
        return 0

    def coefficients(x):
        wa, wb = e1a[6, x], e1b[6, x]
        ya, yb = up_y(wa, wb)
        da, db = down_y(wa, wb)
        for w, wu, wd, yu, yd, dg, kc in (
            (wa, e1a[6, x + 1], e1a[6, x - 1], ya, da, dga, kca),
            (wb, e1b[6, x + 1], e1b[6, x - 1], yb, db, dgb, kcb),
        ):
            zu = jnp.where(not_last, up_z(w), 0.0)
            zd = jnp.where(not_first, down_z(w), 0.0)
            kc[0, x] = link(w, wu)
            kc[1, x] = link(w, yu)
            kc[2, x] = link(w, yd)
            kc[3, x] = link(w, zu)
            kc[4, x] = link(w, zd)
            sx = w + 0.5 * (wu + wd)
            sy = w + 0.5 * (yu + yd)
            sz = w + 0.5 * (zu + zd)
            every = MASS_TERM + SPRING_SHEAR * (sx + sy + sz)
            dg[0, x] = every + SHEAR_REST * sx
            dg[1, x] = every + SHEAR_REST * sy
            dg[2, x] = every + SHEAR_REST * sz

    def edge_link(x):
        kca[0, x] = link(e1a[6, x], e1a[6, x + 1])
        kcb[0, x] = link(e1b[6, x], e1b[6, x + 1])

    edge_link(HALO - 2)
    over_rows(HALO - 1, HALO + X + 1, WIDE_K, all_coefficients)
    finish_recv(recv1, 6 * (REACH - 1), 3 * X)
    lax.fori_loop(0, (X + 2 * HALO) // 2, open1, 0)

    def operate(x, va, vb, base, chosen=slice(0, 2)):
        result = []
        coef = [[kc[j, x] for j in range(5)] + [kc[0, x - 1]] for kc in (kca, kcb)]
        for c in range(3):
            a, b = va[base + c, x], vb[base + c, x]
            ua, ub = up_y(a, b)
            la, lb = down_y(a, b)
            pair = []
            halves = ((a, va, ua, la, coef[0], dga), (b, vb, ub, lb, coef[1], dgb))
            for v, ref, u, l, k, dg in halves[chosen]:
                parts = (
                    k[0] * ref[base + c, x + 1] + k[5] * ref[base + c, x - 1],
                    k[1] * u + k[2] * l,
                    k[3] * up_z(v) + k[4] * down_z(v),
                )
                shear = parts[(c + 1) % 3] + parts[(c + 2) % 3]
                pair.append(dg[c, x] * v - (shear + (SPRING_NORMAL / SPRING_SHEAR) * parts[c]))
            result.append(pair)
        return result

    only_a, only_b = slice(0, 1), slice(1, 2)

    def residual(rows_here, _):
        for x in rows_here:
            image = operate(x, e1a, e1b, 0)
            for c in range(3):
                rqa[c, x] = e1a[3 + c, x] - image[c][0]
                rqb[c, x] = e1b[3 + c, x] - image[c][1]
        return 0

    def solve(step, ship_halo=None):
        def put(x, image):
            for c in range(3):
                rqa[3 + c, x] = image[c][0]
                rqb[3 + c, x] = image[c][1]

        def apply(rows_here, sums):
            rr, rq = sums
            for x in rows_here:
                image = operate(x, rqa, rqb, 0)
                for c in range(3):
                    r = rqa[c, x]
                    rr, rq = rr + r * r, rq + r * image[c][0]
                put(x, image)
            return rr, rq

        zero = jnp.zeros((8, 128), jnp.float32)
        images = [operate(x, rqa, rqb, 0) for x in (HALO - 1, HALO + X)]
        put(HALO - 1, images[0])
        put(HALO + X, images[1])
        rr, rq = over_rows(HALO, HALO + X, WIDE_A, apply, (zero, zero))
        if ship_halo is not None:
            ship_halo()
        rr, rq = total(rr), total(rq)
        mu = jnp.where(rr > 0.0, rq / jnp.where(rr > 0.0, rr, 1.0), 0.0)

        def centred(rows_here, sums):
            ww, wr, mix, wt = sums
            for x in rows_here:
                image = operate(x, rqa, rqb, 3, only_a)
                for c in range(3):
                    r, q, s = rqa[c, x], rqa[3 + c, x], image[c][0]
                    if step == 0:
                        sa[c, x] = s
                    w, t = q - mu * r, s - mu * q
                    ww, wr, mix, wt = ww + w * w, wr + w * r, mix + (r * t + w * q), wt + w * t
            return ww, wr, mix, wt

        sums = over_rows(HALO, HALO + X, WIDE_C, centred, (zero,) * 4)
        ww, wr, mix, wt = [total(v) for v in sums]
        one = lax.broadcasted_iota(jnp.int32, (1, 128), 1)
        row = jnp.zeros((1, 128), jnp.float32)
        for at, value in enumerate((rr, rq, mu, ww, wr, mix, wt)):
            row = jnp.where(one == at, value, row)
        gath[step, me] = row

        if step == 0:
            meet(known.at[len(rounds) - 1], rounds[-1])
        for other in others:
            pltpu.make_async_remote_copy(
                src_ref=gath.at[step, me], dst_ref=gath.at[step, me], send_sem=asend, recv_sem=arecv.at[step],
                device_id=other, device_id_type=MESH).start()

    def collect(step):
        block = gath.at[step, pl.ds(0, count - 1)]
        pltpu.make_async_copy(block, block, arecv.at[step]).wait()
        table = gath[step].reshape(count, 128)
        rr, rq, mu, ww, wr, mix, wt = [table[:, at:at + 1] for at in range(7)]

        def down(v):
            return jnp.sum(v, axis=0, keepdims=True)

        norm = down(rr)
        alpha = norm / down(rq)
        rest = 1.0 - alpha * mu
        after = down(alpha * alpha * ww - 2.0 * alpha * rest * wr + rest * rest * rr)
        curved = down(rest * rest * rq - alpha * rest * mix + alpha * alpha * wt)
        ratio = after / norm
        beta = after / (curved - ratio * after / alpha)
        return jnp.broadcast_to(alpha + beta * (1.0 + ratio), (8, 128)), jnp.broadcast_to(-beta * alpha, (8, 128))

    def drain():
        block = gath.at[:, pl.ds(0, count - 1)]
        pltpu.make_async_copy(block, block, asend).wait()

    def joined(c, x, near, far):
        r, q = rqa[c, x], rqa[3 + c, x]
        return jnp.where(sub == 3, pltpu.roll(r, near, 0), jnp.where(sub == 4, pltpu.roll(r, far, 0), q))

    def split(c, x, tile, row, near, far):
        r = rqb[c, x]
        rqb[c, x] = jnp.where(sub == row, pltpu.roll(tile, near, 0), jnp.where(sub == 7 - row, pltpu.roll(tile, far, 0), r))
        rqb[3 + c, x] = tile

    def ship_halo():
        def pack3(i, _):
            x = HALO + 2 * i
            for c in range(3):
                pack(s3, c, i, joined(c, x, 1, 7), joined(c, x + 1, 1, 7))
            return 0

        lax.fori_loop(0, X // 2, pack3, 0)
        for end, x in ((0, HALO), (1, HALO + X - 2)):
            for c in range(3):
                even, odd = [joined(c, x + o, 2, 6) if o == end else joined(c, x + o, 3, 5) for o in range(2)]
                k3[0, end, c, 0] = jnp.where(upper, even, pltpu.roll(odd, 4, 0))
                k3[1, end, c, 0] = jnp.where(upper, pltpu.roll(even, 4, 0), odd)
        begin(wedges)
        begin(outer)
        begin(third)

    outer_residual(HALO - 2)
    outer_residual(HALO + X + 1)
    over_rows(HALO - 1, HALO + X + 1, WIDE_R, residual)
    solve(0, ship_halo)
    finish_recv(recv2, 3 * (REACH - 1) + 4, 3 * X // 2)
    tip_unpack(tips)
    edge_link(HALO - REACH)
    coefficients(HALO - 2)
    coefficients(HALO + X + 1)

    def open2(i, _):
        for ch in range(3):
            e2b[ch, 2 * i], e2b[ch, 2 * i + 1] = unpack(h2, ch, i)
        return 0

    lax.fori_loop(0, (X + 2 * HALO) // 2, open2, 0)
    finish_recv(recv3, 3 + 3 * (REACH - 1), 3 * X // 2)
    for at, (ds, dg) in enumerate(steps[4:]):
        back = wedges[3 - at][2]

        @pl.when(inside(ds, dg))
        def _():
            back.wait_recv()

    def open3(i, _):
        for c in range(3):
            even, odd = unpack(h3, c, i)
            split(c, 2 * i, even, 2, 7, 1)
            split(c, 2 * i + 1, odd, 2, 7, 1)
        return 0

    lax.fori_loop(HALO // 2, (HALO + X) // 2, open3, 0)
    for pair, one in ((HALO // 2 - 1, 1), ((HALO + X) // 2, 0)):
        for c in range(3):
            for o, tile in enumerate(unpack(h3, c, pair)):
                if o == one:
                    split(c, 2 * pair + o, tile, 1, 6, 2)
                else:
                    split(c, 2 * pair + o, tile, 0, 5, 3)
    finish_send(13 * (REACH - 1) + 7, 13 * X // 2, 6)
    spread_out(outb.at[3], inb.at[3], 3)
    for x in range(HALO - 1, HALO + X + 1):
        image = operate(x, rqa, rqb, 3, only_b)
        for c in range(3):
            sb[c, x] = image[c][0]
            e2a[c, x] = MASS_TERM * e1a[c, x] + e2a[c, x] - e1a[3 + c, x] + rqa[c, x]
            e2b[c, x] = MASS_TERM * e1b[c, x] + e2b[c, x] - e1b[3 + c, x] + rqb[c, x]
    for x in (HALO - 2, HALO + X + 1):
        image = operate(x, e1a, e1b, 0, only_a)
        for c in range(3):
            e2a[c, x] = MASS_TERM * e1a[c, x] + e2a[c, x] - image[c][0]
    for x in (HALO - 2, HALO - 1, HALO + X, HALO + X + 1):
        image = operate(x, rqa, rqb, 3, only_a)
        for c in range(3):
            sa[c, x] = image[c][0]
    c0, c1 = collect(0)

    def step1(x, base, rq, g, s, u1, comps):
        for c in range(3):
            r, q = rq[c, x], rq[3 + c, x]
            grown = c0 * r + c1 * q
            if c in comps:
                u1[c, x] = base[c, x] + grown
            rq[c, x] = g[c, x] + (2.0 * MASS_TERM) * grown - (c0 * q + c1 * s[c, x])

    for x in range(HALO - 2, HALO + X + 2):
        own_row = HALO <= x < HALO + X
        step1(x, e1a, rqa, e2a, sa, u1a, (0, 1, 2) if own_row else ())
        if HALO - 1 <= x <= HALO + X:
            step1(x, e1b, rqb, e2b, sb, u1b, (1,) if own_row else ())

    def early(at, ref, ch):
        for x in range(X):
            rows[at, pl.ds(x, 8, stride=X), :] = ref[ch, HALO + x]
        turn_out(rows[at], outb.at[at])
        spread_out(outb.at[at], inb.at[at], at)
        inb[at, si] = outb[at, si]

    solve(1)
    early(2, u1a, 2)
    early(4, rqa, 2)
    early(5, rqa, 5)
    c0, c1 = collect(1)

    def step2(ra, rb, c, x):
        return ra[c, x] + (c0 * rb[c, x] + c1 * rb[3 + c, x])

    def halves(v):
        high = v.astype(jnp.bfloat16)
        return high, (v - high.astype(jnp.float32)).astype(jnp.bfloat16)

    def finish(c):
        for x in range(X):
            v = step2(u1a, rqa, c, HALO + x)
            disp_ref[c, x] = v
            rows[c, pl.ds(x, 8, stride=X), :] = v
        turned = turn_out(rows[c], outb.at[c])
        spread_out(outb.at[c], inb.at[c], c)
        inb[c, si] = outb[c, si]

    def joint(ref, j, low, high):
        return jnp.concatenate([
            ref[2, j, at:at + 8] + (c0 * ref[4, j, at:at + 8] + c1 * ref[5, j, at:at + 8])
            for at in range(low, high, 8)], axis=0)

    def finish_edges():
        for x in range(X):
            rows[6, pl.ds(x, 8, stride=X), :] = step2(u1b, rqb, 1, HALO + x)
        sides_y = rows[6].T
        zero = jnp.zeros((8, 128), jnp.float32)
        for j in range(ns):
            low, high = sides_y[zrows * j:zrows * j + 8], sides_y[zrows * j + 8:zrows * j + 16]
            tile = jnp.where(lane < 32, pltpu.roll(low, 16, 1),
                             jnp.where(lane < 64, pltpu.roll(pltpu.roll(low, 4, 0), 48, 1),
                                       jnp.where(lane < 96, pltpu.roll(high, 80, 1),
                                                 pltpu.roll(pltpu.roll(high, 4, 0), 112, 1))))
            before = pltpu.roll(joint(outb, j - 1, zrows - 8, zrows), 5, 0) if j else zero
            after = pltpu.roll(joint(outb, j + 1, 0, 8), 5, 0) if j + 1 < ns else zero
            outx[j] = jnp.where(sub == 4, before, jnp.where(sub == 5, after, tile))
        spread_out(outx.at[:, pl.ds(0, 6)], inx.at[:, pl.ds(0, 6)], 6)
        inx[si] = outx[si]

    finish(0)
    finish_edges()
    finish(1)
    for x in range(X):
        disp_ref[2, x] = step2(u1a, rqa, 2, HALO + x)
    fetched[7].wait()

    c1t, c3t = float(np.sqrt(0.5) * np.cos(np.pi / 8)), float(np.sqrt(0.5) * np.cos(3 * np.pi / 8))

    def cosine(v0, v1, v2, v3):
        s03, s12, d03, d12 = v0 + v3, v1 + v2, v0 - v3, v1 - v2
        return [0.5 * (s03 + s12), c1t * d03 + c3t * d12, 0.5 * (s03 - s12), c3t * d03 - c1t * d12]

    def encode(ch, fields):
        for b in range(Y // 4):
            for k, v in enumerate(cosine(*fields[4 * b:4 * b + 4])):
                work[ch, (4 * b + k) * zrows:(4 * b + k + 1) * zrows] = v
        parts = []
        for p in range(Y * zrows // 32):
            parts += cosine(*[work[ch, pl.ds(32 * p + n, 8, stride=4), :] for n in range(4)])
        high, low = halves(jnp.concatenate(parts, axis=0))
        done = jnp.dot(jnp.concatenate([high, low], axis=1), gt_ref[...], preferred_element_type=jnp.float32)
        done = done[:, 0:128] + done[:, 128:256]
        for p in range(Y * zrows // 32):
            for n in range(4):
                coef_ref[ch, pl.ds(32 * p + n, 8, stride=4), :] = done[(4 * p + n) * 8:(4 * p + n + 1) * 8]

    def arrived(c):
        landed(inb.at[c], trecv.at[c])
        return regroup([inb[c, j] for j in range(ns)])

    for at in (2, 4, 5):
        landed(inb.at[at], trecv.at[at])
    along = regroup([joint(inb, j, 0, zrows) for j in range(ns)])
    encode(2, along)
    landed(inb.at[3], trecv.at[3])
    for y, piece in enumerate(regroup([inb[3, j] for j in range(ns)])):
        scale[y] = piece
    field = arrived(0)
    encode(0, field)
    wide = lax.broadcasted_iota(jnp.int32, (zrows, 128), 1)
    encode(3, [scale[y] * (jnp.where(wide < 127, up_z(field[y]), 0.0) - jnp.where(wide > 0, down_z(field[y]), 0.0))
               for y in range(Y)])
    landed(inx.at[:, pl.ds(0, 6)], trecv.at[6])
    edges = regroup([inx[j] for j in range(ns)])
    stress = []
    for y in range(Y):
        low, high = along[y][0:8], along[y][8:16]
        ul, uh, dl, dh = pltpu.roll(low, 7, 0), pltpu.roll(high, 7, 0), pltpu.roll(low, 1, 0), pltpu.roll(high, 1, 0)
        first, last = sub == 0, sub == 7
        low = jnp.where(last, uh, ul) - jnp.where(first, pltpu.roll(edges[y], 4, 0), dl)
        high = jnp.where(last, pltpu.roll(edges[y], 2, 0), uh) - jnp.where(first, dl, dh)
        stress.append(scale[y] * jnp.concatenate([low, high], axis=0))
    encode(5, stress)
    field = arrived(1)
    encode(1, field)
    outside = []
    for side in range(2):
        quarter = [edges[2 * q + side] for q in range(4)]
        outside.append(jnp.concatenate([jnp.where(upper, quarter[q], pltpu.roll(quarter[q + 1], 4, 0)) for q in (0, 2)], axis=0))
    field = [outside[0]] + field + [outside[1]]
    encode(4, [scale[y] * (field[y + 2] - field[y]) for y in range(Y)])
    drain()
    block = inb.at[:, pl.ds(0, ns - 1)]
    pltpu.make_async_copy(block, block, tsend.at[0]).wait()
    landed(inx.at[:, pl.ds(0, 6)], tsend.at[1])


def store(disp_in, coef_in, disp_out, coef_out, sems):
    copies = [pltpu.make_async_copy(disp_in, disp_out, sems.at[0]), pltpu.make_async_copy(coef_in, coef_out, sems.at[1])]
    for copy in copies:
        copy.start()
    for copy in copies:
        copy.wait()


def fused(mesh, u_now, u_prev, force, stiffness, broken, flags):
    ns, ng = mesh.shape["slab"], mesh.shape["grp"]
    _, X, Y, Z = u_now.shape
    xe, pairs, half = X + 2 * HALO, X // 2 + HALO, X // 2
    zrows = Z // ns
    ez = jnp.asarray(np.kron(np.eye(Z // 4), np.ones((1, 4))), jnp.float32)
    gth, gtl = split_table(wavelet_table(X * ns).T)
    gt = jnp.asarray(np.block([[gth, gtl], [gth, np.zeros_like(gtl)]]), jnp.bfloat16)

    def vm(*shape):
        return pltpu.VMEM(shape, jnp.float32)

    def ext(n):
        return vm(n, xe, Y, Z)

    def stage(n):
        return vm(2, n, half, Y, Z)

    def land(n):
        return vm(2, n, pairs, Y, Z)

    dma = pltpu.SemaphoreType.DMA
    shapes = (u_now.shape, (6, Y * zrows, X * ns))
    operands = [pltpu.with_memory_space_constraint(v, pltpu.HBM)
                for v in (u_now, u_prev, force, stiffness, broken, flags, ez, gt)]
    results = pl.pallas_call(
        lambda *refs: kernel(ns, ng, *refs),
        name="lattice",
        out_shape=tuple(vm(*shape) for shape in shapes),
        in_specs=[pl.BlockSpec(memory_space=pltpu.MemorySpace.HBM)] * 8,
        out_specs=(pl.BlockSpec(memory_space=pltpu.VMEM),) * 2,
        scratch_shapes=[
            vm(*u_now.shape), vm(*u_now.shape), vm(*u_now.shape), vm(*stiffness.shape),
            pltpu.VMEM(broken.shape, broken.dtype), pltpu.VMEM(flags.shape, flags.dtype),
            vm(*ez.shape), pltpu.VMEM(gt.shape, gt.dtype), pltpu.SemaphoreType.DMA((6,)),
            ext(7), ext(7), stage(7), land(7),
            ext(3), ext(3), stage(3), land(3),
            ext(6), ext(6), stage(3), land(3), vm(2, 2, 3, 1, Y, Z), vm(2, 3, 2, Y, Z),
            ext(3), ext(3), ext(3), ext(3), vm(Y, zrows, X * ns), ext(3), ext(3), ext(5), ext(5),
            pltpu.SemaphoreType.REGULAR((3,)), vm(2, ns * ng, 1, 128), vm(7, Y * X, Z), vm(6, ns, zrows, 128), vm(6, ns, zrows, 128), vm(ns, 8, 128), vm(ns, 8, 128), vm(6, Y * zrows, X * ns),
            vm(max(9 * X, 13 * X // 2), Y, Z), dma((8,)), vm(2, 2, 2, Y, Z), vm(2, 2, 2, Y, Z), dma((4,)),
            dma((4,)), dma((4,)), dma((4,)), dma((4,)), dma((4,)), vm(2, 2, Y, Z), vm(2, 2, Y, Z), dma((4,)),
            dma, dma((2,)), dma((2,)), dma((7,)),
        ],
        compiler_params=pltpu.CompilerParams(collective_id=0, has_side_effects=True, vmem_limit_bytes=24 << 20),
    )(*operands)
    disp, coef = pl.pallas_call(
        store,
        name="store",
        out_shape=tuple(jax.ShapeDtypeStruct(shape, jnp.float32) for shape in shapes),
        in_specs=[pl.BlockSpec(memory_space=pltpu.VMEM)] * 2,
        out_specs=(pl.BlockSpec(memory_space=pltpu.MemorySpace.HBM),) * 2,
        scratch_shapes=[dma((2,))],
        compiler_params=pltpu.CompilerParams(vmem_limit_bytes=1 << 20),
    )(*[pltpu.with_memory_space_constraint(v, pltpu.VMEM) for v in results])
    return disp, coef.reshape(6, Y, zrows, X * ns)


def fits(mesh, shape):
    ns, ng = mesh.shape["slab"], mesh.shape["grp"]
    x, y, z = shape[1] // ns, shape[2] // ng, shape[3]
    return y == 8 and z == 128 and x * y == 128 and x * ns == 128 and z % (8 * ns) == 0


def entry(mesh, *args):
    ns, ng = mesh.shape["slab"], mesh.shape["grp"]
    _, x, y, z = args[0].shape
    if fits(mesh, (3, x * ns, y * ng, z)):
        return fused(mesh, *args)
    return body(*args)


def solution(mesh):
    return jax.shard_map(
        lambda *args: entry(mesh, *args),
        mesh=mesh,
        in_specs=(
            P(None, "slab", "grp", None),
            P(None, "slab", "grp", None),
            P(None, "slab", "grp", None),
            P("slab", "grp", None),
            P("slab", "grp", None),
            P("slab", "grp", None),
        ),
        out_specs=(P(None, "slab", "grp", None), P(None, "grp", "slab", None)),
        check_vma=False,
    )
```
